32 devices in a mesh: dp: 16 (over z, x, core), tensor: 2 (over y).
Axes of the slice: x: 2, y: 2, z: 4, core: 2. Of those that a mesh axis runs over, the one named last changes fastest.
Arguments:
- tokens: bfloat16 [16, 1024, 768], P('dp'), may hold values from -6 to 6
- lengths: int32 [16], P('dp'), may hold values from 256 to 1024, as said below
- entity_flags: int32 [16, 1024], P('dp'), may hold values 0 or 1
- query_weight: bfloat16 [4, 768, 768], P(None, None, 'tensor'), may hold values from -0.21875 to 0.21875
- query_bias: float32 [4, 768], P(None, 'tensor'), may hold values from -3 to 3
- key_weight: bfloat16 [768, 768], P(None, 'tensor'), may hold values from -0.21875 to 0.21875
- key_bias: float32 [768], P('tensor'), may hold values from -3 to 3
- value_weight: bfloat16 [768, 768], P(None, 'tensor'), may hold values from -0.21875 to 0.21875
- value_bias: float32 [768], P('tensor'), may hold values from -3 to 3
- output_weight: bfloat16 [768, 768], P('tensor'), may hold values from -1.75 to 1.75
- output_bias: float32 [768], replicated, may hold values from -3 to 3
- attn_gain: float32 [768], replicated, may hold values from 0.1 to 1.9
- attn_shift: float32 [768], replicated, may hold values from -3 to 3
- inner_weight: bfloat16 [768, 3072], P(None, 'tensor'), may hold values from -0.21875 to 0.21875
- inner_bias: float32 [3072], P('tensor'), may hold values from -3 to 3
- outer_weight: bfloat16 [3072, 768], P('tensor'), may hold values from -0.109375 to 0.109375
- outer_bias: float32 [768], replicated, may hold values from -3 to 3
- final_gain: float32 [768], replicated, may hold values from 0.1 to 1.9
- final_shift: float32 [768], replicated, may hold values from -3 to 3
- cotangent: bfloat16 [16, 1024, 768], P('dp'), may hold values from -6 to 6
Outputs:
- layer_out: bfloat16 [16, 1024, 768], P('dp')
- input_grad: bfloat16 [16, 1024, 768], P('dp')
- grad_query_weight: float32 [4, 768, 768], P(None, 'dp', 'tensor')
- grad_query_bias: float32 [4, 768], P(None, ('tensor', 'dp'))
- grad_key_weight: float32 [768, 768], P('dp', 'tensor')
- grad_key_bias: float32 [768], P(('tensor', 'dp'))
- grad_value_weight: float32 [768, 768], P('dp', 'tensor')
- grad_value_bias: float32 [768], P(('tensor', 'dp'))
- grad_output_weight: float32 [768, 768], P('tensor', 'dp')
- grad_output_bias: float32 [768], P('dp')
- grad_attn_gain: float32 [768], P('dp')
- grad_attn_shift: float32 [768], P('dp')
- grad_inner_weight: float32 [768, 3072], P('dp', 'tensor')
- grad_inner_bias: float32 [3072], P(('tensor', 'dp'))
- grad_outer_weight: float32 [3072, 768], P('tensor', 'dp')
- grad_outer_bias: float32 [768], P('dp')
- grad_final_gain: float32 [768], P('dp')
- grad_final_shift: float32 [768], P('dp')
The draws below stay inside these ranges and needn't reach their ends.
Inputs may be any that keep to these rules, and one draw needn't show every extreme that they name: `lengths`: each sequence's number of valid leading slots; some sequence has all 1024.
All inputs are finite; a program needn't handle non-finite values. No bound on the sum of `entity_flags` on one device may be relied on, other than what follows from the above.
Results may differ from the reference program's by a relative error of at most 0.019.
Values sent between devices are 32-bit elements; how exact they have to be, the bound alone decides.
No kernel may reach another device: no remote copies, remote signals or barrier semaphores. Data moves between devices by JAX's collectives and lax.ppermute only.
A program may use at most 192 MiB of HBM per device.

```python
import math
import jax
import jax.numpy as jnp
from jax import lax

D = 768
HEADS = 12
HD = 64
FF = 3072
LEN = 1024
SEQS = 16


def draw_lengths(key, part):
    draw_key, place_key = jax.random.split(jax.random.fold_in(key, 7))
    sampled = jax.random.randint(draw_key, (SEQS,), LEN // 4, LEN + 1, dtype=jnp.int32)
    full_at = jax.random.randint(place_key, (), 0, SEQS, dtype=jnp.int32)
    indices = jnp.arange(SEQS, dtype=jnp.int32)
    return jnp.where(indices == full_at, jnp.int32(LEN), sampled).astype(jnp.int32)


def touch_ends(array, stream_key, smallest, high):
    index_at = [jax.random.randint(jax.random.fold_in(stream_key, axis), (), 0, length) for axis, length in enumerate(array.shape)]
    widest = array.shape.index(max(array.shape))
    neighbour = index_at[:widest] + [(index_at[widest] + 1) % array.shape[widest]] + index_at[widest + 1:]
    return array.at[tuple(index_at)].set(smallest).at[tuple(neighbour)].set(high)


def with_spikes(entries, key, source, target, parts, factor):
    def block_of(position):
        return (jnp.arange(entries.shape[position]) // (entries.shape[position] // parts)).reshape((-1,) + (1,) * (entries.ndim - 1 - position))

    near = jax.random.permutation(key, parts)[block_of(target)]
    second = (block_of(target) + parts // 2) % parts
    return jnp.where((block_of(source) == near) | (block_of(source) == second), factor * entries, entries)


def block_levels(own_key, shape, shards, low, high):
    gain, own = 1.0, jax.random.fold_in(own_key, 6)
    for position, parts in shards:
        heights = jnp.exp(jax.random.uniform(jax.random.fold_in(own, position), (parts,), jnp.float32, low / len(shards), high / len(shards)))
        gain = gain * jnp.repeat(heights, shape[position] // parts).reshape([-1 if axis == position else 1 for axis in range(len(shape))])
    return gain


def scatter_about(rng, shape, scale, most, pieces=(), kind=jnp.bfloat16):
    array = scale * jax.random.normal(rng, shape, jnp.float32)
    if pieces:
        array = array * block_levels(rng, shape, pieces, -0.22, 0.18)
    return jnp.clip(array, -most, most).astype(kind)


def gaussian_with(rng, shape, scale, most, cuts, heavy, held_as=jnp.bfloat16):
    values = scale * jax.random.normal(rng, shape, jnp.float32)
    if cuts:
        values = values * block_levels(rng, shape, cuts, -0.22, 0.18)
    return jnp.clip(with_spikes(values, jax.random.fold_in(rng, 3), *heavy), -most, most).astype(held_as)


def setup_inputs(seed: int = 0) -> dict:
    seeds = jax.random.split(jax.random.key(seed), 21)
    tokens = gaussian_with(seeds[0], (SEQS, LEN, D), 1.0, 6.0, ((0, 16),), (0, 2, 16, 2.0))
    lengths = draw_lengths(jax.random.fold_in(seeds[20], 71), 0)
    entity_flags = touch_ends((jax.random.randint(seeds[2], (SEQS, LEN), 0, 4) < 1).astype(jnp.int32), jax.random.fold_in(seeds[2], 1), 0, 1)
    query_weight = scatter_about(seeds[3], (4, D, D), D ** -0.5, 0.21875, ((2, 2),))
    query_bias = scatter_about(seeds[4], (4, D), 0.5, 3.0, ((1, 2),), jnp.float32)
    key_weight = scatter_about(seeds[5], (D, D), D ** -0.5, 0.21875, ((1, 2),))
    key_bias = scatter_about(seeds[6], (D,), 0.5, 3.0, ((0, 2),), jnp.float32)
    value_weight = scatter_about(seeds[7], (D, D), D ** -0.5, 0.21875, ((1, 2),))
    value_bias = scatter_about(seeds[8], (D,), 0.5, 3.0, ((0, 2),), jnp.float32)
    output_weight = scatter_about(seeds[9], (D, D), (D * 16 // LEN) ** -0.5, 1.75, ((0, 2),))
    output_bias = scatter_about(seeds[10], (D,), 0.5, 3.0, (), jnp.float32)
    attn_gain = jnp.clip(1.0 + 0.18 * jax.random.normal(seeds[11], (D,), jnp.float32), 0.1, 1.9)
    attn_shift = scatter_about(seeds[12], (D,), 0.5, 3.0, (), jnp.float32)
    inner_weight = scatter_about(seeds[13], (D, FF), D ** -0.5, 0.21875, ((1, 2),))
    inner_bias = scatter_about(seeds[14], (FF,), 0.5, 3.0, ((0, 2),), jnp.float32)
    outer_weight = scatter_about(seeds[15], (FF, D), FF ** -0.5, 0.109375, ((0, 2),))
    outer_bias = scatter_about(seeds[16], (D,), 0.5, 3.0, (), jnp.float32)
    final_gain = jnp.clip(1.0 + 0.18 * jax.random.normal(seeds[17], (D,), jnp.float32), 0.1, 1.9)
    final_shift = scatter_about(seeds[18], (D,), 0.5, 3.0, (), jnp.float32)
    cotangent = gaussian_with(seeds[19], (SEQS, LEN, D), 1.0, 6.0, ((0, 16),), (0, 2, 16, 2.0))
    return dict(tokens=tokens, lengths=lengths, entity_flags=entity_flags, query_weight=query_weight, query_bias=query_bias, key_weight=key_weight, key_bias=key_bias, value_weight=value_weight, value_bias=value_bias, output_weight=output_weight, output_bias=output_bias, attn_gain=attn_gain, attn_shift=attn_shift, inner_weight=inner_weight, inner_bias=inner_bias, outer_weight=outer_weight, outer_bias=outer_bias, final_gain=final_gain, final_shift=final_shift, cotangent=cotangent)


@jax.custom_vjp
def low(v):
    return lax.optimization_barrier(v.astype(jnp.bfloat16)).astype(jnp.float32)

@jax.custom_vjp
def low_back(v):
    return v

def low_keep(v):
    return (low(v), None)

def low_pass(kept, grad):
    return (grad,)

def back_keep(v):
    return (v, None)

def back_low(kept, grad):
    return (low(grad),)
low.defvjp(low_keep, low_pass)
low_back.defvjp(back_keep, back_low)
highest = lax.Precision.HIGHEST
norm_eps = 1e-05

def layer_norm(values, scaling, offset):
    centre = values - lax.optimization_barrier(jnp.mean(values, axis=-1, keepdims=True))
    spread = lax.optimization_barrier(jnp.mean(centre * centre, axis=-1, keepdims=True))
    return centre * lax.rsqrt(spread + norm_eps) * scaling + offset

def gelu_exact(values):
    return 0.5 * values * (1.0 + jax.scipy.special.erf(values * (1.0 / math.sqrt(2.0))))

def attention(to_word, to_entity, key_rows, value_rows, live_slot, entity_key):
    block_rows = min(512, LEN)
    block_count = LEN // block_rows
    heads_word = to_word.reshape(block_count, block_rows, HEADS, HD)
    heads_entity = to_entity.reshape(block_count, block_rows, HEADS, HD)
    keys_heads = key_rows.reshape(LEN, HEADS, HD)
    values_heads = value_rows.reshape(LEN, HEADS, HD)
    score_scale = 1.0 / math.sqrt(HD)

    def one_block(operands):
        word_block, entity_block = operands
        word_scores = jnp.einsum('qhe,khe->hqk', word_block, keys_heads, precision=highest)
        entity_scores = jnp.einsum('qhe,khe->hqk', entity_block, keys_heads, precision=highest)
        selected = jnp.where(entity_key[None, None, :], entity_scores, word_scores)
        scaled = low_back(selected) * score_scale
        masked = jnp.where(live_slot[None, None, :], scaled, -jnp.inf)
        row_max = lax.optimization_barrier(jnp.max(masked, axis=-1, keepdims=True))
        weights = jnp.exp(masked - row_max)
        attn_probs = weights / lax.optimization_barrier(jnp.sum(weights, axis=-1, keepdims=True))
        return jnp.einsum('hqk,khe->qhe', low(attn_probs), values_heads, precision=highest)
    context = lax.map(jax.checkpoint(one_block), (heads_word, heads_entity))
    return context.reshape(LEN, HEADS * HD)

def block_forward(params, tokens_one, live_slot, flags_one):
    query_weight, query_bias, key_weight, key_bias, value_weight, value_bias, output_weight, output_bias, attn_gain, attn_shift, inner_weight, inner_bias, outer_weight, outer_bias, final_gain, final_shift = params
    queries = low_back(low(jnp.einsum('ld,cde->cle', tokens_one, query_weight, precision=highest) + query_bias[:, None, :]))
    key_rows = low_back(low(jnp.dot(tokens_one, key_weight, precision=highest) + key_bias))
    value_rows = low_back(low(jnp.dot(tokens_one, value_weight, precision=highest) + value_bias))
    entity_key = flags_one == 1
    entity_row = entity_key[:, None]
    to_word = jnp.where(entity_row, queries[2], queries[0])
    to_entity = jnp.where(entity_row, queries[3], queries[1])
    context = low_back(low(attention(to_word, to_entity, key_rows, value_rows, live_slot, entity_key)))
    attn_out = jnp.dot(context, output_weight, precision=highest)
    first_sum = low_back(attn_out) + output_bias + tokens_one
    normed = layer_norm(first_sum, attn_gain, attn_shift)
    inner_pre = low_back(jnp.dot(low(normed), inner_weight, precision=highest) + inner_bias)
    hidden = low(gelu_exact(inner_pre))
    ffn_out = jnp.dot(hidden, outer_weight, precision=highest)
    second_sum = low_back(ffn_out) + outer_bias + normed
    result = layer_norm(second_sum, final_gain, final_shift)
    return jnp.where(live_slot[:, None], result, 0.0)

def add_pair(running, update):
    return running + update

def reference(tokens, lengths, entity_flags, query_weight, query_bias, key_weight, key_bias, value_weight, value_bias, output_weight, output_bias, attn_gain, attn_shift, inner_weight, inner_bias, outer_weight, outer_bias, final_gain, final_shift, cotangent):
    params = tuple((item.astype(jnp.float32) for item in (query_weight, query_bias, key_weight, key_bias, value_weight, value_bias, output_weight, output_bias, attn_gain, attn_shift, inner_weight, inner_bias, outer_weight, outer_bias, final_gain, final_shift)))
    positions = jnp.arange(LEN, dtype=jnp.int32)

    def one_sequence(totals, inputs):
        tokens_one, length_one, flags_one, cot_one = inputs
        live_slot = positions < length_one

        def forward(params_in, tokens_in):
            return block_forward(params_in, tokens_in, live_slot, flags_one)
        result, pullback = jax.vjp(forward, params, tokens_one.astype(jnp.float32))
        grads, token_grad = pullback(cot_one.astype(jnp.float32))
        totals = jax.tree.map(add_pair, totals, grads)
        return (totals, (result.astype(jnp.bfloat16), token_grad.astype(jnp.bfloat16)))
    start = jax.tree.map(jnp.zeros_like, params)
    totals, (layer_out, input_grad) = lax.scan(one_sequence, start, (tokens, lengths, entity_flags, cotangent))
    return (layer_out, input_grad, totals[0], totals[1], totals[2], totals[3], totals[4], totals[5], totals[6], totals[7], totals[8], totals[9], totals[10], totals[11], totals[12], totals[13], totals[14], totals[15])
```

```python
import functools
import math

import jax
import jax.numpy as jnp
from jax import lax
from jax.experimental import pallas as pl
from jax.experimental.pallas import tpu as pltpu
from jax.sharding import PartitionSpec as P

HD = 64
SLICES = 8
MASKED = -1e30
NORM_EPS = 1e-05

F32 = jnp.float32
BF16 = jnp.bfloat16
NN = (((1,), (0,)), ((), ()))
NT = (((1,), (1,)), ((), ()))
TN = (((0,), (0,)), ((), ()))


def mm(left, right, dims):
    return lax.dot_general(left, right, dims, preferred_element_type=F32)


def struct(shape, kind):
    return jax.ShapeDtypeStruct(shape, kind)


def params(mib):
    return pltpu.CompilerParams(vmem_limit_bytes=mib << 20)


def cost(flops, moved, special=0):
    return pl.CostEstimate(flops=int(flops), bytes_accessed=int(moved), transcendentals=int(special))


def whole_block(shape):
    return pl.BlockSpec(shape, lambda *_: (0,) * len(shape), pipeline_mode=pl.Buffered(1))


def three_pieces(value):
    high = value.astype(BF16).astype(F32)
    rest = value - high
    middle = rest.astype(BF16).astype(F32)
    return high, middle, rest - middle


def project_kernel(x_ref, kind_ref, wq_ref, bq_ref, wk_ref, bk_ref, wv_ref, bv_ref, q2_ref, k2_ref, v_ref):
    x = x_ref[...]
    entity = kind_ref[...] > 0.5
    rows = x.shape[0]
    width = wk_ref.shape[1]

    def query(c):
        return mm(x, wq_ref[c], NN) + bq_ref[c : c + 1, :]

    scale = 1.0 / math.sqrt(HD)
    to_word = jnp.where(entity, query(2), query(0)).astype(BF16).astype(F32) * scale
    to_entity = jnp.where(entity, query(3), query(1)).astype(BF16).astype(F32) * scale
    keys = (mm(x, wk_ref[...], NN) + bk_ref[...]).astype(BF16).astype(F32)
    v_ref[...] = (mm(x, wv_ref[...], NN) + bv_ref[...]).astype(BF16)
    left = lax.broadcasted_iota(jnp.int32, (rows, 2 * HD), 1) < HD
    held = left != entity
    for p in range(width // (2 * HD)):
        cols = slice(2 * HD * p, 2 * HD * (p + 1))
        w, e, k = to_word[:, cols], to_entity[:, cols], keys[:, cols]
        w_roll, e_roll, k_roll = (pltpu.roll(t, HD, 1) for t in (w, e, k))
        even = slice(4 * HD * p, 4 * HD * p + 2 * HD)
        odd = slice(4 * HD * p + 2 * HD, 4 * HD * (p + 1))
        q2_ref[:, even] = jnp.where(left, w, e_roll).astype(BF16)
        q2_ref[:, odd] = jnp.where(left, w_roll, e).astype(BF16)
        k2_ref[:, even] = jnp.where(held, jnp.where(left, k, k_roll), 0.0).astype(BF16)
        k2_ref[:, odd] = jnp.where(held, jnp.where(left, k_roll, k), 0.0).astype(BF16)


def project(x, kind, wq, bq, wk, bk, wv, bv, rows=256):
    length, model = x.shape
    width = wk.shape[1]
    rows = min(rows, length)
    tile = lambda w: pl.BlockSpec((rows, w), lambda i: (i, 0))
    return pl.pallas_call(
        project_kernel,
        grid=(length // rows,),
        in_specs=[
            tile(model),
            tile(1),
            whole_block(wq.shape),
            whole_block(bq.shape),
            whole_block(wk.shape),
            whole_block((1, width)),
            whole_block(wv.shape),
            whole_block((1, width)),
        ],
        out_specs=[tile(2 * width), tile(2 * width), tile(width)],
        out_shape=[
            struct((length, 2 * width), BF16),
            struct((length, 2 * width), BF16),
            struct((length, width), BF16),
        ],
        compiler_params=params(48),
        cost_estimate=cost(12 * length * model * width, 16 * model * width + 12 * length * width),
        name="project",
    )(x, kind, wq, bq, wk, bk.reshape(1, width), wv, bv.reshape(1, width))


def key_extra(live, rows):
    lane = lax.broadcasted_iota(jnp.int32, (rows, 2 * HD), 1)
    return jnp.where(
        lane == 0, jnp.where(live, 0.0, MASKED), jnp.where(lane < 4, 1.0, 0.0)
    ).astype(BF16)


def attend_kernel(block, q2_ref, k2_ref, v_ref, live_ref, out_ref, extra_ref):
    length = k2_ref.shape[0]
    total = q2_ref.shape[0]
    extra = key_extra(live_ref[...] > 0.5, length)
    turned = v_ref[...].astype(F32).T.astype(BF16)
    lane = lax.broadcasted_iota(jnp.int32, (block, 2 * HD), 1)
    one = jnp.where(lane == 0, 1.0, 0.0).astype(BF16)
    keys = [
        jnp.concatenate([k2_ref[:, 2 * HD * h : 2 * HD * (h + 1)], extra], axis=1) for h in range(2)
    ]
    for i in range(total // block):
        rows = slice(i * block, (i + 1) * block)
        outs = []
        for h in range(2):
            cols = slice(2 * HD * h, 2 * HD * (h + 1))
            query = jnp.concatenate([q2_ref[rows, cols], one], axis=1)
            scores = mm(keys[h], query, NT)
            top = jnp.max(scores, axis=0, keepdims=True)
            weights = jnp.exp(scores - top)
            norm = jnp.sum(weights, axis=0, keepdims=True)
            summed = mm(turned[HD * h : HD * (h + 1)], weights.astype(BF16), NN)
            outs.append(summed * (1.0 / norm))
            pieces = three_pieces(-(top + jnp.log(norm)))
            filled = jnp.concatenate(
                [jnp.ones((1, block), F32), *pieces, jnp.zeros((2 * HD - 4, block), F32)], axis=0
            )
            extra_ref[rows, cols] = filled.T.astype(BF16)
        out_ref[rows, :] = jnp.concatenate(outs, axis=0).T.astype(BF16)


def attend(q2, k2, v, live, block=1024):
    length, width = v.shape
    block = min(block, length)
    pair = lambda w: pl.BlockSpec((length, w), lambda p: (0, p))
    return pl.pallas_call(
        functools.partial(attend_kernel, block),
        grid=(width // (2 * HD),),
        in_specs=[pair(4 * HD), pair(4 * HD), pair(2 * HD), whole_block((length, 1))],
        out_specs=[pair(2 * HD), pair(4 * HD)],
        out_shape=[struct((length, width), BF16), struct((length, 2 * width), BF16)],
        compiler_params=params(56),
        cost_estimate=cost(10 * length * length * width, 20 * length * width, length * length * width // HD),
        name="attend",
    )(q2, k2, v, live)


def attend_back_kernel(
    block, y_ref, q2_ref, extra_ref, k2_ref, v_ref, o_ref, own_ref, got_ref, live_ref, kind_ref,
    grad_ref, sums_ref, dk_ref, dv_ref, dq_ref,
):
    length = k2_ref.shape[0]
    half = own_ref.shape[0]
    first = y_ref[0] == 0
    own, got = own_ref[...], got_ref[...]
    d_context = jnp.concatenate([jnp.where(first, own, got), jnp.where(first, got, own)], axis=0)
    product = d_context * o_ref[...].astype(F32)
    d_context = d_context.astype(BF16)
    lane = lax.broadcasted_iota(jnp.int32, (length, 2 * HD), 1)
    left = lane < HD
    lane_keys = lax.broadcasted_iota(jnp.int32, (block, 2 * HD), 1)
    for h in range(2):
        mine = left if h == 0 else jnp.logical_not(left)
        delta = jnp.sum(jnp.where(mine, product, 0.0), axis=1, keepdims=True)
        high, middle, low = three_pieces(-delta)
        base = HD * (1 - h)
        pieces = jnp.where(
            lane == base, high, jnp.where(lane == base + 1, middle, jnp.where(lane == base + 2, low, 0.0))
        ).astype(BF16)
        d_wide = jnp.where(mine, d_context, pieces)
        cols = slice(2 * HD * h, 2 * HD * (h + 1))
        q2 = q2_ref[:, cols]
        query = jnp.concatenate([q2, extra_ref[:, cols]], axis=1)
        dq = None
        for j in range(length // block):
            rows = slice(j * block, (j + 1) * block)
            k2 = k2_ref[rows, cols]
            keys = jnp.concatenate([k2, key_extra(live_ref[rows, :] > 0.5, block)], axis=1)
            probs = jnp.exp(mm(keys, query, NT))
            own_keys = (lane_keys < HD) if h == 0 else (lane_keys >= HD)
            ones = jnp.where((lane_keys >= base) & (lane_keys < base + 3), 1.0, 0.0).astype(BF16)
            d_probs = mm(jnp.where(own_keys, v_ref[rows, :], ones), d_wide, NT)
            d_scores = (probs * d_probs).astype(BF16)
            dv_ref[h, rows, :] = mm(probs.astype(BF16), d_context, NN)
            dk_ref[h, rows, :] = mm(d_scores, q2, NN)
            part = mm(k2, d_scores, TN)
            dq = part if dq is None else dq + part
        dq_ref[h] = dq.T * (1.0 / math.sqrt(HD))
    entity = kind_ref[...] > 0.5
    even, odd = dq_ref[0], dq_ref[1]
    to_word = jnp.where(left, even, pltpu.roll(odd, HD, 1)).astype(BF16).astype(F32)
    to_entity = jnp.where(left, pltpu.roll(even, HD, 1), odd).astype(BF16).astype(F32)
    even, odd = dk_ref[0], dk_ref[1]
    even = jnp.where(entity, pltpu.roll(even, HD, 1), even)
    odd = jnp.where(entity, odd, pltpu.roll(odd, HD, 1))
    grads = [
        jnp.where(entity, 0.0, to_word),
        jnp.where(entity, 0.0, to_entity),
        jnp.where(entity, to_word, 0.0),
        jnp.where(entity, to_entity, 0.0),
        jnp.where(left, even, odd).astype(BF16).astype(F32),
        jnp.where(left, dv_ref[0], dv_ref[1]).astype(BF16).astype(F32),
    ]
    for c, grad in enumerate(grads):
        grad_ref[c] = grad.astype(BF16)
    sums = [jnp.sum(grad, axis=0, keepdims=True) for grad in grads]
    sums_ref[...] = jnp.concatenate([*sums, jnp.zeros((2, 2 * HD), F32)], axis=0)


def attend_back(y, q2, extra, k2, v, o, own, got, live, kind, block=1024):
    length, width = v.shape
    half = own.shape[0]
    block = min(block, length)
    pair = lambda w: pl.BlockSpec((length, w), lambda p, *_: (0, p))
    part = pl.BlockSpec((half, 2 * HD), lambda p, *_: (0, p))
    return pl.pallas_call(
        functools.partial(attend_back_kernel, block),
        grid_spec=pltpu.PrefetchScalarGridSpec(
            num_scalar_prefetch=1,
            grid=(width // (2 * HD),),
            in_specs=[
                pair(4 * HD), pair(4 * HD), pair(4 * HD), pair(2 * HD), pair(2 * HD),
                part, part, whole_block((length, 1)), whole_block((length, 1)),
            ],
            out_specs=[
                pl.BlockSpec((6, length, 2 * HD), lambda p, *_: (0, 0, p)),
                pl.BlockSpec((8, 2 * HD), lambda p, *_: (0, p)),
            ],
            scratch_shapes=[pltpu.VMEM((2, length, 2 * HD), F32)] * 3,
        ),
        out_shape=[struct((6, length, width), BF16), struct((8, width), F32)],
        compiler_params=params(60),
        cost_estimate=cost(20 * length * length * width, 40 * length * width, length * length * width // HD),
        name="attend_back",
    )(y, q2, extra, k2, v, o, own, got, live, kind)


def normalise(value):
    centre = value - jnp.mean(value, axis=-1, keepdims=True)
    inverse = lax.rsqrt(jnp.mean(centre * centre, axis=-1, keepdims=True) + NORM_EPS)
    return centre * inverse, inverse


def normalise_back(scaled, normal, inverse):
    return inverse * (
        scaled
        - jnp.mean(scaled, axis=-1, keepdims=True)
        - normal * jnp.mean(scaled * normal, axis=-1, keepdims=True)
    )


def gelu_pair(values):
    cumulative = 0.5 * (1.0 + lax.erf(values * (1.0 / math.sqrt(2.0))))
    density = jnp.exp(-0.5 * values * values) * (1.0 / math.sqrt(2.0 * math.pi))
    return values * cumulative, cumulative + values * density


def column_sum(value):
    return jnp.sum(value, axis=0, keepdims=True)


def middle_kernel(at_ref, x_ref, cot_ref, live_ref, own_ref, got_ref, wo_ref, wi_ref, wu_ref, *rest):
    arrived = rest[:SLICES]
    (
        vec_ref, bias_ref, out_ref, first_ref, dco_ref, dcf_ref, left_ref, right_ref, sums_ref,
        inner_sums_ref, slope_ref, buf_ref,
    ) = rest[SLICES:]
    step = pl.program_id(0)
    me = at_ref[1]
    hidden, model, width = wi_ref.shape[1], x_ref.shape[1], wo_ref.shape[0]
    half = hidden // 2
    ends = [width // SLICES, (width + hidden) // SLICES, (width + hidden + model) // SLICES]
    ends.append(ends[-1] + model // SLICES)

    @pl.when(step == 0)
    def _():
        for k in range(SLICES):
            buf_ref[me ^ k] = arrived[k][...].astype(BF16)

    def foreign(a, b):
        block = buf_ref[:, a:b, :]
        return block.reshape(SLICES * (b - a), model)

    vec = [vec_ref[k : k + 1, :] for k in range(6)]
    got = got_ref[...].astype(BF16)
    own = own_ref[...]
    wo_far = foreign(0, ends[0])
    first = mm(own, wo_ref[...], NN) + mm(got, wo_far, NN) + vec[0] + x_ref[...].astype(F32)
    n1, inv1 = normalise(first)
    normed = n1 * vec[1] + vec[2]
    low = normed.astype(BF16)
    left_ref[0] = low

    def inner(part):
        if part < 2:
            return wi_ref[:, half * part : half * (part + 1)]
        return foreign(ends[part - 1], ends[part])

    def outer(part):
        if part < 2:
            return wu_ref[half * part : half * (part + 1), :]
        per = (ends[1] - ends[0]) // 2
        whole = foreign(ends[0], ends[1])
        return whole[half * (part - 2) : half * (part - 1), :]

    second = vec[3] + normed
    for part in range(4):
        pre = mm(low, inner(part), NN) + bias_ref[part : part + 1, :]
        active, slope = gelu_pair(pre)
        active = active.astype(BF16)
        slope_ref[:, half * part : half * (part + 1)] = slope
        at = hidden + half * (part % 2)
        right_ref[part // 2, :, at : at + half] = active
        second = second + mm(active, outer(part), NN)
    n2, inv2 = normalise(second)
    live = live_ref[...] > 0.5
    out_ref[...] = jnp.where(live, n2 * vec[4] + vec[5], 0.0).astype(BF16).astype(F32)
    dz = jnp.where(live, cot_ref[...].astype(F32), 0.0)
    d_second = normalise_back(dz * vec[4], n2, inv2)
    d_low = d_second.astype(BF16)
    left_ref[1] = d_low
    d_normed = d_second
    inner_sums = []
    for part in range(4):
        d_hidden = mm(d_low, outer(part), NT)
        d_inner = (d_hidden * slope_ref[:, half * part : half * (part + 1)]).astype(BF16)
        at = half * (part % 2)
        right_ref[part // 2, :, at : at + half] = d_inner
        inner_sums.append(column_sum(d_inner.astype(F32)))
        d_normed = d_normed + mm(d_inner, inner(part), NT)
    d_first = normalise_back(d_normed * vec[1], n1, inv1)
    first_ref[...] = d_first
    d_attn = d_first.astype(BF16)
    left_ref[2] = d_attn
    dco_ref[...] = mm(d_attn, wo_ref[...], NT).astype(BF16).astype(F32)
    dcf_ref[...] = mm(d_attn, wo_far, NT).astype(BF16).astype(F32)
    right_ref[0, :, 2 * hidden :] = own
    right_ref[1, :, 2 * hidden :] = got
    sums = jnp.concatenate(
        [
            column_sum(d_first),
            column_sum(d_normed * n1),
            column_sum(d_normed),
            column_sum(d_second),
            column_sum(dz * n2),
            column_sum(dz),
            jnp.zeros((2, model), F32),
        ],
        axis=0,
    )
    inner_sums = jnp.concatenate([*inner_sums, jnp.zeros((4, half), F32)], axis=0)

    @pl.when(step == 0)
    def _():
        sums_ref[...] = sums
        inner_sums_ref[...] = inner_sums

    @pl.when(step != 0)
    def _():
        sums_ref[...] += sums
        inner_sums_ref[...] += inner_sums


def middle(at, x, cot, live, context, got, wo, wi, wu, arrived, vec, bias, rows=256):
    half, width = got.shape
    model, hidden = wi.shape
    rows = min(rows, half)
    steps = half // rows
    mine = lambda w: pl.BlockSpec((rows, w), lambda i, s: (i + s[0] * steps, 0))
    tile = lambda w: pl.BlockSpec((rows, w), lambda i, s: (i, 0))
    packed = 2 * hidden + width
    return pl.pallas_call(
        middle_kernel,
        grid_spec=pltpu.PrefetchScalarGridSpec(
            num_scalar_prefetch=1,
            grid=(steps,),
            in_specs=[
                mine(model), mine(model), mine(1), mine(width), tile(width),
                whole_block(wo.shape), whole_block(wi.shape), whole_block(wu.shape),
                *(whole_block(a.shape) for a in arrived),
                whole_block(vec.shape), whole_block(bias.shape),
            ],
            out_specs=[
                tile(model), tile(model), tile(width), tile(width),
                pl.BlockSpec((3, rows, model), lambda i, s: (0, i, 0)),
                pl.BlockSpec((2, rows, packed), lambda i, s: (0, i, 0)),
                pl.BlockSpec((8, model), lambda i, s: (0, 0)),
                pl.BlockSpec((8, hidden // 2), lambda i, s: (0, 0)),
            ],
            scratch_shapes=[
                pltpu.VMEM((rows, 2 * hidden), F32),
                pltpu.VMEM((SLICES, *arrived[0].shape), BF16),
            ],
        ),
        out_shape=[
            struct((half, model), F32), struct((half, model), F32),
            struct((half, width), F32), struct((half, width), F32),
            struct((3, half, model), BF16), struct((2, half, packed), BF16),
            struct((8, model), F32), struct((8, hidden // 2), F32),
        ],
        compiler_params=params(62),
        cost_estimate=cost(
            16 * half * model * (hidden + width // 2), 12 * model * packed + 40 * half * model, 6 * half * hidden
        ),
        name="middle",
    )(at, x, cot, live, context, got, wo, wi, wu, *arrived, vec, bias)


def weight_kernel(tiles, left_ref, right_ref, *rest):
    out_ref = rest[-1]
    end = 0
    for index, source, target, size in tiles:
        out_ref[0, :, target : target + size] = mm(left_ref[index], right_ref[0, :, source : source + size], TN)
        end = max(end, target + size)
    if len(rest) == 2:
        out_ref[0, :, end:] = rest[0][0]


def weight_grads(left, right, extra, tiles, rows=256):
    kinds, depth, model = left.shape
    pieces, _, packed = right.shape
    columns = sum(tile[3] for tile in tiles) + (extra.shape[-1] if extra is not None else 0)
    args, specs = [left, right], [
        pl.BlockSpec((kinds, depth, rows), lambda k, i: (0, 0, i)),
        pl.BlockSpec((1, depth, packed), lambda k, i: (k, 0, 0)),
    ]
    if extra is not None:
        args.append(extra)
        specs.append(pl.BlockSpec((1, rows, extra.shape[-1]), lambda k, i: (k, i, 0)))
    return pl.pallas_call(
        functools.partial(weight_kernel, tiles),
        grid=(pieces, model // rows),
        in_specs=specs,
        out_specs=pl.BlockSpec((1, rows, columns), lambda k, i: (k, i, 0)),
        out_shape=struct((pieces, model, columns), F32),
        compiler_params=params(56),
        cost_estimate=cost(2 * pieces * depth * model * columns, 4 * pieces * model * columns),
        name="weight_grads",
    )(*args)


def project_weight_kernel(chosen, x_ref, grad_ref, *rest):
    out_ref = rest[-1]
    width = grad_ref.shape[2]
    for k, c in enumerate(chosen):
        out_ref[:, width * k : width * (k + 1)] = mm(x_ref[...], grad_ref[c], TN)
    if len(rest) == 2:
        out_ref[:, width * len(chosen) :] = rest[0][...]


def project_weight_grads(x, grads, chosen, extra, rows=256):
    length, model = x.shape
    width = grads.shape[2]
    columns = width * len(chosen) + (extra.shape[-1] if extra is not None else 0)
    args = [x, grads]
    specs = [pl.BlockSpec((length, rows), lambda i: (0, i)), whole_block(grads.shape)]
    if extra is not None:
        args.append(extra)
        specs.append(pl.BlockSpec((rows, extra.shape[-1]), lambda i: (i, 0)))
    return pl.pallas_call(
        functools.partial(project_weight_kernel, chosen),
        grid=(model // rows,),
        in_specs=specs,
        out_specs=pl.BlockSpec((rows, columns), lambda i: (i, 0)),
        out_shape=struct((model, columns), F32),
        compiler_params=params(48),
        cost_estimate=cost(2 * length * model * columns, 4 * model * columns + 12 * length * width),
        name="project_weight_grads",
    )(*args)


def input_kernel(steps, y_ref, grad_ref, wq_ref, wk_ref, wv_ref, first_ref, out_ref):
    total = mm(grad_ref[4], wk_ref[...], NT) + mm(grad_ref[5], wv_ref[...], NT)
    for c in range(4):
        total = total + mm(grad_ref[c], wq_ref[c], NT)
    mine = pl.program_id(0) // steps == y_ref[0]
    out_ref[...] = total + jnp.where(mine, first_ref[...], 0.0)


def input_part(y, grads, wq, wk, wv, first, rows=256):
    _, length, width = grads.shape
    half, model = first.shape
    rows = min(rows, half)
    steps = half // rows
    return pl.pallas_call(
        functools.partial(input_kernel, steps),
        grid_spec=pltpu.PrefetchScalarGridSpec(
            num_scalar_prefetch=1,
            grid=(length // rows,),
            in_specs=[
                pl.BlockSpec((6, rows, width), lambda i, s: (0, i, 0)),
                whole_block(wq.shape), whole_block(wk.shape), whole_block(wv.shape),
                pl.BlockSpec((rows, model), lambda i, s: (jnp.clip(i - s[0] * steps, 0, steps - 1), 0)),
            ],
            out_specs=pl.BlockSpec((rows, model), lambda i, s: (i, 0)),
        ),
        out_shape=struct((length, model), F32),
        compiler_params=params(48),
        cost_estimate=cost(12 * length * model * width, 16 * model * width + 8 * length * model),
        name="input_part",
    )(y, grads, wq, wk, wv, first)


def place_kernel(y_ref, own_ref, got_ref, out_ref):
    mine = pl.program_id(0) == y_ref[0]
    out_ref[...] = jnp.where(mine, own_ref[...], got_ref[...]).astype(BF16)


def place_rows(y, own, got):
    half, model = own.shape
    return pl.pallas_call(
        place_kernel,
        grid_spec=pltpu.PrefetchScalarGridSpec(
            num_scalar_prefetch=1,
            grid=(2,),
            in_specs=[whole_block(own.shape), whole_block(got.shape)],
            out_specs=pl.BlockSpec((half, model), lambda i, s: (i, 0)),
        ),
        out_shape=struct((2 * half, model), BF16),
        compiler_params=params(32),
        cost_estimate=cost(half * model, 12 * half * model),
        name="place_rows",
    )(y, own, got)


def per_device(
    devices,
    tokens,
    lengths,
    entity_flags,
    query_weight,
    query_bias,
    key_weight,
    key_bias,
    value_weight,
    value_bias,
    output_weight,
    output_bias,
    attn_gain,
    attn_shift,
    inner_weight,
    inner_bias,
    outer_weight,
    outer_bias,
    final_gain,
    final_shift,
    cotangent,
):
    x = tokens[0]
    length, model = x.shape
    width = key_weight.shape[1]
    hidden = inner_weight.shape[1]
    half = length // 2
    bits = devices.bit_length() - 1
    y = lax.axis_index("tensor")
    d = lax.axis_index("dp")

    def swap(value, mask):
        return lax.ppermute(value, "dp", [(i, i ^ mask) for i in range(devices)])

    def cross(value):
        return lax.ppermute(value, "tensor", [(0, 1), (1, 0)])

    me = d % SLICES
    at = jnp.stack([y, me]).astype(jnp.int32)

    def pack(index):
        cut = lambda a: lax.dynamic_slice_in_dim(
            a, index * (a.shape[0] // SLICES), a.shape[0] // SLICES, 0
        )
        wide = cut(inner_weight)
        return jnp.concatenate(
            [cut(output_weight), cut(outer_weight), wide[:, :model], wide[:, model:]], axis=0
        ).astype(F32)

    near = cross(pack(me))
    last = cross(pack(me ^ 6))
    by_two = swap(near, 2)
    by_four = swap(near, 4)
    arrived = []
    for piece in (near, by_two, by_four, last):
        arrived += [piece, swap(piece, 1)]
    arrived = tuple(arrived)
    far_bias = cross(inner_bias)

    live = (lax.broadcasted_iota(jnp.int32, (length, 1), 0) < lengths[0]).astype(F32)
    kind = (entity_flags[0] == 1).astype(F32).reshape(length, 1)

    q2, k2, v = project(
        x, kind, query_weight, query_bias, key_weight, key_bias, value_weight, value_bias
    )
    context, extra = attend(q2, k2, v, live)
    got = cross(lax.dynamic_slice_in_dim(context, half * (1 - y), half, 0).astype(F32))

    vec = jnp.stack(
        [output_bias, attn_gain, attn_shift, outer_bias, final_gain, final_shift, outer_bias, outer_bias]
    )
    bias = jnp.concatenate([inner_bias, far_bias, inner_bias, far_bias]).reshape(8, hidden // 2)
    out_rows, d_first, dco, dcf, left, right, sums, inner_sums = middle(
        at, x, cotangent[0], live, context, got, output_weight, inner_weight, outer_weight,
        arrived, vec, bias,
    )
    d_got = cross(dcf)

    inner_columns = inner_sums[:4].reshape(2, model, 2)
    shared = jnp.broadcast_to(sums[:6].T[None], (2, model, 6))
    columns = jnp.pad(jnp.concatenate([shared, inner_columns], axis=2), ((0, 0), (0, 0), (0, 120)))
    grads_a = weight_grads(left, right, None, ((0, 0, 0, hidden), (2, 2 * hidden, hidden, width)))
    grads_b = weight_grads(left, right, columns, ((1, hidden, 0, hidden),))

    def spread(array):
        return array.reshape(array.shape[0], *([2] * bits), model // devices, array.shape[-1])

    def halve(array, mask):
        axis = 1 + bits - mask.bit_length()
        bit = (d // mask) % 2
        send = lax.dynamic_slice_in_dim(array, 1 - bit, 1, axis)
        keep = lax.dynamic_slice_in_dim(array, bit, 1, axis)
        return keep + swap(send, mask)

    def across(array):
        return array[:1] + cross(array[1:])

    def finish(array, done):
        for k in range(bits):
            if (1 << k) not in done:
                array = halve(array, 1 << k)
        return array.reshape(model // devices, array.shape[-1])

    d_all, bias_sums = attend_back(at, q2, extra, k2, v, context, dco, d_got, live, kind)
    got_out = cross(out_rows)

    a = halve(halve(spread(grads_a), 1), 2)
    b = halve(halve(spread(grads_b), 1), 4)
    a = halve(across(a), 4)
    b = across(halve(b, 2))
    a = finish(a, (1, 2, 4))
    b = finish(b, (1, 2, 4))
    layer_out = place_rows(at, out_rows, got_out)

    part = input_part(at, d_all, query_weight, key_weight, value_weight, d_first)
    input_grad = (part + cross(part)).astype(BF16)

    per = width // devices
    rows = model // devices
    bias_columns = jnp.pad(
        bias_sums[:6].reshape(6, devices, per), ((0, 0), (0, 0), (0, rows - per))
    ).reshape(6, model)
    bias_columns = jnp.pad(bias_columns.T, ((0, 0), (0, 122)))
    grads_c = project_weight_grads(x, d_all, (0, 1, 2), None)[None]
    grads_d = project_weight_grads(x, d_all, (3, 4, 5), bias_columns)[None]
    c = halve(halve(halve(spread(grads_c), 1), 2), 4)
    e = halve(halve(halve(spread(grads_d), 1), 4), 2)
    c = finish(c, (1, 2, 4))
    e = finish(e, (1, 2, 4))

    shared = b[:, hidden:]
    cut = lambda k: c[:, width * k : width * (k + 1)]
    grad_query_weight = jnp.stack([cut(0), cut(1), cut(2), e[:, :width]])
    biases = e[:per, 3 * width : 3 * width + 6].T
    return (
        layer_out[None],
        input_grad[None],
        grad_query_weight,
        biases[:4],
        e[:, width : 2 * width],
        biases[4],
        e[:, 2 * width : 3 * width],
        biases[5],
        a[:, hidden:].T,
        shared[:, 0],
        shared[:, 1],
        shared[:, 2],
        a[:, :hidden],
        shared[:, 6:8].reshape(2 * rows),
        b[:, :hidden].T,
        shared[:, 3],
        shared[:, 4],
        shared[:, 5],
    )


def solution(mesh):
    return jax.shard_map(
        functools.partial(per_device, mesh.shape["dp"]),
        mesh=mesh,
        in_specs=(
            P("dp", None, None),
            P("dp"),
            P("dp", None),
            P(None, None, "tensor"),
            P(None, "tensor"),
            P(None, "tensor"),
            P("tensor"),
            P(None, "tensor"),
            P("tensor"),
            P("tensor", None),
            P(),
            P(),
            P(),
            P(None, "tensor"),
            P("tensor"),
            P("tensor", None),
            P(),
            P(),
            P(),
            P("dp", None, None),
        ),
        out_specs=(
            P("dp", None, None),
            P("dp", None, None),
            P(None, "dp", "tensor"),
            P(None, ("tensor", "dp")),
            P("dp", "tensor"),
            P(("tensor", "dp")),
            P("dp", "tensor"),
            P(("tensor", "dp")),
            P("tensor", "dp"),
            P("dp"),
            P("dp"),
            P("dp"),
            P("dp", "tensor"),
            P(("tensor", "dp")),
            P("tensor", "dp"),
            P("dp"),
            P("dp"),
            P("dp"),
        ),
        check_vma=False,
    )
```

```python
import functools
import math

import jax
import jax.numpy as jnp
from jax import lax
from jax.experimental import pallas as pl
from jax.experimental.pallas import tpu as pltpu
from jax.sharding import PartitionSpec as P

HD = 64
SLICES = 8
MASKED = -1e30
NORM_EPS = 1e-05

F32 = jnp.float32
BF16 = jnp.bfloat16
NN = (((1,), (0,)), ((), ()))
NT = (((1,), (1,)), ((), ()))
TN = (((0,), (0,)), ((), ()))


def mm(left, right, dims):
    return lax.dot_general(left, right, dims, preferred_element_type=F32)


def struct(shape, kind):
    return jax.ShapeDtypeStruct(shape, kind)


def params(mib):
    return pltpu.CompilerParams(vmem_limit_bytes=mib << 20)


def cost(flops, moved, special=0):
    return pl.CostEstimate(flops=int(flops), bytes_accessed=int(moved), transcendentals=int(special))


def whole_block(shape):
    return pl.BlockSpec(shape, lambda *_: (0,) * len(shape), pipeline_mode=pl.Buffered(1))


def three_pieces(value):
    high = value.astype(BF16).astype(F32)
    rest = value - high
    middle = rest.astype(BF16).astype(F32)
    return high, middle, rest - middle


def project_kernel(x_ref, kind_ref, wq_ref, bq_ref, wk_ref, bk_ref, wv_ref, bv_ref, q2_ref, k2_ref, v_ref):
    x = x_ref[...]
    entity = kind_ref[...] > 0.5
    rows = x.shape[0]
    width = wk_ref.shape[1]

    weights = jnp.concatenate([*(wq_ref[c] for c in range(4)), wk_ref[...], wv_ref[...]], axis=1)
    biases = jnp.concatenate([*(bq_ref[c : c + 1, :] for c in range(4)), bk_ref[...], bv_ref[...]], axis=1)
    products = mm(x, weights, NN) + biases

    def query(c):
        return products[:, width * c : width * (c + 1)]

    scale = 1.0 / math.sqrt(HD)
    to_word = jnp.where(entity, query(2), query(0)).astype(BF16).astype(F32) * scale
    to_entity = jnp.where(entity, query(3), query(1)).astype(BF16).astype(F32) * scale
    keys = query(4).astype(BF16).astype(F32)
    v_ref[...] = query(5).astype(BF16)
    left = lax.broadcasted_iota(jnp.int32, (rows, 2 * HD), 1) < HD
    held = left != entity
    for p in range(width // (2 * HD)):
        cols = slice(2 * HD * p, 2 * HD * (p + 1))
        w, e, k = to_word[:, cols], to_entity[:, cols], keys[:, cols]
        w_roll, e_roll, k_roll = (pltpu.roll(t, HD, 1) for t in (w, e, k))
        even = slice(4 * HD * p, 4 * HD * p + 2 * HD)
        odd = slice(4 * HD * p + 2 * HD, 4 * HD * (p + 1))
        q2_ref[:, even] = jnp.where(left, w, e_roll).astype(BF16)
        q2_ref[:, odd] = jnp.where(left, w_roll, e).astype(BF16)
        k2_ref[:, even] = jnp.where(held, jnp.where(left, k, k_roll), 0.0).astype(BF16)
        k2_ref[:, odd] = jnp.where(held, jnp.where(left, k_roll, k), 0.0).astype(BF16)


def project(x, kind, wq, bq, wk, bk, wv, bv, rows=256):
    length, model = x.shape
    width = wk.shape[1]
    rows = min(rows, length)
    tile = lambda w: pl.BlockSpec((rows, w), lambda i: (i, 0))
    return pl.pallas_call(
        project_kernel,
        grid=(length // rows,),
        in_specs=[
            tile(model),
            tile(1),
            whole_block(wq.shape),
            whole_block(bq.shape),
            whole_block(wk.shape),
            whole_block((1, width)),
            whole_block(wv.shape),
            whole_block((1, width)),
        ],
        out_specs=[tile(2 * width), tile(2 * width), tile(width)],
        out_shape=[
            struct((length, 2 * width), BF16),
            struct((length, 2 * width), BF16),
            struct((length, width), BF16),
        ],
        compiler_params=params(48),
        cost_estimate=cost(12 * length * model * width, 16 * model * width + 12 * length * width),
        name="project",
    )(x, kind, wq, bq, wk, bk.reshape(1, width), wv, bv.reshape(1, width))


def key_extra(live, rows):
    lane = lax.broadcasted_iota(jnp.int32, (rows, 2 * HD), 1)
    return jnp.where(
        lane == 0, jnp.where(live, 0.0, MASKED), jnp.where(lane < 4, 1.0, 0.0)
    ).astype(BF16)


def attend_kernel(q2_ref, k2_ref, v_ref, live_ref, out_ref, extra_ref, turned_ref, both_ref):
    length = k2_ref.shape[0]
    h = pl.program_id(1)

    @pl.when(h == 0)
    def _():
        turned = v_ref[...].astype(F32).T.astype(BF16)
        turned_ref[0] = turned[:HD]
        turned_ref[1] = turned[HD:]

    lane = lax.broadcasted_iota(jnp.int32, (length, 2 * HD), 1)
    one = jnp.where(lane == 0, 1.0, 0.0).astype(BF16)
    keys = jnp.concatenate([k2_ref[...], key_extra(live_ref[...] > 0.5, length)], axis=1)
    query = jnp.concatenate([q2_ref[...], one], axis=1)
    scores = mm(keys, query, NT)
    top = jnp.max(scores, axis=0, keepdims=True)
    weights = jnp.exp(scores - top)
    norm = jnp.sum(weights, axis=0, keepdims=True)
    summed = mm(turned_ref[h], weights.astype(BF16), NN)
    both_ref[h] = summed * (1.0 / norm)
    pieces = three_pieces(-(top + jnp.log(norm)))
    filled = jnp.concatenate(
        [jnp.ones((1, length), F32), *pieces, jnp.zeros((2 * HD - 4, length), F32)], axis=0
    )
    extra_ref[...] = filled.T.astype(BF16)

    @pl.when(h == 1)
    def _():
        out_ref[...] = jnp.concatenate([both_ref[0], both_ref[1]], axis=0).T.astype(BF16)


def attend(q2, k2, v, live):
    length, width = v.shape
    head = pl.BlockSpec((length, 2 * HD), lambda p, h: (0, 2 * p + h))
    pair = pl.BlockSpec((length, 2 * HD), lambda p, h: (0, p))
    return pl.pallas_call(
        attend_kernel,
        grid=(width // (2 * HD), 2),
        in_specs=[head, head, pair, whole_block((length, 1))],
        out_specs=[pair, head],
        out_shape=[struct((length, width), BF16), struct((length, 2 * width), BF16)],
        scratch_shapes=[pltpu.VMEM((2, HD, length), BF16), pltpu.VMEM((2, HD, length), F32)],
        compiler_params=params(56),
        cost_estimate=cost(10 * length * length * width, 20 * length * width, length * length * width // HD),
        name="attend",
    )(q2, k2, v, live)


def attend_back_kernel(
    y_ref, q2_ref, extra_ref, k2_ref, v_ref, o_ref, own_ref, got_ref, live_ref, kind_ref,
    grad_ref, sums_ref, dk_ref, dv_ref, dq_ref, product_ref, d_ref,
):
    length = k2_ref.shape[0]
    h = pl.program_id(1)
    lane = lax.broadcasted_iota(jnp.int32, (length, 2 * HD), 1)
    left = lane < HD

    @pl.when(h == 0)
    def _():
        first = y_ref[0] == 0
        own, got = own_ref[...], got_ref[...]
        joined = jnp.concatenate([jnp.where(first, own, got), jnp.where(first, got, own)], axis=0)
        product_ref[...] = joined * o_ref[...].astype(F32)
        d_ref[...] = joined.astype(BF16)

    d_context = d_ref[...]
    base = HD * (1 - h)
    mine = jnp.logical_and(lane >= HD - base, lane < 2 * HD - base)
    delta = jnp.sum(jnp.where(mine, product_ref[...], 0.0), axis=1, keepdims=True)
    high, middle, low = three_pieces(-delta)
    pieces = jnp.where(
        lane == base, high, jnp.where(lane == base + 1, middle, jnp.where(lane == base + 2, low, 0.0))
    ).astype(BF16)
    d_wide = jnp.where(mine, d_context, pieces)
    q2, k2 = q2_ref[...], k2_ref[...]
    query = jnp.concatenate([q2, extra_ref[...]], axis=1)
    keys = jnp.concatenate([k2, key_extra(live_ref[...] > 0.5, length)], axis=1)
    probs = jnp.exp(mm(keys, query, NT))
    ones = jnp.where((lane >= base) & (lane < base + 3), 1.0, 0.0).astype(BF16)
    d_probs = mm(jnp.where(mine, v_ref[...], ones), d_wide, NT)
    d_scores = (probs * d_probs).astype(BF16)
    dv_ref[h] = mm(probs.astype(BF16), d_context, NN)
    dk_ref[h] = mm(d_scores, q2, NN)
    dq_ref[h] = mm(k2, d_scores, TN).T * (1.0 / math.sqrt(HD))

    @pl.when(h == 1)
    def _():
        entity = kind_ref[...] > 0.5
        even, odd = dq_ref[0], dq_ref[1]
        to_word = jnp.where(left, even, pltpu.roll(odd, HD, 1)).astype(BF16).astype(F32)
        to_entity = jnp.where(left, pltpu.roll(even, HD, 1), odd).astype(BF16).astype(F32)
        even, odd = dk_ref[0], dk_ref[1]
        even = jnp.where(entity, pltpu.roll(even, HD, 1), even)
        odd = jnp.where(entity, odd, pltpu.roll(odd, HD, 1))
        grads = [
            jnp.where(entity, 0.0, to_word),
            jnp.where(entity, 0.0, to_entity),
            jnp.where(entity, to_word, 0.0),
            jnp.where(entity, to_entity, 0.0),
            jnp.where(left, even, odd).astype(BF16).astype(F32),
            jnp.where(left, dv_ref[0], dv_ref[1]).astype(BF16).astype(F32),
        ]
        for c, grad in enumerate(grads):
            grad_ref[c] = grad.astype(BF16)
        sums = [jnp.sum(grad, axis=0, keepdims=True) for grad in grads]
        sums_ref[...] = jnp.concatenate([*sums, jnp.zeros((2, 2 * HD), F32)], axis=0)


def attend_back(y, q2, extra, k2, v, o, own, got, live, kind):
    length, width = v.shape
    half = own.shape[0]
    head = pl.BlockSpec((length, 2 * HD), lambda p, h, *_: (0, 2 * p + h))
    pair = pl.BlockSpec((length, 2 * HD), lambda p, h, *_: (0, p))
    part = pl.BlockSpec((half, 2 * HD), lambda p, h, *_: (0, p))
    return pl.pallas_call(
        attend_back_kernel,
        grid_spec=pltpu.PrefetchScalarGridSpec(
            num_scalar_prefetch=1,
            grid=(width // (2 * HD), 2),
            in_specs=[
                head, head, head, pair, pair, part, part, whole_block((length, 1)), whole_block((length, 1)),
            ],
            out_specs=[
                pl.BlockSpec((6, length, 2 * HD), lambda p, h, *_: (0, 0, p)),
                pl.BlockSpec((8, 2 * HD), lambda p, h, *_: (0, p)),
            ],
            scratch_shapes=[
                *[pltpu.VMEM((2, length, 2 * HD), F32)] * 3,
                pltpu.VMEM((length, 2 * HD), F32),
                pltpu.VMEM((length, 2 * HD), BF16),
            ],
        ),
        out_shape=[struct((6, length, width), BF16), struct((8, width), F32)],
        compiler_params=params(60),
        cost_estimate=cost(20 * length * length * width, 40 * length * width, length * length * width // HD),
        name="attend_back",
    )(y, q2, extra, k2, v, o, own, got, live, kind)


def normalise(value):
    centre = value - jnp.mean(value, axis=-1, keepdims=True)
    inverse = lax.rsqrt(jnp.mean(centre * centre, axis=-1, keepdims=True) + NORM_EPS)
    return centre * inverse, inverse


def normalise_back(scaled, normal, inverse):
    return inverse * (
        scaled
        - jnp.mean(scaled, axis=-1, keepdims=True)
        - normal * jnp.mean(scaled * normal, axis=-1, keepdims=True)
    )


def gelu_pair(values):
    cumulative = 0.5 * (1.0 + lax.erf(values * (1.0 / math.sqrt(2.0))))
    density = jnp.exp(-0.5 * values * values) * (1.0 / math.sqrt(2.0 * math.pi))
    return values * cumulative, cumulative + values * density


def column_sum(value):
    return jnp.sum(value, axis=0, keepdims=True)


def group_cuts(half):
    return half // 2, half // 128 * 5 // 6 * 128


def middle_kernel(at_ref, x_ref, cot_ref, live_ref, own_ref, got_ref, wo_ref, wi_ref, wu_ref, *rest):
    arrived = rest[:SLICES]
    arrived_late = rest[SLICES : 2 * SLICES]
    (
        vec_ref, bias_ref, out_ref, first_ref, dco_ref, cross_ref, late_out_ref, left_ref,
        keep0_ref, keep1_ref, keep2_ref, left_send_ref, send0_ref, send1_ref, send2_ref,
        sums_ref, inner_sums_ref, slope_ref, early_ref, late_ref,
    ) = rest[2 * SLICES :]
    step = pl.program_id(0)
    me = at_ref[1]
    lower = me % 2 == 0
    hidden, model, width = wi_ref.shape[1], x_ref.shape[1], wo_ref.shape[0]
    half = hidden // 2
    ca, cb = group_cuts(half)

    @pl.when(step == 0)
    def _():
        for k in range(SLICES):
            early_ref[me ^ k] = arrived[k][...].astype(BF16)
            late_ref[me ^ k] = arrived_late[k][...].astype(BF16)

    def foreign(ref, a, b):
        return ref[:, a:b, :].reshape(SLICES * (b - a), model)

    vec = [vec_ref[k : k + 1, :] for k in range(6)]
    got = got_ref[...].astype(BF16)
    own = own_ref[...]
    cut = [width // SLICES, (width + model) // SLICES, (width + 2 * model) // SLICES]
    wo_far = foreign(early_ref, 0, cut[0])
    first = mm(own, wo_ref[...], NN) + mm(got, wo_far, NN) + vec[0] + x_ref[...].astype(F32)
    n1, inv1 = normalise(first)
    normed = n1 * vec[1] + vec[2]
    low = normed.astype(BF16)

    def inner(part):
        if part < 2:
            return wi_ref[:, half * part : half * (part + 1)]
        return foreign(early_ref, cut[part - 2], cut[part - 1])

    def outer(part):
        if part < 2:
            return wu_ref[half * part : half * (part + 1), :]
        per = SLICES // 2
        block = late_ref[per * (part - 2) : per * (part - 1), :, :]
        return block.reshape(half, model)

    def both(index, value):
        turned = value.astype(F32).T
        left_ref[index] = turned.astype(BF16)
        left_send_ref[model * index : model * (index + 1), :] = turned

    def split(values):
        first, second = (value.astype(F32) for value in values)
        keep = jnp.where(lower, first, second).astype(BF16)
        return keep, jnp.where(lower, second, first)

    both(0, low)
    second = vec[3] + normed
    for far in range(2):
        pair = []
        for part in (2 * far, 2 * far + 1):
            pre = mm(low, inner(part), NN) + bias_ref[part : part + 1, :]
            active, slope = gelu_pair(pre)
            active = active.astype(BF16)
            slope_ref[:, half * part : half * (part + 1)] = slope
            pair.append(active)
            second = second + mm(active, outer(part), NN)
        keep, send = split(pair)
        at1 = (half - ca + half - cb) * far + half - ca
        for value, ref1, ref2 in ((keep, keep1_ref, keep2_ref), (send, send1_ref, send2_ref)):
            ref2[:, cb * far : cb * (far + 1)] = value[:, :cb]
            ref1[:, at1 : at1 + half - cb] = value[:, cb:]
    n2, inv2 = normalise(second)
    live = live_ref[...] > 0.5
    result = jnp.where(live, n2 * vec[4] + vec[5], 0.0).astype(BF16)
    out_ref[...] = result
    cross_ref[:, width:] = result[:, : model // 2].astype(F32)
    late_out_ref[...] = result[:, model // 2 :].astype(F32)
    dz = jnp.where(live, cot_ref[...].astype(F32), 0.0)
    d_second = normalise_back(dz * vec[4], n2, inv2)
    d_low = d_second.astype(BF16)
    both(1, d_low)
    d_normed = d_second
    inner_sums = []
    for far in range(2):
        pair = []
        for part in (2 * far, 2 * far + 1):
            d_hidden = mm(d_low, outer(part), NT)
            d_inner = (d_hidden * slope_ref[:, half * part : half * (part + 1)]).astype(BF16)
            pair.append(d_inner)
            inner_sums.append(column_sum(d_inner.astype(F32)))
            d_normed = d_normed + mm(d_inner, inner(part), NT)
        keep, send = split(pair)
        at1 = (half - ca + half - cb) * far
        for value, ref0, ref1 in ((keep, keep0_ref, keep1_ref), (send, send0_ref, send1_ref)):
            ref0[:, ca * far : ca * (far + 1)] = value[:, :ca]
            ref1[:, at1 : at1 + half - ca] = value[:, ca:]
    d_first = normalise_back(d_normed * vec[1], n1, inv1)
    first_ref[...] = d_first
    d_attn = d_first.astype(BF16)
    both(2, d_attn)
    dco_ref[...] = mm(d_attn, wo_ref[...], NT).astype(BF16).astype(F32)
    cross_ref[:, :width] = mm(d_attn, wo_far, NT).astype(BF16).astype(F32)
    keep, send = split((own, got))
    keep0_ref[:, 2 * ca :] = keep
    send0_ref[:, 2 * ca :] = send
    sums = jnp.concatenate(
        [
            column_sum(d_first),
            column_sum(d_normed * n1),
            column_sum(d_normed),
            column_sum(d_second),
            column_sum(dz * n2),
            column_sum(dz),
            jnp.zeros((2, model), F32),
        ],
        axis=0,
    )
    inner_sums = jnp.concatenate([*inner_sums, jnp.zeros((4, half), F32)], axis=0)

    @pl.when(step == 0)
    def _():
        sums_ref[...] = sums
        inner_sums_ref[...] = inner_sums

    @pl.when(step != 0)
    def _():
        sums_ref[...] += sums
        inner_sums_ref[...] += inner_sums


def middle(at, x, cot, live, context, got, wo, wi, wu, early, late, vec, bias, rows=256):
    half, width = got.shape
    model, hidden = wi.shape
    rows = min(rows, half)
    steps = half // rows
    mine = lambda w: pl.BlockSpec((rows, w), lambda i, s: (i + s[0] * steps, 0))
    tile = lambda w: pl.BlockSpec((rows, w), lambda i, s: (i, 0))
    ca, cb = group_cuts(hidden // 2)
    widths = (2 * ca + width, 2 * (hidden - ca - cb), 2 * cb)
    return pl.pallas_call(
        middle_kernel,
        grid_spec=pltpu.PrefetchScalarGridSpec(
            num_scalar_prefetch=1,
            grid=(steps,),
            in_specs=[
                mine(model), mine(model), mine(1), mine(width), tile(width),
                whole_block(wo.shape), whole_block(wi.shape), whole_block(wu.shape),
                *(whole_block(a.shape) for a in (*early, *late)),
                whole_block(vec.shape), whole_block(bias.shape),
            ],
            out_specs=[
                tile(model), tile(model), tile(width), tile(width + model // 2), tile(model // 2),
                pl.BlockSpec((3, model, rows), lambda i, s: (0, 0, i)),
                *(tile(w) for w in widths),
                pl.BlockSpec((3 * model, rows), lambda i, s: (0, i)),
                *(tile(w) for w in widths),
                pl.BlockSpec((8, model), lambda i, s: (0, 0)),
                pl.BlockSpec((8, hidden // 2), lambda i, s: (0, 0)),
            ],
            scratch_shapes=[
                pltpu.VMEM((rows, 2 * hidden), F32),
                pltpu.VMEM((SLICES, *early[0].shape), BF16),
                pltpu.VMEM((SLICES, *late[0].shape), BF16),
            ],
        ),
        out_shape=[
            struct((half, model), BF16), struct((half, model), F32),
            struct((half, width), F32), struct((half, width + model // 2), F32),
            struct((half, model // 2), F32),
            struct((3, model, half), BF16),
            *(struct((half, w), BF16) for w in widths),
            struct((3 * model, half), F32),
            *(struct((half, w), F32) for w in widths),
            struct((8, model), F32), struct((8, hidden // 2), F32),
        ],
        compiler_params=params(63),
        cost_estimate=cost(
            16 * half * model * (hidden + width // 2), 24 * model * hidden + 80 * half * model, 6 * half * hidden
        ),
        name="middle",
    )(at, x, cot, live, context, got, wo, wi, wu, *early, *late, vec, bias)


def weight_kernel(slot, group, tiles, bit_ref, right_ref, right_got_ref, *rest):
    keep_ref, send_ref = rest[-2:]
    lefts = [rest[2 * k][0] for k in range(len(rest) // 2 - 1)]
    lefts_got = [rest[2 * k + 1][...].astype(BF16) for k in range(len(rest) // 2 - 1)]

    def product(index, a, b):
        value = mm(lefts[index], right_ref[:, a:b], NN)
        return value + mm(lefts_got[index], right_got_ref[:, a:b].astype(BF16), NN)

    if slot is None:
        middle_column = right_ref.shape[1] // 2
        for index, a, b in tiles:
            ref, base = (keep_ref, 0) if b <= middle_column else (send_ref, middle_column)
            ref[:, a - base : b - base] = product(index, a, b)
        return
    kept = bit_ref[slot] == 0
    for index, a, b in tiles:
        value = product(index, a, b)
        pairs = value.reshape(value.shape[0] // (2 * group), 2, group, b - a)
        first, second = pairs[:, 0], pairs[:, 1]
        keep_ref[:, :, a:b] = jnp.where(kept, first, second)
        send_ref[:, :, a:b] = jnp.where(kept, second, first)


def weight_grads(at, slot, left, left_got, right, right_got, indices, tiles, group):
    _, model, depth = left.shape
    rows = model // 2
    columns = right.shape[1]
    args = [right, right_got]
    specs = [whole_block(right.shape), whole_block(right_got.shape)]
    for index in indices:
        args += [left, left_got]
        specs += [
            pl.BlockSpec((1, rows, depth), lambda i, s, index=index: (index, i, 0)),
            pl.BlockSpec((rows, depth), lambda i, s, index=index: (2 * index + i, 0)),
        ]
    if slot is None:
        shape = (model, columns // 2)
        out = pl.BlockSpec((rows, columns // 2), lambda i, s: (i, 0))
    else:
        blocks = rows // (2 * group)
        shape = (2 * blocks, group, columns)
        out = pl.BlockSpec((blocks, group, columns), lambda i, s: (i, 0, 0))
    return pl.pallas_call(
        functools.partial(weight_kernel, slot, group, tiles),
        grid_spec=pltpu.PrefetchScalarGridSpec(
            num_scalar_prefetch=1, grid=(2,), in_specs=specs, out_specs=[out, out]
        ),
        out_shape=[struct(shape, F32)] * 2,
        compiler_params=params(56),
        cost_estimate=cost(4 * depth * model * columns, 4 * model * columns + 8 * depth * columns),
        name="weight_grads",
    )(at, *args)


def project_weight_kernel(turned_ref, grad_ref, extra_ref, out_ref):
    width = grad_ref.shape[2]
    grads = jnp.concatenate([grad_ref[c] for c in range(6)], axis=1)
    out_ref[:, : 6 * width] = mm(turned_ref[...], grads, NN)
    out_ref[:, 6 * width :] = extra_ref[...]


def project_weight_grads(turned, grads, extra, rows=256):
    model, length = turned.shape
    width = grads.shape[2]
    columns = 6 * width + extra.shape[1]
    return pl.pallas_call(
        project_weight_kernel,
        grid=(model // rows,),
        in_specs=[
            pl.BlockSpec((rows, length), lambda i: (i, 0)),
            whole_block(grads.shape),
            pl.BlockSpec((rows, extra.shape[1]), lambda i: (i, 0)),
        ],
        out_specs=pl.BlockSpec((rows, columns), lambda i: (i, 0)),
        out_shape=struct((model, columns), F32),
        compiler_params=params(48),
        cost_estimate=cost(2 * length * model * columns, 4 * model * columns + 12 * length * width),
        name="project_weight_grads",
    )(turned, grads, extra)


def turn_kernel(value_ref, out_ref):
    out_ref[...] = value_ref[...].astype(F32).T.astype(BF16)


def turn(value, columns=256):
    length, model = value.shape
    return pl.pallas_call(
        turn_kernel,
        grid=(model // columns,),
        in_specs=[pl.BlockSpec((length, columns), lambda i: (0, i))],
        out_specs=pl.BlockSpec((columns, length), lambda i: (i, 0)),
        out_shape=struct((model, length), BF16),
        compiler_params=params(32),
        cost_estimate=cost(length * model, 4 * length * model),
        name="turn",
    )(value)


def input_kernel(steps, y_ref, grad_ref, wq_ref, wk_ref, wv_ref, first_ref, out_ref):
    grads = jnp.concatenate([grad_ref[c] for c in range(6)], axis=1)
    weights = jnp.concatenate([*(wq_ref[c] for c in range(4)), wk_ref[...], wv_ref[...]], axis=1)
    total = mm(grads, weights, NT)
    mine = pl.program_id(0) // steps == y_ref[0]
    out_ref[...] = total + jnp.where(mine, first_ref[...], 0.0)


def input_part(y, grads, wq, wk, wv, first, rows=256):
    _, length, width = grads.shape
    half, model = first.shape
    rows = min(rows, half)
    steps = half // rows
    return pl.pallas_call(
        functools.partial(input_kernel, steps),
        grid_spec=pltpu.PrefetchScalarGridSpec(
            num_scalar_prefetch=1,
            grid=(length // rows,),
            in_specs=[
                pl.BlockSpec((6, rows, width), lambda i, s: (0, i, 0)),
                whole_block(wq.shape), whole_block(wk.shape), whole_block(wv.shape),
                pl.BlockSpec((rows, model), lambda i, s: (jnp.clip(i - s[0] * steps, 0, steps - 1), 0)),
            ],
            out_specs=pl.BlockSpec((rows, model), lambda i, s: (i, 0)),
        ),
        out_shape=struct((length, model), F32),
        compiler_params=params(48),
        cost_estimate=cost(12 * length * model * width, 16 * model * width + 8 * length * model),
        name="input_part",
    )(y, grads, wq, wk, wv, first)


def place_kernel(y_ref, own_ref, first_ref, second_ref, out_ref):
    mine = pl.program_id(0) == y_ref[0]
    got = jnp.concatenate([first_ref[...], second_ref[...]], axis=1)
    out_ref[...] = jnp.where(mine, own_ref[...].astype(F32), got).astype(BF16)


def place_rows(y, own, first, second):
    half, model = own.shape
    return pl.pallas_call(
        place_kernel,
        grid_spec=pltpu.PrefetchScalarGridSpec(
            num_scalar_prefetch=1,
            grid=(2,),
            in_specs=[
                whole_block(own.shape),
                pl.BlockSpec((half, model // 2), lambda i, s: (0, 1)),
                whole_block(second.shape),
            ],
            out_specs=pl.BlockSpec((half, model), lambda i, s: (i, 0)),
        ),
        out_shape=struct((2 * half, model), BF16),
        compiler_params=params(32),
        cost_estimate=cost(half * model, 12 * half * model),
        name="place_rows",
    )(y, own, first, second)


def round_kernel(value_ref, out_ref):
    out_ref[...] = value_ref[...].astype(BF16)


def round_rows(value):
    length, model = value.shape
    rows = min(512, length)
    tile = pl.BlockSpec((rows, model), lambda i: (i, 0))
    return pl.pallas_call(
        round_kernel,
        grid=(length // rows,),
        in_specs=[tile],
        out_specs=tile,
        out_shape=struct((length, model), BF16),
        cost_estimate=cost(length * model, 6 * length * model),
        name="round_rows",
    )(value)


def per_device(
    devices,
    tokens,
    lengths,
    entity_flags,
    query_weight,
    query_bias,
    key_weight,
    key_bias,
    value_weight,
    value_bias,
    output_weight,
    output_bias,
    attn_gain,
    attn_shift,
    inner_weight,
    inner_bias,
    outer_weight,
    outer_bias,
    final_gain,
    final_shift,
    cotangent,
):
    x = tokens[0]
    length, model = x.shape
    width = key_weight.shape[1]
    hidden = inner_weight.shape[1]
    half = length // 2
    bits = devices.bit_length() - 1
    y = lax.axis_index("tensor")
    d = lax.axis_index("dp")

    def swap(value, mask):
        return lax.ppermute(value, "dp", [(i, i ^ mask) for i in range(devices)])

    def cross(value):
        return lax.ppermute(value, "tensor", [(0, 1), (1, 0)])

    me = d % SLICES
    core = d % 2
    rows = model // devices
    near_mask, far_mask = 96 // rows, 192 // rows
    at = jnp.stack([y, me, (d // near_mask) % 2, (d // far_mask) % 2]).astype(jnp.int32)
    tie = lax.optimization_barrier

    def cut(array, index):
        size = array.shape[0] // SLICES
        return lax.dynamic_slice_in_dim(array, index * size, size, 0)

    def pack(index):
        wide = cut(inner_weight, index)
        early = jnp.concatenate([cut(output_weight, index), wide[:, :model], wide[:, model:]], axis=0)
        return early.astype(F32)

    def pack_late(index):
        return cut(outer_weight, index).astype(F32)

    live = (lax.broadcasted_iota(jnp.int32, (length, 1), 0) < lengths[0]).astype(F32)
    kind = (entity_flags[0] == 1).astype(F32).reshape(length, 1)

    e0 = cross(pack(me))
    far_bias = cross(inner_bias)
    q2, k2, v = project(
        x, kind, query_weight, query_bias, key_weight, key_bias, value_weight, value_bias
    )
    e0, l0, q2 = tie((e0, pack_late(me), q2))
    e2 = swap(e0, 2)
    e4 = swap(e0, 4)
    e1 = swap(e0, 1)
    l0 = cross(l0)
    context, extra = attend(q2, k2, v, live)
    sent = lax.dynamic_slice_in_dim(context, half * (1 - y), half, 0).astype(F32)
    e1, e2, e4, l0, sent, l6 = tie((e1, e2, e4, l0, sent, pack_late(me ^ 6)))
    got = cross(sent)
    l2 = swap(l0, 2)
    l4 = swap(l0, 4)
    e6 = swap(e4, 2)
    l6 = cross(l6)
    l1 = swap(l0, 1)
    e3 = swap(e2, 1)
    e5 = swap(e4, 1)
    x_turned = turn(x)
    got, l2, l4, e6, l6, l1, e3, e5, x_turned = tie((got, l2, l4, e6, l6, l1, e3, e5, x_turned))
    e7 = swap(e6, 1)
    l3 = swap(l2, 1)
    l5 = swap(l4, 1)
    l7 = swap(l6, 1)
    early = (e0, e1, e2, e3, e4, e5, e6, e7)
    late = (l0, l1, l2, l3, l4, l5, l6, l7)

    vec = jnp.stack(
        [output_bias, attn_gain, attn_shift, outer_bias, final_gain, final_shift, outer_bias, outer_bias]
    )
    bias = jnp.concatenate([inner_bias, far_bias, inner_bias, far_bias]).reshape(8, hidden // 2)
    (
        out_rows, d_first, dco, first_cross, out_late, left, keep0, keep1, keep2, left_send, send0, send1, send2,
        sums, inner_sums,
    ) = middle(
        at, x, cotangent[0], live, context, got, output_weight, inner_weight, outer_weight,
        early, late, vec, bias,
    )
    d_got = cross(first_cross)
    left_got = swap(left_send, 1)
    got0 = swap(send0, 1)
    got1 = swap(send1, 1)
    got2 = swap(send2, 1)

    ca, cb = group_cuts(hidden // 2)
    da, db = hidden // 2 - ca, hidden // 2 - cb
    g0_keep, g0_send = weight_grads(
        at, 2, left, left_got, keep0, got0, (0, 2),
        ((0, 0, ca), (0, ca, 2 * ca), (1, 2 * ca, 2 * ca + width)), near_mask * rows,
    )
    g2_keep, g2_send = weight_grads(
        at, 3, left, left_got, keep2, got2, (1,), ((0, 0, cb), (0, cb, 2 * cb)), far_mask * rows
    )
    g1_keep, g1_send = weight_grads(
        at, None, left, left_got, keep1, got1, (0, 1),
        (
            (0, 0, da), (1, da, da + db),
            (0, da + db, 2 * da + db), (1, 2 * da + db, 2 * (da + db)),
        ),
        None,
    )
    g0_got = swap(g0_send, near_mask)
    g2_got = swap(g2_send, far_mask)
    g1_got = cross(g1_send)

    inner_columns = inner_sums[:4].reshape(2, model, 2)
    shared = jnp.broadcast_to(sums[:6].T[None], (2, model, 6))
    columns = jnp.concatenate([shared, inner_columns], axis=2)
    columns = columns[0] + cross(columns[1])

    g0_send, g1_send, g2_send, dco, d_got = tie((g0_send, g1_send, g2_send, dco, d_got))
    d_all, bias_sums = attend_back(at, q2, extra, k2, v, context, dco, d_got, live, kind)
    part = input_part(at, d_all, query_weight, key_weight, value_weight, d_first)
    per = width // devices
    bias_columns = jnp.pad(
        bias_sums[:6].reshape(6, devices, per), ((0, 0), (0, 0), (0, rows - per))
    ).reshape(6, model)
    extra_columns = jnp.pad(jnp.concatenate([bias_columns.T, columns], axis=1), ((0, 0), (0, 114)))
    projections = project_weight_grads(x_turned, d_all, extra_columns)
    got_late = cross(out_late)
    input_sum = lax.psum(part, "tensor")
    summed = lax.psum_scatter(projections, "dp", scatter_dimension=0, tiled=True)

    def spread(array, done):
        dims = [1 if (1 << (bits - 1 - k)) in done else 2 for k in range(bits)]
        return array.reshape(*dims, rows, array.shape[-1])

    def halves(array, mask):
        axis = bits - mask.bit_length()
        bit = (d // mask) % 2
        send = lax.dynamic_slice_in_dim(array, 1 - bit, 1, axis)
        return lax.dynamic_slice_in_dim(array, bit, 1, axis), send

    g0_got, g1_got, g2_got, got_late, part, projections = tie(
        (g0_got, g1_got, g2_got, got_late, part, projections)
    )
    g0 = spread(g0_keep + g0_got, (near_mask,))
    g1 = spread(g1_keep + g1_got, ())
    g2 = spread(g2_keep + g2_got, (far_mask,))
    g0_keep, g0_send = g0[..., :ca], g0[..., ca : 2 * ca]
    t_keep, t_send = halves(g0[..., 2 * ca :], far_mask)
    g1_keep, g1_send = halves(g1, far_mask)
    g2_keep, g2_send = halves(g2, near_mask)
    g0_got = cross(g0_send)
    t_got = swap(t_send, far_mask)
    g1_got = swap(g1_send, far_mask)
    g2_got = swap(g2_send, near_mask)
    g0_got, g1_got, g2_got, t_got = tie((g0_got, g1_got, g2_got, t_got))
    t_send = t_keep + t_got
    g0_keep, g0_send = halves(g0_keep + g0_got, far_mask)
    g1_keep, g1_send = halves(g1_keep + g1_got, near_mask)
    g2 = g2_keep + g2_got
    g2_keep, g2_send = g2[..., :cb], g2[..., cb:]
    g0_got = swap(g0_send, far_mask)
    t_got = cross(t_send)
    g1_got = swap(g1_send, near_mask)
    g2_got = cross(g2_send)
    g0_got, g1_got, g2_got, t_got = tie((g0_got, g1_got, g2_got, t_got))
    t_sum = jnp.where(core == 0, t_send, t_got)
    whole = jnp.concatenate([g0_keep + g0_got, t_sum, g1_keep + g1_got, g2_keep + g2_got], axis=-1)
    for k in range(1, bits):
        if (1 << k) not in (near_mask, far_mask):
            keep, send = halves(whole, 1 << k)
            whole = keep + swap(send, 1 << k)
    keep, send = halves(whole, 1)
    got_last = swap(send, 1).reshape(rows, -1)
    keep = keep.reshape(rows, -1)
    low_half = jnp.where(core == 0, keep, got_last)
    high_half = jnp.where(core == 0, got_last, keep)
    at1 = ca + width
    at2 = at1 + da + db

    def inner_half(array):
        return [array[:, :ca], array[:, at1 : at1 + da]]

    def outer_half(array):
        return [array[:, at2:], array[:, at1 + da : at2]]

    grad_inner = jnp.concatenate(inner_half(low_half) + inner_half(high_half), axis=1)
    grad_outer = jnp.concatenate(outer_half(low_half) + outer_half(high_half), axis=1).T
    grad_output = (keep[:, ca:at1] + got_last[:, ca:at1]).T
    layer_out = place_rows(at, out_rows, d_got, got_late)
    input_grad = round_rows(input_sum)

    small = summed[:, 6 * width + 6 :]
    piece = lambda k: summed[:, width * k : width * (k + 1)]
    grad_query_weight = jnp.stack([piece(0), piece(1), piece(2), piece(3)])
    biases = summed[:per, 6 * width : 6 * width + 6].T
    return (
        layer_out[None],
        input_grad[None],
        grad_query_weight,
        biases[:4],
        piece(4),
        biases[4],
        piece(5),
        biases[5],
        grad_output,
        small[:, 0],
        small[:, 1],
        small[:, 2],
        grad_inner,
        small[:, 6:8].reshape(2 * rows),
        grad_outer,
        small[:, 3],
        small[:, 4],
        small[:, 5],
    )


def solution(mesh):
    return jax.shard_map(
        functools.partial(per_device, mesh.shape["dp"]),
        mesh=mesh,
        in_specs=(
            P("dp", None, None),
            P("dp"),
            P("dp", None),
            P(None, None, "tensor"),
            P(None, "tensor"),
            P(None, "tensor"),
            P("tensor"),
            P(None, "tensor"),
            P("tensor"),
            P("tensor", None),
            P(),
            P(),
            P(),
            P(None, "tensor"),
            P("tensor"),
            P("tensor", None),
            P(),
            P(),
            P(),
            P("dp", None, None),
        ),
        out_specs=(
            P("dp", None, None),
            P("dp", None, None),
            P(None, "dp", "tensor"),
            P(None, ("tensor", "dp")),
            P("dp", "tensor"),
            P(("tensor", "dp")),
            P("dp", "tensor"),
            P(("tensor", "dp")),
            P("tensor", "dp"),
            P("dp"),
            P("dp"),
            P("dp"),
            P("dp", "tensor"),
            P(("tensor", "dp")),
            P("tensor", "dp"),
            P("dp"),
            P("dp"),
            P("dp"),
        ),
        check_vma=False,
    )
```

```python
import functools
import math

import jax
import jax.numpy as jnp
from jax import lax
from jax.experimental import pallas as pl
from jax.experimental.pallas import tpu as pltpu
from jax.sharding import PartitionSpec as P

HD = 64
SLICES = 8
MASKED = -1e30
NORM_EPS = 1e-05

F32 = jnp.float32
BF16 = jnp.bfloat16
NN = (((1,), (0,)), ((), ()))
NT = (((1,), (1,)), ((), ()))
TN = (((0,), (0,)), ((), ()))


def mm(left, right, dims):
    return lax.dot_general(left, right, dims, preferred_element_type=F32)


def struct(shape, kind):
    return jax.ShapeDtypeStruct(shape, kind)


def params(mib):
    return pltpu.CompilerParams(vmem_limit_bytes=mib << 20)


def cost(flops, moved, special=0):
    return pl.CostEstimate(flops=int(flops), bytes_accessed=int(moved), transcendentals=int(special))


def whole_block(shape):
    return pl.BlockSpec(shape, lambda *_: (0,) * len(shape), pipeline_mode=pl.Buffered(1))


def three_pieces(value):
    high = value.astype(BF16).astype(F32)
    rest = value - high
    middle = rest.astype(BF16).astype(F32)
    return high, middle, rest - middle


def project_kernel(x_ref, kind_ref, wq_ref, bq_ref, wk_ref, bk_ref, wv_ref, bv_ref, q2_ref, k2_ref, v_ref):
    x = x_ref[...]
    entity = kind_ref[...] > 0.5
    rows = x.shape[0]
    width = wk_ref.shape[1]

    weights = jnp.concatenate([*(wq_ref[c] for c in range(4)), wk_ref[...], wv_ref[...]], axis=1)
    biases = jnp.concatenate([*(bq_ref[c : c + 1, :] for c in range(4)), bk_ref[...], bv_ref[...]], axis=1)
    products = mm(x, weights, NN) + biases

    def query(c):
        return products[:, width * c : width * (c + 1)]

    scale = 1.0 / math.sqrt(HD)
    to_word = jnp.where(entity, query(2), query(0)).astype(BF16).astype(F32) * scale
    to_entity = jnp.where(entity, query(3), query(1)).astype(BF16).astype(F32) * scale
    keys = query(4).astype(BF16).astype(F32)
    v_ref[...] = query(5).astype(BF16)
    left = lax.broadcasted_iota(jnp.int32, (rows, 2 * HD), 1) < HD
    held = left != entity
    for p in range(width // (2 * HD)):
        cols = slice(2 * HD * p, 2 * HD * (p + 1))
        w, e, k = to_word[:, cols], to_entity[:, cols], keys[:, cols]
        w_roll, e_roll, k_roll = (pltpu.roll(t, HD, 1) for t in (w, e, k))
        even = slice(4 * HD * p, 4 * HD * p + 2 * HD)
        odd = slice(4 * HD * p + 2 * HD, 4 * HD * (p + 1))
        q2_ref[:, even] = jnp.where(left, w, e_roll).astype(BF16)
        q2_ref[:, odd] = jnp.where(left, w_roll, e).astype(BF16)
        k2_ref[:, even] = jnp.where(held, jnp.where(left, k, k_roll), 0.0).astype(BF16)
        k2_ref[:, odd] = jnp.where(held, jnp.where(left, k_roll, k), 0.0).astype(BF16)


def project(x, kind, wq, bq, wk, bk, wv, bv, rows=512):
    length, model = x.shape
    width = wk.shape[1]
    rows = min(rows, length)
    tile = lambda w: pl.BlockSpec((rows, w), lambda i: (i, 0))
    return pl.pallas_call(
        project_kernel,
        grid=(length // rows,),
        in_specs=[
            tile(model),
            tile(1),
            whole_block(wq.shape),
            whole_block(bq.shape),
            whole_block(wk.shape),
            whole_block((1, width)),
            whole_block(wv.shape),
            whole_block((1, width)),
        ],
        out_specs=[tile(2 * width), tile(2 * width), tile(width)],
        out_shape=[
            struct((length, 2 * width), BF16),
            struct((length, 2 * width), BF16),
            struct((length, width), BF16),
        ],
        compiler_params=params(63),
        cost_estimate=cost(12 * length * model * width, 16 * model * width + 12 * length * width),
        name="project",
    )(x, kind, wq, bq, wk, bk.reshape(1, width), wv, bv.reshape(1, width))


def key_extra(live, rows):
    lane = lax.broadcasted_iota(jnp.int32, (rows, 2 * HD), 1)
    return jnp.where(
        lane == 0, jnp.where(live, 0.0, MASKED), jnp.where(lane < 4, 1.0, 0.0)
    ).astype(BF16)


def attend_kernel(q2_ref, k2_ref, v_ref, live_ref, out_ref, extra_ref, turned_ref, both_ref):
    length = k2_ref.shape[0]
    h = pl.program_id(1)

    @pl.when(h == 0)
    def _():
        turned = v_ref[...].astype(F32).T.astype(BF16)
        turned_ref[0] = turned[:HD]
        turned_ref[1] = turned[HD:]

    lane = lax.broadcasted_iota(jnp.int32, (length, 2 * HD), 1)
    one = jnp.where(lane == 0, 1.0, 0.0).astype(BF16)
    keys = jnp.concatenate([k2_ref[...], key_extra(live_ref[...] > 0.5, length)], axis=1)
    query = jnp.concatenate([q2_ref[...], one], axis=1)
    scores = mm(keys, query, NT)
    top = jnp.max(scores, axis=0, keepdims=True)
    weights = jnp.exp(scores - top)
    norm = jnp.sum(weights, axis=0, keepdims=True)
    summed = mm(turned_ref[h], weights.astype(BF16), NN)
    both_ref[h] = summed * (1.0 / norm)
    pieces = three_pieces(-(top + jnp.log(norm)))
    filled = jnp.concatenate(
        [jnp.ones((1, length), F32), *pieces, jnp.zeros((2 * HD - 4, length), F32)], axis=0
    )
    extra_ref[...] = filled.T.astype(BF16)

    @pl.when(h == 1)
    def _():
        out_ref[...] = jnp.concatenate([both_ref[0], both_ref[1]], axis=0).T.astype(BF16)


def attend(q2, k2, v, live):
    length, width = v.shape
    head = pl.BlockSpec((length, 2 * HD), lambda p, h: (0, 2 * p + h))
    pair = pl.BlockSpec((length, 2 * HD), lambda p, h: (0, p))
    return pl.pallas_call(
        attend_kernel,
        grid=(width // (2 * HD), 2),
        in_specs=[head, head, pair, whole_block((length, 1))],
        out_specs=[pair, head],
        out_shape=[struct((length, width), BF16), struct((length, 2 * width), BF16)],
        scratch_shapes=[pltpu.VMEM((2, HD, length), BF16), pltpu.VMEM((2, HD, length), F32)],
        compiler_params=params(63),
        cost_estimate=cost(10 * length * length * width, 20 * length * width, length * length * width // HD),
        name="attend",
    )(q2, k2, v, live)


def attend_back_kernel(
    count, group, y_ref, q2_ref, extra_ref, k2_ref, v_ref, o_ref, own_ref, got_ref, live_ref, kind_ref, columns_ref, pick_ref,
    wq_hbm, wk_hbm, wv_hbm, turned_hbm, first_hbm, *rest,
):
    outs = count + (2 if group is None else 4)
    part_hbm, grads_hbm = rest[:count], rest[count:outs]
    (
        dk_ref, dv_ref, dq_ref, product_ref, d_ref, all_ref, sums_ref, weights_ref, turned_ref, first_ref,
        part_ref, grads_ref, in_sem, out_sem,
    ) = rest[outs:]
    length = k2_ref.shape[0]
    width = wk_hbm.shape[1]
    p, h = pl.program_id(0), pl.program_id(1)
    pairs = width // (2 * HD)
    lane = lax.broadcasted_iota(jnp.int32, (length, 2 * HD), 1)
    left = lane < HD

    def arriving():
        copies = [
            pltpu.make_async_copy(wq_hbm.at[c], weights_ref.at[:, width * c : width * (c + 1)], in_sem.at[c])
            for c in range(4)
        ]
        copies.append(pltpu.make_async_copy(wk_hbm, weights_ref.at[:, 4 * width : 5 * width], in_sem.at[4]))
        copies.append(pltpu.make_async_copy(wv_hbm, weights_ref.at[:, 5 * width : 6 * width], in_sem.at[5]))
        copies.append(pltpu.make_async_copy(turned_hbm, turned_ref, in_sem.at[6]))
        copies.append(pltpu.make_async_copy(first_hbm, first_ref, in_sem.at[7]))
        return copies

    @pl.when(jnp.logical_and(p == 0, h == 0))
    def _():
        for copy in arriving():
            copy.start()

    @pl.when(h == 0)
    def _():
        first = y_ref[0] == 0
        own, got = own_ref[...], got_ref[...]
        joined = jnp.concatenate([jnp.where(first, own, got), jnp.where(first, got, own)], axis=0)
        product_ref[...] = joined * o_ref[...].astype(F32)
        d_ref[...] = joined.astype(BF16)

    d_context = d_ref[...]
    base = HD * (1 - h)
    mine = jnp.logical_and(lane >= HD - base, lane < 2 * HD - base)
    delta = jnp.sum(jnp.where(mine, product_ref[...], 0.0), axis=1, keepdims=True)
    high, middle, low = three_pieces(-delta)
    pieces = jnp.where(
        lane == base, high, jnp.where(lane == base + 1, middle, jnp.where(lane == base + 2, low, 0.0))
    ).astype(BF16)
    d_wide = jnp.where(mine, d_context, pieces)
    q2, k2 = q2_ref[...], k2_ref[...]
    query = jnp.concatenate([q2, extra_ref[...]], axis=1)
    keys = jnp.concatenate([k2, key_extra(live_ref[...] > 0.5, length)], axis=1)
    probs = jnp.exp(mm(keys, query, NT))
    ones = jnp.where((lane >= base) & (lane < base + 3), 1.0, 0.0).astype(BF16)
    d_probs = mm(jnp.where(mine, v_ref[...], ones), d_wide, NT)
    d_scores = (probs * d_probs).astype(BF16)
    dv_ref[h] = mm(probs.astype(BF16), d_context, NN)
    dk_ref[h] = mm(d_scores, q2, NN)
    dq_ref[h] = mm(k2, d_scores, TN).T * (1.0 / math.sqrt(HD))

    @pl.when(h == 1)
    def _():
        entity = kind_ref[...] > 0.5
        even, odd = dq_ref[0], dq_ref[1]
        to_word = jnp.where(left, even, pltpu.roll(odd, HD, 1)).astype(BF16).astype(F32)
        to_entity = jnp.where(left, pltpu.roll(even, HD, 1), odd).astype(BF16).astype(F32)
        even, odd = dk_ref[0], dk_ref[1]
        even = jnp.where(entity, pltpu.roll(even, HD, 1), even)
        odd = jnp.where(entity, odd, pltpu.roll(odd, HD, 1))
        grads = [
            jnp.where(entity, 0.0, to_word),
            jnp.where(entity, 0.0, to_entity),
            jnp.where(entity, to_word, 0.0),
            jnp.where(entity, to_entity, 0.0),
            jnp.where(left, even, odd).astype(BF16).astype(F32),
            jnp.where(left, dv_ref[0], dv_ref[1]).astype(BF16).astype(F32),
        ]
        for c, grad in enumerate(grads):
            all_ref[p, c] = grad.astype(BF16)
        sums = [jnp.sum(grad, axis=0, keepdims=True) for grad in grads]
        sums_ref[p] = jnp.concatenate([*sums, jnp.zeros((2, 2 * HD), F32)], axis=0)

    @pl.when(jnp.logical_and(p == pairs - 1, h == 1))
    def _():
        for copy in arriving():
            copy.wait()
        grads = jnp.concatenate([all_ref[k, c] for c in range(6) for k in range(pairs)], axis=1)
        half = first_ref.shape[0]
        leaving = []

        def leave(source, target):
            copy = pltpu.make_async_copy(source, target, out_sem.at[len(leaving)])
            copy.start()
            leaving.append(copy)

        for i in range(2):
            rows = slice(i * half, (i + 1) * half)
            total = mm(grads[rows], weights_ref[...], NT)
            part_ref[rows, :] = total + jnp.where(y_ref[0] == i, first_ref[...], 0.0)
        begin = 0
        for target in part_hbm:
            leave(part_ref.at[begin : begin + target.shape[0], :], target)
            begin += target.shape[0]
        model = turned_ref.shape[0]
        sums = jnp.concatenate([sums_ref[k] for k in range(pairs)], axis=1)
        pieces = jnp.concatenate([piece.astype(BF16) for piece in three_pieces(sums)], axis=0)
        picked = mm(pick_ref[...], pieces, NT)
        biases = picked[:, :6] + picked[:, 8:14] + picked[:, 16:22]
        extra = jnp.concatenate(
            [biases, columns_ref[...], jnp.zeros((model, 128 - 6 - columns_ref.shape[1]), F32)], axis=1
        )
        lower = y_ref[1] % 2 == 0

        def place(array, a, b, value):
            if group is None:
                grads_ref[array, :, a:b] = value
                return
            blocks = value.reshape(model // (2 * group), 2, group, b - a)
            first, second = blocks[:, 0], blocks[:, 1]
            for k, (one, other) in enumerate(((first, second), (second, first))):
                picked_rows = jnp.where(lower, one, other).reshape(model // 2, b - a)
                grads_ref[array, k * (model // 2) : (k + 1) * (model // 2), a:b] = picked_rows

        for array in range(2):
            for i in range(3):
                cols = slice(width * (3 * array + i), width * (3 * array + i + 1))
                place(array, width * i, width * (i + 1), mm(turned_ref[...], grads[:, cols], NN))
            wide = 3 * width
            if array:
                place(array, wide, wide + 128, extra)
                wide += 128
            if group is None:
                leave(grads_ref.at[array, :, :wide], grads_hbm[array])
            else:
                for k in (1, 0):
                    rows = slice(k * (model // 2), (k + 1) * (model // 2))
                    leave(grads_ref.at[array, rows, :wide], grads_hbm[2 * array + k])
        for copy in leaving:
            copy.wait()


def attend_back(
    y, q2, extra, k2, v, o, own, got, live, kind, columns, pick, wq, wk, wv, turned, first, chunks, group
):
    length, width = v.shape
    half, model = first.shape
    pairs = width // (2 * HD)
    head = pl.BlockSpec((length, 2 * HD), lambda p, h, *_: (0, 2 * p + h))
    pair = pl.BlockSpec((length, 2 * HD), lambda p, h, *_: (0, p))
    part = pl.BlockSpec((half, 2 * HD), lambda p, h, *_: (0, p))
    anywhere = pl.BlockSpec(memory_space=pl.ANY)
    shapes = [struct((rows, model), F32) for rows in chunks]
    for wide in (3 * width, 3 * width + 128):
        shapes += [struct((model, wide), F32)] if group is None else [struct((model // 2, wide), F32)] * 2
    return pl.pallas_call(
        functools.partial(attend_back_kernel, len(chunks), group),
        grid_spec=pltpu.PrefetchScalarGridSpec(
            num_scalar_prefetch=1,
            grid=(pairs, 2),
            in_specs=[
                head, head, head, pair, pair, part, part, whole_block((length, 1)), whole_block((length, 1)),
                whole_block(columns.shape), whole_block(pick.shape),
                *[anywhere] * 5,
            ],
            out_specs=[anywhere] * len(shapes),
            scratch_shapes=[
                *[pltpu.VMEM((2, length, 2 * HD), F32)] * 3,
                pltpu.VMEM((length, 2 * HD), F32),
                pltpu.VMEM((length, 2 * HD), BF16),
                pltpu.VMEM((pairs, 6, length, 2 * HD), BF16),
                pltpu.VMEM((pairs, 8, 2 * HD), F32),
                pltpu.VMEM((model, 6 * width), BF16),
                pltpu.VMEM((model, length), BF16),
                pltpu.VMEM((half, model), F32),
                pltpu.VMEM((length, model), F32),
                pltpu.VMEM((2, model, 3 * width + 128), F32),
                pltpu.SemaphoreType.DMA((8,)),
                pltpu.SemaphoreType.DMA((len(shapes),)),
            ],
        ),
        out_shape=shapes,
        compiler_params=params(63),
        cost_estimate=cost(20 * length * length * width, 40 * length * width, length * length * width // HD),
        name="attend_back",
    )(y, q2, extra, k2, v, o, own, got, live, kind, columns, pick, wq, wk, wv, turned, first)


def normalise(value):
    centre = value - jnp.mean(value, axis=-1, keepdims=True)
    inverse = lax.rsqrt(jnp.mean(centre * centre, axis=-1, keepdims=True) + NORM_EPS)
    return centre * inverse, inverse


def normalise_back(scaled, normal, inverse):
    return inverse * (
        scaled
        - jnp.mean(scaled, axis=-1, keepdims=True)
        - normal * jnp.mean(scaled * normal, axis=-1, keepdims=True)
    )


def gelu_pair(values):
    cumulative = 0.5 * (1.0 + lax.erf(values * (1.0 / math.sqrt(2.0))))
    density = jnp.exp(-0.5 * values * values) * (1.0 / math.sqrt(2.0 * math.pi))
    return values * cumulative, cumulative + values * density


def column_sum(value):
    return jnp.sum(value, axis=0, keepdims=True)


def group_cuts(half):
    return half // 384 * 256, half // 128 * 5 // 6 * 128


def middle_kernel(at_ref, x_ref, cot_ref, live_ref, own_ref, got_ref, wo_ref, wi_hbm, wu_hbm, *rest):
    arrived = rest[:SLICES]
    arrived_late = rest[SLICES : 2 * SLICES]
    (
        vec_ref, bias_ref, out_ref, out_late_ref, first_ref, dco_ref, cross_ref, left_ref,
        keep0_ref, keep1_ref, keep2_ref, early_send_ref, late_send_ref,
        sums_ref, inner_sums_ref, slope_ref, early_ref, late_ref, wi_ref, wu_ref, raw_ref, raw_late_ref, in_sem,
    ) = rest[2 * SLICES :]
    step = pl.program_id(0)
    me = at_ref[1]
    lower = me % 2 == 0
    hidden, model, width = wi_hbm.shape[1], x_ref.shape[1], wo_ref.shape[0]
    half = hidden // 2
    cut = [width // SLICES, (width + model) // SLICES, (width + 2 * model) // SLICES]
    ca, cb = group_cuts(half)
    left_sends = ((late_send_ref, 0), (early_send_ref, 0), (late_send_ref, model))
    start0, start1 = 2 * model, 2 * model + 2 * ca + width

    def weight_copies():
        stages = [[], [], [], [], []]
        for k in range(SLICES):
            for stage, source, target in (
                (0, arrived[k].at[: cut[0], :], raw_ref.at[k, : cut[0], :]),
                (2, arrived[k].at[cut[0] :, :], raw_ref.at[k, cut[0] :, :]),
                (4, arrived_late[k], raw_late_ref.at[k]),
            ):
                stages[stage].append(pltpu.make_async_copy(source, target, in_sem.at[stage * SLICES + k]))
        stages[1].append(pltpu.make_async_copy(wi_hbm, wi_ref, in_sem.at[SLICES]))
        stages[3].append(pltpu.make_async_copy(wu_hbm, wu_ref, in_sem.at[3 * SLICES]))
        return stages

    def arrive(*wanted):
        @pl.when(step == 0)
        def _():
            stages = weight_copies()
            for stage in wanted:
                for copy in stages[stage]:
                    copy.wait()
            for k in range(SLICES):
                if 0 in wanted:
                    early_ref[me ^ k, : cut[0], :] = raw_ref[k, : cut[0], :].astype(BF16)
                if 2 in wanted:
                    early_ref[me ^ k, cut[0] :, :] = raw_ref[k, cut[0] :, :].astype(BF16)
                if 4 in wanted:
                    late_ref[me ^ k] = raw_late_ref[k].astype(BF16)

    @pl.when(step == 0)
    def _():
        for stage in weight_copies():
            for copy in stage:
                copy.start()

    arrive(0)

    def foreign(ref, a, b):
        return ref[:, a:b, :].reshape(SLICES * (b - a), model)

    vec = [vec_ref[k : k + 1, :] for k in range(6)]
    got = got_ref[...].astype(BF16)
    own = own_ref[...]
    wo_far = foreign(early_ref, 0, cut[0])
    first = mm(own, wo_ref[...], NN) + mm(got, wo_far, NN) + vec[0] + x_ref[...].astype(F32)
    n1, inv1 = normalise(first)
    normed = n1 * vec[1] + vec[2]
    low = normed.astype(BF16)

    def inner(part):
        if part < 2:
            return wi_ref[:, half * part : half * (part + 1)]
        return foreign(early_ref, cut[part - 2], cut[part - 1])

    def outer(part):
        if part < 2:
            return wu_ref[half * part : half * (part + 1), :]
        per = SLICES // 2
        block = late_ref[per * (part - 2) : per * (part - 1), :, :]
        return block.reshape(half, model)

    def both(index, value):
        left_ref[index] = value
        ref, at = left_sends[index]
        ref[:, at : at + model] = value.astype(F32)

    def split(values):
        first, second = (value.astype(F32) for value in values)
        keep = jnp.where(lower, first, second).astype(BF16)
        return keep, jnp.where(lower, second, first)

    both(0, low)
    second = vec[3] + normed
    arrive(1, 3)
    for far in range(2):
        if far:
            arrive(2, 4)
        pair = []
        for part in (2 * far, 2 * far + 1):
            pre = mm(low, inner(part), NN) + bias_ref[part : part + 1, :]
            active, slope = gelu_pair(pre)
            active = active.astype(BF16)
            slope_ref[:, half * part : half * (part + 1)] = slope
            pair.append(active)
            second = second + mm(active, outer(part), NN)
        keep, send = split(pair)
        at1 = (half - ca + half - cb) * far + half - ca
        keep2_ref[:, cb * far : cb * (far + 1)] = keep[:, :cb]
        keep1_ref[:, at1 : at1 + half - cb] = keep[:, cb:]
        early_send_ref[:, model + cb * far : model + cb * (far + 1)] = send[:, :cb]
        late_send_ref[:, start1 + at1 : start1 + at1 + half - cb] = send[:, cb:]
    n2, inv2 = normalise(second)
    live = live_ref[...] > 0.5
    result = jnp.where(live, n2 * vec[4] + vec[5], 0.0).astype(BF16)
    out_ref[...] = result
    cross_ref[:, width:] = result[:, : model // 2].astype(F32)
    out_late_ref[...] = result[:, model // 2 :].astype(F32)
    dz = jnp.where(live, cot_ref[...].astype(F32), 0.0)
    d_second = normalise_back(dz * vec[4], n2, inv2)
    d_low = d_second.astype(BF16)
    both(1, d_low)
    d_normed = d_second
    inner_sums = []
    for far in range(2):
        pair = []
        for part in (2 * far, 2 * far + 1):
            d_hidden = mm(d_low, outer(part), NT)
            d_inner = (d_hidden * slope_ref[:, half * part : half * (part + 1)]).astype(BF16)
            pair.append(d_inner)
            inner_sums.append(column_sum(d_inner.astype(F32)))
            d_normed = d_normed + mm(d_inner, inner(part), NT)
        keep, send = split(pair)
        at1 = (half - ca + half - cb) * far
        keep0_ref[:, ca * far : ca * (far + 1)] = keep[:, :ca]
        keep1_ref[:, at1 : at1 + half - ca] = keep[:, ca:]
        late_send_ref[:, start0 + ca * far : start0 + ca * (far + 1)] = send[:, :ca]
        late_send_ref[:, start1 + at1 : start1 + at1 + half - ca] = send[:, ca:]
    d_first = normalise_back(d_normed * vec[1], n1, inv1)
    first_ref[...] = d_first
    d_attn = d_first.astype(BF16)
    both(2, d_attn)
    dco_ref[...] = mm(d_attn, wo_ref[...], NT).astype(BF16).astype(F32)
    cross_ref[:, :width] = mm(d_attn, wo_far, NT).astype(BF16).astype(F32)
    keep, send = split((own, got))
    keep0_ref[:, 2 * ca :] = keep
    late_send_ref[:, start0 + 2 * ca : start1] = send
    sums = jnp.concatenate(
        [
            column_sum(d_first),
            column_sum(d_normed * n1),
            column_sum(d_normed),
            column_sum(d_second),
            column_sum(dz * n2),
            column_sum(dz),
            jnp.zeros((2, model), F32),
        ],
        axis=0,
    )
    inner_sums = jnp.concatenate([*inner_sums, jnp.zeros((4, half), F32)], axis=0)

    @pl.when(step == 0)
    def _():
        sums_ref[...] = sums
        inner_sums_ref[...] = inner_sums

    @pl.when(step != 0)
    def _():
        sums_ref[...] += sums
        inner_sums_ref[...] += inner_sums


def middle(at, x, cot, live, context, got, wo, wi, wu, early, late, vec, bias, rows=256):
    half, width = got.shape
    model, hidden = wi.shape
    rows = min(rows, half)
    steps = half // rows
    mine = lambda w: pl.BlockSpec((rows, w), lambda i, s: (i + s[0] * steps, 0))
    tile = lambda w: pl.BlockSpec((rows, w), lambda i, s: (i, 0))
    ca, cb = group_cuts(hidden // 2)
    widths = (2 * ca + width, 2 * (hidden - ca - cb), 2 * cb)
    return pl.pallas_call(
        middle_kernel,
        grid_spec=pltpu.PrefetchScalarGridSpec(
            num_scalar_prefetch=1,
            grid=(steps,),
            in_specs=[
                mine(model), mine(model), mine(1), mine(width), tile(width),
                whole_block(wo.shape), *[pl.BlockSpec(memory_space=pl.ANY)] * (2 + 2 * SLICES),
                whole_block(vec.shape), whole_block(bias.shape),
            ],
            out_specs=[
                tile(model), tile(model // 2), tile(model), tile(width), tile(width + model // 2),
                pl.BlockSpec((3, rows, model), lambda i, s: (0, i, 0)),
                *(tile(w) for w in widths),
                tile(model + widths[2]), tile(2 * model + widths[0] + widths[1]),
                pl.BlockSpec((8, model), lambda i, s: (0, 0)),
                pl.BlockSpec((8, hidden // 2), lambda i, s: (0, 0)),
            ],
            scratch_shapes=[
                pltpu.VMEM((rows, 2 * hidden), F32),
                pltpu.VMEM((SLICES, *early[0].shape), BF16),
                pltpu.VMEM((SLICES, *late[0].shape), BF16),
                pltpu.VMEM(wi.shape, BF16),
                pltpu.VMEM(wu.shape, BF16),
                pltpu.VMEM((SLICES, *early[0].shape), F32),
                pltpu.VMEM((SLICES, *late[0].shape), F32),
                pltpu.SemaphoreType.DMA((5 * SLICES,)),
            ],
        ),
        out_shape=[
            struct((half, model), BF16), struct((half, model // 2), F32), struct((half, model), F32),
            struct((half, width), F32), struct((half, width + model // 2), F32),
            struct((3, half, model), BF16),
            *(struct((half, w), BF16) for w in widths),
            struct((half, model + widths[2]), F32),
            struct((half, 2 * model + widths[0] + widths[1]), F32),
            struct((8, model), F32), struct((8, hidden // 2), F32),
        ],
        compiler_params=params(63),
        cost_estimate=cost(
            16 * half * model * (hidden + width // 2), 24 * model * hidden + 80 * half * model, 6 * half * hidden
        ),
        name="middle",
    )(at, x, cot, live, context, got, wo, wi, wu, *early, *late, vec, bias)


def weight_kernel(plan, count, bit_ref, left_hbm, *rest):
    groups = len(plan)
    keep_hbm, rest = rest[:groups], rest[groups:]
    got_hbm, rest = rest[:count], rest[count:]
    outs, rest = rest[: 2 * groups], rest[2 * groups :]
    left_ref, left_got_ref, rest = rest[0], rest[1], rest[2:]
    keep_refs, rest = rest[:groups], rest[groups:]
    got_refs, rest = rest[:groups], rest[groups:]
    stage_refs, (in_sem, out_sem) = rest[:groups], rest[groups:]
    model = left_ref.shape[2]

    arriving, ready = [], {}

    def bring(key, source, target):
        if key not in ready:
            ready[key] = pltpu.make_async_copy(source, target, in_sem.at[len(arriving)])
            arriving.append(ready[key])

    for g, (_, _, tiles, (right_array, right_at)) in enumerate(plan):
        for index, (left_array, left_at), a, b in tiles:
            bring(("left", index), left_hbm.at[index], left_ref.at[index])
            bring(
                ("left got", index), got_hbm[left_array].at[:, left_at : left_at + model], left_got_ref.at[index]
            )
            bring(("keep", g, a), keep_hbm[g].at[:, a:b], keep_refs[g].at[:, a:b])
            bring(
                ("got", g, a), got_hbm[right_array].at[:, right_at + a : right_at + b], got_refs[g].at[:, a:b]
            )
    for copy in arriving:
        copy.start()
    waited = set()

    def need(*keys):
        for key in keys:
            if key not in waited:
                waited.add(key)
                ready[key].wait()

    leaving = []
    for g, (slot, group, tiles, _) in enumerate(plan):
        width = keep_refs[g].shape[1]
        for index, _, a, b in tiles:
            need(("left", index), ("left got", index), ("keep", g, a), ("got", g, a))
            left = jnp.concatenate([left_ref[index], left_got_ref[index].astype(BF16)], axis=0)
            right = jnp.concatenate([keep_refs[g][:, a:b], got_refs[g][:, a:b].astype(BF16)], axis=0)
            value = mm(left, right, TN)
            if slot is None:
                part, base = (0, 0) if 2 * b <= width else (1, width // 2)
                stage_refs[g][part, :, a - base : b - base] = value
                parts = ((part, a - base, b - base),)
            else:
                pairs = value.reshape(model // (2 * group), 2, group, b - a)
                kept = bit_ref[slot] == 0
                first, second = pairs[:, 0], pairs[:, 1]
                for part, (one, other) in enumerate(((first, second), (second, first))):
                    picked = jnp.where(kept, one, other)
                    stage_refs[g][part, :, a:b] = picked.reshape(model // 2, b - a)
                parts = ((1, a, b), (0, a, b))
            for part, a, b in parts:
                copy = pltpu.make_async_copy(
                    stage_refs[g].at[part, :, a:b], outs[2 * g + part].at[:, a:b], out_sem.at[len(leaving)]
                )
                copy.start()
                leaving.append(copy)
    for copy in leaving:
        copy.wait()


def weight_grads(at, left, keeps, received, plan):
    _, depth, model = left.shape
    stages, shapes, steps = [], [], 0
    for (slot, _, tiles, _), keep in zip(plan, keeps):
        width = keep.shape[1]
        shape = (model, width // 2) if slot is None else (model // 2, width)
        stages.append(pltpu.VMEM((2, *shape), F32))
        shapes += [struct(shape, F32)] * 2
        steps += len(tiles)
    columns = sum(keep.shape[1] for keep in keeps)
    anywhere = pl.BlockSpec(memory_space=pl.ANY)
    return pl.pallas_call(
        functools.partial(weight_kernel, plan, len(received)),
        grid_spec=pltpu.PrefetchScalarGridSpec(
            num_scalar_prefetch=1,
            grid=(1,),
            in_specs=[anywhere] * (1 + len(keeps) + len(received)),
            out_specs=[anywhere] * len(shapes),
            scratch_shapes=[
                pltpu.VMEM(left.shape, BF16),
                pltpu.VMEM(left.shape, F32),
                *(pltpu.VMEM(keep.shape, BF16) for keep in keeps),
                *(pltpu.VMEM(keep.shape, F32) for keep in keeps),
                *stages,
                pltpu.SemaphoreType.DMA((6 + 2 * steps,)),
                pltpu.SemaphoreType.DMA((2 * steps,)),
            ],
        ),
        out_shape=shapes,
        compiler_params=params(63),
        cost_estimate=cost(4 * depth * model * columns, 4 * model * columns + 8 * depth * columns),
        name="weight_grads",
    )(at, left, *keeps, *received)


def combine_kernel(plan, count, bits_ref, *rest):
    outs = len(plan)
    arrays, targets = rest[:count], rest[count : count + outs]
    buffers, (in_sem, out_sem) = rest[count + outs : -2], rest[-2:]
    copies = []
    for pieces in plan:
        for _, terms in pieces:
            for array, chosen, a, b, _ in terms:
                index = [slice(None)] * len(arrays[array].shape)
                for axis, (bit, mine) in chosen:
                    index[axis] = pl.ds(bits_ref[bit] if mine else 1 - bits_ref[bit], 1)
                index[-1] = slice(a, b)
                k = len(copies)
                copies.append(pltpu.make_async_copy(arrays[array].at[tuple(index)], buffers[k], in_sem.at[k]))
    for copy in copies:
        copy.start()
    k = 0
    leaving = []
    for target, pieces in zip(targets, plan):
        for at, terms in pieces:
            first = k
            total = None
            for *_, gate in terms:
                copies[k].wait()
                value = buffers[k][...]
                if gate is not None:
                    value = jnp.where(bits_ref[0] == gate, value, 0.0)
                total = value if total is None else total + value
                k += 1
            if len(terms) > 1:
                buffers[first][...] = total
            width = buffers[first].shape[-1]
            index = (*[slice(None)] * (len(target.shape) - 1), slice(at, at + width))
            copy = pltpu.make_async_copy(buffers[first], target.at[index], out_sem.at[len(leaving)])
            copy.start()
            leaving.append(copy)
    for copy in leaving:
        copy.wait()


def combine(bit_values, outputs):
    arrays, plan, shapes, buffers, moved = [], [], [], [], 0
    for pieces in outputs:
        at, planned = 0, []
        for terms in pieces:
            named = []
            for array, chosen, a, b, gate in terms:
                place = [k for k, other in enumerate(arrays) if other is array]
                if not place:
                    place = [len(arrays)]
                    arrays.append(array)
                named.append((place[0], tuple(sorted(chosen.items())), a, b, gate))
                block = tuple(1 if k in chosen else size for k, size in enumerate(array.shape[:-1]))
                buffers.append(pltpu.VMEM((*block, b - a), F32))
                moved += 4 * math.prod(block) * (b - a)
            planned.append((at, named))
            at += b - a
        plan.append(planned)
        shapes.append(struct((*block, at), F32))
    anywhere = pl.BlockSpec(memory_space=pl.ANY)
    pieces = sum(len(planned) for planned in plan)
    return pl.pallas_call(
        functools.partial(combine_kernel, plan, len(arrays)),
        grid_spec=pltpu.PrefetchScalarGridSpec(
            num_scalar_prefetch=1,
            grid=(1,),
            in_specs=[anywhere] * len(arrays),
            out_specs=[anywhere] * len(shapes),
            scratch_shapes=[
                *buffers,
                pltpu.SemaphoreType.DMA((len(buffers),)),
                pltpu.SemaphoreType.DMA((pieces,)),
            ],
        ),
        out_shape=shapes,
        compiler_params=params(63),
        cost_estimate=cost(moved, 2 * moved),
        name="combine",
    )(bit_values, *arrays)


def turn_kernel(value_ref, out_ref):
    out_ref[...] = value_ref[...].astype(F32).T.astype(BF16)


def turn(value, columns=256):
    length, model = value.shape
    return pl.pallas_call(
        turn_kernel,
        grid=(model // columns,),
        in_specs=[pl.BlockSpec((length, columns), lambda i: (0, i))],
        out_specs=pl.BlockSpec((columns, length), lambda i: (i, 0)),
        out_shape=struct((model, length), BF16),
        compiler_params=params(63),
        cost_estimate=cost(length * model, 4 * length * model),
        name="turn",
    )(value)


def place_kernel(y_ref, own_ref, first_ref, second_ref, out_ref):
    mine = pl.program_id(0) == y_ref[0]
    got = jnp.concatenate([first_ref[...], second_ref[...]], axis=1)
    out_ref[...] = jnp.where(mine, own_ref[...].astype(F32), got).astype(BF16)


def place_rows(y, own, first, second):
    half, model = own.shape
    return pl.pallas_call(
        place_kernel,
        grid_spec=pltpu.PrefetchScalarGridSpec(
            num_scalar_prefetch=1,
            grid=(2,),
            in_specs=[
                whole_block(own.shape),
                pl.BlockSpec((half, model // 2), lambda i, s: (0, 1)),
                whole_block(second.shape),
            ],
            out_specs=pl.BlockSpec((half, model), lambda i, s: (i, 0)),
        ),
        out_shape=struct((2 * half, model), BF16),
        compiler_params=params(63),
        cost_estimate=cost(half * model, 12 * half * model),
        name="place_rows",
    )(y, own, first, second)


def per_device(
    devices,
    tokens,
    lengths,
    entity_flags,
    query_weight,
    query_bias,
    key_weight,
    key_bias,
    value_weight,
    value_bias,
    output_weight,
    output_bias,
    attn_gain,
    attn_shift,
    inner_weight,
    inner_bias,
    outer_weight,
    outer_bias,
    final_gain,
    final_shift,
    cotangent,
):
    x = tokens[0]
    length, model = x.shape
    width = key_weight.shape[1]
    hidden = inner_weight.shape[1]
    half = length // 2
    bits = devices.bit_length() - 1
    y = lax.axis_index("tensor")
    d = lax.axis_index("dp")

    def swap(value, mask):
        return lax.ppermute(value, "dp", [(i, i ^ mask) for i in range(devices)])

    def cross(value):
        return lax.ppermute(value, "tensor", [(0, 1), (1, 0)])

    me = d % SLICES
    core = d % 2
    rows = model // devices
    near_mask, far_mask = 96 // rows, 192 // rows
    at = jnp.stack([y, me, (d // near_mask) % 2, (d // far_mask) % 2]).astype(jnp.int32)
    tie = lax.optimization_barrier

    def cut(array, index):
        size = array.shape[0] // SLICES
        return lax.dynamic_slice_in_dim(array, index * size, size, 0)

    def pack(index):
        wide = cut(inner_weight, index)
        early = jnp.concatenate([cut(output_weight, index), wide[:, :model], wide[:, model:]], axis=0)
        return early.astype(F32)

    def pack_late(index):
        return cut(outer_weight, index).astype(F32)

    live = (lax.broadcasted_iota(jnp.int32, (length, 1), 0) < lengths[0]).astype(F32)
    kind = (entity_flags[0] == 1).astype(F32).reshape(length, 1)

    e0 = cross(pack(me))
    far_bias = cross(inner_bias)
    q2, k2, v = project(
        x, kind, query_weight, query_bias, key_weight, key_bias, value_weight, value_bias
    )
    e0, far_bias, l0, l6, q2 = tie((e0, far_bias, pack_late(me), pack_late(me ^ 6), q2))
    e2 = swap(e0, 2)
    e4 = swap(e0, 4)
    l0 = cross(l0)
    e1 = swap(e0, 1)
    context, extra = attend(q2, k2, v, live)
    sent = lax.dynamic_slice_in_dim(context, half * (1 - y), half, 0).astype(F32)
    e1, e2, e4, l0, l6, sent = tie((e1, e2, e4, l0, l6, sent))
    l2 = swap(l0, 2)
    l4 = swap(l0, 4)
    got = cross(sent)
    e6 = swap(e4, 2)
    l6 = cross(l6)
    per = width // devices
    where_row = lax.broadcasted_iota(jnp.int32, (model, width), 0)
    where_bias = lax.broadcasted_iota(jnp.int32, (model, width), 1)
    pick = (where_row == (where_bias // per) * rows + where_bias % per).astype(BF16)
    x_turned = turn(x)
    l2, l4, e2, e4, pick, x_turned = tie((l2, l4, e2, e4, pick, x_turned))
    e3 = swap(e2, 1)
    e5 = swap(e4, 1)
    got, e6, l6, e3, e5, l0, l2, l4 = tie((got, e6, l6, e3, e5, l0, l2, l4))
    l1 = swap(l0, 1)
    l3 = swap(l2, 1)
    l5 = swap(l4, 1)
    l7 = swap(l6, 1)
    e7 = swap(e6, 1)
    early = (e0, e1, e2, e3, e4, e5, e6, e7)
    late = (l0, l1, l2, l3, l4, l5, l6, l7)

    vec = jnp.stack(
        [output_bias, attn_gain, attn_shift, outer_bias, final_gain, final_shift, outer_bias, outer_bias]
    )
    bias = jnp.concatenate([inner_bias, far_bias, inner_bias, far_bias]).reshape(8, hidden // 2)
    (
        out_rows, out_late, d_first, dco, first_cross, left, keep0, keep1, keep2, early_send, late_send,
        sums, inner_sums,
    ) = middle(
        at, x, cotangent[0], live, context, got, output_weight, inner_weight, outer_weight,
        early, late, vec, bias,
    )
    inner_columns = inner_sums[:4].reshape(2, model, 2)
    columns = jnp.concatenate([sums[:6].T, inner_columns[0], inner_columns[1]], axis=1)
    d_got = cross(first_cross)
    early_got = swap(early_send, 1)
    late_got = swap(late_send, 1)
    early_got, columns = tie((early_got, columns))

    ca, cb = group_cuts(hidden // 2)
    da, db = hidden // 2 - ca, hidden // 2 - cb
    normed_at, d_second_at, d_attn_at = (1, 0), (0, 0), (1, model)
    g0_keep, g0_send, g1_keep, g1_send = weight_grads(
        at, left, (keep0, keep1), (early_got, late_got),
        (
            (
                2, near_mask * rows,
                (
                    (0, normed_at, 0, ca), (0, normed_at, ca, 2 * ca),
                    (2, d_attn_at, 2 * ca, 2 * ca + width),
                ),
                (1, 2 * model),
            ),
            (
                None, None,
                (
                    (0, normed_at, 0, da), (1, d_second_at, da, da + db),
                    (0, normed_at, da + db, 2 * da + db), (1, d_second_at, 2 * da + db, 2 * (da + db)),
                ),
                (1, 2 * model + 2 * ca + width),
            ),
        ),
    )
    early_got, g0_send = tie((early_got, g0_send))
    g2_keep, g2_send = weight_grads(
        at, left, (keep2,), (early_got,),
        ((3, far_mask * rows, ((1, (0, 0), 0, cb), (1, (0, 0), cb, 2 * cb)), (0, model)),),
    )
    g0_got = swap(g0_send, near_mask)
    g2_got = swap(g2_send, far_mask)
    g1_got = cross(g1_send)

    g0_send, g1_send, g2_send, dco, d_got = tie((g0_send, g1_send, g2_send, dco, d_got))
    chunks = tuple(length * k // 32 for k in (2, 4, 14, 12))
    group = rows if rows % 8 == 0 else None
    results = attend_back(
        at, q2, extra, k2, v, context, dco, d_got, live, kind, columns, pick,
        query_weight, key_weight, value_weight, x_turned, d_first, chunks, group,
    )
    parts, products = results[: len(chunks)], results[len(chunks) :]
    got_out = cross(out_late)

    def spread(array, done):
        dims = [1 if (1 << (bits - 1 - k)) in done else 2 for k in range(bits)]
        return array.reshape(*dims, rows, array.shape[-1])

    bit_values = jnp.stack([(d >> k) % 2 for k in range(bits)]).astype(jnp.int32)
    rest_masks = [1 << k for k in range(1, bits) if (1 << k) not in (near_mask, far_mask)]

    def term(array, *done):
        array = spread(array, done)
        return (array, {}, 0, array.shape[-1], None)

    def half_of(terms, mask, mine):
        k = mask.bit_length() - 1
        return [(array, {**chosen, bits - 1 - k: (k, mine)}, a, b, gate) for array, chosen, a, b, gate in terms]

    def kept(terms, mask):
        return half_of(terms, mask, True)

    def other(terms, mask):
        return half_of(terms, mask, False)

    def columns_of(terms, first, last):
        return [(array, chosen, a + first, a + last, gate) for array, chosen, a, _, gate in terms]

    def on_core(terms, core_index):
        return [(array, chosen, a, b, core_index) for array, chosen, a, b, _ in terms]

    def whole_of(array):
        return (array, {}, 0, array.shape[-1], None)

    def part_of(array, a, b):
        return (array, {}, a, b, None)

    g0_got, g1_got, g2_got, got_out, parts, products = tie((g0_got, g1_got, g2_got, got_out, parts, products))
    if group is None:
        c = [term(products[0])]
        e = [term(products[1])]
        c_send, e_send = combine(bit_values, [[other(c, 1)], [other(e, 1)]])
        c, e = kept(c, 1), kept(e, 1)
    else:
        c, e = [term(products[0], 1)], [term(products[2], 1)]
        c_send, e_send = spread(products[1], (1,)), spread(products[3], (1,))
    e_got = swap(e_send, 1)
    c_got = swap(c_send, 1)
    g0 = [term(g0_keep, near_mask), term(g0_got, near_mask)]
    g1 = [term(g1_keep), term(g1_got)]
    g2 = [term(g2_keep, far_mask), term(g2_got, far_mask)]
    sends = combine(
        bit_values, [[columns_of(g0, ca, 2 * ca + width)], [other(g1, near_mask)], [other(g2, near_mask)]]
    )
    e_got, c_got, sends, parts = tie((e_got, c_got, sends, parts))
    e.append(whole_of(e_got))
    c.append(whole_of(c_got))
    g0_got = cross(sends[0])
    g2_got = swap(sends[2], near_mask)
    g1_got = swap(sends[1], near_mask)
    (e_send,) = combine(bit_values, [[other(e, far_mask)]])
    e_got = swap(e_send, far_mask)
    part0 = cross(parts[0])
    g0_got, g1_got, g2_got, e_got, part0, parts = tie((g0_got, g1_got, g2_got, e_got, part0, parts))
    t = [
        *on_core(columns_of(g0, 2 * ca, 2 * ca + width), 0),
        *on_core([part_of(g0_got, ca, ca + width)], 1),
    ]
    g0 = [*columns_of(g0, 0, ca), part_of(g0_got, 0, ca)]
    g1 = [*kept(g1, near_mask), whole_of(g1_got)]
    g2 = [*kept(g2, near_mask), whole_of(g2_got)]
    e = [*kept(e, far_mask), whole_of(e_got)]

    sends = combine(
        bit_values,
        [
            [other(terms, far_mask) for terms in (g0, t, g1)],
            [columns_of(g2, cb, 2 * cb)],
            [other(c, near_mask)],
        ],
    )
    sends, parts = tie((sends, parts))
    g2_got = cross(sends[1])
    three_got = swap(sends[0], far_mask)
    c_got = swap(sends[2], near_mask)
    part1 = cross(parts[1])
    three_got, g2_got, c_got, part1, parts = tie((three_got, g2_got, c_got, part1, parts))
    g0 = [*kept(g0, far_mask), part_of(three_got, 0, ca)]
    t = [*kept(t, far_mask), part_of(three_got, ca, ca + width)]
    g1 = [*kept(g1, far_mask), part_of(three_got, ca + width, three_got.shape[-1])]
    g2 = [*columns_of(g2, 0, cb), whole_of(g2_got)]
    c = [*kept(c, near_mask), whole_of(c_got)]

    main = (g0, g1, g2, t)
    sizes = (ca, da + db, cb, width)
    ends = [sum(sizes[:k]) for k in range(len(sizes) + 1)]
    mask = rest_masks[0]
    sends = combine(
        bit_values,
        [[other(terms, mask) for terms in main], [other(e, near_mask)], [other(c, far_mask)]],
    )
    sends, parts = tie((sends, parts))
    got_z = swap(sends[0], mask)
    part2 = cross(parts[2])
    c_got = swap(sends[2], far_mask)
    e_got = swap(sends[1], near_mask)
    layer_out = place_rows(at, out_rows, d_got, got_out)
    got_z, e_got, c_got, part2, parts, layer_out = tie((got_z, e_got, c_got, part2, parts, layer_out))
    main = [[*kept(terms, mask), part_of(got_z, ends[n], ends[n + 1])] for n, terms in enumerate(main)]
    e = [*kept(e, near_mask), whole_of(e_got)]
    c = [*kept(c, far_mask), whole_of(c_got)]
    for mask in rest_masks[1:]:
        (send,) = combine(bit_values, [[other(terms, mask) for terms in main]])
        got_z = swap(send, mask)
        main = [[*kept(terms, mask), part_of(got_z, ends[n], ends[n + 1])] for n, terms in enumerate(main)]

    for k, mask in enumerate(rest_masks):
        outputs = [[other(c, mask), other(e, mask)], [kept(c, mask), kept(e, mask)]]
        if k == 0:
            outputs += [[other(terms, 1) for terms in main], [kept(terms, 1) for terms in main]]
        sends = combine(bit_values, outputs)
        if k == 0:
            sends, parts = tie((sends, parts))
        pair_got = swap(sends[0], mask)
        if k == 0:
            part3 = cross(parts[3])
            got_last = swap(sends[2], 1)
            keep = sends[3]
            pair_got, got_last, part3 = tie((pair_got, got_last, part3))
        c = [part_of(sends[1], 0, 3 * width), part_of(pair_got, 0, 3 * width)]
        e = [part_of(sends[1], 3 * width, sends[1].shape[-1]), part_of(pair_got, 3 * width, sends[1].shape[-1])]
    pair = (sends[1] + pair_got).reshape(rows, -1)
    c, e = pair[:, : 3 * width], pair[:, 3 * width :]
    last = e[:, 3 * width + 6 : 3 * width + 16]
    last_got = cross(last)
    small = last[:, :6] + last_got[:, :6]
    inner_two = last[:, 6:8] + last_got[:, 8:]

    got_last = got_last.reshape(rows, -1)
    keep = keep.reshape(rows, -1)
    low_half = jnp.where(core == 0, keep, got_last)
    high_half = jnp.where(core == 0, got_last, keep)
    at2 = ca + da + db
    inner_half = lambda array: [array[:, : ca + da]]
    at3 = at2 + cb
    outer_half = lambda array: [array[:, at2:at3], array[:, ca + da : at2]]
    t = keep[:, at3:] + got_last[:, at3:]
    grad_inner = jnp.concatenate(inner_half(low_half) + inner_half(high_half), axis=1)
    grad_outer = jnp.concatenate(outer_half(low_half) + outer_half(high_half), axis=1).T
    sent_parts = (part0, part1, part2, part3)
    input_grad = jnp.concatenate([(a + b).astype(BF16) for a, b in zip(parts, sent_parts)], axis=0)

    piece = lambda array, k: array[:, width * k : width * (k + 1)]
    grad_query_weight = jnp.stack([piece(c, 0), piece(c, 1), piece(c, 2), piece(e, 0)])
    biases = e[:per, 3 * width : 3 * width + 6].T
    return (
        layer_out[None],
        input_grad[None],
        grad_query_weight,
        biases[:4],
        piece(e, 1),
        biases[4],
        piece(e, 2),
        biases[5],
        t.T,
        small[:, 0],
        small[:, 1],
        small[:, 2],
        grad_inner,
        inner_two.reshape(2 * rows),
        grad_outer,
        small[:, 3],
        small[:, 4],
        small[:, 5],
    )


def solution(mesh):
    return jax.shard_map(
        functools.partial(per_device, mesh.shape["dp"]),
        mesh=mesh,
        in_specs=(
            P("dp", None, None),
            P("dp"),
            P("dp", None),
            P(None, None, "tensor"),
            P(None, "tensor"),
            P(None, "tensor"),
            P("tensor"),
            P(None, "tensor"),
            P("tensor"),
            P("tensor", None),
            P(),
            P(),
            P(),
            P(None, "tensor"),
            P("tensor"),
            P("tensor", None),
            P(),
            P(),
            P(),
            P("dp", None, None),
        ),
        out_specs=(
            P("dp", None, None),
            P("dp", None, None),
            P(None, "dp", "tensor"),
            P(None, ("tensor", "dp")),
            P("dp", "tensor"),
            P(("tensor", "dp")),
            P("dp", "tensor"),
            P(("tensor", "dp")),
            P("tensor", "dp"),
            P("dp"),
            P("dp"),
            P("dp"),
            P("dp", "tensor"),
            P(("tensor", "dp")),
            P("tensor", "dp"),
            P("dp"),
            P("dp"),
            P("dp"),
        ),
        check_vma=False,
    )
```

```python
import functools
import math

import jax
import jax.numpy as jnp
from jax import lax
from jax.experimental import pallas as pl
from jax.experimental.pallas import tpu as pltpu
from jax.sharding import PartitionSpec as P

HD = 64
SLICES = 8
MASKED = -1e30
NORM_EPS = 1e-05

F32 = jnp.float32
BF16 = jnp.bfloat16
NN = (((1,), (0,)), ((), ()))
NT = (((1,), (1,)), ((), ()))
TN = (((0,), (0,)), ((), ()))


def mm(left, right, dims):
    return lax.dot_general(left, right, dims, preferred_element_type=F32)


def struct(shape, kind):
    return jax.ShapeDtypeStruct(shape, kind)


def params(mib):
    return pltpu.CompilerParams(vmem_limit_bytes=mib << 20)


def cost(flops, moved, special=0):
    return pl.CostEstimate(flops=int(flops), bytes_accessed=int(moved), transcendentals=int(special))


def whole_block(shape):
    return pl.BlockSpec(shape, lambda *_: (0,) * len(shape), pipeline_mode=pl.Buffered(1))


def three_pieces(value):
    high = value.astype(BF16).astype(F32)
    rest = value - high
    middle = rest.astype(BF16).astype(F32)
    return high, middle, rest - middle


def project_kernel(x_ref, kind_ref, wq_ref, bq_ref, wk_ref, bk_ref, wv_ref, bv_ref, q2_ref, k2_ref, v_ref):
    x = x_ref[...]
    entity = kind_ref[...] > 0.5
    rows = x.shape[0]
    width = wk_ref.shape[1]

    weights = jnp.concatenate([*(wq_ref[c] for c in range(4)), wk_ref[...], wv_ref[...]], axis=1)
    biases = jnp.concatenate([*(bq_ref[c : c + 1, :] for c in range(4)), bk_ref[...], bv_ref[...]], axis=1)
    products = mm(x, weights, NN) + biases

    def query(c):
        return products[:, width * c : width * (c + 1)]

    scale = 1.0 / math.sqrt(HD)
    to_word = jnp.where(entity, query(2), query(0)).astype(BF16).astype(F32) * scale
    to_entity = jnp.where(entity, query(3), query(1)).astype(BF16).astype(F32) * scale
    keys = query(4).astype(BF16).astype(F32)
    v_ref[...] = query(5).astype(BF16)
    left = lax.broadcasted_iota(jnp.int32, (rows, 2 * HD), 1) < HD
    held = left != entity
    for p in range(width // (2 * HD)):
        cols = slice(2 * HD * p, 2 * HD * (p + 1))
        w, e, k = to_word[:, cols], to_entity[:, cols], keys[:, cols]
        w_roll, e_roll, k_roll = (pltpu.roll(t, HD, 1) for t in (w, e, k))
        even = slice(4 * HD * p, 4 * HD * p + 2 * HD)
        odd = slice(4 * HD * p + 2 * HD, 4 * HD * (p + 1))
        q2_ref[:, even] = jnp.where(left, w, e_roll).astype(BF16)
        q2_ref[:, odd] = jnp.where(left, w_roll, e).astype(BF16)
        k2_ref[:, even] = jnp.where(held, jnp.where(left, k, k_roll), 0.0).astype(BF16)
        k2_ref[:, odd] = jnp.where(held, jnp.where(left, k_roll, k), 0.0).astype(BF16)


def project(x, kind, wq, bq, wk, bk, wv, bv, rows=256):
    length, model = x.shape
    width = wk.shape[1]
    rows = min(rows, length)
    tile = lambda w: pl.BlockSpec((rows, w), lambda i: (i, 0))
    return pl.pallas_call(
        project_kernel,
        grid=(length // rows,),
        in_specs=[
            tile(model),
            tile(1),
            whole_block(wq.shape),
            whole_block(bq.shape),
            whole_block(wk.shape),
            whole_block((1, width)),
            whole_block(wv.shape),
            whole_block((1, width)),
        ],
        out_specs=[tile(2 * width), tile(2 * width), tile(width)],
        out_shape=[
            struct((length, 2 * width), BF16),
            struct((length, 2 * width), BF16),
            struct((length, width), BF16),
        ],
        compiler_params=params(63),
        cost_estimate=cost(12 * length * model * width, 16 * model * width + 12 * length * width),
        name="project",
    )(x, kind, wq, bq, wk, bk.reshape(1, width), wv, bv.reshape(1, width))


def key_extra(live, rows):
    lane = lax.broadcasted_iota(jnp.int32, (rows, 2 * HD), 1)
    return jnp.where(
        lane == 0, jnp.where(live, 0.0, MASKED), jnp.where(lane < 4, 1.0, 0.0)
    ).astype(BF16)


def attend_kernel(q2_ref, k2_ref, v_ref, live_ref, out_ref, extra_ref, turned_ref, both_ref):
    length = k2_ref.shape[0]
    h = pl.program_id(1)

    @pl.when(h == 0)
    def _():
        turned = v_ref[...].astype(F32).T.astype(BF16)
        turned_ref[0] = turned[:HD]
        turned_ref[1] = turned[HD:]

    lane = lax.broadcasted_iota(jnp.int32, (length, 2 * HD), 1)
    one = jnp.where(lane == 0, 1.0, 0.0).astype(BF16)
    keys = jnp.concatenate([k2_ref[...], key_extra(live_ref[...] > 0.5, length)], axis=1)
    query = jnp.concatenate([q2_ref[...], one], axis=1)
    scores = mm(keys, query, NT)
    top = jnp.max(scores, axis=0, keepdims=True)
    weights = jnp.exp(scores - top)
    norm = jnp.sum(weights, axis=0, keepdims=True)
    summed = mm(turned_ref[h], weights.astype(BF16), NN)
    both_ref[h] = summed * (1.0 / norm)
    pieces = three_pieces(-(top + jnp.log(norm)))
    filled = jnp.concatenate(
        [jnp.ones((1, length), F32), *pieces, jnp.zeros((2 * HD - 4, length), F32)], axis=0
    )
    extra_ref[...] = filled.T.astype(BF16)

    @pl.when(h == 1)
    def _():
        out_ref[...] = jnp.concatenate([both_ref[0], both_ref[1]], axis=0).T.astype(BF16)


def attend(q2, k2, v, live):
    length, width = v.shape
    head = pl.BlockSpec((length, 2 * HD), lambda p, h: (0, 2 * p + h))
    pair = pl.BlockSpec((length, 2 * HD), lambda p, h: (0, p))
    return pl.pallas_call(
        attend_kernel,
        grid=(width // (2 * HD), 2),
        in_specs=[head, head, pair, whole_block((length, 1))],
        out_specs=[pair, head],
        out_shape=[struct((length, width), BF16), struct((length, 2 * width), BF16)],
        scratch_shapes=[pltpu.VMEM((2, HD, length), BF16), pltpu.VMEM((2, HD, length), F32)],
        compiler_params=params(63),
        cost_estimate=cost(10 * length * length * width, 20 * length * width, length * length * width // HD),
        name="attend",
    )(q2, k2, v, live)


def attend_back_kernel(
    count, group, y_ref, q2_ref, extra_ref, k2_ref, v_ref, o_ref, own_ref, got_ref, live_ref, kind_ref, columns_ref, pick_ref,
    wq_hbm, wk_hbm, wv_hbm, turned_hbm, first_hbm, *rest,
):
    outs = count + (2 if group is None else 4)
    part_hbm, grads_hbm = rest[:count], rest[count:outs]
    (
        dk_ref, dv_ref, dq_ref, product_ref, d_ref, all_ref, sums_ref, weights_ref, turned_ref, first_ref,
        part_ref, grads_ref, in_sem, out_sem,
    ) = rest[outs:]
    length = k2_ref.shape[0]
    width = wk_hbm.shape[1]
    p, h = pl.program_id(0), pl.program_id(1)
    pairs = width // (2 * HD)
    lane = lax.broadcasted_iota(jnp.int32, (length, 2 * HD), 1)
    left = lane < HD

    def arriving():
        copies = [
            pltpu.make_async_copy(wq_hbm.at[c], weights_ref.at[:, width * c : width * (c + 1)], in_sem.at[c])
            for c in range(4)
        ]
        copies.append(pltpu.make_async_copy(wk_hbm, weights_ref.at[:, 4 * width : 5 * width], in_sem.at[4]))
        copies.append(pltpu.make_async_copy(wv_hbm, weights_ref.at[:, 5 * width : 6 * width], in_sem.at[5]))
        copies.append(pltpu.make_async_copy(turned_hbm, turned_ref, in_sem.at[6]))
        copies.append(pltpu.make_async_copy(first_hbm, first_ref, in_sem.at[7]))
        return copies

    @pl.when(jnp.logical_and(p == 0, h == 0))
    def _():
        for copy in arriving():
            copy.start()

    @pl.when(h == 0)
    def _():
        first = y_ref[0] == 0
        own, got = own_ref[...], got_ref[...]
        joined = jnp.concatenate([jnp.where(first, own, got), jnp.where(first, got, own)], axis=0)
        product_ref[...] = joined * o_ref[...].astype(F32)
        d_ref[...] = joined.astype(BF16)

    d_context = d_ref[...]
    base = HD * (1 - h)
    mine = jnp.logical_and(lane >= HD - base, lane < 2 * HD - base)
    delta = jnp.sum(jnp.where(mine, product_ref[...], 0.0), axis=1, keepdims=True)
    high, middle, low = three_pieces(-delta)
    pieces = jnp.where(
        lane == base, high, jnp.where(lane == base + 1, middle, jnp.where(lane == base + 2, low, 0.0))
    ).astype(BF16)
    d_wide = jnp.where(mine, d_context, pieces)
    q2, k2 = q2_ref[...], k2_ref[...]
    query = jnp.concatenate([q2, extra_ref[...]], axis=1)
    keys = jnp.concatenate([k2, key_extra(live_ref[...] > 0.5, length)], axis=1)
    probs = jnp.exp(mm(keys, query, NT))
    ones = jnp.where((lane >= base) & (lane < base + 3), 1.0, 0.0).astype(BF16)
    d_probs = mm(jnp.where(mine, v_ref[...], ones), d_wide, NT)
    d_scores = (probs * d_probs).astype(BF16)
    dv_ref[h] = mm(probs.astype(BF16), d_context, NN)
    dk_ref[h] = mm(d_scores, q2, NN)
    dq_ref[h] = mm(k2, d_scores, TN).T * (1.0 / math.sqrt(HD))

    @pl.when(h == 1)
    def _():
        entity = kind_ref[...] > 0.5
        even, odd = dq_ref[0], dq_ref[1]
        to_word = jnp.where(left, even, pltpu.roll(odd, HD, 1)).astype(BF16).astype(F32)
        to_entity = jnp.where(left, pltpu.roll(even, HD, 1), odd).astype(BF16).astype(F32)
        even, odd = dk_ref[0], dk_ref[1]
        even = jnp.where(entity, pltpu.roll(even, HD, 1), even)
        odd = jnp.where(entity, odd, pltpu.roll(odd, HD, 1))
        grads = [
            jnp.where(entity, 0.0, to_word),
            jnp.where(entity, 0.0, to_entity),
            jnp.where(entity, to_word, 0.0),
            jnp.where(entity, to_entity, 0.0),
            jnp.where(left, even, odd).astype(BF16).astype(F32),
            jnp.where(left, dv_ref[0], dv_ref[1]).astype(BF16).astype(F32),
        ]
        for c, grad in enumerate(grads):
            all_ref[p, c] = grad.astype(BF16)
        sums = [jnp.sum(grad, axis=0, keepdims=True) for grad in grads]
        sums_ref[p] = jnp.concatenate([*sums, jnp.zeros((2, 2 * HD), F32)], axis=0)

    @pl.when(jnp.logical_and(p == pairs - 1, h == 1))
    def _():
        for copy in arriving():
            copy.wait()
        grads = jnp.concatenate([all_ref[k, c] for c in range(6) for k in range(pairs)], axis=1)
        half = first_ref.shape[0]
        leaving = []

        def leave(source, target):
            copy = pltpu.make_async_copy(source, target, out_sem.at[len(leaving)])
            copy.start()
            leaving.append(copy)

        for i in range(2):
            rows = slice(i * half, (i + 1) * half)
            total = mm(grads[rows], weights_ref[...], NT)
            part_ref[rows, :] = total + jnp.where(y_ref[0] == i, first_ref[...], 0.0)
        begin = 0
        for target in part_hbm:
            leave(part_ref.at[begin : begin + target.shape[0], :], target)
            begin += target.shape[0]
        model = turned_ref.shape[0]
        sums = jnp.concatenate([sums_ref[k] for k in range(pairs)], axis=1)
        pieces = jnp.concatenate([piece.astype(BF16) for piece in three_pieces(sums)], axis=0)
        picked = mm(pick_ref[...], pieces, NT)
        biases = picked[:, :6] + picked[:, 8:14] + picked[:, 16:22]
        extra = jnp.concatenate(
            [biases, columns_ref[...], jnp.zeros((model, 128 - 6 - columns_ref.shape[1]), F32)], axis=1
        )
        lower = y_ref[1] % 2 == 0

        def place(array, cols, value):
            if group is None:
                grads_ref[array, :, cols] = value
                return
            blocks = value.reshape(model // (2 * group), 2, group, value.shape[1])
            first, second = blocks[:, 0], blocks[:, 1]
            for k, (one, other) in enumerate(((first, second), (second, first))):
                picked_rows = jnp.where(lower, one, other).reshape(model // 2, value.shape[1])
                grads_ref[array, k * (model // 2) : (k + 1) * (model // 2), cols] = picked_rows

        for array in range(2):

            def one(i, carry, array=array):
                grad = jnp.concatenate([all_ref[k, 3 * array + i] for k in range(pairs)], axis=1)
                at = pl.multiple_of(width * i, 128)
                place(array, pl.ds(at, width), mm(turned_ref[...], grad, NN))
                return carry

            lax.fori_loop(0, 3, one, 0)
            wide = 3 * width
            if array:
                place(array, slice(wide, wide + 128), extra)
                wide += 128
            if group is None:
                leave(grads_ref.at[array, :, :wide], grads_hbm[array])
            else:
                for k in (1, 0):
                    rows = slice(k * (model // 2), (k + 1) * (model // 2))
                    leave(grads_ref.at[array, rows, :wide], grads_hbm[2 * array + k])
        for copy in leaving:
            copy.wait()


def attend_back(
    y, q2, extra, k2, v, o, own, got, live, kind, columns, pick, wq, wk, wv, turned, first, chunks, group
):
    length, width = v.shape
    half, model = first.shape
    pairs = width // (2 * HD)
    head = pl.BlockSpec((length, 2 * HD), lambda p, h, *_: (0, 2 * p + h))
    pair = pl.BlockSpec((length, 2 * HD), lambda p, h, *_: (0, p))
    part = pl.BlockSpec((half, 2 * HD), lambda p, h, *_: (0, p))
    anywhere = pl.BlockSpec(memory_space=pl.ANY)
    shapes = [struct((rows, model), F32) for rows in chunks]
    for wide in (3 * width, 3 * width + 128):
        shapes += [struct((model, wide), F32)] if group is None else [struct((model // 2, wide), F32)] * 2
    return pl.pallas_call(
        functools.partial(attend_back_kernel, len(chunks), group),
        grid_spec=pltpu.PrefetchScalarGridSpec(
            num_scalar_prefetch=1,
            grid=(pairs, 2),
            in_specs=[
                head, head, head, pair, pair, part, part, whole_block((length, 1)), whole_block((length, 1)),
                whole_block(columns.shape), whole_block(pick.shape),
                *[anywhere] * 5,
            ],
            out_specs=[anywhere] * len(shapes),
            scratch_shapes=[
                *[pltpu.VMEM((2, length, 2 * HD), F32)] * 3,
                pltpu.VMEM((length, 2 * HD), F32),
                pltpu.VMEM((length, 2 * HD), BF16),
                pltpu.VMEM((pairs, 6, length, 2 * HD), BF16),
                pltpu.VMEM((pairs, 8, 2 * HD), F32),
                pltpu.VMEM((model, 6 * width), BF16),
                pltpu.VMEM((model, length), BF16),
                pltpu.VMEM((half, model), F32),
                pltpu.VMEM((length, model), F32),
                pltpu.VMEM((2, model, 3 * width + 128), F32),
                pltpu.SemaphoreType.DMA((8,)),
                pltpu.SemaphoreType.DMA((len(shapes),)),
            ],
        ),
        out_shape=shapes,
        compiler_params=params(63),
        cost_estimate=cost(20 * length * length * width, 40 * length * width, length * length * width // HD),
        name="attend_back",
    )(y, q2, extra, k2, v, o, own, got, live, kind, columns, pick, wq, wk, wv, turned, first)


def normalise(value):
    centre = value - jnp.mean(value, axis=-1, keepdims=True)
    inverse = lax.rsqrt(jnp.mean(centre * centre, axis=-1, keepdims=True) + NORM_EPS)
    return centre * inverse, inverse


def normalise_back(scaled, normal, inverse):
    return inverse * (
        scaled
        - jnp.mean(scaled, axis=-1, keepdims=True)
        - normal * jnp.mean(scaled * normal, axis=-1, keepdims=True)
    )


def gelu_pair(values):
    cumulative = 0.5 * (1.0 + lax.erf(values * (1.0 / math.sqrt(2.0))))
    density = jnp.exp(-0.5 * values * values) * (1.0 / math.sqrt(2.0 * math.pi))
    return values * cumulative, cumulative + values * density


def column_sum(value):
    return jnp.sum(value, axis=0, keepdims=True)


def first_cut(half):
    return half // 2


def middle_sizes(wi, wo, early):
    hidden, model, width = wi.shape[1], wo.shape[1], wo.shape[0]
    cut = [width // SLICES, (width + model) // SLICES, (width + 2 * model) // SLICES]
    return hidden, hidden // 2, model, width, cut


def far_block(ref, a, b):
    return ref[:, a:b, :].reshape(SLICES * (b - a), ref.shape[2])


def far_outer(ref, part, half):
    per = SLICES // 2
    return ref[per * (part - 2) : per * (part - 1), :, :].reshape(half, ref.shape[2])


def by_core(lower, values):
    first, second = (value.astype(F32) for value in values)
    keep = jnp.where(lower, first, second).astype(BF16)
    return keep, jnp.where(lower, second, first)


def forward_kernel(at_ref, x_ref, cot_ref, live_ref, own_ref, got_ref, wo_ref, wi_hbm, wu_hbm, *rest):
    arrived = rest[:SLICES]
    arrived_late = rest[SLICES : 2 * SLICES]
    (
        vec_ref, bias_ref, out_ref, out_first_ref, out_late_ref, low_ref, d_low_ref, keep_ref, send_ref,
        slope_ref, n1_ref, inv1_ref, d_second_ref, sums_ref, early_hbm, late_hbm,
        early_ref, late_ref, wi_ref, wu_ref, raw_ref, raw_late_ref, in_sem, out_sem,
    ) = rest[2 * SLICES :]
    step = pl.program_id(0)
    me = at_ref[1]
    lower = me % 2 == 0
    hidden, half, model, width, cut = middle_sizes(wi_hbm, wo_ref, early_ref)

    def weight_copies():
        stages = [[], [], [], [], []]
        for k in range(SLICES):
            for stage, source, target in (
                (0, arrived[k].at[: cut[0], :], raw_ref.at[k, : cut[0], :]),
                (2, arrived[k].at[cut[0] :, :], raw_ref.at[k, cut[0] :, :]),
                (4, arrived_late[k], raw_late_ref.at[k]),
            ):
                stages[stage].append(pltpu.make_async_copy(source, target, in_sem.at[stage * SLICES + k]))
        stages[1].append(pltpu.make_async_copy(wi_hbm, wi_ref, in_sem.at[SLICES]))
        stages[3].append(pltpu.make_async_copy(wu_hbm, wu_ref, in_sem.at[3 * SLICES]))
        return stages

    def leaving():
        return [
            pltpu.make_async_copy(early_ref, early_hbm, out_sem.at[0]),
            pltpu.make_async_copy(late_ref, late_hbm, out_sem.at[1]),
        ]

    def arrive(*wanted):
        @pl.when(step == 0)
        def _():
            stages = weight_copies()
            for stage in wanted:
                for copy in stages[stage]:
                    copy.wait()
            for k in range(SLICES):
                if 0 in wanted:
                    early_ref[me ^ k, : cut[0], :] = raw_ref[k, : cut[0], :].astype(BF16)
                if 2 in wanted:
                    early_ref[me ^ k, cut[0] :, :] = raw_ref[k, cut[0] :, :].astype(BF16)
                if 4 in wanted:
                    late_ref[me ^ k] = raw_late_ref[k].astype(BF16)
            if 4 in wanted:
                for copy in leaving():
                    copy.start()

    @pl.when(step == 0)
    def _():
        for stage in weight_copies():
            for copy in stage:
                copy.start()

    arrive(0)
    vec = [vec_ref[k : k + 1, :] for k in range(6)]
    got = got_ref[...].astype(BF16)
    own = own_ref[...]
    first = mm(own, wo_ref[...], NN) + mm(got, far_block(early_ref, 0, cut[0]), NN) + vec[0] + x_ref[...].astype(F32)
    n1, inv1 = normalise(first)
    n1_ref[...] = n1
    inv1_ref[...] = inv1
    normed = n1 * vec[1] + vec[2]
    low = normed.astype(BF16)
    low_ref[...] = low
    at_low = model + hidden
    send_ref[:, at_low : at_low + model] = low.astype(F32)
    _, send = by_core(lower, (own, got))
    send_ref[:, at_low + model :] = send
    second = vec[3] + normed
    arrive(1, 3)
    for far in range(2):
        if far:
            arrive(2, 4)
        pair = []
        for part in (2 * far, 2 * far + 1):
            inner = wi_ref[:, half * part : half * (part + 1)] if part < 2 else far_block(early_ref, cut[part - 2], cut[part - 1])
            pre = mm(low, inner, NN) + bias_ref[part : part + 1, :]
            active, slope = gelu_pair(pre)
            active = active.astype(BF16)
            slope_ref[:, half * part : half * (part + 1)] = slope.astype(BF16)
            pair.append(active)
            outer = wu_ref[half * part : half * (part + 1), :] if part < 2 else far_outer(late_ref, part, half)
            second = second + mm(active, outer, NN)
        keep, send = by_core(lower, pair)
        keep_ref[:, half * far : half * (far + 1)] = keep
        send_ref[:, model + half * far : model + half * (far + 1)] = send
    n2, inv2 = normalise(second)
    live = live_ref[...] > 0.5
    result = jnp.where(live, n2 * vec[4] + vec[5], 0.0).astype(BF16)
    out_ref[...] = result
    out_first_ref[...] = result[:, : model // 2].astype(F32)
    out_late_ref[...] = result[:, model // 2 :].astype(F32)
    dz = jnp.where(live, cot_ref[...].astype(F32), 0.0)
    d_second = normalise_back(dz * vec[4], n2, inv2)
    d_second_ref[...] = d_second
    d_low = d_second.astype(BF16)
    d_low_ref[...] = d_low
    send_ref[:, :model] = d_low.astype(F32)
    sums = jnp.concatenate(
        [column_sum(d_second), column_sum(dz * n2), column_sum(dz), jnp.zeros((5, model), F32)], axis=0
    )

    @pl.when(step == 0)
    def _():
        sums_ref[...] = sums

    @pl.when(step != 0)
    def _():
        sums_ref[...] += sums

    @pl.when(step == pl.num_programs(0) - 1)
    def _():
        for copy in leaving():
            copy.wait()


def forward(at, x, cot, live, context, got, wo, wi, wu, early, late, vec, bias, rows=256):
    half, width = got.shape
    model, hidden = wi.shape
    rows = min(rows, half)
    steps = half // rows
    mine = lambda w: pl.BlockSpec((rows, w), lambda i, s: (i + s[0] * steps, 0))
    tile = lambda w: pl.BlockSpec((rows, w), lambda i, s: (i, 0))
    anywhere = pl.BlockSpec(memory_space=pl.ANY)
    widths = (
        (model, BF16), (model // 2, F32), (model // 2, F32), (model, BF16), (model, BF16), (hidden, BF16),
        (2 * model + hidden + width, F32), (2 * hidden, BF16), (model, F32), (1, F32), (model, F32),
    )
    far_shapes = [(SLICES, *early[0].shape), (SLICES, *late[0].shape)]
    return pl.pallas_call(
        forward_kernel,
        grid_spec=pltpu.PrefetchScalarGridSpec(
            num_scalar_prefetch=1,
            grid=(steps,),
            in_specs=[
                mine(model), mine(model), mine(1), mine(width), tile(width),
                whole_block(wo.shape), *[anywhere] * (2 + 2 * SLICES),
                whole_block(vec.shape), whole_block(bias.shape),
            ],
            out_specs=[
                *(tile(w) for w, _ in widths), pl.BlockSpec((8, model), lambda i, s: (0, 0)), anywhere, anywhere,
            ],
            scratch_shapes=[
                *(pltpu.VMEM(shape, BF16) for shape in far_shapes),
                pltpu.VMEM(wi.shape, BF16),
                pltpu.VMEM(wu.shape, BF16),
                *(pltpu.VMEM(shape, F32) for shape in far_shapes),
                pltpu.SemaphoreType.DMA((5 * SLICES,)),
                pltpu.SemaphoreType.DMA((2,)),
            ],
        ),
        out_shape=[
            *(struct((half, w), kind) for w, kind in widths), struct((8, model), F32),
            *(struct(shape, BF16) for shape in far_shapes),
        ],
        compiler_params=params(63),
        cost_estimate=cost(8 * half * model * hidden, 24 * model * hidden, 4 * half * hidden),
        name="forward",
    )(at, x, cot, live, context, got, wo, wi, wu, *early, *late, vec, bias)


def backward_kernel(
    at_ref, slope_ref, n1_ref, inv1_ref, d_second_ref, d_low_ref, own_ref, got_ref, wo_ref, vec_ref,
    wi_hbm, wu_hbm, early_hbm, late_hbm,
    first_ref, dco_ref, dcf_ref, d_attn_ref, keep0_ref, keep1_ref, send_ref, sums_ref, inner_sums_ref,
    wi_ref, wu_ref, early_ref, late_ref, in_sem,
):
    step = pl.program_id(0)
    lower = at_ref[1] % 2 == 0
    hidden, half, model, width, cut = middle_sizes(wi_hbm, wo_ref, early_ref)
    ca = first_cut(half)

    def copies():
        pairs = ((wu_hbm, wu_ref), (wi_hbm, wi_ref), (late_hbm, late_ref), (early_hbm, early_ref))
        return [pltpu.make_async_copy(*pair, in_sem.at[k]) for k, pair in enumerate(pairs)]

    @pl.when(step == 0)
    def _():
        for copy in copies():
            copy.start()

    d_low = d_low_ref[...]
    n1 = n1_ref[...]
    d_normed = d_second_ref[...]
    inner_sums = []
    for far in range(2):

        @pl.when(step == 0)
        def _():
            for copy in copies()[2 * far : 2 * far + 2]:
                copy.wait()

        pair = []
        for part in (2 * far, 2 * far + 1):
            outer = wu_ref[half * part : half * (part + 1), :] if part < 2 else far_outer(late_ref, part, half)
            inner = wi_ref[:, half * part : half * (part + 1)] if part < 2 else far_block(early_ref, cut[part - 2], cut[part - 1])
            d_hidden = mm(d_low, outer, NT)
            d_inner = (d_hidden * slope_ref[:, half * part : half * (part + 1)].astype(F32)).astype(BF16)
            pair.append(d_inner)
            inner_sums.append(column_sum(d_inner.astype(F32)))
            d_normed = d_normed + mm(d_inner, inner, NT)
        keep, send = by_core(lower, pair)
        da = half - ca
        keep0_ref[:, ca * far : ca * (far + 1)] = keep[:, :ca]
        keep1_ref[:, da * far : da * (far + 1)] = keep[:, ca:]
        send_ref[:, ca * far : ca * (far + 1)] = send[:, :ca]
        send_ref[:, 2 * ca + da * far : 2 * ca + da * (far + 1)] = send[:, ca:]
    d_first = normalise_back(d_normed * vec_ref[1:2, :], n1, inv1_ref[...])
    first_ref[...] = d_first
    d_attn = d_first.astype(BF16)
    d_attn_ref[...] = d_attn
    send_ref[:, hidden:] = d_attn.astype(F32)
    dco_ref[...] = mm(d_attn, wo_ref[...], NT).astype(BF16).astype(F32)
    dcf_ref[...] = mm(d_attn, far_block(early_ref, 0, cut[0]), NT).astype(BF16).astype(F32)
    keep, _ = by_core(lower, (own_ref[...], got_ref[...]))
    keep0_ref[:, 2 * ca :] = keep
    sums = jnp.concatenate(
        [column_sum(d_first), column_sum(d_normed * n1), column_sum(d_normed), jnp.zeros((5, model), F32)], axis=0
    )
    inner_sums = jnp.concatenate([*inner_sums, jnp.zeros((4, half), F32)], axis=0)

    @pl.when(step == 0)
    def _():
        sums_ref[...] = sums
        inner_sums_ref[...] = inner_sums

    @pl.when(step != 0)
    def _():
        sums_ref[...] += sums
        inner_sums_ref[...] += inner_sums


def backward(at, slope, n1, inv1, d_second, d_low, context, got, wo, vec, wi, wu, early, late, rows=256):
    half, width = got.shape
    model, hidden = wi.shape
    rows = min(rows, half)
    steps = half // rows
    ca = first_cut(hidden // 2)
    mine = lambda w: pl.BlockSpec((rows, w), lambda i, s: (i + s[0] * steps, 0))
    tile = lambda w: pl.BlockSpec((rows, w), lambda i, s: (i, 0))
    anywhere = pl.BlockSpec(memory_space=pl.ANY)
    widths = (
        (model, F32), (width, F32), (width, F32), (model, BF16), (2 * ca + width, BF16), (hidden - 2 * ca, BF16),
        (hidden + model, F32),
    )
    return pl.pallas_call(
        backward_kernel,
        grid_spec=pltpu.PrefetchScalarGridSpec(
            num_scalar_prefetch=1,
            grid=(steps,),
            in_specs=[
                tile(2 * hidden), tile(model), tile(1), tile(model), tile(model), mine(width), tile(width),
                whole_block(wo.shape), whole_block(vec.shape), *[anywhere] * 4,
            ],
            out_specs=[
                *(tile(w) for w, _ in widths),
                pl.BlockSpec((8, model), lambda i, s: (0, 0)),
                pl.BlockSpec((8, hidden // 2), lambda i, s: (0, 0)),
            ],
            scratch_shapes=[
                *(pltpu.VMEM(a.shape, BF16) for a in (wi, wu, early, late)),
                pltpu.SemaphoreType.DMA((4,)),
            ],
        ),
        out_shape=[
            *(struct((half, w), kind) for w, kind in widths), struct((8, model), F32), struct((8, hidden // 2), F32),
        ],
        compiler_params=params(63),
        cost_estimate=cost(8 * half * model * hidden, 24 * model * hidden),
        name="backward",
    )(at, slope, n1, inv1, d_second, d_low, context, got, wo, vec, wi, wu, early, late)


def weight_kernel(plan, count, kinds, bit_ref, *rest):
    groups = len(plan)
    left_hbm, rest = rest[:kinds], rest[kinds:]
    keep_hbm, rest = rest[:groups], rest[groups:]
    got_hbm, rest = rest[:count], rest[count:]
    outs, rest = rest[: 2 * groups], rest[2 * groups :]
    left_ref, left_got_ref, rest = rest[0], rest[1], rest[2:]
    keep_refs, rest = rest[:groups], rest[groups:]
    got_refs, rest = rest[:groups], rest[groups:]
    stage_refs, (in_sem, out_sem) = rest[:groups], rest[groups:]
    model = left_ref.shape[2]

    arriving, ready = [], {}

    def bring(key, source, target):
        if key not in ready:
            ready[key] = pltpu.make_async_copy(source, target, in_sem.at[len(arriving)])
            ready[key].start()
            arriving.append(key)

    for g, (_, _, tiles) in enumerate(plan):
        for index, (left_array, left_at), (right_array, right_at), a, b in tiles:
            bring(("left", index), left_hbm[index], left_ref.at[index])
            if ("left got", index) not in ready:
                columns = slice(left_at, left_at + model)
                bring(("left got", index), got_hbm[left_array].at[:, columns], left_got_ref.at[index])
            bring(("keep", g, a), keep_hbm[g].at[:, a:b], keep_refs[g].at[:, a:b])
            columns = slice(right_at, right_at + b - a)
            bring(("got", g, a), got_hbm[right_array].at[:, columns], got_refs[g].at[:, a:b])
    waited = set()

    def need(*keys):
        for key in keys:
            if key not in waited:
                waited.add(key)
                ready[key].wait()

    leaving = []
    for g, (slot, group, tiles) in enumerate(plan):
        width = keep_refs[g].shape[1]
        for index, _, _, a, b in tiles:
            need(("left", index), ("left got", index), ("keep", g, a), ("got", g, a))
            left = jnp.concatenate([left_ref[index], left_got_ref[index].astype(BF16)], axis=0)
            right = jnp.concatenate([keep_refs[g][:, a:b], got_refs[g][:, a:b].astype(BF16)], axis=0)
            value = mm(left, right, TN)
            if slot is None:
                part, base = (0, 0) if 2 * b <= width else (1, width // 2)
                stage_refs[g][part, :, a - base : b - base] = value
                parts = ((part, a - base, b - base),)
            else:
                pairs = value.reshape(model // (2 * group), 2, group, b - a)
                kept = bit_ref[slot] == 0
                first, second = pairs[:, 0], pairs[:, 1]
                for part, (one, other) in enumerate(((first, second), (second, first))):
                    picked = jnp.where(kept, one, other)
                    stage_refs[g][part, :, a:b] = picked.reshape(model // 2, b - a)
                parts = ((1, a, b), (0, a, b))
            for part, a, b in parts:
                copy = pltpu.make_async_copy(
                    stage_refs[g].at[part, :, a:b], outs[2 * g + part].at[:, a:b], out_sem.at[len(leaving)]
                )
                copy.start()
                leaving.append(copy)
    for copy in leaving:
        copy.wait()


def weight_grads(at, lefts, keeps, received, plan):
    depth, model = lefts[0].shape
    stages, shapes, steps = [], [], 0
    for (slot, _, tiles), keep in zip(plan, keeps):
        width = keep.shape[1]
        shape = (model, width // 2) if slot is None else (model // 2, width)
        stages.append(pltpu.VMEM((2, *shape), F32))
        shapes += [struct(shape, F32)] * 2
        steps += len(tiles)
    columns = sum(keep.shape[1] for keep in keeps)
    anywhere = pl.BlockSpec(memory_space=pl.ANY)
    return pl.pallas_call(
        functools.partial(weight_kernel, plan, len(received), len(lefts)),
        grid_spec=pltpu.PrefetchScalarGridSpec(
            num_scalar_prefetch=1,
            grid=(1,),
            in_specs=[anywhere] * (len(lefts) + len(keeps) + len(received)),
            out_specs=[anywhere] * len(shapes),
            scratch_shapes=[
                pltpu.VMEM((len(lefts), depth, model), BF16),
                pltpu.VMEM((len(lefts), depth, model), F32),
                *(pltpu.VMEM(keep.shape, BF16) for keep in keeps),
                *(pltpu.VMEM(keep.shape, F32) for keep in keeps),
                *stages,
                pltpu.SemaphoreType.DMA((2 * len(lefts) + 2 * steps,)),
                pltpu.SemaphoreType.DMA((2 * steps,)),
            ],
        ),
        out_shape=shapes,
        compiler_params=params(63),
        cost_estimate=cost(4 * depth * model * columns, 4 * model * columns + 8 * depth * columns),
        name="weight_grads",
    )(at, *lefts, *keeps, *received)


def combine_kernel(plan, count, bits_ref, *rest):
    outs = len(plan)
    arrays, targets = rest[:count], rest[count : count + outs]
    buffers, (in_sem, out_sem) = rest[count + outs : -2], rest[-2:]
    copies = []
    for pieces in plan:
        for _, terms in pieces:
            for array, chosen, a, b, _ in terms:
                index = [slice(None)] * len(arrays[array].shape)
                for axis, (bit, mine) in chosen:
                    index[axis] = pl.ds(bits_ref[bit] if mine else 1 - bits_ref[bit], 1)
                index[-1] = slice(a, b)
                k = len(copies)
                copies.append(pltpu.make_async_copy(arrays[array].at[tuple(index)], buffers[k], in_sem.at[k]))
    for copy in copies:
        copy.start()
    k = 0
    leaving = []
    for target, pieces in zip(targets, plan):
        for at, terms in pieces:
            first = k
            total = None
            for *_, gate in terms:
                copies[k].wait()
                value = buffers[k][...]
                if gate is not None:
                    value = jnp.where(bits_ref[0] == gate, value, 0.0)
                total = value if total is None else total + value
                k += 1
            if len(terms) > 1:
                buffers[first][...] = total
            width = buffers[first].shape[-1]
            index = (*[slice(None)] * (len(target.shape) - 1), slice(at, at + width))
            copy = pltpu.make_async_copy(buffers[first], target.at[index], out_sem.at[len(leaving)])
            copy.start()
            leaving.append(copy)
    for copy in leaving:
        copy.wait()


def combine(bit_values, outputs):
    arrays, plan, shapes, buffers, moved = [], [], [], [], 0
    for pieces in outputs:
        at, planned = 0, []
        for terms in pieces:
            named = []
            for array, chosen, a, b, gate in terms:
                place = [k for k, other in enumerate(arrays) if other is array]
                if not place:
                    place = [len(arrays)]
                    arrays.append(array)
                named.append((place[0], tuple(sorted(chosen.items())), a, b, gate))
                block = tuple(1 if k in chosen else size for k, size in enumerate(array.shape[:-1]))
                buffers.append(pltpu.VMEM((*block, b - a), F32))
                moved += 4 * math.prod(block) * (b - a)
            planned.append((at, named))
            at += b - a
        plan.append(planned)
        shapes.append(struct((*block, at), F32))
    anywhere = pl.BlockSpec(memory_space=pl.ANY)
    pieces = sum(len(planned) for planned in plan)
    return pl.pallas_call(
        functools.partial(combine_kernel, plan, len(arrays)),
        grid_spec=pltpu.PrefetchScalarGridSpec(
            num_scalar_prefetch=1,
            grid=(1,),
            in_specs=[anywhere] * len(arrays),
            out_specs=[anywhere] * len(shapes),
            scratch_shapes=[
                *buffers,
                pltpu.SemaphoreType.DMA((len(buffers),)),
                pltpu.SemaphoreType.DMA((pieces,)),
            ],
        ),
        out_shape=shapes,
        compiler_params=params(63),
        cost_estimate=cost(moved, 2 * moved),
        name="combine",
    )(bit_values, *arrays)


def turn_kernel(value_ref, out_ref):
    out_ref[...] = value_ref[...].astype(F32).T.astype(BF16)


def turn(value, columns=256):
    length, model = value.shape
    return pl.pallas_call(
        turn_kernel,
        grid=(model // columns,),
        in_specs=[pl.BlockSpec((length, columns), lambda i: (0, i))],
        out_specs=pl.BlockSpec((columns, length), lambda i: (i, 0)),
        out_shape=struct((model, length), BF16),
        compiler_params=params(63),
        cost_estimate=cost(length * model, 4 * length * model),
        name="turn",
    )(value)


def place_kernel(steps, y_ref, own_ref, first_ref, second_ref, out_ref):
    mine = pl.program_id(0) // steps == y_ref[0]
    got = jnp.concatenate([first_ref[...], second_ref[...]], axis=1)
    out_ref[...] = jnp.where(mine, own_ref[...].astype(F32), got).astype(BF16)


def place_rows(y, own, first, second):
    half, model = own.shape
    rows = min(128, half)
    steps = half // rows
    tile = lambda w: pl.BlockSpec((rows, w), lambda i, s: (i % steps, 0))
    return pl.pallas_call(
        functools.partial(place_kernel, steps),
        grid_spec=pltpu.PrefetchScalarGridSpec(
            num_scalar_prefetch=1,
            grid=(2 * steps,),
            in_specs=[tile(model), tile(model // 2), tile(model // 2)],
            out_specs=pl.BlockSpec((rows, model), lambda i, s: (i, 0)),
        ),
        out_shape=struct((2 * half, model), BF16),
        compiler_params=params(63),
        cost_estimate=cost(half * model, 12 * half * model),
        name="place_rows",
    )(y, own, first, second)


def per_device(
    devices,
    tokens,
    lengths,
    entity_flags,
    query_weight,
    query_bias,
    key_weight,
    key_bias,
    value_weight,
    value_bias,
    output_weight,
    output_bias,
    attn_gain,
    attn_shift,
    inner_weight,
    inner_bias,
    outer_weight,
    outer_bias,
    final_gain,
    final_shift,
    cotangent,
):
    x = tokens[0]
    length, model = x.shape
    width = key_weight.shape[1]
    hidden = inner_weight.shape[1]
    half = length // 2
    bits = devices.bit_length() - 1
    y = lax.axis_index("tensor")
    d = lax.axis_index("dp")

    def swap(value, mask):
        return lax.ppermute(value, "dp", [(i, i ^ mask) for i in range(devices)])

    def cross(value):
        return lax.ppermute(value, "tensor", [(0, 1), (1, 0)])

    me = d % SLICES
    core = d % 2
    rows = model // devices
    near_mask, far_mask = 192 // rows, 96 // rows
    at = jnp.stack([y, me, (d // near_mask) % 2, (d // far_mask) % 2]).astype(jnp.int32)
    tie = lax.optimization_barrier

    def cut(array, index):
        size = array.shape[0] // SLICES
        return lax.dynamic_slice_in_dim(array, index * size, size, 0)

    def pack(index):
        wide = cut(inner_weight, index)
        early = jnp.concatenate([cut(output_weight, index), wide[:, :model], wide[:, model:]], axis=0)
        return early.astype(F32)

    def pack_late(index):
        return cut(outer_weight, index).astype(F32)

    live = (lax.broadcasted_iota(jnp.int32, (length, 1), 0) < lengths[0]).astype(F32)
    kind = (entity_flags[0] == 1).astype(F32).reshape(length, 1)

    e0 = cross(pack(me))
    far_bias = cross(inner_bias)
    q2, k2, v = project(
        x, kind, query_weight, query_bias, key_weight, key_bias, value_weight, value_bias
    )
    e0, far_bias, l0, l6, q2 = tie((e0, far_bias, pack_late(me), pack_late(me ^ 6), q2))
    e2 = swap(e0, 2)
    e4 = swap(e0, 4)
    l0 = cross(l0)
    e1 = swap(e0, 1)
    context, extra = attend(q2, k2, v, live)
    sent = lax.dynamic_slice_in_dim(context, half * (1 - y), half, 0).astype(F32)
    e1, e2, e4, l0, l6, sent = tie((e1, e2, e4, l0, l6, sent))
    l2 = swap(l0, 2)
    l4 = swap(l0, 4)
    got = cross(sent)
    e6 = swap(e4, 2)
    l6 = cross(l6)
    per = width // devices
    where_row = lax.broadcasted_iota(jnp.int32, (model, width), 0)
    where_bias = lax.broadcasted_iota(jnp.int32, (model, width), 1)
    pick = (where_row == (where_bias // per) * rows + where_bias % per).astype(BF16)
    x_turned = turn(x)
    l2, l4, e2, e4, pick, x_turned = tie((l2, l4, e2, e4, pick, x_turned))
    e3 = swap(e2, 1)
    e5 = swap(e4, 1)
    got, e6, l6, e3, e5, l0, l2, l4 = tie((got, e6, l6, e3, e5, l0, l2, l4))
    l1 = swap(l0, 1)
    l3 = swap(l2, 1)
    l5 = swap(l4, 1)
    l7 = swap(l6, 1)
    e7 = swap(e6, 1)
    early = (e0, e1, e2, e3, e4, e5, e6, e7)
    late = (l0, l1, l2, l3, l4, l5, l6, l7)

    vec = jnp.stack(
        [output_bias, attn_gain, attn_shift, outer_bias, final_gain, final_shift, outer_bias, outer_bias]
    )
    bias = jnp.concatenate([inner_bias, far_bias, inner_bias, far_bias]).reshape(8, hidden // 2)
    ca, cb = first_cut(hidden // 2), hidden // 2
    da, db = hidden // 2 - ca, 0
    (
        out_rows, out_first, out_late, low, d_low, keep2, early_send, slope, n1, inv1, d_second, late_sums,
        far_early, far_late,
    ) = forward(
        at, x, cotangent[0], live, context, got, output_weight, inner_weight, outer_weight,
        early, late, vec, bias,
    )
    early_got = swap(early_send, 1)
    got_first = cross(out_first)
    d_first, dco, dcf, d_attn, keep0, keep1, late_send, first_sums, inner_sums = backward(
        at, slope, n1, inv1, d_second, d_low, context, got, output_weight, vec, inner_weight, outer_weight,
        far_early, far_late,
    )
    inner_columns = inner_sums[:4].reshape(2, model, 2)
    columns = jnp.concatenate([first_sums[:3].T, late_sums[:3].T, inner_columns[0], inner_columns[1]], axis=1)
    early_got, got_first, late_send, dcf, columns = tie((early_got, got_first, late_send, dcf, columns))
    late_got = swap(late_send, 1)
    d_got = cross(dcf)

    low_at, d_attn_at = (0, 2 * cb + model), (1, hidden)
    g2_keep, g2_send = weight_grads(
        at, (d_low,), (keep2,), (early_got,),
        (
            (
                3, far_mask * rows,
                ((0, (0, 0), (0, model), 0, cb), (0, (0, 0), (0, model + cb), cb, 2 * cb)),
            ),
        ),
    )
    g0_keep, g0_send, g1_keep, g1_send = weight_grads(
        at, (low, d_attn), (keep0, keep1), (early_got, late_got),
        (
            (
                2, near_mask * rows,
                (
                    (0, low_at, (1, 0), 0, ca), (0, low_at, (1, ca), ca, 2 * ca),
                    (1, d_attn_at, (0, 2 * model + hidden), 2 * ca, 2 * ca + width),
                ),
            ),
            (
                None, None,
                ((0, low_at, (1, 2 * ca), 0, da), (0, low_at, (1, 2 * ca + da), da, 2 * da)),
            ),
        ),
    )
    g0_send, g1_send, d_got = tie((g0_send, g1_send, d_got))
    g0_got = swap(g0_send, near_mask)
    g2_got = swap(g2_send, far_mask)
    g1_got = cross(g1_send)

    g0_send, g1_send, g2_send, dco, d_got = tie((g0_send, g1_send, g2_send, dco, d_got))
    chunks = tuple(length * k // 32 for k in (3, 4, 14, 11))
    group = rows if rows % 8 == 0 else None
    results = attend_back(
        at, q2, extra, k2, v, context, dco, d_got, live, kind, columns, pick,
        query_weight, key_weight, value_weight, x_turned, d_first, chunks, group,
    )
    parts, products = results[: len(chunks)], results[len(chunks) :]
    got_out = cross(out_late)

    def spread(array, done):
        dims = [1 if (1 << (bits - 1 - k)) in done else 2 for k in range(bits)]
        return array.reshape(*dims, rows, array.shape[-1])

    bit_values = jnp.stack([(d >> k) % 2 for k in range(bits)]).astype(jnp.int32)
    rest_masks = [1 << k for k in range(1, bits) if (1 << k) not in (near_mask, far_mask)]

    def term(array, *done):
        array = spread(array, done)
        return (array, {}, 0, array.shape[-1], None)

    def half_of(terms, mask, mine):
        k = mask.bit_length() - 1
        return [(array, {**chosen, bits - 1 - k: (k, mine)}, a, b, gate) for array, chosen, a, b, gate in terms]

    def kept(terms, mask):
        return half_of(terms, mask, True)

    def other(terms, mask):
        return half_of(terms, mask, False)

    def columns_of(terms, first, last):
        return [(array, chosen, a + first, a + last, gate) for array, chosen, a, _, gate in terms]

    def on_core(terms, core_index):
        return [(array, chosen, a, b, core_index) for array, chosen, a, b, _ in terms]

    def whole_of(array):
        return (array, {}, 0, array.shape[-1], None)

    def part_of(array, a, b):
        return (array, {}, a, b, None)

    g0_got, g1_got, g2_got, got_out, parts, products = tie((g0_got, g1_got, g2_got, got_out, parts, products))
    if group is None:
        c = [term(products[0])]
        e = [term(products[1])]
        c_send, e_send = combine(bit_values, [[other(c, 1)], [other(e, 1)]])
        c, e = kept(c, 1), kept(e, 1)
    else:
        c, e = [term(products[0], 1)], [term(products[2], 1)]
        c_send, e_send = spread(products[1], (1,)), spread(products[3], (1,))
    e_got = swap(e_send, 1)
    c_got = swap(c_send, 1)
    g0 = [term(g0_keep, near_mask), term(g0_got, near_mask)]
    g1 = [term(g1_keep), term(g1_got)]
    g2 = [term(g2_keep, far_mask), term(g2_got, far_mask)]
    (g2_send,) = combine(bit_values, [[other(g2, near_mask)]])
    sends = combine(bit_values, [[columns_of(g0, ca, 2 * ca + width)], [other(g1, near_mask)]])
    e_got, c_got, sends, parts = tie((e_got, c_got, sends, parts))
    e.append(whole_of(e_got))
    c.append(whole_of(c_got))
    g2_got = swap(g2_send, near_mask)
    g0_got = cross(sends[0])
    g1_got = swap(sends[1], near_mask)
    (e_send,) = combine(bit_values, [[other(e, far_mask)]])
    e_got = swap(e_send, far_mask)
    part0 = cross(parts[0])
    g0_got, g1_got, g2_got, e_got, part0, parts = tie((g0_got, g1_got, g2_got, e_got, part0, parts))
    t = [
        *on_core(columns_of(g0, 2 * ca, 2 * ca + width), 0),
        *on_core([part_of(g0_got, ca, ca + width)], 1),
    ]
    g0 = [*columns_of(g0, 0, ca), part_of(g0_got, 0, ca)]
    g1 = [*kept(g1, near_mask), whole_of(g1_got)]
    g2 = [*kept(g2, near_mask), whole_of(g2_got)]
    e = [*kept(e, far_mask), whole_of(e_got)]

    (three_send,) = combine(bit_values, [[other(terms, far_mask) for terms in (g0, t, g1)]])
    sends = combine(bit_values, [[columns_of(g2, cb, 2 * cb)], [other(c, near_mask)]])
    sends, parts = tie((sends, parts))
    three_got = swap(three_send, far_mask)
    g2_got = cross(sends[0])
    c_got = swap(sends[1], near_mask)
    part1 = cross(parts[1])
    three_got, g2_got, c_got, part1, parts = tie((three_got, g2_got, c_got, part1, parts))
    g0 = [*kept(g0, far_mask), part_of(three_got, 0, ca)]
    t = [*kept(t, far_mask), part_of(three_got, ca, ca + width)]
    g1 = [*kept(g1, far_mask), part_of(three_got, ca + width, three_got.shape[-1])]
    g2 = [*columns_of(g2, 0, cb), whole_of(g2_got)]
    c = [*kept(c, near_mask), whole_of(c_got)]

    main = (g0, g1, g2, t)
    sizes = (ca, da + db, cb, width)
    ends = [sum(sizes[:k]) for k in range(len(sizes) + 1)]
    mask = rest_masks[0]
    (main_send,) = combine(bit_values, [[other(terms, mask) for terms in main]])
    main_send, late_bits = tie((main_send, bit_values))
    sends = combine(late_bits, [[other(e, near_mask)], [other(c, far_mask)]])
    sends, parts = tie((sends, parts))
    got_z = swap(main_send, mask)
    part2 = cross(parts[2])
    c_got = swap(sends[1], far_mask)
    e_got = swap(sends[0], near_mask)
    layer_out = place_rows(at, out_rows, got_first, got_out)
    got_z, e_got, c_got, part2, parts, layer_out = tie((got_z, e_got, c_got, part2, parts, layer_out))
    main = [[*kept(terms, mask), part_of(got_z, ends[n], ends[n + 1])] for n, terms in enumerate(main)]
    e = [*kept(e, near_mask), whole_of(e_got)]
    c = [*kept(c, far_mask), whole_of(c_got)]
    for mask in rest_masks[1:]:
        (send,) = combine(bit_values, [[other(terms, mask) for terms in main]])
        got_z = swap(send, mask)
        main = [[*kept(terms, mask), part_of(got_z, ends[n], ends[n + 1])] for n, terms in enumerate(main)]

    for k, mask in enumerate(rest_masks):
        (pair_send,) = combine(bit_values, [[other(c, mask), other(e, mask)]])
        outputs = [[kept(c, mask), kept(e, mask)]]
        if k == 0:
            outputs += [[other(terms, 1) for terms in main], [kept(terms, 1) for terms in main]]
        sends = combine(bit_values, outputs)
        if k == 0:
            sends, parts = tie((sends, parts))
        pair_got = swap(pair_send, mask)
        if k == 0:
            part3 = cross(parts[3])
            got_last = swap(sends[1], 1)
            keep = sends[2]
        pair_keep = sends[0]
        wide = pair_keep.shape[-1]
        c = [part_of(pair_keep, 0, 3 * width), part_of(pair_got, 0, 3 * width)]
        e = [part_of(pair_keep, 3 * width, wide), part_of(pair_got, 3 * width, wide)]

    got_last = got_last.reshape(rows, -1)
    keep = keep.reshape(rows, -1)
    low_half = jnp.where(core == 0, keep, got_last)
    high_half = jnp.where(core == 0, got_last, keep)
    at2 = ca + da + db
    inner_half = lambda array: [array[:, : ca + da]]
    at3 = at2 + cb
    outer_half = lambda array: [array[:, at2:at3], array[:, ca + da : at2]]
    t = keep[:, at3:] + got_last[:, at3:]
    grad_inner = jnp.concatenate(inner_half(low_half) + inner_half(high_half), axis=1)
    grad_outer = jnp.concatenate(outer_half(low_half) + outer_half(high_half), axis=1).T
    grad_output = t.T
    sent_parts = (part0, part1, part2)
    input_first = jnp.concatenate([(a + b).astype(BF16) for a, b in zip(parts, sent_parts)], axis=0)
    pair_got, part3, input_first = tie((pair_got, part3, input_first))
    pair = (pair_keep + pair_got).reshape(rows, -1)
    c, e = pair[:, : 3 * width], pair[:, 3 * width :]
    last = e[:, 3 * width + 6 : 3 * width + 16]
    last_got = cross(last)
    small = last[:, :6] + last_got[:, :6]
    inner_two = last[:, 6:8] + last_got[:, 8:]
    input_grad = jnp.concatenate([input_first, (parts[3] + part3).astype(BF16)], axis=0)

    piece = lambda array, k: array[:, width * k : width * (k + 1)]
    grad_query_weight = jnp.stack([piece(c, 0), piece(c, 1), piece(c, 2), piece(e, 0)])
    biases = e[:per, 3 * width : 3 * width + 6].T
    return (
        layer_out[None],
        input_grad[None],
        grad_query_weight,
        biases[:4],
        piece(e, 1),
        biases[4],
        piece(e, 2),
        biases[5],
        grad_output,
        small[:, 0],
        small[:, 1],
        small[:, 2],
        grad_inner,
        inner_two.reshape(2 * rows),
        grad_outer,
        small[:, 3],
        small[:, 4],
        small[:, 5],
    )


def solution(mesh):
    return jax.shard_map(
        functools.partial(per_device, mesh.shape["dp"]),
        mesh=mesh,
        in_specs=(
            P("dp", None, None),
            P("dp"),
            P("dp", None),
            P(None, None, "tensor"),
            P(None, "tensor"),
            P(None, "tensor"),
            P("tensor"),
            P(None, "tensor"),
            P("tensor"),
            P("tensor", None),
            P(),
            P(),
            P(),
            P(None, "tensor"),
            P("tensor"),
            P("tensor", None),
            P(),
            P(),
            P(),
            P("dp", None, None),
        ),
        out_specs=(
            P("dp", None, None),
            P("dp", None, None),
            P(None, "dp", "tensor"),
            P(None, ("tensor", "dp")),
            P("dp", "tensor"),
            P(("tensor", "dp")),
            P("dp", "tensor"),
            P(("tensor", "dp")),
            P("tensor", "dp"),
            P("dp"),
            P("dp"),
            P("dp"),
            P("dp", "tensor"),
            P(("tensor", "dp")),
            P("tensor", "dp"),
            P("dp"),
            P("dp"),
            P("dp"),
        ),
        check_vma=False,
    )
```

```python
import functools
import math

import jax
import jax.numpy as jnp
from jax import lax
from jax.experimental import pallas as pl
from jax.experimental.pallas import tpu as pltpu
from jax.sharding import PartitionSpec as P

HD = 64
SLICES = 8
MASKED = -1e30
NORM_EPS = 1e-05

F32 = jnp.float32
BF16 = jnp.bfloat16
NN = (((1,), (0,)), ((), ()))
NT = (((1,), (1,)), ((), ()))
TN = (((0,), (0,)), ((), ()))


def mm(left, right, dims):
    return lax.dot_general(left, right, dims, preferred_element_type=F32)


def struct(shape, kind):
    return jax.ShapeDtypeStruct(shape, kind)


def params(mib):
    return pltpu.CompilerParams(vmem_limit_bytes=mib << 20)


def cost(flops, moved, special=0):
    return pl.CostEstimate(flops=int(flops), bytes_accessed=int(moved), transcendentals=int(special))


def whole_block(shape):
    return pl.BlockSpec(shape, lambda *_: (0,) * len(shape), pipeline_mode=pl.Buffered(1))


def three_pieces(value):
    high = value.astype(BF16).astype(F32)
    rest = value - high
    middle = rest.astype(BF16).astype(F32)
    return high, middle, rest - middle


def project_kernel(x_ref, kind_ref, wq_ref, bq_ref, wk_ref, bk_ref, wv_ref, bv_ref, q2_ref, k2_ref, v_ref):
    x = x_ref[...]
    entity = kind_ref[...] > 0.5
    rows = x.shape[0]
    width = wk_ref.shape[1]

    weights = jnp.concatenate([*(wq_ref[c] for c in range(4)), wk_ref[...], wv_ref[...]], axis=1)
    biases = jnp.concatenate([*(bq_ref[c : c + 1, :] for c in range(4)), bk_ref[...], bv_ref[...]], axis=1)
    products = mm(x, weights, NN) + biases

    def query(c):
        return products[:, width * c : width * (c + 1)]

    scale = 1.0 / math.sqrt(HD)
    to_word = jnp.where(entity, query(2), query(0)).astype(BF16).astype(F32) * scale
    to_entity = jnp.where(entity, query(3), query(1)).astype(BF16).astype(F32) * scale
    keys = query(4).astype(BF16).astype(F32)
    v_ref[...] = query(5).astype(BF16)
    left = lax.broadcasted_iota(jnp.int32, (rows, 2 * HD), 1) < HD
    held = left != entity
    for p in range(width // (2 * HD)):
        cols = slice(2 * HD * p, 2 * HD * (p + 1))
        w, e, k = to_word[:, cols], to_entity[:, cols], keys[:, cols]
        w_roll, e_roll, k_roll = (pltpu.roll(t, HD, 1) for t in (w, e, k))
        even = slice(4 * HD * p, 4 * HD * p + 2 * HD)
        odd = slice(4 * HD * p + 2 * HD, 4 * HD * (p + 1))
        q2_ref[:, even] = jnp.where(left, w, e_roll).astype(BF16)
        q2_ref[:, odd] = jnp.where(left, w_roll, e).astype(BF16)
        k2_ref[:, even] = jnp.where(held, jnp.where(left, k, k_roll), 0.0).astype(BF16)
        k2_ref[:, odd] = jnp.where(held, jnp.where(left, k_roll, k), 0.0).astype(BF16)


def project(x, kind, wq, bq, wk, bk, wv, bv, rows=256):
    length, model = x.shape
    width = wk.shape[1]
    rows = min(rows, length)
    tile = lambda w: pl.BlockSpec((rows, w), lambda i: (i, 0))
    return pl.pallas_call(
        project_kernel,
        grid=(length // rows,),
        in_specs=[
            tile(model),
            tile(1),
            whole_block(wq.shape),
            whole_block(bq.shape),
            whole_block(wk.shape),
            whole_block((1, width)),
            whole_block(wv.shape),
            whole_block((1, width)),
        ],
        out_specs=[tile(2 * width), tile(2 * width), tile(width)],
        out_shape=[
            struct((length, 2 * width), BF16),
            struct((length, 2 * width), BF16),
            struct((length, width), BF16),
        ],
        compiler_params=params(63),
        cost_estimate=cost(12 * length * model * width, 16 * model * width + 12 * length * width),
        name="project",
    )(x, kind, wq, bq, wk, bk.reshape(1, width), wv, bv.reshape(1, width))


def key_extra(live, rows):
    lane = lax.broadcasted_iota(jnp.int32, (rows, 2 * HD), 1)
    return jnp.where(
        lane == 0, jnp.where(live, 0.0, MASKED), jnp.where(lane < 4, 1.0, 0.0)
    ).astype(BF16)


def attend_kernel(q2_ref, k2_ref, v_ref, live_ref, out_ref, extra_ref, turned_ref, both_ref):
    length = k2_ref.shape[0]
    h = pl.program_id(1)

    @pl.when(h == 0)
    def _():
        turned = v_ref[...].astype(F32).T.astype(BF16)
        turned_ref[0] = turned[:HD]
        turned_ref[1] = turned[HD:]

    lane = lax.broadcasted_iota(jnp.int32, (length, 2 * HD), 1)
    one = jnp.where(lane == 0, 1.0, 0.0).astype(BF16)
    keys = jnp.concatenate([k2_ref[...], key_extra(live_ref[...] > 0.5, length)], axis=1)
    query = jnp.concatenate([q2_ref[...], one], axis=1)
    scores = mm(keys, query, NT)
    top = jnp.max(scores, axis=0, keepdims=True)
    weights = jnp.exp(scores - top)
    norm = jnp.sum(weights, axis=0, keepdims=True)
    summed = mm(turned_ref[h], weights.astype(BF16), NN)
    both_ref[h] = summed * (1.0 / norm)
    pieces = three_pieces(-(top + jnp.log(norm)))
    filled = jnp.concatenate(
        [jnp.ones((1, length), F32), *pieces, jnp.zeros((2 * HD - 4, length), F32)], axis=0
    )
    extra_ref[...] = filled.T.astype(BF16)

    @pl.when(h == 1)
    def _():
        out_ref[...] = jnp.concatenate([both_ref[0], both_ref[1]], axis=0).T.astype(BF16)


def attend(q2, k2, v, live):
    length, width = v.shape
    head = pl.BlockSpec((length, 2 * HD), lambda p, h: (0, 2 * p + h))
    pair = pl.BlockSpec((length, 2 * HD), lambda p, h: (0, p))
    return pl.pallas_call(
        attend_kernel,
        grid=(width // (2 * HD), 2),
        in_specs=[head, head, pair, whole_block((length, 1))],
        out_specs=[pair, head],
        out_shape=[struct((length, width), BF16), struct((length, 2 * width), BF16)],
        scratch_shapes=[pltpu.VMEM((2, HD, length), BF16), pltpu.VMEM((2, HD, length), F32)],
        compiler_params=params(63),
        cost_estimate=cost(10 * length * length * width, 20 * length * width, length * length * width // HD),
        name="attend",
    )(q2, k2, v, live)


def attend_back_kernel(
    count, group, y_ref, q2_ref, extra_ref, k2_ref, v_ref, o_ref, own_ref, got_ref, live_ref, kind_ref, columns_ref, pick_ref,
    wq_hbm, wk_hbm, wv_hbm, turned_hbm, first_hbm, *rest,
):
    outs = count + (2 if group is None else 4)
    part_hbm, grads_hbm = rest[:count], rest[count:outs]
    (
        dk_ref, dv_ref, dq_ref, product_ref, d_ref, all_ref, sums_ref, weights_ref, turned_ref, first_ref,
        part_ref, grads_ref, in_sem, out_sem,
    ) = rest[outs:]
    length = k2_ref.shape[0]
    width = wk_hbm.shape[1]
    p, h = pl.program_id(0), pl.program_id(1)
    pairs = width // (2 * HD)
    lane = lax.broadcasted_iota(jnp.int32, (length, 2 * HD), 1)
    left = lane < HD

    def arriving():
        copies = [
            pltpu.make_async_copy(wq_hbm.at[c], weights_ref.at[:, width * c : width * (c + 1)], in_sem.at[c])
            for c in range(4)
        ]
        copies.append(pltpu.make_async_copy(wk_hbm, weights_ref.at[:, 4 * width : 5 * width], in_sem.at[4]))
        copies.append(pltpu.make_async_copy(wv_hbm, weights_ref.at[:, 5 * width : 6 * width], in_sem.at[5]))
        copies.append(pltpu.make_async_copy(turned_hbm, turned_ref, in_sem.at[6]))
        copies.append(pltpu.make_async_copy(first_hbm, first_ref, in_sem.at[7]))
        return copies

    @pl.when(jnp.logical_and(p == 0, h == 0))
    def _():
        for copy in arriving():
            copy.start()

    @pl.when(h == 0)
    def _():
        first = y_ref[0] == 0
        own, got = own_ref[...], got_ref[...]
        joined = jnp.concatenate([jnp.where(first, own, got), jnp.where(first, got, own)], axis=0)
        product_ref[...] = joined * o_ref[...].astype(F32)
        d_ref[...] = joined.astype(BF16)

    d_context = d_ref[...]
    base = HD * (1 - h)
    mine = jnp.logical_and(lane >= HD - base, lane < 2 * HD - base)
    delta = jnp.sum(jnp.where(mine, product_ref[...], 0.0), axis=1, keepdims=True)
    high, middle, low = three_pieces(-delta)
    pieces = jnp.where(
        lane == base, high, jnp.where(lane == base + 1, middle, jnp.where(lane == base + 2, low, 0.0))
    ).astype(BF16)
    d_wide = jnp.where(mine, d_context, pieces)
    q2, k2 = q2_ref[...], k2_ref[...]
    query = jnp.concatenate([q2, extra_ref[...]], axis=1)
    keys = jnp.concatenate([k2, key_extra(live_ref[...] > 0.5, length)], axis=1)
    probs = jnp.exp(mm(keys, query, NT))
    ones = jnp.where((lane >= base) & (lane < base + 3), 1.0, 0.0).astype(BF16)
    d_probs = mm(jnp.where(mine, v_ref[...], ones), d_wide, NT)
    d_scores = (probs * d_probs).astype(BF16)
    dv_ref[h] = mm(probs.astype(BF16), d_context, NN)
    dk_ref[h] = mm(d_scores, q2, NN)
    dq_ref[h] = mm(k2, d_scores, TN).T * (1.0 / math.sqrt(HD))

    @pl.when(h == 1)
    def _():
        entity = kind_ref[...] > 0.5
        even, odd = dq_ref[0], dq_ref[1]
        to_word = jnp.where(left, even, pltpu.roll(odd, HD, 1)).astype(BF16).astype(F32)
        to_entity = jnp.where(left, pltpu.roll(even, HD, 1), odd).astype(BF16).astype(F32)
        even, odd = dk_ref[0], dk_ref[1]
        even = jnp.where(entity, pltpu.roll(even, HD, 1), even)
        odd = jnp.where(entity, odd, pltpu.roll(odd, HD, 1))
        grads = [
            jnp.where(entity, 0.0, to_word),
            jnp.where(entity, 0.0, to_entity),
            jnp.where(entity, to_word, 0.0),
            jnp.where(entity, to_entity, 0.0),
            jnp.where(left, even, odd).astype(BF16).astype(F32),
            jnp.where(left, dv_ref[0], dv_ref[1]).astype(BF16).astype(F32),
        ]
        for c, grad in enumerate(grads):
            all_ref[p, c] = grad.astype(BF16)
        sums = [jnp.sum(grad, axis=0, keepdims=True) for grad in grads]
        sums_ref[p] = jnp.concatenate([*sums, jnp.zeros((2, 2 * HD), F32)], axis=0)

    @pl.when(jnp.logical_and(p == pairs - 1, h == 1))
    def _():
        for copy in arriving():
            copy.wait()
        grads = jnp.concatenate([all_ref[k, c] for c in range(6) for k in range(pairs)], axis=1)
        half = first_ref.shape[0]
        leaving = []

        def leave(source, target):
            copy = pltpu.make_async_copy(source, target, out_sem.at[len(leaving)])
            copy.start()
            leaving.append(copy)

        for i in range(2):
            rows = slice(i * half, (i + 1) * half)
            total = mm(grads[rows], weights_ref[...], NT)
            part_ref[rows, :] = total + jnp.where(y_ref[0] == i, first_ref[...], 0.0)
        begin = 0
        for target in part_hbm:
            leave(part_ref.at[begin : begin + target.shape[0], :], target)
            begin += target.shape[0]
        model = turned_ref.shape[0]
        sums = jnp.concatenate([sums_ref[k] for k in range(pairs)], axis=1)
        pieces = jnp.concatenate([piece.astype(BF16) for piece in three_pieces(sums)], axis=0)
        picked = mm(pick_ref[...], pieces, NT)
        biases = picked[:, :6] + picked[:, 8:14] + picked[:, 16:22]
        seen = columns_ref.shape[1] // 2
        rest_zero = jnp.zeros((model, 128 - 6 - seen), F32)
        extra = jnp.concatenate(
            [
                biases, columns_ref[:, :seen], rest_zero,
                jnp.zeros((model, 6), F32), columns_ref[:, seen:], rest_zero,
            ],
            axis=1,
        )
        lower = y_ref[1] % 2 == 0

        def place(array, cols, value):
            if group is None:
                grads_ref[array, :, cols] = value
                return
            blocks = value.reshape(model // (2 * group), 2, group, value.shape[1])
            first, second = blocks[:, 0], blocks[:, 1]
            for k, (one, other) in enumerate(((first, second), (second, first))):
                picked_rows = jnp.where(lower, one, other).reshape(model // 2, value.shape[1])
                grads_ref[array, k * (model // 2) : (k + 1) * (model // 2), cols] = picked_rows

        for array in range(2):

            def one(i, carry, array=array):
                grad = jnp.concatenate([all_ref[k, 3 * array + i] for k in range(pairs)], axis=1)
                at = pl.multiple_of(width * i, 128)
                place(array, pl.ds(at, width), mm(turned_ref[...], grad, NN))
                return carry

            lax.fori_loop(0, 3, one, 0)
            wide = 3 * width
            if array:
                place(array, slice(wide, wide + 256), extra)
                wide += 256
            if group is None:
                leave(grads_ref.at[array, :, :wide], grads_hbm[array])
            else:
                for k in (1, 0):
                    rows = slice(k * (model // 2), (k + 1) * (model // 2))
                    leave(grads_ref.at[array, rows, :wide], grads_hbm[2 * array + k])
        for copy in leaving:
            copy.wait()


def attend_back(
    y, q2, extra, k2, v, o, own, got, live, kind, columns, pick, wq, wk, wv, turned, first, chunks, group
):
    length, width = v.shape
    half, model = first.shape
    pairs = width // (2 * HD)
    head = pl.BlockSpec((length, 2 * HD), lambda p, h, *_: (0, 2 * p + h))
    pair = pl.BlockSpec((length, 2 * HD), lambda p, h, *_: (0, p))
    part = pl.BlockSpec((half, 2 * HD), lambda p, h, *_: (0, p))
    anywhere = pl.BlockSpec(memory_space=pl.ANY)
    shapes = [struct((rows, model), F32) for rows in chunks]
    for wide in (3 * width, 3 * width + 256):
        shapes += [struct((model, wide), F32)] if group is None else [struct((model // 2, wide), F32)] * 2
    return pl.pallas_call(
        functools.partial(attend_back_kernel, len(chunks), group),
        grid_spec=pltpu.PrefetchScalarGridSpec(
            num_scalar_prefetch=1,
            grid=(pairs, 2),
            in_specs=[
                head, head, head, pair, pair, part, part, whole_block((length, 1)), whole_block((length, 1)),
                whole_block(columns.shape), whole_block(pick.shape),
                *[anywhere] * 5,
            ],
            out_specs=[anywhere] * len(shapes),
            scratch_shapes=[
                *[pltpu.VMEM((2, length, 2 * HD), F32)] * 3,
                pltpu.VMEM((length, 2 * HD), F32),
                pltpu.VMEM((length, 2 * HD), BF16),
                pltpu.VMEM((pairs, 6, length, 2 * HD), BF16),
                pltpu.VMEM((pairs, 8, 2 * HD), F32),
                pltpu.VMEM((model, 6 * width), BF16),
                pltpu.VMEM((model, length), BF16),
                pltpu.VMEM((half, model), F32),
                pltpu.VMEM((length, model), F32),
                pltpu.VMEM((2, model, 3 * width + 256), F32),
                pltpu.SemaphoreType.DMA((8,)),
                pltpu.SemaphoreType.DMA((len(shapes),)),
            ],
        ),
        out_shape=shapes,
        compiler_params=params(63),
        cost_estimate=cost(20 * length * length * width, 40 * length * width, length * length * width // HD),
        name="attend_back",
    )(y, q2, extra, k2, v, o, own, got, live, kind, columns, pick, wq, wk, wv, turned, first)


def normalise(value):
    centre = value - jnp.mean(value, axis=-1, keepdims=True)
    inverse = lax.rsqrt(jnp.mean(centre * centre, axis=-1, keepdims=True) + NORM_EPS)
    return centre * inverse, inverse


def normalise_back(scaled, normal, inverse):
    return inverse * (
        scaled
        - jnp.mean(scaled, axis=-1, keepdims=True)
        - normal * jnp.mean(scaled * normal, axis=-1, keepdims=True)
    )


def gelu_pair(values):
    cumulative = 0.5 * (1.0 + lax.erf(values * (1.0 / math.sqrt(2.0))))
    density = jnp.exp(-0.5 * values * values) * (1.0 / math.sqrt(2.0 * math.pi))
    return values * cumulative, cumulative + values * density


def column_sum(value):
    return jnp.sum(value, axis=0, keepdims=True)


def first_cut(half):
    return half // 2


def middle_sizes(wi, wo, early):
    hidden, model, width = wi.shape[1], wo.shape[1], wo.shape[0]
    cut = [width // SLICES, (width + model) // SLICES, (width + 2 * model) // SLICES]
    return hidden, hidden // 2, model, width, cut


def far_block(ref, a, b):
    return ref[:, a:b, :].reshape(SLICES * (b - a), ref.shape[2])


def far_outer(ref, part, half):
    per = SLICES // 2
    return ref[per * (part - 2) : per * (part - 1), :, :].reshape(half, ref.shape[2])


def by_core(lower, values):
    first, second = (value.astype(F32) for value in values)
    keep = jnp.where(lower, first, second).astype(BF16)
    return keep, jnp.where(lower, second, first)


def forward_kernel(at_ref, x_ref, cot_ref, live_ref, own_ref, got_ref, wo_ref, wi_hbm, wu_hbm, *rest):
    arrived = rest[:SLICES]
    arrived_late = rest[SLICES : 2 * SLICES]
    (
        vec_ref, bias_ref, out_ref, out_first_ref, out_late_ref, low_ref, d_low_ref, keep_ref, send_ref,
        slope_ref, n1_ref, inv1_ref, d_second_ref, sums_ref, early_hbm, late_hbm,
        early_ref, late_ref, wi_ref, wu_ref, raw_ref, raw_late_ref, in_sem, out_sem,
    ) = rest[2 * SLICES :]
    step = pl.program_id(0)
    me = at_ref[1]
    lower = me % 2 == 0
    hidden, half, model, width, cut = middle_sizes(wi_hbm, wo_ref, early_ref)

    def weight_copies():
        stages = [[], [], [], [], []]
        for k in range(SLICES):
            for stage, source, target in (
                (0, arrived[k].at[: cut[0], :], raw_ref.at[k, : cut[0], :]),
                (2, arrived[k].at[cut[0] :, :], raw_ref.at[k, cut[0] :, :]),
                (4, arrived_late[k], raw_late_ref.at[k]),
            ):
                stages[stage].append(pltpu.make_async_copy(source, target, in_sem.at[stage * SLICES + k]))
        stages[1].append(pltpu.make_async_copy(wi_hbm, wi_ref, in_sem.at[SLICES]))
        stages[3].append(pltpu.make_async_copy(wu_hbm, wu_ref, in_sem.at[3 * SLICES]))
        return stages

    def leaving():
        return [
            pltpu.make_async_copy(early_ref, early_hbm, out_sem.at[0]),
            pltpu.make_async_copy(late_ref, late_hbm, out_sem.at[1]),
        ]

    def arrive(*wanted):
        @pl.when(step == 0)
        def _():
            stages = weight_copies()
            for stage in wanted:
                for copy in stages[stage]:
                    copy.wait()
            for k in range(SLICES):
                if 0 in wanted:
                    early_ref[me ^ k, : cut[0], :] = raw_ref[k, : cut[0], :].astype(BF16)
                if 2 in wanted:
                    early_ref[me ^ k, cut[0] :, :] = raw_ref[k, cut[0] :, :].astype(BF16)
                if 4 in wanted:
                    late_ref[me ^ k] = raw_late_ref[k].astype(BF16)
            if 4 in wanted:
                for copy in leaving():
                    copy.start()

    @pl.when(step == 0)
    def _():
        for stage in weight_copies():
            for copy in stage:
                copy.start()

    arrive(0)
    vec = [vec_ref[k : k + 1, :] for k in range(6)]
    got = got_ref[...].astype(BF16)
    own = own_ref[...]
    first = mm(own, wo_ref[...], NN) + mm(got, far_block(early_ref, 0, cut[0]), NN) + vec[0] + x_ref[...].astype(F32)
    n1, inv1 = normalise(first)
    n1_ref[...] = n1
    inv1_ref[...] = inv1
    normed = n1 * vec[1] + vec[2]
    low = normed.astype(BF16)
    low_ref[...] = low
    at_low = model + hidden
    send_ref[:, at_low : at_low + model] = low.astype(F32)
    _, send = by_core(lower, (own, got))
    send_ref[:, at_low + model :] = send
    second = vec[3] + normed
    arrive(1, 3)
    for far in range(2):
        if far:
            arrive(2, 4)
        pair = []
        for part in (2 * far, 2 * far + 1):
            inner = wi_ref[:, half * part : half * (part + 1)] if part < 2 else far_block(early_ref, cut[part - 2], cut[part - 1])
            pre = mm(low, inner, NN) + bias_ref[part : part + 1, :]
            active, slope = gelu_pair(pre)
            active = active.astype(BF16)
            slope_ref[:, half * part : half * (part + 1)] = slope.astype(BF16)
            pair.append(active)
            outer = wu_ref[half * part : half * (part + 1), :] if part < 2 else far_outer(late_ref, part, half)
            second = second + mm(active, outer, NN)
        keep, send = by_core(lower, pair)
        keep_ref[:, half * far : half * (far + 1)] = keep
        send_ref[:, model + half * far : model + half * (far + 1)] = send
    n2, inv2 = normalise(second)
    live = live_ref[...] > 0.5
    result = jnp.where(live, n2 * vec[4] + vec[5], 0.0).astype(BF16)
    out_ref[...] = result
    out_first_ref[...] = result[:, : model // 2].astype(F32)
    out_late_ref[...] = result[:, model // 2 :].astype(F32)
    dz = jnp.where(live, cot_ref[...].astype(F32), 0.0)
    d_second = normalise_back(dz * vec[4], n2, inv2)
    d_second_ref[...] = d_second
    d_low = d_second.astype(BF16)
    d_low_ref[...] = d_low
    send_ref[:, :model] = d_low.astype(F32)
    sums = jnp.concatenate(
        [column_sum(d_second), column_sum(dz * n2), column_sum(dz), jnp.zeros((5, model), F32)], axis=0
    )

    @pl.when(step == 0)
    def _():
        sums_ref[...] = sums

    @pl.when(step != 0)
    def _():
        sums_ref[...] += sums

    @pl.when(step == pl.num_programs(0) - 1)
    def _():
        for copy in leaving():
            copy.wait()


def forward(at, x, cot, live, context, got, wo, wi, wu, early, late, vec, bias, rows=256):
    half, width = got.shape
    model, hidden = wi.shape
    rows = min(rows, half)
    steps = half // rows
    mine = lambda w: pl.BlockSpec((rows, w), lambda i, s: (i + s[0] * steps, 0))
    tile = lambda w: pl.BlockSpec((rows, w), lambda i, s: (i, 0))
    anywhere = pl.BlockSpec(memory_space=pl.ANY)
    widths = (
        (model, BF16), (model // 2, F32), (model // 2, F32), (model, BF16), (model, BF16), (hidden, BF16),
        (2 * model + hidden + width, F32), (2 * hidden, BF16), (model, F32), (1, F32), (model, F32),
    )
    far_shapes = [(SLICES, *early[0].shape), (SLICES, *late[0].shape)]
    return pl.pallas_call(
        forward_kernel,
        grid_spec=pltpu.PrefetchScalarGridSpec(
            num_scalar_prefetch=1,
            grid=(steps,),
            in_specs=[
                mine(model), mine(model), mine(1), mine(width), tile(width),
                whole_block(wo.shape), *[anywhere] * (2 + 2 * SLICES),
                whole_block(vec.shape), whole_block(bias.shape),
            ],
            out_specs=[
                *(tile(w) for w, _ in widths), pl.BlockSpec((8, model), lambda i, s: (0, 0)), anywhere, anywhere,
            ],
            scratch_shapes=[
                *(pltpu.VMEM(shape, BF16) for shape in far_shapes),
                pltpu.VMEM(wi.shape, BF16),
                pltpu.VMEM(wu.shape, BF16),
                *(pltpu.VMEM(shape, F32) for shape in far_shapes),
                pltpu.SemaphoreType.DMA((5 * SLICES,)),
                pltpu.SemaphoreType.DMA((2,)),
            ],
        ),
        out_shape=[
            *(struct((half, w), kind) for w, kind in widths), struct((8, model), F32),
            *(struct(shape, BF16) for shape in far_shapes),
        ],
        compiler_params=params(63),
        cost_estimate=cost(8 * half * model * hidden, 24 * model * hidden, 4 * half * hidden),
        name="forward",
    )(at, x, cot, live, context, got, wo, wi, wu, *early, *late, vec, bias)


def backward_kernel(
    at_ref, slope_ref, n1_ref, inv1_ref, d_second_ref, d_low_ref, own_ref, got_ref, wo_ref, vec_ref,
    wi_hbm, wu_hbm, early_hbm, late_hbm,
    first_ref, dco_ref, dcf_ref, d_attn_ref, keep0_ref, keep1_ref, send_ref, sums_ref, inner_sums_ref,
    wi_ref, wu_ref, early_ref, late_ref, in_sem,
):
    step = pl.program_id(0)
    lower = at_ref[1] % 2 == 0
    hidden, half, model, width, cut = middle_sizes(wi_hbm, wo_ref, early_ref)
    ca = first_cut(half)

    def copies():
        pairs = ((wu_hbm, wu_ref), (wi_hbm, wi_ref), (late_hbm, late_ref), (early_hbm, early_ref))
        return [pltpu.make_async_copy(*pair, in_sem.at[k]) for k, pair in enumerate(pairs)]

    @pl.when(step == 0)
    def _():
        for copy in copies():
            copy.start()

    d_low = d_low_ref[...]
    n1 = n1_ref[...]
    d_normed = d_second_ref[...]
    inner_sums = []
    for far in range(2):

        @pl.when(step == 0)
        def _():
            for copy in copies()[2 * far : 2 * far + 2]:
                copy.wait()

        pair = []
        for part in (2 * far, 2 * far + 1):
            outer = wu_ref[half * part : half * (part + 1), :] if part < 2 else far_outer(late_ref, part, half)
            inner = wi_ref[:, half * part : half * (part + 1)] if part < 2 else far_block(early_ref, cut[part - 2], cut[part - 1])
            d_hidden = mm(d_low, outer, NT)
            d_inner = (d_hidden * slope_ref[:, half * part : half * (part + 1)].astype(F32)).astype(BF16)
            pair.append(d_inner)
            inner_sums.append(column_sum(d_inner.astype(F32)))
            d_normed = d_normed + mm(d_inner, inner, NT)
        keep, send = by_core(lower, pair)
        da = half - ca
        keep0_ref[:, ca * far : ca * (far + 1)] = keep[:, :ca]
        keep1_ref[:, da * far : da * (far + 1)] = keep[:, ca:]
        send_ref[:, ca * far : ca * (far + 1)] = send[:, :ca]
        send_ref[:, 2 * ca + da * far : 2 * ca + da * (far + 1)] = send[:, ca:]
    d_first = normalise_back(d_normed * vec_ref[1:2, :], n1, inv1_ref[...])
    first_ref[...] = d_first
    d_attn = d_first.astype(BF16)
    d_attn_ref[...] = d_attn
    send_ref[:, hidden:] = d_attn.astype(F32)
    dco_ref[...] = mm(d_attn, wo_ref[...], NT).astype(BF16).astype(F32)
    dcf_ref[...] = mm(d_attn, far_block(early_ref, 0, cut[0]), NT).astype(BF16).astype(F32)
    keep, _ = by_core(lower, (own_ref[...], got_ref[...]))
    keep0_ref[:, 2 * ca :] = keep
    sums = jnp.concatenate(
        [column_sum(d_first), column_sum(d_normed * n1), column_sum(d_normed), jnp.zeros((5, model), F32)], axis=0
    )
    inner_sums = jnp.concatenate([*inner_sums, jnp.zeros((4, half), F32)], axis=0)

    @pl.when(step == 0)
    def _():
        sums_ref[...] = sums
        inner_sums_ref[...] = inner_sums

    @pl.when(step != 0)
    def _():
        sums_ref[...] += sums
        inner_sums_ref[...] += inner_sums


def backward(at, slope, n1, inv1, d_second, d_low, context, got, wo, vec, wi, wu, early, late, rows=256):
    half, width = got.shape
    model, hidden = wi.shape
    rows = min(rows, half)
    steps = half // rows
    ca = first_cut(hidden // 2)
    mine = lambda w: pl.BlockSpec((rows, w), lambda i, s: (i + s[0] * steps, 0))
    tile = lambda w: pl.BlockSpec((rows, w), lambda i, s: (i, 0))
    anywhere = pl.BlockSpec(memory_space=pl.ANY)
    widths = (
        (model, F32), (width, F32), (width, F32), (model, BF16), (2 * ca + width, BF16), (hidden - 2 * ca, BF16),
        (hidden + model, F32),
    )
    return pl.pallas_call(
        backward_kernel,
        grid_spec=pltpu.PrefetchScalarGridSpec(
            num_scalar_prefetch=1,
            grid=(steps,),
            in_specs=[
                tile(2 * hidden), tile(model), tile(1), tile(model), tile(model), mine(width), tile(width),
                whole_block(wo.shape), whole_block(vec.shape), *[anywhere] * 4,
            ],
            out_specs=[
                *(tile(w) for w, _ in widths),
                pl.BlockSpec((8, model), lambda i, s: (0, 0)),
                pl.BlockSpec((8, hidden // 2), lambda i, s: (0, 0)),
            ],
            scratch_shapes=[
                *(pltpu.VMEM(a.shape, BF16) for a in (wi, wu, early, late)),
                pltpu.SemaphoreType.DMA((4,)),
            ],
        ),
        out_shape=[
            *(struct((half, w), kind) for w, kind in widths), struct((8, model), F32), struct((8, hidden // 2), F32),
        ],
        compiler_params=params(63),
        cost_estimate=cost(8 * half * model * hidden, 24 * model * hidden),
        name="backward",
    )(at, slope, n1, inv1, d_second, d_low, context, got, wo, vec, wi, wu, early, late)


def weight_kernel(plan, count, kinds, bit_ref, *rest):
    groups = len(plan)
    left_hbm, rest = rest[:kinds], rest[kinds:]
    keep_hbm, rest = rest[:groups], rest[groups:]
    got_hbm, rest = rest[:count], rest[count:]
    outs, rest = rest[: 2 * groups], rest[2 * groups :]
    left_ref, left_got_ref, rest = rest[0], rest[1], rest[2:]
    keep_refs, rest = rest[:groups], rest[groups:]
    got_refs, rest = rest[:groups], rest[groups:]
    stage_refs, (in_sem, out_sem) = rest[:groups], rest[groups:]
    model = left_ref.shape[2]

    arriving, ready = [], {}

    def bring(key, source, target):
        if key not in ready:
            ready[key] = pltpu.make_async_copy(source, target, in_sem.at[len(arriving)])
            ready[key].start()
            arriving.append(key)

    for g, (_, _, tiles) in enumerate(plan):
        for index, (left_array, left_at), (right_array, right_at), a, b in tiles:
            bring(("left", index), left_hbm[index], left_ref.at[index])
            if ("left got", index) not in ready:
                columns = slice(left_at, left_at + model)
                bring(("left got", index), got_hbm[left_array].at[:, columns], left_got_ref.at[index])
            bring(("keep", g, a), keep_hbm[g].at[:, a:b], keep_refs[g].at[:, a:b])
            columns = slice(right_at, right_at + b - a)
            bring(("got", g, a), got_hbm[right_array].at[:, columns], got_refs[g].at[:, a:b])
    waited = set()

    def need(*keys):
        for key in keys:
            if key not in waited:
                waited.add(key)
                ready[key].wait()

    leaving = []
    for g, (slot, group, tiles) in enumerate(plan):
        width = keep_refs[g].shape[1]
        for index, _, _, a, b in tiles:
            need(("left", index), ("left got", index), ("keep", g, a), ("got", g, a))
            left = jnp.concatenate([left_ref[index], left_got_ref[index].astype(BF16)], axis=0)
            right = jnp.concatenate([keep_refs[g][:, a:b], got_refs[g][:, a:b].astype(BF16)], axis=0)
            value = mm(left, right, TN)
            if slot is None:
                part, base = (0, 0) if 2 * b <= width else (1, width // 2)
                stage_refs[g][part, :, a - base : b - base] = value
                parts = ((part, a - base, b - base),)
            else:
                pairs = value.reshape(model // (2 * group), 2, group, b - a)
                kept = bit_ref[slot] == 0
                first, second = pairs[:, 0], pairs[:, 1]
                for part, (one, other) in enumerate(((first, second), (second, first))):
                    picked = jnp.where(kept, one, other)
                    stage_refs[g][part, :, a:b] = picked.reshape(model // 2, b - a)
                parts = ((1, a, b), (0, a, b))
            for part, a, b in parts:
                copy = pltpu.make_async_copy(
                    stage_refs[g].at[part, :, a:b], outs[2 * g + part].at[:, a:b], out_sem.at[len(leaving)]
                )
                copy.start()
                leaving.append(copy)
    for copy in leaving:
        copy.wait()


def weight_grads(at, lefts, keeps, received, plan):
    depth, model = lefts[0].shape
    stages, shapes, steps = [], [], 0
    for (slot, _, tiles), keep in zip(plan, keeps):
        width = keep.shape[1]
        shape = (model, width // 2) if slot is None else (model // 2, width)
        stages.append(pltpu.VMEM((2, *shape), F32))
        shapes += [struct(shape, F32)] * 2
        steps += len(tiles)
    columns = sum(keep.shape[1] for keep in keeps)
    anywhere = pl.BlockSpec(memory_space=pl.ANY)
    return pl.pallas_call(
        functools.partial(weight_kernel, plan, len(received), len(lefts)),
        grid_spec=pltpu.PrefetchScalarGridSpec(
            num_scalar_prefetch=1,
            grid=(1,),
            in_specs=[anywhere] * (len(lefts) + len(keeps) + len(received)),
            out_specs=[anywhere] * len(shapes),
            scratch_shapes=[
                pltpu.VMEM((len(lefts), depth, model), BF16),
                pltpu.VMEM((len(lefts), depth, model), F32),
                *(pltpu.VMEM(keep.shape, BF16) for keep in keeps),
                *(pltpu.VMEM(keep.shape, F32) for keep in keeps),
                *stages,
                pltpu.SemaphoreType.DMA((2 * len(lefts) + 2 * steps,)),
                pltpu.SemaphoreType.DMA((2 * steps,)),
            ],
        ),
        out_shape=shapes,
        compiler_params=params(63),
        cost_estimate=cost(4 * depth * model * columns, 4 * model * columns + 8 * depth * columns),
        name="weight_grads",
    )(at, *lefts, *keeps, *received)


def combine_kernel(plan, count, bits_ref, *rest):
    outs = len(plan)
    arrays, targets = rest[:count], rest[count : count + outs]
    buffers, (in_sem, out_sem) = rest[count + outs : -2], rest[-2:]
    copies = []
    for pieces in plan:
        for _, terms in pieces:
            for array, chosen, a, b, _ in terms:
                index = [slice(None)] * len(arrays[array].shape)
                for axis, (bit, mine) in chosen:
                    index[axis] = pl.ds(bits_ref[bit] if mine else 1 - bits_ref[bit], 1)
                index[-1] = slice(a, b)
                k = len(copies)
                copies.append(pltpu.make_async_copy(arrays[array].at[tuple(index)], buffers[k], in_sem.at[k]))
    for copy in copies:
        copy.start()
    k = 0
    leaving = []
    for target, pieces in zip(targets, plan):
        for at, terms in pieces:
            first = k
            total = None
            for *_, gate in terms:
                copies[k].wait()
                value = buffers[k][...]
                if gate is not None:
                    value = jnp.where(bits_ref[0] == gate, value, 0.0)
                total = value if total is None else total + value
                k += 1
            if len(terms) > 1:
                buffers[first][...] = total
            width = buffers[first].shape[-1]
            index = (*[slice(None)] * (len(target.shape) - 1), slice(at, at + width))
            copy = pltpu.make_async_copy(buffers[first], target.at[index], out_sem.at[len(leaving)])
            copy.start()
            leaving.append(copy)
    for copy in leaving:
        copy.wait()


def combine(bit_values, outputs):
    arrays, plan, shapes, buffers, moved = [], [], [], [], 0
    for pieces in outputs:
        at, planned = 0, []
        for terms in pieces:
            named = []
            for array, chosen, a, b, gate in terms:
                place = [k for k, other in enumerate(arrays) if other is array]
                if not place:
                    place = [len(arrays)]
                    arrays.append(array)
                named.append((place[0], tuple(sorted(chosen.items())), a, b, gate))
                block = tuple(1 if k in chosen else size for k, size in enumerate(array.shape[:-1]))
                buffers.append(pltpu.VMEM((*block, b - a), F32))
                moved += 4 * math.prod(block) * (b - a)
            planned.append((at, named))
            at += b - a
        plan.append(planned)
        shapes.append(struct((*block, at), F32))
    anywhere = pl.BlockSpec(memory_space=pl.ANY)
    pieces = sum(len(planned) for planned in plan)
    return pl.pallas_call(
        functools.partial(combine_kernel, plan, len(arrays)),
        grid_spec=pltpu.PrefetchScalarGridSpec(
            num_scalar_prefetch=1,
            grid=(1,),
            in_specs=[anywhere] * len(arrays),
            out_specs=[anywhere] * len(shapes),
            scratch_shapes=[
                *buffers,
                pltpu.SemaphoreType.DMA((len(buffers),)),
                pltpu.SemaphoreType.DMA((pieces,)),
            ],
        ),
        out_shape=shapes,
        compiler_params=params(63),
        cost_estimate=cost(moved, 2 * moved),
        name="combine",
    )(bit_values, *arrays)


def turn_kernel(value_ref, out_ref):
    out_ref[...] = value_ref[...].astype(F32).T.astype(BF16)


def turn(value, columns=256):
    length, model = value.shape
    return pl.pallas_call(
        turn_kernel,
        grid=(model // columns,),
        in_specs=[pl.BlockSpec((length, columns), lambda i: (0, i))],
        out_specs=pl.BlockSpec((columns, length), lambda i: (i, 0)),
        out_shape=struct((model, length), BF16),
        compiler_params=params(63),
        cost_estimate=cost(length * model, 4 * length * model),
        name="turn",
    )(value)


def place_kernel(steps, y_ref, own_ref, first_ref, second_ref, out_ref):
    mine = pl.program_id(0) // steps == y_ref[0]
    got = jnp.concatenate([first_ref[...], second_ref[...]], axis=1)
    out_ref[...] = jnp.where(mine, own_ref[...].astype(F32), got).astype(BF16)


def place_rows(y, own, first, second):
    half, model = own.shape
    rows = min(128, half)
    steps = half // rows
    tile = lambda w: pl.BlockSpec((rows, w), lambda i, s: (i % steps, 0))
    return pl.pallas_call(
        functools.partial(place_kernel, steps),
        grid_spec=pltpu.PrefetchScalarGridSpec(
            num_scalar_prefetch=1,
            grid=(2 * steps,),
            in_specs=[tile(model), tile(model // 2), tile(model // 2)],
            out_specs=pl.BlockSpec((rows, model), lambda i, s: (i, 0)),
        ),
        out_shape=struct((2 * half, model), BF16),
        compiler_params=params(63),
        cost_estimate=cost(half * model, 12 * half * model),
        name="place_rows",
    )(y, own, first, second)


def per_device(
    devices,
    tokens,
    lengths,
    entity_flags,
    query_weight,
    query_bias,
    key_weight,
    key_bias,
    value_weight,
    value_bias,
    output_weight,
    output_bias,
    attn_gain,
    attn_shift,
    inner_weight,
    inner_bias,
    outer_weight,
    outer_bias,
    final_gain,
    final_shift,
    cotangent,
):
    x = tokens[0]
    length, model = x.shape
    width = key_weight.shape[1]
    hidden = inner_weight.shape[1]
    half = length // 2
    bits = devices.bit_length() - 1
    y = lax.axis_index("tensor")
    d = lax.axis_index("dp")

    def swap(value, mask):
        return lax.ppermute(value, "dp", [(i, i ^ mask) for i in range(devices)])

    def cross(value):
        return lax.ppermute(value, "tensor", [(0, 1), (1, 0)])

    me = d % SLICES
    core = d % 2
    rows = model // devices
    near_mask, far_mask = 192 // rows, 96 // rows
    at = jnp.stack([y, me, (d // near_mask) % 2, (d // far_mask) % 2]).astype(jnp.int32)
    tie = lax.optimization_barrier

    def cut(array, index):
        size = array.shape[0] // SLICES
        return lax.dynamic_slice_in_dim(array, index * size, size, 0)

    def pack(index):
        wide = cut(inner_weight, index)
        early = jnp.concatenate([cut(output_weight, index), wide[:, :model], wide[:, model:]], axis=0)
        return early.astype(F32)

    def pack_late(index):
        return cut(outer_weight, index).astype(F32)

    live = (lax.broadcasted_iota(jnp.int32, (length, 1), 0) < lengths[0]).astype(F32)
    kind = (entity_flags[0] == 1).astype(F32).reshape(length, 1)

    e0 = cross(pack(me))
    far_bias = cross(inner_bias)
    q2, k2, v = project(
        x, kind, query_weight, query_bias, key_weight, key_bias, value_weight, value_bias
    )
    e0, far_bias, l0, l6, q2 = tie((e0, far_bias, pack_late(me), pack_late(me ^ 6), q2))
    e2 = swap(e0, 2)
    e4 = swap(e0, 4)
    l0 = cross(l0)
    e1 = swap(e0, 1)
    context, extra = attend(q2, k2, v, live)
    sent = lax.dynamic_slice_in_dim(context, half * (1 - y), half, 0).astype(F32)
    e1, e2, e4, l0, l6, sent = tie((e1, e2, e4, l0, l6, sent))
    l2 = swap(l0, 2)
    l4 = swap(l0, 4)
    got = cross(sent)
    e6 = swap(e4, 2)
    l6 = cross(l6)
    per = width // devices
    where_row = lax.broadcasted_iota(jnp.int32, (model, width), 0)
    where_bias = lax.broadcasted_iota(jnp.int32, (model, width), 1)
    pick = (where_row == (where_bias // per) * rows + where_bias % per).astype(BF16)
    x_turned = turn(x)
    l2, l4, e2, e4, pick, x_turned = tie((l2, l4, e2, e4, pick, x_turned))
    e3 = swap(e2, 1)
    e5 = swap(e4, 1)
    got, e6, l6, e3, e5, l0, l2, l4 = tie((got, e6, l6, e3, e5, l0, l2, l4))
    l1 = swap(l0, 1)
    l3 = swap(l2, 1)
    l5 = swap(l4, 1)
    l7 = swap(l6, 1)
    e7 = swap(e6, 1)
    early = (e0, e1, e2, e3, e4, e5, e6, e7)
    late = (l0, l1, l2, l3, l4, l5, l6, l7)

    vec = jnp.stack(
        [output_bias, attn_gain, attn_shift, outer_bias, final_gain, final_shift, outer_bias, outer_bias]
    )
    bias = jnp.concatenate([inner_bias, far_bias, inner_bias, far_bias]).reshape(8, hidden // 2)
    ca, cb = first_cut(hidden // 2), hidden // 2
    da, db = hidden // 2 - ca, 0
    (
        out_rows, out_first, out_late, low, d_low, keep2, early_send, slope, n1, inv1, d_second, late_sums,
        far_early, far_late,
    ) = forward(
        at, x, cotangent[0], live, context, got, output_weight, inner_weight, outer_weight,
        early, late, vec, bias,
    )
    early_got = swap(early_send, 1)
    got_first = cross(out_first)
    d_first, dco, dcf, d_attn, keep0, keep1, late_send, first_sums, inner_sums = backward(
        at, slope, n1, inv1, d_second, d_low, context, got, output_weight, vec, inner_weight, outer_weight,
        far_early, far_late,
    )
    inner_columns = inner_sums[:4].reshape(2, model, 2)
    shared = [first_sums[:3].T, late_sums[:3].T]
    columns = jnp.concatenate([*shared, inner_columns[0], *shared, inner_columns[1]], axis=1)
    early_got, got_first, late_send, dcf, columns = tie((early_got, got_first, late_send, dcf, columns))
    late_got = swap(late_send, 1)
    d_got = cross(dcf)

    low_at, d_attn_at = (0, 2 * cb + model), (1, hidden)
    g2_keep, g2_send = weight_grads(
        at, (d_low,), (keep2,), (early_got,),
        (
            (
                3, far_mask * rows,
                ((0, (0, 0), (0, model), 0, cb), (0, (0, 0), (0, model + cb), cb, 2 * cb)),
            ),
        ),
    )
    g0_keep, g0_send, g1_keep, g1_send = weight_grads(
        at, (low, d_attn), (keep0, keep1), (early_got, late_got),
        (
            (
                2, near_mask * rows,
                (
                    (0, low_at, (1, 0), 0, ca), (0, low_at, (1, ca), ca, 2 * ca),
                    (1, d_attn_at, (0, 2 * model + hidden), 2 * ca, 2 * ca + width),
                ),
            ),
            (
                None, None,
                ((0, low_at, (1, 2 * ca), 0, da), (0, low_at, (1, 2 * ca + da), da, 2 * da)),
            ),
        ),
    )
    g0_send, g1_send, d_got = tie((g0_send, g1_send, d_got))
    g0_got = swap(g0_send, near_mask)
    g2_got = swap(g2_send, far_mask)
    g1_got = cross(g1_send)

    g0_send, g1_send, g2_send, dco, d_got = tie((g0_send, g1_send, g2_send, dco, d_got))
    chunks = tuple(length * k // 32 for k in (3, 4, 16, 9))
    group = rows if rows % 8 == 0 else None
    results = attend_back(
        at, q2, extra, k2, v, context, dco, d_got, live, kind, columns, pick,
        query_weight, key_weight, value_weight, x_turned, d_first, chunks, group,
    )
    parts, products = results[: len(chunks)], results[len(chunks) :]
    got_out = cross(out_late)

    def spread(array, done):
        dims = [1 if (1 << (bits - 1 - k)) in done else 2 for k in range(bits)]
        return array.reshape(*dims, rows, array.shape[-1])

    bit_values = jnp.stack([(d >> k) % 2 for k in range(bits)]).astype(jnp.int32)
    rest_masks = [1 << k for k in range(1, bits) if (1 << k) not in (near_mask, far_mask)]

    def term(array, *done):
        array = spread(array, done)
        return (array, {}, 0, array.shape[-1], None)

    def half_of(terms, mask, mine):
        k = mask.bit_length() - 1
        return [(array, {**chosen, bits - 1 - k: (k, mine)}, a, b, gate) for array, chosen, a, b, gate in terms]

    def kept(terms, mask):
        return half_of(terms, mask, True)

    def other(terms, mask):
        return half_of(terms, mask, False)

    def columns_of(terms, first, last):
        return [(array, chosen, a + first, a + last, gate) for array, chosen, a, _, gate in terms]

    def on_core(terms, core_index):
        return [(array, chosen, a, b, core_index) for array, chosen, a, b, _ in terms]

    def whole_of(array):
        return (array, {}, 0, array.shape[-1], None)

    def part_of(array, a, b):
        return (array, {}, a, b, None)

    g0_got, g1_got, g2_got, got_out, parts, products = tie((g0_got, g1_got, g2_got, got_out, parts, products))
    if group is None:
        c = [term(products[0])]
        e = [term(products[1])]
        c_send, e_send = combine(bit_values, [[other(c, 1)], [other(e, 1)]])
        c, e = kept(c, 1), kept(e, 1)
    else:
        c, e = [term(products[0], 1)], [term(products[2], 1)]
        c_send, e_send = spread(products[1], (1,)), spread(products[3], (1,))
    e_got = swap(e_send, 1)
    c_got = swap(c_send, 1)
    g0 = [term(g0_keep, near_mask), term(g0_got, near_mask)]
    g1 = [term(g1_keep), term(g1_got)]
    g2 = [term(g2_keep, far_mask), term(g2_got, far_mask)]
    (g2_send,) = combine(bit_values, [[other(g2, near_mask)]])
    sends = combine(bit_values, [[columns_of(g0, ca, 2 * ca + width)], [other(g1, near_mask)]])
    e_got, c_got, sends, parts = tie((e_got, c_got, sends, parts))
    e.append(whole_of(e_got))
    c.append(whole_of(c_got))
    g2_got = swap(g2_send, near_mask)
    g0_got = cross(sends[0])
    g1_got = swap(sends[1], near_mask)
    e_send, c_send = combine(bit_values, [[other(e, far_mask)], [other(c, near_mask)]])
    e_got = swap(e_send, far_mask)
    part0 = cross(parts[0])
    g0_got, g1_got, g2_got, e_got, part0, parts, c_send = tie(
        (g0_got, g1_got, g2_got, e_got, part0, parts, c_send)
    )
    t = [
        *on_core(columns_of(g0, 2 * ca, 2 * ca + width), 0),
        *on_core([part_of(g0_got, ca, ca + width)], 1),
    ]
    g0 = [*columns_of(g0, 0, ca), part_of(g0_got, 0, ca)]
    g1 = [*kept(g1, near_mask), whole_of(g1_got)]
    g2 = [*kept(g2, near_mask), whole_of(g2_got)]
    e = [*kept(e, far_mask), whole_of(e_got)]

    (three_send,) = combine(bit_values, [[other(terms, far_mask) for terms in (g0, t, g1)]])
    sends = combine(
        bit_values, [[columns_of(g2, cb, 2 * cb)], [columns_of(e, 3 * width + 128, 3 * width + 256)]]
    )
    three_got = swap(three_send, far_mask)
    g2_got = cross(sends[0])
    small_got = cross(sends[1])
    c_got = swap(c_send, near_mask)
    in1 = (parts[1] + cross(parts[1])).astype(BF16)
    in1, own0, part0 = tie((in1, parts[0], part0))
    in0 = (own0 + part0).astype(BF16)
    three_got, g2_got, c_got, small_got, in0, in1, parts = tie(
        (three_got, g2_got, c_got, small_got, in0, in1, parts)
    )
    small = [*columns_of(e, 3 * width, 3 * width + 128), whole_of(small_got)]
    e = columns_of(e, 0, 3 * width)
    g0 = [*kept(g0, far_mask), part_of(three_got, 0, ca)]
    t = [*kept(t, far_mask), part_of(three_got, ca, ca + width)]
    g1 = [*kept(g1, far_mask), part_of(three_got, ca + width, three_got.shape[-1])]
    g2 = [*columns_of(g2, 0, cb), whole_of(g2_got)]
    c = [*kept(c, near_mask), whole_of(c_got)]

    main = (g0, g1, g2, t)
    sizes = (ca, da + db, cb, width)
    ends = [sum(sizes[:k]) for k in range(len(sizes) + 1)]
    mask = rest_masks[0]
    (main_send,) = combine(bit_values, [[other(terms, mask) for terms in main]])
    _, late_bits = tie((main_send, bit_values))
    sends = combine(late_bits, [[other(e, near_mask), other(small, near_mask)], [other(c, far_mask)]])
    got_z = swap(main_send, mask)
    in2 = (parts[2] + cross(parts[2])).astype(BF16)
    c_got = swap(sends[1], far_mask)
    e_got = swap(sends[0], near_mask)
    layer_out = place_rows(at, out_rows, got_first, got_out)
    got_z, e_got, c_got, in2, parts, layer_out = tie((got_z, e_got, c_got, in2, parts, layer_out))
    main = [[*kept(terms, mask), part_of(got_z, ends[n], ends[n + 1])] for n, terms in enumerate(main)]
    e = [*kept(e, near_mask), part_of(e_got, 0, 3 * width)]
    small = [*kept(small, near_mask), part_of(e_got, 3 * width, 3 * width + 128)]
    c = [*kept(c, far_mask), whole_of(c_got)]
    for mask in rest_masks[1:]:
        (send,) = combine(bit_values, [[other(terms, mask) for terms in main]])
        got_z = swap(send, mask)
        main = [[*kept(terms, mask), part_of(got_z, ends[n], ends[n + 1])] for n, terms in enumerate(main)]

    for k, mask in enumerate(rest_masks):
        (pair_send,) = combine(bit_values, [[other(c, mask), other(e, mask), other(small, mask)]])
        outputs = [[kept(c, mask), kept(e, mask), kept(small, mask)]]
        if k == 0:
            outputs += [[other(terms, 1) for terms in main], [kept(terms, 1) for terms in main]]
        _, late_bits = tie((pair_send, bit_values))
        sends = combine(late_bits, outputs)
        pair_got = swap(pair_send, mask)
        if k == 0:
            in3 = (parts[3] + cross(parts[3])).astype(BF16)
            got_last = swap(sends[1], 1)
            keep = sends[2]
        pair_keep = sends[0]
        wide = pair_keep.shape[-1]
        c = [part_of(pair_keep, 0, 3 * width), part_of(pair_got, 0, 3 * width)]
        e = [part_of(pair_keep, 3 * width, 6 * width), part_of(pair_got, 3 * width, 6 * width)]
        small = [part_of(pair_keep, 6 * width, wide), part_of(pair_got, 6 * width, wide)]

    input_grad = jnp.concatenate([in0, in1, in2, in3], axis=0)
    got_last, keep, input_grad = tie((got_last, keep, input_grad))
    got_last = got_last.reshape(rows, -1)
    keep = keep.reshape(rows, -1)
    low_half = jnp.where(core == 0, keep, got_last)
    high_half = jnp.where(core == 0, got_last, keep)
    at2 = ca + da + db
    inner_half = lambda array: [array[:, : ca + da]]
    at3 = at2 + cb
    outer_half = lambda array: [array[:, at2:at3], array[:, ca + da : at2]]
    t = keep[:, at3:] + got_last[:, at3:]
    grad_inner = jnp.concatenate(inner_half(low_half) + inner_half(high_half), axis=1)
    grad_outer = jnp.concatenate(outer_half(low_half) + outer_half(high_half), axis=1).T
    grad_output = t.T
    pair_got, grad_inner, grad_outer, grad_output = tie((pair_got, grad_inner, grad_outer, grad_output))
    pair = (pair_keep + pair_got).reshape(rows, -1)
    c, e = pair[:, : 3 * width], pair[:, 3 * width :]
    small = e[:, 3 * width + 6 : 3 * width + 12]
    inner_two = e[:, 3 * width + 12 : 3 * width + 14]

    piece = lambda array, k: array[:, width * k : width * (k + 1)]
    grad_query_weight = jnp.stack([piece(c, 0), piece(c, 1), piece(c, 2), piece(e, 0)])
    biases = e[:per, 3 * width : 3 * width + 6].T
    return (
        layer_out[None],
        input_grad[None],
        grad_query_weight,
        biases[:4],
        piece(e, 1),
        biases[4],
        piece(e, 2),
        biases[5],
        grad_output,
        small[:, 0],
        small[:, 1],
        small[:, 2],
        grad_inner,
        inner_two.reshape(2 * rows),
        grad_outer,
        small[:, 3],
        small[:, 4],
        small[:, 5],
    )


def solution(mesh):
    return jax.shard_map(
        functools.partial(per_device, mesh.shape["dp"]),
        mesh=mesh,
        in_specs=(
            P("dp", None, None),
            P("dp"),
            P("dp", None),
            P(None, None, "tensor"),
            P(None, "tensor"),
            P(None, "tensor"),
            P("tensor"),
            P(None, "tensor"),
            P("tensor"),
            P("tensor", None),
            P(),
            P(),
            P(),
            P(None, "tensor"),
            P("tensor"),
            P("tensor", None),
            P(),
            P(),
            P(),
            P("dp", None, None),
        ),
        out_specs=(
            P("dp", None, None),
            P("dp", None, None),
            P(None, "dp", "tensor"),
            P(None, ("tensor", "dp")),
            P("dp", "tensor"),
            P(("tensor", "dp")),
            P("dp", "tensor"),
            P(("tensor", "dp")),
            P("tensor", "dp"),
            P("dp"),
            P("dp"),
            P("dp"),
            P("dp", "tensor"),
            P(("tensor", "dp")),
            P("tensor", "dp"),
            P("dp"),
            P("dp"),
            P("dp"),
        ),
        check_vma=False,
    )
```

```python
import functools
import math

import jax
import jax.numpy as jnp
from jax import lax
from jax.experimental import pallas as pl
from jax.experimental.pallas import tpu as pltpu
from jax.sharding import PartitionSpec as P

HD = 64
SLICES = 8
MASKED = -1e30
NORM_EPS = 1e-05

F32 = jnp.float32
BF16 = jnp.bfloat16
NN = (((1,), (0,)), ((), ()))
NT = (((1,), (1,)), ((), ()))
TN = (((0,), (0,)), ((), ()))


def mm(left, right, dims):
    return lax.dot_general(left, right, dims, preferred_element_type=F32)


def struct(shape, kind):
    return jax.ShapeDtypeStruct(shape, kind)


def params(mib):
    return pltpu.CompilerParams(vmem_limit_bytes=mib << 20)


def cost(flops, moved, special=0):
    return pl.CostEstimate(flops=int(flops), bytes_accessed=int(moved), transcendentals=int(special))


def whole_block(shape):
    return pl.BlockSpec(shape, lambda *_: (0,) * len(shape), pipeline_mode=pl.Buffered(1))


def three_pieces(value):
    high = value.astype(BF16).astype(F32)
    rest = value - high
    middle = rest.astype(BF16).astype(F32)
    return high, middle, rest - middle


def project_kernel(x_ref, kind_ref, wq_ref, bq_ref, wk_ref, bk_ref, wv_ref, bv_ref, q2_ref, k2_ref, v_ref):
    x = x_ref[...]
    entity = kind_ref[...] > 0.5
    rows = x.shape[0]
    width = wk_ref.shape[1]

    weights = jnp.concatenate([*(wq_ref[c] for c in range(4)), wk_ref[...], wv_ref[...]], axis=1)
    biases = jnp.concatenate([*(bq_ref[c : c + 1, :] for c in range(4)), bk_ref[...], bv_ref[...]], axis=1)
    products = mm(x, weights, NN) + biases

    def query(c):
        return products[:, width * c : width * (c + 1)]

    scale = 1.0 / math.sqrt(HD)
    to_word = jnp.where(entity, query(2), query(0)).astype(BF16).astype(F32) * scale
    to_entity = jnp.where(entity, query(3), query(1)).astype(BF16).astype(F32) * scale
    keys = query(4).astype(BF16).astype(F32)
    v_ref[...] = query(5).astype(BF16)
    left = lax.broadcasted_iota(jnp.int32, (rows, 2 * HD), 1) < HD
    held = left != entity
    for p in range(width // (2 * HD)):
        cols = slice(2 * HD * p, 2 * HD * (p + 1))
        w, e, k = to_word[:, cols], to_entity[:, cols], keys[:, cols]
        w_roll, e_roll, k_roll = (pltpu.roll(t, HD, 1) for t in (w, e, k))
        even = slice(4 * HD * p, 4 * HD * p + 2 * HD)
        odd = slice(4 * HD * p + 2 * HD, 4 * HD * (p + 1))
        q2_ref[:, even] = jnp.where(left, w, e_roll).astype(BF16)
        q2_ref[:, odd] = jnp.where(left, w_roll, e).astype(BF16)
        k2_ref[:, even] = jnp.where(held, jnp.where(left, k, k_roll), 0.0).astype(BF16)
        k2_ref[:, odd] = jnp.where(held, jnp.where(left, k_roll, k), 0.0).astype(BF16)


def project(x, kind, wq, bq, wk, bk, wv, bv, rows=256):
    length, model = x.shape
    width = wk.shape[1]
    rows = min(rows, length)
    tile = lambda w: pl.BlockSpec((rows, w), lambda i: (i, 0))
    return pl.pallas_call(
        project_kernel,
        grid=(length // rows,),
        in_specs=[
            tile(model),
            tile(1),
            whole_block(wq.shape),
            whole_block(bq.shape),
            whole_block(wk.shape),
            whole_block((1, width)),
            whole_block(wv.shape),
            whole_block((1, width)),
        ],
        out_specs=[tile(2 * width), tile(2 * width), tile(width)],
        out_shape=[
            struct((length, 2 * width), BF16),
            struct((length, 2 * width), BF16),
            struct((length, width), BF16),
        ],
        compiler_params=params(63),
        cost_estimate=cost(12 * length * model * width, 16 * model * width + 12 * length * width),
        name="project",
    )(x, kind, wq, bq, wk, bk.reshape(1, width), wv, bv.reshape(1, width))


def key_extra(live, rows):
    lane = lax.broadcasted_iota(jnp.int32, (rows, 2 * HD), 1)
    return jnp.where(
        lane == 0, jnp.where(live, 0.0, MASKED), jnp.where(lane < 4, 1.0, 0.0)
    ).astype(BF16)


def attend_kernel(q2_ref, k2_ref, v_ref, live_ref, out_ref, extra_ref, turned_ref, both_ref):
    length = k2_ref.shape[0]
    h = pl.program_id(1)

    @pl.when(h == 0)
    def _():
        turned = v_ref[...].astype(F32).T.astype(BF16)
        turned_ref[0] = turned[:HD]
        turned_ref[1] = turned[HD:]

    lane = lax.broadcasted_iota(jnp.int32, (length, 2 * HD), 1)
    one = jnp.where(lane == 0, 1.0, 0.0).astype(BF16)
    keys = jnp.concatenate([k2_ref[...], key_extra(live_ref[...] > 0.5, length)], axis=1)
    query = jnp.concatenate([q2_ref[...], one], axis=1)
    scores = mm(keys, query, NT)
    top = jnp.max(scores, axis=0, keepdims=True)
    weights = jnp.exp(scores - top)
    norm = jnp.sum(weights, axis=0, keepdims=True)
    summed = mm(turned_ref[h], weights.astype(BF16), NN)
    both_ref[h] = summed * (1.0 / norm)
    pieces = three_pieces(-(top + jnp.log(norm)))
    filled = jnp.concatenate(
        [jnp.ones((1, length), F32), *pieces, jnp.zeros((2 * HD - 4, length), F32)], axis=0
    )
    extra_ref[...] = filled.T.astype(BF16)

    @pl.when(h == 1)
    def _():
        out_ref[...] = jnp.concatenate([both_ref[0], both_ref[1]], axis=0).T.astype(BF16)


def attend(q2, k2, v, live):
    length, width = v.shape
    head = pl.BlockSpec((length, 2 * HD), lambda p, h: (0, 2 * p + h))
    pair = pl.BlockSpec((length, 2 * HD), lambda p, h: (0, p))
    return pl.pallas_call(
        attend_kernel,
        grid=(width // (2 * HD), 2),
        in_specs=[head, head, pair, whole_block((length, 1))],
        out_specs=[pair, head],
        out_shape=[struct((length, width), BF16), struct((length, 2 * width), BF16)],
        scratch_shapes=[pltpu.VMEM((2, HD, length), BF16), pltpu.VMEM((2, HD, length), F32)],
        compiler_params=params(63),
        cost_estimate=cost(10 * length * length * width, 20 * length * width, length * length * width // HD),
        name="attend",
    )(q2, k2, v, live)


def attend_back_kernel(
    count, group, y_ref, q2_ref, extra_ref, k2_ref, v_ref, o_ref, own_ref, got_ref, live_ref, kind_ref, columns_ref, pick_ref,
    wq_hbm, wk_hbm, wv_hbm, turned_hbm, first_hbm, *rest,
):
    outs = count + (2 if group is None else 4)
    part_hbm, grads_hbm = rest[:count], rest[count:outs]
    (
        dk_ref, dv_ref, dq_ref, product_ref, d_ref, all_ref, sums_ref, weights_ref, turned_ref, first_ref,
        part_ref, grads_ref, in_sem, out_sem,
    ) = rest[outs:]
    length = k2_ref.shape[0]
    width = wk_hbm.shape[1]
    p, h = pl.program_id(0), pl.program_id(1)
    pairs = width // (2 * HD)
    lane = lax.broadcasted_iota(jnp.int32, (length, 2 * HD), 1)
    left = lane < HD

    def arriving():
        copies = [
            pltpu.make_async_copy(wq_hbm.at[c], weights_ref.at[:, width * c : width * (c + 1)], in_sem.at[c])
            for c in range(4)
        ]
        copies.append(pltpu.make_async_copy(wk_hbm, weights_ref.at[:, 4 * width : 5 * width], in_sem.at[4]))
        copies.append(pltpu.make_async_copy(wv_hbm, weights_ref.at[:, 5 * width : 6 * width], in_sem.at[5]))
        copies.append(pltpu.make_async_copy(turned_hbm, turned_ref, in_sem.at[6]))
        copies.append(pltpu.make_async_copy(first_hbm, first_ref, in_sem.at[7]))
        return copies

    @pl.when(jnp.logical_and(p == 0, h == 0))
    def _():
        for copy in arriving():
            copy.start()

    @pl.when(h == 0)
    def _():
        first = y_ref[0] == 0
        own, got = own_ref[...], got_ref[...]
        joined = jnp.concatenate([jnp.where(first, own, got), jnp.where(first, got, own)], axis=0)
        product_ref[...] = joined * o_ref[...].astype(F32)
        d_ref[...] = joined.astype(BF16)

    d_context = d_ref[...]
    base = HD * (1 - h)
    mine = jnp.logical_and(lane >= HD - base, lane < 2 * HD - base)
    delta = jnp.sum(jnp.where(mine, product_ref[...], 0.0), axis=1, keepdims=True)
    high, middle, low = three_pieces(-delta)
    pieces = jnp.where(
        lane == base, high, jnp.where(lane == base + 1, middle, jnp.where(lane == base + 2, low, 0.0))
    ).astype(BF16)
    d_wide = jnp.where(mine, d_context, pieces)
    q2, k2 = q2_ref[...], k2_ref[...]
    query = jnp.concatenate([q2, extra_ref[...]], axis=1)
    keys = jnp.concatenate([k2, key_extra(live_ref[...] > 0.5, length)], axis=1)
    probs = jnp.exp(mm(keys, query, NT))
    ones = jnp.where((lane >= base) & (lane < base + 3), 1.0, 0.0).astype(BF16)
    d_probs = mm(jnp.where(mine, v_ref[...], ones), d_wide, NT)
    d_scores = (probs * d_probs).astype(BF16)
    dv_ref[h] = mm(probs.astype(BF16), d_context, NN)
    dk_ref[h] = mm(d_scores, q2, NN)
    dq_ref[h] = mm(k2, d_scores, TN).T * (1.0 / math.sqrt(HD))

    @pl.when(h == 1)
    def _():
        entity = kind_ref[...] > 0.5
        even, odd = dq_ref[0], dq_ref[1]
        to_word = jnp.where(left, even, pltpu.roll(odd, HD, 1)).astype(BF16).astype(F32)
        to_entity = jnp.where(left, pltpu.roll(even, HD, 1), odd).astype(BF16).astype(F32)
        even, odd = dk_ref[0], dk_ref[1]
        even = jnp.where(entity, pltpu.roll(even, HD, 1), even)
        odd = jnp.where(entity, odd, pltpu.roll(odd, HD, 1))
        grads = [
            jnp.where(entity, 0.0, to_word),
            jnp.where(entity, 0.0, to_entity),
            jnp.where(entity, to_word, 0.0),
            jnp.where(entity, to_entity, 0.0),
            jnp.where(left, even, odd).astype(BF16).astype(F32),
            jnp.where(left, dv_ref[0], dv_ref[1]).astype(BF16).astype(F32),
        ]
        for c, grad in enumerate(grads):
            all_ref[p, c] = grad.astype(BF16)
        sums = [jnp.sum(grad, axis=0, keepdims=True) for grad in grads]
        sums_ref[p] = jnp.concatenate([*sums, jnp.zeros((2, 2 * HD), F32)], axis=0)

    @pl.when(jnp.logical_and(p == pairs - 1, h == 1))
    def _():
        for copy in arriving():
            copy.wait()
        grads = jnp.concatenate([all_ref[k, c] for c in range(6) for k in range(pairs)], axis=1)
        half = first_ref.shape[0]
        leaving = []

        def leave(source, target):
            copy = pltpu.make_async_copy(source, target, out_sem.at[len(leaving)])
            copy.start()
            leaving.append(copy)

        for i in range(2):
            rows = slice(i * half, (i + 1) * half)
            total = mm(grads[rows], weights_ref[...], NT)
            part_ref[rows, :] = total + jnp.where(y_ref[0] == i, first_ref[...], 0.0)
        begin = 0
        for target in part_hbm:
            leave(part_ref.at[begin : begin + target.shape[0], :], target)
            begin += target.shape[0]
        model = turned_ref.shape[0]
        sums = jnp.concatenate([sums_ref[k] for k in range(pairs)], axis=1)
        pieces = jnp.concatenate([piece.astype(BF16) for piece in three_pieces(sums)], axis=0)
        picked = mm(pick_ref[...], pieces, NT)
        biases = picked[:, :6] + picked[:, 8:14] + picked[:, 16:22]
        seen = columns_ref.shape[1] // 2
        rest_zero = jnp.zeros((model, 128 - 6 - seen), F32)
        extra = jnp.concatenate(
            [
                biases, columns_ref[:, :seen], rest_zero,
                jnp.zeros((model, 6), F32), columns_ref[:, seen:], rest_zero,
            ],
            axis=1,
        )
        lower = y_ref[1] % 2 == 0

        def place(array, cols, value):
            if group is None:
                grads_ref[array, :, cols] = value
                return
            blocks = value.reshape(model // (2 * group), 2, group, value.shape[1])
            first, second = blocks[:, 0], blocks[:, 1]
            for k, (one, other) in enumerate(((first, second), (second, first))):
                picked_rows = jnp.where(lower, one, other).reshape(model // 2, value.shape[1])
                grads_ref[array, k * (model // 2) : (k + 1) * (model // 2), cols] = picked_rows

        for array in range(2):

            def one(i, carry, array=array):
                grad = jnp.concatenate([all_ref[k, 3 * array + i] for k in range(pairs)], axis=1)
                at = pl.multiple_of(width * i, 128)
                place(array, pl.ds(at, width), mm(turned_ref[...], grad, NN))
                return carry

            lax.fori_loop(0, 3, one, 0)
            wide = 3 * width
            if array:
                place(array, slice(wide, wide + 256), extra)
                wide += 256
            if group is None:
                leave(grads_ref.at[array, :, :wide], grads_hbm[array])
            else:
                for k in (1, 0):
                    rows = slice(k * (model // 2), (k + 1) * (model // 2))
                    leave(grads_ref.at[array, rows, :wide], grads_hbm[2 * array + k])
        for copy in leaving:
            copy.wait()


def attend_back(
    y, q2, extra, k2, v, o, own, got, live, kind, columns, pick, wq, wk, wv, turned, first, chunks, group
):
    length, width = v.shape
    half, model = first.shape
    pairs = width // (2 * HD)
    head = pl.BlockSpec((length, 2 * HD), lambda p, h, *_: (0, 2 * p + h))
    pair = pl.BlockSpec((length, 2 * HD), lambda p, h, *_: (0, p))
    part = pl.BlockSpec((half, 2 * HD), lambda p, h, *_: (0, p))
    anywhere = pl.BlockSpec(memory_space=pl.ANY)
    shapes = [struct((rows, model), F32) for rows in chunks]
    for wide in (3 * width, 3 * width + 256):
        shapes += [struct((model, wide), F32)] if group is None else [struct((model // 2, wide), F32)] * 2
    return pl.pallas_call(
        functools.partial(attend_back_kernel, len(chunks), group),
        grid_spec=pltpu.PrefetchScalarGridSpec(
            num_scalar_prefetch=1,
            grid=(pairs, 2),
            in_specs=[
                head, head, head, pair, pair, part, part, whole_block((length, 1)), whole_block((length, 1)),
                whole_block(columns.shape), whole_block(pick.shape),
                *[anywhere] * 5,
            ],
            out_specs=[anywhere] * len(shapes),
            scratch_shapes=[
                *[pltpu.VMEM((2, length, 2 * HD), F32)] * 3,
                pltpu.VMEM((length, 2 * HD), F32),
                pltpu.VMEM((length, 2 * HD), BF16),
                pltpu.VMEM((pairs, 6, length, 2 * HD), BF16),
                pltpu.VMEM((pairs, 8, 2 * HD), F32),
                pltpu.VMEM((model, 6 * width), BF16),
                pltpu.VMEM((model, length), BF16),
                pltpu.VMEM((half, model), F32),
                pltpu.VMEM((length, model), F32),
                pltpu.VMEM((2, model, 3 * width + 256), F32),
                pltpu.SemaphoreType.DMA((8,)),
                pltpu.SemaphoreType.DMA((len(shapes),)),
            ],
        ),
        out_shape=shapes,
        compiler_params=params(63),
        cost_estimate=cost(20 * length * length * width, 40 * length * width, length * length * width // HD),
        name="attend_back",
    )(y, q2, extra, k2, v, o, own, got, live, kind, columns, pick, wq, wk, wv, turned, first)


def normalise(value):
    centre = value - jnp.mean(value, axis=-1, keepdims=True)
    inverse = lax.rsqrt(jnp.mean(centre * centre, axis=-1, keepdims=True) + NORM_EPS)
    return centre * inverse, inverse


def normalise_back(scaled, normal, inverse):
    return inverse * (
        scaled
        - jnp.mean(scaled, axis=-1, keepdims=True)
        - normal * jnp.mean(scaled * normal, axis=-1, keepdims=True)
    )


def gelu_pair(values):
    cumulative = 0.5 * (1.0 + lax.erf(values * (1.0 / math.sqrt(2.0))))
    density = jnp.exp(-0.5 * values * values) * (1.0 / math.sqrt(2.0 * math.pi))
    return values * cumulative, cumulative + values * density


def column_sum(value):
    return jnp.sum(value, axis=0, keepdims=True)


def first_cut(half):
    return half // 2


def middle_sizes(wi, wo, early):
    hidden, model, width = wi.shape[1], wo.shape[1], wo.shape[0]
    cut = [width // SLICES, (width + model) // SLICES, (width + 2 * model) // SLICES]
    return hidden, hidden // 2, model, width, cut


def far_block(ref, a, b):
    return ref[:, a:b, :].reshape(SLICES * (b - a), ref.shape[2])


def far_outer(ref, part, half):
    per = SLICES // 2
    return ref[per * (part - 2) : per * (part - 1), :, :].reshape(half, ref.shape[2])


def by_core(lower, values):
    first, second = (value.astype(F32) for value in values)
    keep = jnp.where(lower, first, second).astype(BF16)
    return keep, jnp.where(lower, second, first)


def forward_kernel(at_ref, x_ref, cot_ref, live_ref, own_ref, got_ref, wo_ref, wi_hbm, wu_hbm, *rest):
    arrived = rest[:SLICES]
    arrived_late = rest[SLICES : 2 * SLICES]
    (
        vec_ref, bias_ref, out_ref, out_first_ref, out_late_ref, low_ref, d_low_ref, keep_ref, send_ref,
        slope_ref, n1_ref, inv1_ref, d_second_ref, sums_ref, early_hbm, late_hbm,
        early_ref, late_ref, wi_ref, wu_ref, raw_ref, raw_late_ref, in_sem, out_sem,
    ) = rest[2 * SLICES :]
    step = pl.program_id(0)
    me = at_ref[1]
    lower = me % 2 == 0
    hidden, half, model, width, cut = middle_sizes(wi_hbm, wo_ref, early_ref)

    def weight_copies():
        stages = [[], [], [], [], []]
        for k in range(SLICES):
            for stage, source, target in (
                (0, arrived[k].at[: cut[0], :], raw_ref.at[k, : cut[0], :]),
                (2, arrived[k].at[cut[0] :, :], raw_ref.at[k, cut[0] :, :]),
                (4, arrived_late[k], raw_late_ref.at[k]),
            ):
                stages[stage].append(pltpu.make_async_copy(source, target, in_sem.at[stage * SLICES + k]))
        stages[1].append(pltpu.make_async_copy(wi_hbm, wi_ref, in_sem.at[SLICES]))
        stages[3].append(pltpu.make_async_copy(wu_hbm, wu_ref, in_sem.at[3 * SLICES]))
        return stages

    def leaving():
        return [
            pltpu.make_async_copy(early_ref, early_hbm, out_sem.at[0]),
            pltpu.make_async_copy(late_ref, late_hbm, out_sem.at[1]),
        ]

    def arrive(*wanted):
        @pl.when(step == 0)
        def _():
            stages = weight_copies()
            for stage in wanted:
                for copy in stages[stage]:
                    copy.wait()
            for k in range(SLICES):
                if 0 in wanted:
                    early_ref[me ^ k, : cut[0], :] = raw_ref[k, : cut[0], :].astype(BF16)
                if 2 in wanted:
                    early_ref[me ^ k, cut[0] :, :] = raw_ref[k, cut[0] :, :].astype(BF16)
                if 4 in wanted:
                    late_ref[me ^ k] = raw_late_ref[k].astype(BF16)
            if 4 in wanted:
                for copy in leaving():
                    copy.start()

    @pl.when(step == 0)
    def _():
        for stage in weight_copies():
            for copy in stage:
                copy.start()

    arrive(0)
    vec = [vec_ref[k : k + 1, :] for k in range(6)]
    got = got_ref[...].astype(BF16)
    own = own_ref[...]
    first = mm(own, wo_ref[...], NN) + mm(got, far_block(early_ref, 0, cut[0]), NN) + vec[0] + x_ref[...].astype(F32)
    n1, inv1 = normalise(first)
    n1_ref[...] = n1
    inv1_ref[...] = inv1
    normed = n1 * vec[1] + vec[2]
    low = normed.astype(BF16)
    low_ref[...] = low
    at_low = model + hidden
    send_ref[:, at_low : at_low + model] = low.astype(F32)
    _, send = by_core(lower, (own, got))
    send_ref[:, at_low + model :] = send
    second = vec[3] + normed
    arrive(1, 3)
    for far in range(2):
        if far:
            arrive(2, 4)
        pair = []
        for part in (2 * far, 2 * far + 1):
            inner = wi_ref[:, half * part : half * (part + 1)] if part < 2 else far_block(early_ref, cut[part - 2], cut[part - 1])
            pre = mm(low, inner, NN) + bias_ref[part : part + 1, :]
            active, slope = gelu_pair(pre)
            active = active.astype(BF16)
            slope_ref[:, half * part : half * (part + 1)] = slope.astype(BF16)
            pair.append(active)
            outer = wu_ref[half * part : half * (part + 1), :] if part < 2 else far_outer(late_ref, part, half)
            second = second + mm(active, outer, NN)
        keep, send = by_core(lower, pair)
        keep_ref[:, half * far : half * (far + 1)] = keep
        send_ref[:, model + half * far : model + half * (far + 1)] = send
    n2, inv2 = normalise(second)
    live = live_ref[...] > 0.5
    result = jnp.where(live, n2 * vec[4] + vec[5], 0.0).astype(BF16)
    out_ref[...] = result
    out_first_ref[...] = result[:, : model // 2].astype(F32)
    out_late_ref[...] = result[:, model // 2 :].astype(F32)
    dz = jnp.where(live, cot_ref[...].astype(F32), 0.0)
    d_second = normalise_back(dz * vec[4], n2, inv2)
    d_second_ref[...] = d_second
    d_low = d_second.astype(BF16)
    d_low_ref[...] = d_low
    send_ref[:, :model] = d_low.astype(F32)
    sums = jnp.concatenate(
        [column_sum(d_second), column_sum(dz * n2), column_sum(dz), jnp.zeros((5, model), F32)], axis=0
    )

    @pl.when(step == 0)
    def _():
        sums_ref[...] = sums

    @pl.when(step != 0)
    def _():
        sums_ref[...] += sums

    @pl.when(step == pl.num_programs(0) - 1)
    def _():
        for copy in leaving():
            copy.wait()


def forward(at, x, cot, live, context, got, wo, wi, wu, early, late, vec, bias, rows=256):
    half, width = got.shape
    model, hidden = wi.shape
    rows = min(rows, half)
    steps = half // rows
    mine = lambda w: pl.BlockSpec((rows, w), lambda i, s: (i + s[0] * steps, 0))
    tile = lambda w: pl.BlockSpec((rows, w), lambda i, s: (i, 0))
    anywhere = pl.BlockSpec(memory_space=pl.ANY)
    widths = (
        (model, BF16), (model // 2, F32), (model // 2, F32), (model, BF16), (model, BF16), (hidden, BF16),
        (2 * model + hidden + width, F32), (2 * hidden, BF16), (model, F32), (1, F32), (model, F32),
    )
    far_shapes = [(SLICES, *early[0].shape), (SLICES, *late[0].shape)]
    return pl.pallas_call(
        forward_kernel,
        grid_spec=pltpu.PrefetchScalarGridSpec(
            num_scalar_prefetch=1,
            grid=(steps,),
            in_specs=[
                mine(model), mine(model), mine(1), mine(width), tile(width),
                whole_block(wo.shape), *[anywhere] * (2 + 2 * SLICES),
                whole_block(vec.shape), whole_block(bias.shape),
            ],
            out_specs=[
                *(tile(w) for w, _ in widths), pl.BlockSpec((8, model), lambda i, s: (0, 0)), anywhere, anywhere,
            ],
            scratch_shapes=[
                *(pltpu.VMEM(shape, BF16) for shape in far_shapes),
                pltpu.VMEM(wi.shape, BF16),
                pltpu.VMEM(wu.shape, BF16),
                *(pltpu.VMEM(shape, F32) for shape in far_shapes),
                pltpu.SemaphoreType.DMA((5 * SLICES,)),
                pltpu.SemaphoreType.DMA((2,)),
            ],
        ),
        out_shape=[
            *(struct((half, w), kind) for w, kind in widths), struct((8, model), F32),
            *(struct(shape, BF16) for shape in far_shapes),
        ],
        compiler_params=params(63),
        cost_estimate=cost(8 * half * model * hidden, 24 * model * hidden, 4 * half * hidden),
        name="forward",
    )(at, x, cot, live, context, got, wo, wi, wu, *early, *late, vec, bias)


def backward_kernel(
    at_ref, slope_ref, n1_ref, inv1_ref, d_second_ref, d_low_ref, own_ref, got_ref, wo_ref, vec_ref,
    wi_hbm, wu_hbm, early_hbm, late_hbm,
    first_ref, dco_ref, dcf_ref, d_attn_ref, keep0_ref, keep1_ref, send_ref, sums_ref, inner_sums_ref,
    wi_ref, wu_ref, early_ref, late_ref, in_sem,
):
    step = pl.program_id(0)
    lower = at_ref[1] % 2 == 0
    hidden, half, model, width, cut = middle_sizes(wi_hbm, wo_ref, early_ref)
    ca = first_cut(half)

    def copies():
        pairs = ((wu_hbm, wu_ref), (wi_hbm, wi_ref), (late_hbm, late_ref), (early_hbm, early_ref))
        return [pltpu.make_async_copy(*pair, in_sem.at[k]) for k, pair in enumerate(pairs)]

    @pl.when(step == 0)
    def _():
        for copy in copies():
            copy.start()

    d_low = d_low_ref[...]
    n1 = n1_ref[...]
    d_normed = d_second_ref[...]
    inner_sums = []
    for far in range(2):

        @pl.when(step == 0)
        def _():
            for copy in copies()[2 * far : 2 * far + 2]:
                copy.wait()

        pair = []
        for part in (2 * far, 2 * far + 1):
            outer = wu_ref[half * part : half * (part + 1), :] if part < 2 else far_outer(late_ref, part, half)
            inner = wi_ref[:, half * part : half * (part + 1)] if part < 2 else far_block(early_ref, cut[part - 2], cut[part - 1])
            d_hidden = mm(d_low, outer, NT)
            d_inner = (d_hidden * slope_ref[:, half * part : half * (part + 1)].astype(F32)).astype(BF16)
            pair.append(d_inner)
            inner_sums.append(column_sum(d_inner.astype(F32)))
            d_normed = d_normed + mm(d_inner, inner, NT)
        keep, send = by_core(lower, pair)
        da = half - ca
        keep0_ref[:, ca * far : ca * (far + 1)] = keep[:, :ca]
        keep1_ref[:, da * far : da * (far + 1)] = keep[:, ca:]
        send_ref[:, ca * far : ca * (far + 1)] = send[:, :ca]
        send_ref[:, 2 * ca + da * far : 2 * ca + da * (far + 1)] = send[:, ca:]
    d_first = normalise_back(d_normed * vec_ref[1:2, :], n1, inv1_ref[...])
    first_ref[...] = d_first
    d_attn = d_first.astype(BF16)
    d_attn_ref[...] = d_attn
    send_ref[:, hidden:] = d_attn.astype(F32)
    dco_ref[...] = mm(d_attn, wo_ref[...], NT).astype(BF16).astype(F32)
    dcf_ref[...] = mm(d_attn, far_block(early_ref, 0, cut[0]), NT).astype(BF16).astype(F32)
    keep, _ = by_core(lower, (own_ref[...], got_ref[...]))
    keep0_ref[:, 2 * ca :] = keep
    sums = jnp.concatenate(
        [column_sum(d_first), column_sum(d_normed * n1), column_sum(d_normed), jnp.zeros((5, model), F32)], axis=0
    )
    inner_sums = jnp.concatenate([*inner_sums, jnp.zeros((4, half), F32)], axis=0)

    @pl.when(step == 0)
    def _():
        sums_ref[...] = sums
        inner_sums_ref[...] = inner_sums

    @pl.when(step != 0)
    def _():
        sums_ref[...] += sums
        inner_sums_ref[...] += inner_sums


def backward(at, slope, n1, inv1, d_second, d_low, context, got, wo, vec, wi, wu, early, late, rows=256):
    half, width = got.shape
    model, hidden = wi.shape
    rows = min(rows, half)
    steps = half // rows
    ca = first_cut(hidden // 2)
    mine = lambda w: pl.BlockSpec((rows, w), lambda i, s: (i + s[0] * steps, 0))
    tile = lambda w: pl.BlockSpec((rows, w), lambda i, s: (i, 0))
    anywhere = pl.BlockSpec(memory_space=pl.ANY)
    widths = (
        (model, F32), (width, F32), (width, F32), (model, BF16), (2 * ca + width, BF16), (hidden - 2 * ca, BF16),
        (hidden + model, F32),
    )
    return pl.pallas_call(
        backward_kernel,
        grid_spec=pltpu.PrefetchScalarGridSpec(
            num_scalar_prefetch=1,
            grid=(steps,),
            in_specs=[
                tile(2 * hidden), tile(model), tile(1), tile(model), tile(model), mine(width), tile(width),
                whole_block(wo.shape), whole_block(vec.shape), *[anywhere] * 4,
            ],
            out_specs=[
                *(tile(w) for w, _ in widths),
                pl.BlockSpec((8, model), lambda i, s: (0, 0)),
                pl.BlockSpec((8, hidden // 2), lambda i, s: (0, 0)),
            ],
            scratch_shapes=[
                *(pltpu.VMEM(a.shape, BF16) for a in (wi, wu, early, late)),
                pltpu.SemaphoreType.DMA((4,)),
            ],
        ),
        out_shape=[
            *(struct((half, w), kind) for w, kind in widths), struct((8, model), F32), struct((8, hidden // 2), F32),
        ],
        compiler_params=params(63),
        cost_estimate=cost(8 * half * model * hidden, 24 * model * hidden),
        name="backward",
    )(at, slope, n1, inv1, d_second, d_low, context, got, wo, vec, wi, wu, early, late)


def weight_kernel(plan, count, kinds, bit_ref, *rest):
    groups = len(plan)
    left_hbm, rest = rest[:kinds], rest[kinds:]
    keep_hbm, rest = rest[:groups], rest[groups:]
    got_hbm, rest = rest[:count], rest[count:]
    outs, rest = rest[: 2 * groups], rest[2 * groups :]
    left_ref, left_got_ref, rest = rest[0], rest[1], rest[2:]
    keep_refs, rest = rest[:groups], rest[groups:]
    got_refs, rest = rest[:groups], rest[groups:]
    stage_refs, (in_sem, out_sem) = rest[:groups], rest[groups:]
    model = left_ref.shape[2]

    arriving, ready = [], {}

    def bring(key, source, target):
        if key not in ready:
            ready[key] = pltpu.make_async_copy(source, target, in_sem.at[len(arriving)])
            ready[key].start()
            arriving.append(key)

    for g, (_, _, tiles) in enumerate(plan):
        for index, (left_array, left_at), (right_array, right_at), a, b in tiles:
            bring(("left", index), left_hbm[index], left_ref.at[index])
            if ("left got", index) not in ready:
                columns = slice(left_at, left_at + model)
                bring(("left got", index), got_hbm[left_array].at[:, columns], left_got_ref.at[index])
            bring(("keep", g, a), keep_hbm[g].at[:, a:b], keep_refs[g].at[:, a:b])
            columns = slice(right_at, right_at + b - a)
            bring(("got", g, a), got_hbm[right_array].at[:, columns], got_refs[g].at[:, a:b])
    waited = set()

    def need(*keys):
        for key in keys:
            if key not in waited:
                waited.add(key)
                ready[key].wait()

    leaving = []
    for g, (slot, group, tiles) in enumerate(plan):
        width = keep_refs[g].shape[1]
        for index, _, _, a, b in tiles:
            need(("left", index), ("left got", index), ("keep", g, a), ("got", g, a))
            left = jnp.concatenate([left_ref[index], left_got_ref[index].astype(BF16)], axis=0)
            right = jnp.concatenate([keep_refs[g][:, a:b], got_refs[g][:, a:b].astype(BF16)], axis=0)
            value = mm(left, right, TN)
            if slot is None:
                part, base = (0, 0) if 2 * b <= width else (1, width // 2)
                stage_refs[g][part, :, a - base : b - base] = value
                parts = ((part, a - base, b - base),)
            else:
                pairs = value.reshape(model // (2 * group), 2, group, b - a)
                kept = bit_ref[slot] == 0
                first, second = pairs[:, 0], pairs[:, 1]
                for part, (one, other) in enumerate(((first, second), (second, first))):
                    picked = jnp.where(kept, one, other)
                    stage_refs[g][part, :, a:b] = picked.reshape(model // 2, b - a)
                parts = ((1, a, b), (0, a, b))
            for part, a, b in parts:
                copy = pltpu.make_async_copy(
                    stage_refs[g].at[part, :, a:b], outs[2 * g + part].at[:, a:b], out_sem.at[len(leaving)]
                )
                copy.start()
                leaving.append(copy)
    for copy in leaving:
        copy.wait()


def weight_grads(at, lefts, keeps, received, plan):
    depth, model = lefts[0].shape
    stages, shapes, steps = [], [], 0
    for (slot, _, tiles), keep in zip(plan, keeps):
        width = keep.shape[1]
        shape = (model, width // 2) if slot is None else (model // 2, width)
        stages.append(pltpu.VMEM((2, *shape), F32))
        shapes += [struct(shape, F32)] * 2
        steps += len(tiles)
    columns = sum(keep.shape[1] for keep in keeps)
    anywhere = pl.BlockSpec(memory_space=pl.ANY)
    return pl.pallas_call(
        functools.partial(weight_kernel, plan, len(received), len(lefts)),
        grid_spec=pltpu.PrefetchScalarGridSpec(
            num_scalar_prefetch=1,
            grid=(1,),
            in_specs=[anywhere] * (len(lefts) + len(keeps) + len(received)),
            out_specs=[anywhere] * len(shapes),
            scratch_shapes=[
                pltpu.VMEM((len(lefts), depth, model), BF16),
                pltpu.VMEM((len(lefts), depth, model), F32),
                *(pltpu.VMEM(keep.shape, BF16) for keep in keeps),
                *(pltpu.VMEM(keep.shape, F32) for keep in keeps),
                *stages,
                pltpu.SemaphoreType.DMA((2 * len(lefts) + 2 * steps,)),
                pltpu.SemaphoreType.DMA((2 * steps,)),
            ],
        ),
        out_shape=shapes,
        compiler_params=params(63),
        cost_estimate=cost(4 * depth * model * columns, 4 * model * columns + 8 * depth * columns),
        name="weight_grads",
    )(at, *lefts, *keeps, *received)


def combine_kernel(plan, count, bits_ref, *rest):
    outs = len(plan)
    arrays, targets = rest[:count], rest[count : count + outs]
    buffers, (in_sem, out_sem) = rest[count + outs : -2], rest[-2:]
    copies = []
    for pieces in plan:
        for _, terms in pieces:
            for array, chosen, a, b, _ in terms:
                index = [slice(None)] * len(arrays[array].shape)
                for axis, (bit, mine) in chosen:
                    index[axis] = pl.ds(bits_ref[bit] if mine else 1 - bits_ref[bit], 1)
                index[-1] = slice(a, b)
                k = len(copies)
                copies.append(pltpu.make_async_copy(arrays[array].at[tuple(index)], buffers[k], in_sem.at[k]))
    for copy in copies:
        copy.start()
    k = 0
    leaving = []
    for target, pieces in zip(targets, plan):
        for at, terms in pieces:
            first = k
            total = None
            for *_, gate in terms:
                copies[k].wait()
                value = buffers[k][...]
                if gate is not None:
                    value = jnp.where(bits_ref[0] == gate, value, 0.0)
                total = value if total is None else total + value
                k += 1
            if len(terms) > 1:
                buffers[first][...] = total
            width = buffers[first].shape[-1]
            index = (*[slice(None)] * (len(target.shape) - 1), slice(at, at + width))
            copy = pltpu.make_async_copy(buffers[first], target.at[index], out_sem.at[len(leaving)])
            copy.start()
            leaving.append(copy)
    for copy in leaving:
        copy.wait()


def combine(bit_values, outputs):
    arrays, plan, shapes, buffers, moved = [], [], [], [], 0
    for pieces in outputs:
        at, planned = 0, []
        for terms in pieces:
            named = []
            for array, chosen, a, b, gate in terms:
                place = [k for k, other in enumerate(arrays) if other is array]
                if not place:
                    place = [len(arrays)]
                    arrays.append(array)
                named.append((place[0], tuple(sorted(chosen.items())), a, b, gate))
                block = tuple(1 if k in chosen else size for k, size in enumerate(array.shape[:-1]))
                buffers.append(pltpu.VMEM((*block, b - a), F32))
                moved += 4 * math.prod(block) * (b - a)
            planned.append((at, named))
            at += b - a
        plan.append(planned)
        shapes.append(struct((*block, at), F32))
    anywhere = pl.BlockSpec(memory_space=pl.ANY)
    pieces = sum(len(planned) for planned in plan)
    return pl.pallas_call(
        functools.partial(combine_kernel, plan, len(arrays)),
        grid_spec=pltpu.PrefetchScalarGridSpec(
            num_scalar_prefetch=1,
            grid=(1,),
            in_specs=[anywhere] * len(arrays),
            out_specs=[anywhere] * len(shapes),
            scratch_shapes=[
                *buffers,
                pltpu.SemaphoreType.DMA((len(buffers),)),
                pltpu.SemaphoreType.DMA((pieces,)),
            ],
        ),
        out_shape=shapes,
        compiler_params=params(63),
        cost_estimate=cost(moved, 2 * moved),
        name="combine",
    )(bit_values, *arrays)


def turn_kernel(value_ref, out_ref):
    out_ref[...] = value_ref[...].astype(F32).T.astype(BF16)


def turn(value, columns=256):
    length, model = value.shape
    return pl.pallas_call(
        turn_kernel,
        grid=(model // columns,),
        in_specs=[pl.BlockSpec((length, columns), lambda i: (0, i))],
        out_specs=pl.BlockSpec((columns, length), lambda i: (i, 0)),
        out_shape=struct((model, length), BF16),
        compiler_params=params(63),
        cost_estimate=cost(length * model, 4 * length * model),
        name="turn",
    )(value)


def place_kernel(steps, y_ref, own_ref, first_ref, second_ref, out_ref):
    mine = pl.program_id(0) // steps == y_ref[0]
    got = jnp.concatenate([first_ref[...], second_ref[...]], axis=1)
    out_ref[...] = jnp.where(mine, own_ref[...].astype(F32), got).astype(BF16)


def place_rows(y, own, first, second):
    half, model = own.shape
    rows = min(128, half)
    steps = half // rows
    tile = lambda w: pl.BlockSpec((rows, w), lambda i, s: (i % steps, 0))
    return pl.pallas_call(
        functools.partial(place_kernel, steps),
        grid_spec=pltpu.PrefetchScalarGridSpec(
            num_scalar_prefetch=1,
            grid=(2 * steps,),
            in_specs=[tile(model), tile(model // 2), tile(model // 2)],
            out_specs=pl.BlockSpec((rows, model), lambda i, s: (i, 0)),
        ),
        out_shape=struct((2 * half, model), BF16),
        compiler_params=params(63),
        cost_estimate=cost(half * model, 12 * half * model),
        name="place_rows",
    )(y, own, first, second)


def per_device(
    devices,
    tokens,
    lengths,
    entity_flags,
    query_weight,
    query_bias,
    key_weight,
    key_bias,
    value_weight,
    value_bias,
    output_weight,
    output_bias,
    attn_gain,
    attn_shift,
    inner_weight,
    inner_bias,
    outer_weight,
    outer_bias,
    final_gain,
    final_shift,
    cotangent,
):
    x = tokens[0]
    length, model = x.shape
    width = key_weight.shape[1]
    hidden = inner_weight.shape[1]
    half = length // 2
    bits = devices.bit_length() - 1
    y = lax.axis_index("tensor")
    d = lax.axis_index("dp")

    def swap(value, mask):
        return lax.ppermute(value, "dp", [(i, i ^ mask) for i in range(devices)])

    def cross(value):
        return lax.ppermute(value, "tensor", [(0, 1), (1, 0)])

    me = d % SLICES
    core = d % 2
    rows = model // devices
    near_mask, far_mask = 192 // rows, 96 // rows
    at = jnp.stack([y, me, (d // near_mask) % 2, (d // far_mask) % 2]).astype(jnp.int32)
    tie = lax.optimization_barrier

    def cut(array, index):
        size = array.shape[0] // SLICES
        return lax.dynamic_slice_in_dim(array, index * size, size, 0)

    def pack(index):
        wide = cut(inner_weight, index)
        early = jnp.concatenate([cut(output_weight, index), wide[:, :model], wide[:, model:]], axis=0)
        return early.astype(F32)

    def pack_late(index):
        return cut(outer_weight, index).astype(F32)

    live = (lax.broadcasted_iota(jnp.int32, (length, 1), 0) < lengths[0]).astype(F32)
    kind = (entity_flags[0] == 1).astype(F32).reshape(length, 1)

    e0 = cross(pack(me))
    far_bias = cross(inner_bias)
    q2, k2, v = project(
        x, kind, query_weight, query_bias, key_weight, key_bias, value_weight, value_bias
    )
    e0, far_bias, l0, l6, q2 = tie((e0, far_bias, pack_late(me), pack_late(me ^ 6), q2))
    e2 = swap(e0, 2)
    e4 = swap(e0, 4)
    l0 = cross(l0)
    e1 = swap(e0, 1)
    context, extra = attend(q2, k2, v, live)
    sent = lax.dynamic_slice_in_dim(context, half * (1 - y), half, 0).astype(F32)
    e1, e2, e4, l0, l6, sent = tie((e1, e2, e4, l0, l6, sent))
    l2 = swap(l0, 2)
    l4 = swap(l0, 4)
    got = cross(sent)
    e6 = swap(e4, 2)
    l6 = cross(l6)
    per = width // devices
    where_row = lax.broadcasted_iota(jnp.int32, (model, width), 0)
    where_bias = lax.broadcasted_iota(jnp.int32, (model, width), 1)
    pick = (where_row == (where_bias // per) * rows + where_bias % per).astype(BF16)
    x_turned = turn(x)
    l2, l4, e2, e4, pick, x_turned = tie((l2, l4, e2, e4, pick, x_turned))
    e3 = swap(e2, 1)
    e5 = swap(e4, 1)
    got, e6, l6, e3, e5, l0, l2, l4 = tie((got, e6, l6, e3, e5, l0, l2, l4))
    l1 = swap(l0, 1)
    l3 = swap(l2, 1)
    l5 = swap(l4, 1)
    l7 = swap(l6, 1)
    e7 = swap(e6, 1)
    early = (e0, e1, e2, e3, e4, e5, e6, e7)
    late = (l0, l1, l2, l3, l4, l5, l6, l7)

    vec = jnp.stack(
        [output_bias, attn_gain, attn_shift, outer_bias, final_gain, final_shift, outer_bias, outer_bias]
    )
    bias = jnp.concatenate([inner_bias, far_bias, inner_bias, far_bias]).reshape(8, hidden // 2)
    ca, cb = first_cut(hidden // 2), hidden // 2
    da, db = hidden // 2 - ca, 0
    (
        out_rows, out_first, out_late, low, d_low, keep2, early_send, slope, n1, inv1, d_second, late_sums,
        far_early, far_late,
    ) = forward(
        at, x, cotangent[0], live, context, got, output_weight, inner_weight, outer_weight,
        early, late, vec, bias,
    )
    early_got = swap(early_send, 1)
    got_first = cross(out_first)
    d_first, dco, dcf, d_attn, keep0, keep1, late_send, first_sums, inner_sums = backward(
        at, slope, n1, inv1, d_second, d_low, context, got, output_weight, vec, inner_weight, outer_weight,
        far_early, far_late,
    )
    inner_columns = inner_sums[:4].reshape(2, model, 2)
    shared = [first_sums[:3].T, late_sums[:3].T]
    columns = jnp.concatenate([*shared, inner_columns[0], *shared, inner_columns[1]], axis=1)
    early_got, got_first, late_send, dcf, columns = tie((early_got, got_first, late_send, dcf, columns))
    late_got = swap(late_send, 1)
    d_got = cross(dcf)

    low_at, d_attn_at = (0, 2 * cb + model), (1, hidden)
    g2_keep, g2_send = weight_grads(
        at, (d_low,), (keep2,), (early_got,),
        (
            (
                3, far_mask * rows,
                ((0, (0, 0), (0, model), 0, cb), (0, (0, 0), (0, model + cb), cb, 2 * cb)),
            ),
        ),
    )
    g0_keep, g0_send, g1_keep, g1_send = weight_grads(
        at, (low, d_attn), (keep0, keep1), (early_got, late_got),
        (
            (
                2, near_mask * rows,
                (
                    (0, low_at, (1, 0), 0, ca), (0, low_at, (1, ca), ca, 2 * ca),
                    (1, d_attn_at, (0, 2 * model + hidden), 2 * ca, 2 * ca + width),
                ),
            ),
            (
                None, None,
                ((0, low_at, (1, 2 * ca), 0, da), (0, low_at, (1, 2 * ca + da), da, 2 * da)),
            ),
        ),
    )
    g0_send, g1_send, d_got = tie((g0_send, g1_send, d_got))
    g0_got = swap(g0_send, near_mask)
    g2_got = swap(g2_send, far_mask)
    g1_got = cross(g1_send)

    g0_send, g1_send, g2_send, dco, d_got = tie((g0_send, g1_send, g2_send, dco, d_got))
    chunks = tuple(length * k // 32 for k in (7, 16, 9))
    group = rows if rows % 8 == 0 else None
    results = attend_back(
        at, q2, extra, k2, v, context, dco, d_got, live, kind, columns, pick,
        query_weight, key_weight, value_weight, x_turned, d_first, chunks, group,
    )
    parts, products = results[: len(chunks)], results[len(chunks) :]
    got_out = cross(out_late)

    def spread(array, done):
        dims = [1 if (1 << (bits - 1 - k)) in done else 2 for k in range(bits)]
        return array.reshape(*dims, rows, array.shape[-1])

    bit_values = jnp.stack([(d >> k) % 2 for k in range(bits)]).astype(jnp.int32)
    rest_masks = [1 << k for k in range(1, bits) if (1 << k) not in (near_mask, far_mask)]

    def term(array, *done):
        array = spread(array, done)
        return (array, {}, 0, array.shape[-1], None)

    def half_of(terms, mask, mine):
        k = mask.bit_length() - 1
        return [(array, {**chosen, bits - 1 - k: (k, mine)}, a, b, gate) for array, chosen, a, b, gate in terms]

    def kept(terms, mask):
        return half_of(terms, mask, True)

    def other(terms, mask):
        return half_of(terms, mask, False)

    def columns_of(terms, first, last):
        return [(array, chosen, a + first, a + last, gate) for array, chosen, a, _, gate in terms]

    def on_core(terms, core_index):
        return [(array, chosen, a, b, core_index) for array, chosen, a, b, _ in terms]

    def whole_of(array):
        return (array, {}, 0, array.shape[-1], None)

    def part_of(array, a, b):
        return (array, {}, a, b, None)

    g0_got, g1_got, g2_got, got_out, parts, products = tie((g0_got, g1_got, g2_got, got_out, parts, products))
    if group is None:
        c = [term(products[0])]
        e = [term(products[1])]
        c_send, e_send = combine(bit_values, [[other(c, 1)], [other(e, 1)]])
        c, e = kept(c, 1), kept(e, 1)
    else:
        c, e = [term(products[0], 1)], [term(products[2], 1)]
        c_send, e_send = spread(products[1], (1,)), spread(products[3], (1,))
    e_got = swap(e_send, 1)
    c_got = swap(c_send, 1)
    g0 = [term(g0_keep, near_mask), term(g0_got, near_mask)]
    g1 = [term(g1_keep), term(g1_got)]
    g2 = [term(g2_keep, far_mask), term(g2_got, far_mask)]
    sends = combine(bit_values, [[columns_of(g0, ca, 2 * ca + width)], [other(g1, near_mask)]])
    _, late_bits = tie((sends, bit_values))
    (g2_send,) = combine(late_bits, [[other(g2, near_mask)]])
    e_got, c_got, parts, _ = tie((e_got, c_got, parts, g2_send))
    e.append(whole_of(e_got))
    c.append(whole_of(c_got))
    g1_got = swap(sends[1], near_mask)
    g0_got = cross(sends[0])
    g2_got = swap(g2_send, near_mask)
    e_send, c_send = combine(bit_values, [[other(e, far_mask)], [other(c, near_mask)]])
    e_got = swap(e_send, far_mask)
    part0 = cross(parts[0])
    near_bit, near_axis = (d // near_mask) % 2, bits - near_mask.bit_length()
    for array, *_ in g1:
        g1_got = tie(g1_got + lax.dynamic_slice_in_dim(array, near_bit, 1, near_axis))
    g0_got, g1_sum = tie((g0_got, g1_got))
    t = [
        *on_core(columns_of(g0, 2 * ca, 2 * ca + width), 0),
        *on_core([part_of(g0_got, ca, ca + width)], 1),
    ]
    g0 = [*columns_of(g0, 0, ca), part_of(g0_got, 0, ca)]
    g1 = [whole_of(g1_sum)]

    (three_send,) = combine(bit_values, [[other(terms, far_mask) for terms in (g0, t, g1)]])
    three_got = swap(three_send, far_mask)
    g2_got, e_got, part0, parts, _ = tie((g2_got, e_got, part0, parts, three_send))
    g2 = [*kept(g2, near_mask), whole_of(g2_got)]
    e = [*kept(e, far_mask), whole_of(e_got)]
    sends = combine(
        bit_values, [[columns_of(g2, cb, 2 * cb)], [columns_of(e, 3 * width + 128, 3 * width + 256)]]
    )
    g2_got = cross(sends[0])
    small_got = cross(sends[1])
    c_got = swap(c_send, near_mask)
    three_got, c_got, own0, part0 = tie((three_got, c_got, parts[0], part0))
    in0 = (own0 + part0).astype(BF16)
    three_got, g2_got, c_got, small_got, in0, parts = tie((three_got, g2_got, c_got, small_got, in0, parts))
    small = [*columns_of(e, 3 * width, 3 * width + 128), whole_of(small_got)]
    e = columns_of(e, 0, 3 * width)
    g0 = [*kept(g0, far_mask), part_of(three_got, 0, ca)]
    t = [*kept(t, far_mask), part_of(three_got, ca, ca + width)]
    g1 = [*kept(g1, far_mask), part_of(three_got, ca + width, three_got.shape[-1])]
    g2 = [*columns_of(g2, 0, cb), whole_of(g2_got)]
    c = [*kept(c, near_mask), whole_of(c_got)]

    main = (g0, g1, g2, t)
    sizes = (ca, da + db, cb, width)
    ends = [sum(sizes[:k]) for k in range(len(sizes) + 1)]
    mask = rest_masks[0]
    (main_send,) = combine(bit_values, [[other(terms, mask) for terms in main]])
    _, late_bits = tie((main_send, bit_values))
    sends = combine(late_bits, [[other(e, near_mask), other(small, near_mask)], [other(c, far_mask)]])
    got_z = swap(main_send, mask)
    in1 = (parts[1] + cross(parts[1])).astype(BF16)
    c_got = swap(sends[1], far_mask)
    e_got = swap(sends[0], near_mask)
    layer_out = place_rows(at, out_rows, got_first, got_out)
    got_z, e_got, c_got, in1, parts, layer_out = tie((got_z, e_got, c_got, in1, parts, layer_out))
    main = [[*kept(terms, mask), part_of(got_z, ends[n], ends[n + 1])] for n, terms in enumerate(main)]
    e = [*kept(e, near_mask), part_of(e_got, 0, 3 * width)]
    small = [*kept(small, near_mask), part_of(e_got, 3 * width, 3 * width + 128)]
    c = [*kept(c, far_mask), whole_of(c_got)]
    for mask in rest_masks[1:]:
        (send,) = combine(bit_values, [[other(terms, mask) for terms in main]])
        got_z = swap(send, mask)
        main = [[*kept(terms, mask), part_of(got_z, ends[n], ends[n + 1])] for n, terms in enumerate(main)]

    for k, mask in enumerate(rest_masks):
        (pair_send,) = combine(bit_values, [[other(c, mask), other(e, mask), other(small, mask)]])
        outputs = [[kept(c, mask), kept(e, mask), kept(small, mask)]]
        if k == 0:
            outputs += [[other(terms, 1) for terms in main], [kept(terms, 1) for terms in main]]
        _, late_bits = tie((pair_send, bit_values))
        sends = combine(late_bits, outputs)
        pair_got = swap(pair_send, mask)
        if k == 0:
            in2 = (parts[2] + cross(parts[2])).astype(BF16)
            got_last = swap(sends[1], 1)
            keep = sends[2]
        pair_keep = sends[0]
        wide = pair_keep.shape[-1]
        c = [part_of(pair_keep, 0, 3 * width), part_of(pair_got, 0, 3 * width)]
        e = [part_of(pair_keep, 3 * width, 6 * width), part_of(pair_got, 3 * width, 6 * width)]
        small = [part_of(pair_keep, 6 * width, wide), part_of(pair_got, 6 * width, wide)]

    input_grad = jnp.concatenate([in0, in1, in2], axis=0)
    got_last, keep, input_grad = tie((got_last, keep, input_grad))
    got_last = got_last.reshape(rows, -1)
    keep = keep.reshape(rows, -1)
    low_half = jnp.where(core == 0, keep, got_last)
    high_half = jnp.where(core == 0, got_last, keep)
    at2 = ca + da + db
    inner_half = lambda array: [array[:, : ca + da]]
    at3 = at2 + cb
    outer_half = lambda array: [array[:, at2:at3], array[:, ca + da : at2]]
    t = keep[:, at3:] + got_last[:, at3:]
    grad_inner = jnp.concatenate(inner_half(low_half) + inner_half(high_half), axis=1)
    grad_outer = jnp.concatenate(outer_half(low_half) + outer_half(high_half), axis=1).T
    grad_output = t.T
    pair_got, grad_inner, grad_outer, grad_output = tie((pair_got, grad_inner, grad_outer, grad_output))
    pair = (pair_keep + pair_got).reshape(rows, -1)
    c, e = pair[:, : 3 * width], pair[:, 3 * width :]
    small = e[:, 3 * width + 6 : 3 * width + 12]
    inner_two = e[:, 3 * width + 12 : 3 * width + 14]

    piece = lambda array, k: array[:, width * k : width * (k + 1)]
    grad_query_weight = jnp.stack([piece(c, 0), piece(c, 1), piece(c, 2), piece(e, 0)])
    biases = e[:per, 3 * width : 3 * width + 6].T
    return (
        layer_out[None],
        input_grad[None],
        grad_query_weight,
        biases[:4],
        piece(e, 1),
        biases[4],
        piece(e, 2),
        biases[5],
        grad_output,
        small[:, 0],
        small[:, 1],
        small[:, 2],
        grad_inner,
        inner_two.reshape(2 * rows),
        grad_outer,
        small[:, 3],
        small[:, 4],
        small[:, 5],
    )


def solution(mesh):
    return jax.shard_map(
        functools.partial(per_device, mesh.shape["dp"]),
        mesh=mesh,
        in_specs=(
            P("dp", None, None),
            P("dp"),
            P("dp", None),
            P(None, None, "tensor"),
            P(None, "tensor"),
            P(None, "tensor"),
            P("tensor"),
            P(None, "tensor"),
            P("tensor"),
            P("tensor", None),
            P(),
            P(),
            P(),
            P(None, "tensor"),
            P("tensor"),
            P("tensor", None),
            P(),
            P(),
            P(),
            P("dp", None, None),
        ),
        out_specs=(
            P("dp", None, None),
            P("dp", None, None),
            P(None, "dp", "tensor"),
            P(None, ("tensor", "dp")),
            P("dp", "tensor"),
            P(("tensor", "dp")),
            P("dp", "tensor"),
            P(("tensor", "dp")),
            P("tensor", "dp"),
            P("dp"),
            P("dp"),
            P("dp"),
            P("dp", "tensor"),
            P(("tensor", "dp")),
            P("tensor", "dp"),
            P("dp"),
            P("dp"),
            P("dp"),
        ),
        check_vma=False,
    )
```

```python
import functools
import math

import jax
import jax.numpy as jnp
from jax import lax
from jax.experimental import pallas as pl
from jax.experimental.pallas import tpu as pltpu
from jax.sharding import PartitionSpec as P

HD = 64
SLICES = 8
MASKED = -1e30
NORM_EPS = 1e-05

F32 = jnp.float32
BF16 = jnp.bfloat16
NN = (((1,), (0,)), ((), ()))
NT = (((1,), (1,)), ((), ()))
TN = (((0,), (0,)), ((), ()))


def mm(left, right, dims):
    return lax.dot_general(left, right, dims, preferred_element_type=F32)


def struct(shape, kind):
    return jax.ShapeDtypeStruct(shape, kind)


def params(mib):
    return pltpu.CompilerParams(vmem_limit_bytes=mib << 20)


def cost(flops, moved, special=0):
    return pl.CostEstimate(flops=int(flops), bytes_accessed=int(moved), transcendentals=int(special))


def whole_block(shape):
    return pl.BlockSpec(shape, lambda *_: (0,) * len(shape), pipeline_mode=pl.Buffered(1))


def three_pieces(value):
    high = value.astype(BF16).astype(F32)
    rest = value - high
    middle = rest.astype(BF16).astype(F32)
    return high, middle, rest - middle


def project_kernel(x_ref, kind_ref, wq_ref, bq_ref, wk_ref, bk_ref, wv_ref, bv_ref, q2_ref, k2_ref, v_ref):
    x = x_ref[...]
    entity = kind_ref[...] > 0.5
    rows = x.shape[0]
    width = wk_ref.shape[1]

    weights = jnp.concatenate([*(wq_ref[c] for c in range(4)), wk_ref[...], wv_ref[...]], axis=1)
    biases = jnp.concatenate([*(bq_ref[c : c + 1, :] for c in range(4)), bk_ref[...], bv_ref[...]], axis=1)
    products = mm(x, weights, NN) + biases

    def query(c):
        return products[:, width * c : width * (c + 1)]

    scale = 1.0 / math.sqrt(HD)
    to_word = jnp.where(entity, query(2), query(0)).astype(BF16).astype(F32) * scale
    to_entity = jnp.where(entity, query(3), query(1)).astype(BF16).astype(F32) * scale
    keys = query(4).astype(BF16).astype(F32)
    v_ref[...] = query(5).astype(BF16)
    left = lax.broadcasted_iota(jnp.int32, (rows, 2 * HD), 1) < HD
    held = left != entity
    for p in range(width // (2 * HD)):
        cols = slice(2 * HD * p, 2 * HD * (p + 1))
        w, e, k = to_word[:, cols], to_entity[:, cols], keys[:, cols]
        w_roll, e_roll, k_roll = (pltpu.roll(t, HD, 1) for t in (w, e, k))
        even = slice(4 * HD * p, 4 * HD * p + 2 * HD)
        odd = slice(4 * HD * p + 2 * HD, 4 * HD * (p + 1))
        q2_ref[:, even] = jnp.where(left, w, e_roll).astype(BF16)
        q2_ref[:, odd] = jnp.where(left, w_roll, e).astype(BF16)
        k2_ref[:, even] = jnp.where(held, jnp.where(left, k, k_roll), 0.0).astype(BF16)
        k2_ref[:, odd] = jnp.where(held, jnp.where(left, k_roll, k), 0.0).astype(BF16)


def project(x, kind, wq, bq, wk, bk, wv, bv, rows=256):
    length, model = x.shape
    width = wk.shape[1]
    rows = min(rows, length)
    tile = lambda w: pl.BlockSpec((rows, w), lambda i: (i, 0))
    return pl.pallas_call(
        project_kernel,
        grid=(length // rows,),
        in_specs=[
            tile(model),
            tile(1),
            whole_block(wq.shape),
            whole_block(bq.shape),
            whole_block(wk.shape),
            whole_block((1, width)),
            whole_block(wv.shape),
            whole_block((1, width)),
        ],
        out_specs=[tile(2 * width), tile(2 * width), tile(width)],
        out_shape=[
            struct((length, 2 * width), BF16),
            struct((length, 2 * width), BF16),
            struct((length, width), BF16),
        ],
        compiler_params=params(63),
        cost_estimate=cost(12 * length * model * width, 16 * model * width + 12 * length * width),
        name="project",
    )(x, kind, wq, bq, wk, bk.reshape(1, width), wv, bv.reshape(1, width))


def key_extra(live, rows):
    lane = lax.broadcasted_iota(jnp.int32, (rows, 2 * HD), 1)
    return jnp.where(
        lane == 0, jnp.where(live, 0.0, MASKED), jnp.where(lane < 4, 1.0, 0.0)
    ).astype(BF16)


def attend_kernel(q2_ref, k2_ref, v_ref, live_ref, out_ref, extra_ref, turned_ref, both_ref):
    length = k2_ref.shape[0]
    h = pl.program_id(1)

    @pl.when(h == 0)
    def _():
        turned = v_ref[...].astype(F32).T.astype(BF16)
        turned_ref[0] = turned[:HD]
        turned_ref[1] = turned[HD:]

    lane = lax.broadcasted_iota(jnp.int32, (length, 2 * HD), 1)
    one = jnp.where(lane == 0, 1.0, 0.0).astype(BF16)
    keys = jnp.concatenate([k2_ref[...], key_extra(live_ref[...] > 0.5, length)], axis=1)
    query = jnp.concatenate([q2_ref[...], one], axis=1)
    scores = mm(keys, query, NT)
    top = jnp.max(scores, axis=0, keepdims=True)
    weights = jnp.exp(scores - top)
    norm = jnp.sum(weights, axis=0, keepdims=True)
    summed = mm(turned_ref[h], weights.astype(BF16), NN)
    both_ref[h] = summed * (1.0 / norm)
    pieces = three_pieces(-(top + jnp.log(norm)))
    filled = jnp.concatenate(
        [jnp.ones((1, length), F32), *pieces, jnp.zeros((2 * HD - 4, length), F32)], axis=0
    )
    extra_ref[...] = filled.T.astype(BF16)

    @pl.when(h == 1)
    def _():
        out_ref[...] = jnp.concatenate([both_ref[0], both_ref[1]], axis=0).T.astype(BF16)


def attend(q2, k2, v, live):
    length, width = v.shape
    head = pl.BlockSpec((length, 2 * HD), lambda p, h: (0, 2 * p + h))
    pair = pl.BlockSpec((length, 2 * HD), lambda p, h: (0, p))
    return pl.pallas_call(
        attend_kernel,
        grid=(width // (2 * HD), 2),
        in_specs=[head, head, pair, whole_block((length, 1))],
        out_specs=[pair, head],
        out_shape=[struct((length, width), BF16), struct((length, 2 * width), BF16)],
        scratch_shapes=[pltpu.VMEM((2, HD, length), BF16), pltpu.VMEM((2, HD, length), F32)],
        compiler_params=params(63),
        cost_estimate=cost(10 * length * length * width, 20 * length * width, length * length * width // HD),
        name="attend",
    )(q2, k2, v, live)


def attend_back_kernel(
    count, group, y_ref, q2_ref, extra_ref, k2_ref, v_ref, o_ref, own_ref, got_ref, live_ref, kind_ref, columns_ref, pick_ref,
    wq_hbm, wk_hbm, wv_hbm, turned_hbm, first_hbm, *rest,
):
    outs = count + (2 if group is None else 4)
    part_hbm, grads_hbm = rest[:count], rest[count:outs]
    (
        dk_ref, dv_ref, dq_ref, product_ref, d_ref, all_ref, sums_ref, weights_ref, turned_ref, first_ref,
        part_ref, grads_ref, in_sem, out_sem,
    ) = rest[outs:]
    length = k2_ref.shape[0]
    width = wk_hbm.shape[1]
    p, h = pl.program_id(0), pl.program_id(1)
    pairs = width // (2 * HD)
    lane = lax.broadcasted_iota(jnp.int32, (length, 2 * HD), 1)
    left = lane < HD

    def arriving():
        copies = [
            pltpu.make_async_copy(wq_hbm.at[c], weights_ref.at[:, width * c : width * (c + 1)], in_sem.at[c])
            for c in range(4)
        ]
        copies.append(pltpu.make_async_copy(wk_hbm, weights_ref.at[:, 4 * width : 5 * width], in_sem.at[4]))
        copies.append(pltpu.make_async_copy(wv_hbm, weights_ref.at[:, 5 * width : 6 * width], in_sem.at[5]))
        copies.append(pltpu.make_async_copy(turned_hbm, turned_ref, in_sem.at[6]))
        copies.append(pltpu.make_async_copy(first_hbm, first_ref, in_sem.at[7]))
        return copies

    @pl.when(jnp.logical_and(p == 0, h == 0))
    def _():
        for copy in arriving():
            copy.start()

    @pl.when(h == 0)
    def _():
        first = y_ref[0] == 0
        own, got = own_ref[...], got_ref[...]
        joined = jnp.concatenate([jnp.where(first, own, got), jnp.where(first, got, own)], axis=0)
        product_ref[...] = joined * o_ref[...].astype(F32)
        d_ref[...] = joined.astype(BF16)

    d_context = d_ref[...]
    base = HD * (1 - h)
    mine = jnp.logical_and(lane >= HD - base, lane < 2 * HD - base)
    delta = jnp.sum(jnp.where(mine, product_ref[...], 0.0), axis=1, keepdims=True)
    high, middle, low = three_pieces(-delta)
    pieces = jnp.where(
        lane == base, high, jnp.where(lane == base + 1, middle, jnp.where(lane == base + 2, low, 0.0))
    ).astype(BF16)
    d_wide = jnp.where(mine, d_context, pieces)
    q2, k2 = q2_ref[...], k2_ref[...]
    query = jnp.concatenate([q2, extra_ref[...]], axis=1)
    keys = jnp.concatenate([k2, key_extra(live_ref[...] > 0.5, length)], axis=1)
    probs = jnp.exp(mm(keys, query, NT))
    ones = jnp.where((lane >= base) & (lane < base + 3), 1.0, 0.0).astype(BF16)
    d_probs = mm(jnp.where(mine, v_ref[...], ones), d_wide, NT)
    d_scores = (probs * d_probs).astype(BF16)
    dv_ref[h] = mm(probs.astype(BF16), d_context, NN)
    dk_ref[h] = mm(d_scores, q2, NN)
    dq_ref[h] = mm(k2, d_scores, TN).T * (1.0 / math.sqrt(HD))

    @pl.when(h == 1)
    def _():
        entity = kind_ref[...] > 0.5
        even, odd = dq_ref[0], dq_ref[1]
        to_word = jnp.where(left, even, pltpu.roll(odd, HD, 1)).astype(BF16).astype(F32)
        to_entity = jnp.where(left, pltpu.roll(even, HD, 1), odd).astype(BF16).astype(F32)
        even, odd = dk_ref[0], dk_ref[1]
        even = jnp.where(entity, pltpu.roll(even, HD, 1), even)
        odd = jnp.where(entity, odd, pltpu.roll(odd, HD, 1))
        grads = [
            jnp.where(entity, 0.0, to_word),
            jnp.where(entity, 0.0, to_entity),
            jnp.where(entity, to_word, 0.0),
            jnp.where(entity, to_entity, 0.0),
            jnp.where(left, even, odd).astype(BF16).astype(F32),
            jnp.where(left, dv_ref[0], dv_ref[1]).astype(BF16).astype(F32),
        ]
        for c, grad in enumerate(grads):
            all_ref[p, c] = grad.astype(BF16)
        sums = [jnp.sum(grad, axis=0, keepdims=True) for grad in grads]
        sums_ref[p] = jnp.concatenate([*sums, jnp.zeros((2, 2 * HD), F32)], axis=0)

    @pl.when(jnp.logical_and(p == pairs - 1, h == 1))
    def _():
        for copy in arriving():
            copy.wait()
        grads = jnp.concatenate([all_ref[k, c] for c in range(6) for k in range(pairs)], axis=1)
        half = first_ref.shape[0]
        leaving = []

        def leave(source, target):
            copy = pltpu.make_async_copy(source, target, out_sem.at[len(leaving)])
            copy.start()
            leaving.append(copy)

        for i in range(2):
            rows = slice(i * half, (i + 1) * half)
            total = mm(grads[rows], weights_ref[...], NT)
            part_ref[rows, :] = total + jnp.where(y_ref[0] == i, first_ref[...], 0.0)
        begin = 0
        for target in part_hbm:
            leave(part_ref.at[begin : begin + target.shape[0], :], target)
            begin += target.shape[0]
        model = turned_ref.shape[0]
        sums = jnp.concatenate([sums_ref[k] for k in range(pairs)], axis=1)
        pieces = jnp.concatenate([piece.astype(BF16) for piece in three_pieces(sums)], axis=0)
        picked = mm(pick_ref[...], pieces, NT)
        biases = picked[:, :6] + picked[:, 8:14] + picked[:, 16:22]
        seen = columns_ref.shape[1] // 2
        rest_zero = jnp.zeros((model, 128 - 6 - seen), F32)
        extra = jnp.concatenate(
            [
                biases, columns_ref[:, :seen], rest_zero,
                jnp.zeros((model, 6), F32), columns_ref[:, seen:], rest_zero,
            ],
            axis=1,
        )
        lower = y_ref[1] % 2 == 0

        def place(array, cols, value):
            if group is None:
                grads_ref[array, :, cols] = value
                return
            blocks = value.reshape(model // (2 * group), 2, group, value.shape[1])
            first, second = blocks[:, 0], blocks[:, 1]
            for k, (one, other) in enumerate(((first, second), (second, first))):
                picked_rows = jnp.where(lower, one, other).reshape(model // 2, value.shape[1])
                grads_ref[array, k * (model // 2) : (k + 1) * (model // 2), cols] = picked_rows

        for array in range(2):

            def one(i, carry, array=array):
                grad = jnp.concatenate([all_ref[k, 3 * array + i] for k in range(pairs)], axis=1)
                at = pl.multiple_of(width * i, 128)
                place(array, pl.ds(at, width), mm(turned_ref[...], grad, NN))
                return carry

            lax.fori_loop(0, 3, one, 0)
            wide = 3 * width
            if array:
                place(array, slice(wide, wide + 256), extra)
                wide += 256
            if group is None:
                leave(grads_ref.at[array, :, :wide], grads_hbm[array])
            else:
                for k in (1, 0):
                    rows = slice(k * (model // 2), (k + 1) * (model // 2))
                    leave(grads_ref.at[array, rows, :wide], grads_hbm[2 * array + k])
        for copy in leaving:
            copy.wait()


def attend_back(
    y, q2, extra, k2, v, o, own, got, live, kind, columns, pick, wq, wk, wv, turned, first, chunks, group
):
    length, width = v.shape
    half, model = first.shape
    pairs = width // (2 * HD)
    head = pl.BlockSpec((length, 2 * HD), lambda p, h, *_: (0, 2 * p + h))
    pair = pl.BlockSpec((length, 2 * HD), lambda p, h, *_: (0, p))
    part = pl.BlockSpec((half, 2 * HD), lambda p, h, *_: (0, p))
    anywhere = pl.BlockSpec(memory_space=pl.ANY)
    shapes = [struct((rows, model), F32) for rows in chunks]
    for wide in (3 * width, 3 * width + 256):
        shapes += [struct((model, wide), F32)] if group is None else [struct((model // 2, wide), F32)] * 2
    return pl.pallas_call(
        functools.partial(attend_back_kernel, len(chunks), group),
        grid_spec=pltpu.PrefetchScalarGridSpec(
            num_scalar_prefetch=1,
            grid=(pairs, 2),
            in_specs=[
                head, head, head, pair, pair, part, part, whole_block((length, 1)), whole_block((length, 1)),
                whole_block(columns.shape), whole_block(pick.shape),
                *[anywhere] * 5,
            ],
            out_specs=[anywhere] * len(shapes),
            scratch_shapes=[
                *[pltpu.VMEM((2, length, 2 * HD), F32)] * 3,
                pltpu.VMEM((length, 2 * HD), F32),
                pltpu.VMEM((length, 2 * HD), BF16),
                pltpu.VMEM((pairs, 6, length, 2 * HD), BF16),
                pltpu.VMEM((pairs, 8, 2 * HD), F32),
                pltpu.VMEM((model, 6 * width), BF16),
                pltpu.VMEM((model, length), BF16),
                pltpu.VMEM((half, model), F32),
                pltpu.VMEM((length, model), F32),
                pltpu.VMEM((2, model, 3 * width + 256), F32),
                pltpu.SemaphoreType.DMA((8,)),
                pltpu.SemaphoreType.DMA((len(shapes),)),
            ],
        ),
        out_shape=shapes,
        compiler_params=params(63),
        cost_estimate=cost(20 * length * length * width, 40 * length * width, length * length * width // HD),
        name="attend_back",
    )(y, q2, extra, k2, v, o, own, got, live, kind, columns, pick, wq, wk, wv, turned, first)


def normalise(value):
    centre = value - jnp.mean(value, axis=-1, keepdims=True)
    inverse = lax.rsqrt(jnp.mean(centre * centre, axis=-1, keepdims=True) + NORM_EPS)
    return centre * inverse, inverse


def normalise_back(scaled, normal, inverse):
    return inverse * (
        scaled
        - jnp.mean(scaled, axis=-1, keepdims=True)
        - normal * jnp.mean(scaled * normal, axis=-1, keepdims=True)
    )


def gelu_pair(values):
    cumulative = 0.5 * (1.0 + lax.erf(values * (1.0 / math.sqrt(2.0))))
    density = jnp.exp(-0.5 * values * values) * (1.0 / math.sqrt(2.0 * math.pi))
    return values * cumulative, cumulative + values * density


def column_sum(value):
    return jnp.sum(value, axis=0, keepdims=True)


def first_cut(half):
    return half // 2


def middle_sizes(wi, wo, early):
    hidden, model, width = wi.shape[1], wo.shape[1], wo.shape[0]
    cut = [width // SLICES, (width + model) // SLICES, (width + 2 * model) // SLICES]
    return hidden, hidden // 2, model, width, cut


def far_block(ref, a, b):
    return ref[:, a:b, :].reshape(SLICES * (b - a), ref.shape[2])


def far_outer(ref, part, half):
    per = SLICES // 2
    return ref[per * (part - 2) : per * (part - 1), :, :].reshape(half, ref.shape[2])


def by_core(lower, values):
    first, second = (value.astype(F32) for value in values)
    keep = jnp.where(lower, first, second).astype(BF16)
    return keep, jnp.where(lower, second, first)


def forward_kernel(at_ref, x_ref, cot_ref, live_ref, own_ref, got_ref, wo_ref, wi_hbm, wu_hbm, *rest):
    arrived = rest[:SLICES]
    arrived_late = rest[SLICES : 2 * SLICES]
    (
        vec_ref, bias_ref, out_ref, out_first_ref, out_late_ref, low_ref, d_low_ref, keep_ref, send_ref,
        slope_ref, n1_ref, inv1_ref, d_second_ref, sums_ref, early_hbm, late_hbm,
        early_ref, late_ref, wi_ref, wu_ref, raw_ref, raw_late_ref, in_sem, out_sem,
    ) = rest[2 * SLICES :]
    step = pl.program_id(0)
    me = at_ref[1]
    lower = me % 2 == 0
    hidden, half, model, width, cut = middle_sizes(wi_hbm, wo_ref, early_ref)

    def weight_copies():
        stages = [[], [], [], [], []]
        for k in range(SLICES):
            for stage, source, target in (
                (0, arrived[k].at[: cut[0], :], raw_ref.at[k, : cut[0], :]),
                (2, arrived[k].at[cut[0] :, :], raw_ref.at[k, cut[0] :, :]),
                (4, arrived_late[k], raw_late_ref.at[k]),
            ):
                stages[stage].append(pltpu.make_async_copy(source, target, in_sem.at[stage * SLICES + k]))
        stages[1].append(pltpu.make_async_copy(wi_hbm, wi_ref, in_sem.at[SLICES]))
        stages[3].append(pltpu.make_async_copy(wu_hbm, wu_ref, in_sem.at[3 * SLICES]))
        return stages

    def leaving():
        return [
            pltpu.make_async_copy(early_ref, early_hbm, out_sem.at[0]),
            pltpu.make_async_copy(late_ref, late_hbm, out_sem.at[1]),
        ]

    def arrive(*wanted):
        @pl.when(step == 0)
        def _():
            stages = weight_copies()
            for stage in wanted:
                for copy in stages[stage]:
                    copy.wait()
            for k in range(SLICES):
                if 0 in wanted:
                    early_ref[me ^ k, : cut[0], :] = raw_ref[k, : cut[0], :].astype(BF16)
                if 2 in wanted:
                    early_ref[me ^ k, cut[0] :, :] = raw_ref[k, cut[0] :, :].astype(BF16)
                if 4 in wanted:
                    late_ref[me ^ k] = raw_late_ref[k].astype(BF16)
            if 4 in wanted:
                for copy in leaving():
                    copy.start()

    @pl.when(step == 0)
    def _():
        for stage in weight_copies():
            for copy in stage:
                copy.start()

    arrive(0)
    vec = [vec_ref[k : k + 1, :] for k in range(6)]
    got = got_ref[...].astype(BF16)
    own = own_ref[...]
    first = mm(own, wo_ref[...], NN) + mm(got, far_block(early_ref, 0, cut[0]), NN) + vec[0] + x_ref[...].astype(F32)
    n1, inv1 = normalise(first)
    n1_ref[...] = n1
    inv1_ref[...] = inv1
    normed = n1 * vec[1] + vec[2]
    low = normed.astype(BF16)
    low_ref[...] = low
    at_low = model + hidden
    send_ref[:, at_low : at_low + model] = low.astype(F32)
    _, send = by_core(lower, (own, got))
    send_ref[:, at_low + model :] = send
    second = vec[3] + normed
    arrive(1, 3)
    for far in range(2):
        if far:
            arrive(2, 4)
        pair = []
        for part in (2 * far, 2 * far + 1):
            inner = wi_ref[:, half * part : half * (part + 1)] if part < 2 else far_block(early_ref, cut[part - 2], cut[part - 1])
            pre = mm(low, inner, NN) + bias_ref[part : part + 1, :]
            active, slope = gelu_pair(pre)
            active = active.astype(BF16)
            slope_ref[:, half * part : half * (part + 1)] = slope.astype(BF16)
            pair.append(active)
            outer = wu_ref[half * part : half * (part + 1), :] if part < 2 else far_outer(late_ref, part, half)
            second = second + mm(active, outer, NN)
        keep, send = by_core(lower, pair)
        keep_ref[:, half * far : half * (far + 1)] = keep
        send_ref[:, model + half * far : model + half * (far + 1)] = send
    n2, inv2 = normalise(second)
    live = live_ref[...] > 0.5
    result = jnp.where(live, n2 * vec[4] + vec[5], 0.0).astype(BF16)
    out_ref[...] = result
    out_first_ref[...] = result[:, : model // 2].astype(F32)
    out_late_ref[...] = result[:, model // 2 :].astype(F32)
    dz = jnp.where(live, cot_ref[...].astype(F32), 0.0)
    d_second = normalise_back(dz * vec[4], n2, inv2)
    d_second_ref[...] = d_second
    d_low = d_second.astype(BF16)
    d_low_ref[...] = d_low
    send_ref[:, :model] = d_low.astype(F32)
    sums = jnp.concatenate(
        [column_sum(d_second), column_sum(dz * n2), column_sum(dz), jnp.zeros((5, model), F32)], axis=0
    )

    @pl.when(step == 0)
    def _():
        sums_ref[...] = sums

    @pl.when(step != 0)
    def _():
        sums_ref[...] += sums

    @pl.when(step == pl.num_programs(0) - 1)
    def _():
        for copy in leaving():
            copy.wait()


def forward(at, x, cot, live, context, got, wo, wi, wu, early, late, vec, bias, rows=256):
    half, width = got.shape
    model, hidden = wi.shape
    rows = min(rows, half)
    steps = half // rows
    mine = lambda w: pl.BlockSpec((rows, w), lambda i, s: (i + s[0] * steps, 0))
    tile = lambda w: pl.BlockSpec((rows, w), lambda i, s: (i, 0))
    anywhere = pl.BlockSpec(memory_space=pl.ANY)
    widths = (
        (model, BF16), (model // 2, F32), (model // 2, F32), (model, BF16), (model, BF16), (hidden, BF16),
        (2 * model + hidden + width, F32), (2 * hidden, BF16), (model, F32), (1, F32), (model, F32),
    )
    far_shapes = [(SLICES, *early[0].shape), (SLICES, *late[0].shape)]
    return pl.pallas_call(
        forward_kernel,
        grid_spec=pltpu.PrefetchScalarGridSpec(
            num_scalar_prefetch=1,
            grid=(steps,),
            in_specs=[
                mine(model), mine(model), mine(1), mine(width), tile(width),
                whole_block(wo.shape), *[anywhere] * (2 + 2 * SLICES),
                whole_block(vec.shape), whole_block(bias.shape),
            ],
            out_specs=[
                *(tile(w) for w, _ in widths), pl.BlockSpec((8, model), lambda i, s: (0, 0)), anywhere, anywhere,
            ],
            scratch_shapes=[
                *(pltpu.VMEM(shape, BF16) for shape in far_shapes),
                pltpu.VMEM(wi.shape, BF16),
                pltpu.VMEM(wu.shape, BF16),
                *(pltpu.VMEM(shape, F32) for shape in far_shapes),
                pltpu.SemaphoreType.DMA((5 * SLICES,)),
                pltpu.SemaphoreType.DMA((2,)),
            ],
        ),
        out_shape=[
            *(struct((half, w), kind) for w, kind in widths), struct((8, model), F32),
            *(struct(shape, BF16) for shape in far_shapes),
        ],
        compiler_params=params(63),
        cost_estimate=cost(8 * half * model * hidden, 24 * model * hidden, 4 * half * hidden),
        name="forward",
    )(at, x, cot, live, context, got, wo, wi, wu, *early, *late, vec, bias)


def backward_kernel(
    at_ref, slope_ref, n1_ref, inv1_ref, d_second_ref, d_low_ref, own_ref, got_ref, wo_ref, vec_ref,
    wi_hbm, wu_hbm, early_hbm, late_hbm,
    first_ref, dco_ref, dcf_ref, d_attn_ref, keep0_ref, keep1_ref, send_ref, sums_ref, inner_sums_ref,
    wi_ref, wu_ref, early_ref, late_ref, in_sem,
):
    step = pl.program_id(0)
    lower = at_ref[1] % 2 == 0
    hidden, half, model, width, cut = middle_sizes(wi_hbm, wo_ref, early_ref)
    ca = first_cut(half)

    def copies():
        pairs = ((wu_hbm, wu_ref), (wi_hbm, wi_ref), (late_hbm, late_ref), (early_hbm, early_ref))
        return [pltpu.make_async_copy(*pair, in_sem.at[k]) for k, pair in enumerate(pairs)]

    @pl.when(step == 0)
    def _():
        for copy in copies():
            copy.start()

    d_low = d_low_ref[...]
    n1 = n1_ref[...]
    d_normed = d_second_ref[...]
    inner_sums = []
    for far in range(2):

        @pl.when(step == 0)
        def _():
            for copy in copies()[2 * far : 2 * far + 2]:
                copy.wait()

        pair = []
        for part in (2 * far, 2 * far + 1):
            outer = wu_ref[half * part : half * (part + 1), :] if part < 2 else far_outer(late_ref, part, half)
            inner = wi_ref[:, half * part : half * (part + 1)] if part < 2 else far_block(early_ref, cut[part - 2], cut[part - 1])
            d_hidden = mm(d_low, outer, NT)
            d_inner = (d_hidden * slope_ref[:, half * part : half * (part + 1)].astype(F32)).astype(BF16)
            pair.append(d_inner)
            inner_sums.append(column_sum(d_inner.astype(F32)))
            d_normed = d_normed + mm(d_inner, inner, NT)
        keep, send = by_core(lower, pair)
        da = half - ca
        keep0_ref[:, ca * far : ca * (far + 1)] = keep[:, :ca]
        keep1_ref[:, da * far : da * (far + 1)] = keep[:, ca:]
        send_ref[:, ca * far : ca * (far + 1)] = send[:, :ca]
        send_ref[:, 2 * ca + da * far : 2 * ca + da * (far + 1)] = send[:, ca:]
    d_first = normalise_back(d_normed * vec_ref[1:2, :], n1, inv1_ref[...])
    first_ref[...] = d_first
    d_attn = d_first.astype(BF16)
    d_attn_ref[...] = d_attn
    send_ref[:, hidden:] = d_attn.astype(F32)
    dco_ref[...] = mm(d_attn, wo_ref[...], NT).astype(BF16).astype(F32)
    dcf_ref[...] = mm(d_attn, far_block(early_ref, 0, cut[0]), NT).astype(BF16).astype(F32)
    keep, _ = by_core(lower, (own_ref[...], got_ref[...]))
    keep0_ref[:, 2 * ca :] = keep
    sums = jnp.concatenate(
        [column_sum(d_first), column_sum(d_normed * n1), column_sum(d_normed), jnp.zeros((5, model), F32)], axis=0
    )
    inner_sums = jnp.concatenate([*inner_sums, jnp.zeros((4, half), F32)], axis=0)

    @pl.when(step == 0)
    def _():
        sums_ref[...] = sums
        inner_sums_ref[...] = inner_sums

    @pl.when(step != 0)
    def _():
        sums_ref[...] += sums
        inner_sums_ref[...] += inner_sums


def backward(at, slope, n1, inv1, d_second, d_low, context, got, wo, vec, wi, wu, early, late, rows=256):
    half, width = got.shape
    model, hidden = wi.shape
    rows = min(rows, half)
    steps = half // rows
    ca = first_cut(hidden // 2)
    mine = lambda w: pl.BlockSpec((rows, w), lambda i, s: (i + s[0] * steps, 0))
    tile = lambda w: pl.BlockSpec((rows, w), lambda i, s: (i, 0))
    anywhere = pl.BlockSpec(memory_space=pl.ANY)
    widths = (
        (model, F32), (width, F32), (width, F32), (model, BF16), (2 * ca + width, BF16), (hidden - 2 * ca, BF16),
        (hidden + model, F32),
    )
    return pl.pallas_call(
        backward_kernel,
        grid_spec=pltpu.PrefetchScalarGridSpec(
            num_scalar_prefetch=1,
            grid=(steps,),
            in_specs=[
                tile(2 * hidden), tile(model), tile(1), tile(model), tile(model), mine(width), tile(width),
                whole_block(wo.shape), whole_block(vec.shape), *[anywhere] * 4,
            ],
            out_specs=[
                *(tile(w) for w, _ in widths),
                pl.BlockSpec((8, model), lambda i, s: (0, 0)),
                pl.BlockSpec((8, hidden // 2), lambda i, s: (0, 0)),
            ],
            scratch_shapes=[
                *(pltpu.VMEM(a.shape, BF16) for a in (wi, wu, early, late)),
                pltpu.SemaphoreType.DMA((4,)),
            ],
        ),
        out_shape=[
            *(struct((half, w), kind) for w, kind in widths), struct((8, model), F32), struct((8, hidden // 2), F32),
        ],
        compiler_params=params(63),
        cost_estimate=cost(8 * half * model * hidden, 24 * model * hidden),
        name="backward",
    )(at, slope, n1, inv1, d_second, d_low, context, got, wo, vec, wi, wu, early, late)


def weight_kernel(plan, count, kinds, bit_ref, *rest):
    groups = len(plan)
    left_hbm, rest = rest[:kinds], rest[kinds:]
    keep_hbm, rest = rest[:groups], rest[groups:]
    got_hbm, rest = rest[:count], rest[count:]
    outs, rest = rest[: 2 * groups], rest[2 * groups :]
    left_ref, left_got_ref, rest = rest[0], rest[1], rest[2:]
    keep_refs, rest = rest[:groups], rest[groups:]
    got_refs, rest = rest[:groups], rest[groups:]
    stage_refs, (in_sem, out_sem) = rest[:groups], rest[groups:]
    model = left_ref.shape[2]

    arriving, ready = [], {}

    def bring(key, source, target):
        if key not in ready:
            ready[key] = pltpu.make_async_copy(source, target, in_sem.at[len(arriving)])
            ready[key].start()
            arriving.append(key)

    for g, (_, _, tiles) in enumerate(plan):
        for index, (left_array, left_at), (right_array, right_at), a, b in tiles:
            bring(("left", index), left_hbm[index], left_ref.at[index])
            if ("left got", index) not in ready:
                columns = slice(left_at, left_at + model)
                bring(("left got", index), got_hbm[left_array].at[:, columns], left_got_ref.at[index])
            bring(("keep", g, a), keep_hbm[g].at[:, a:b], keep_refs[g].at[:, a:b])
            columns = slice(right_at, right_at + b - a)
            bring(("got", g, a), got_hbm[right_array].at[:, columns], got_refs[g].at[:, a:b])
    waited = set()

    def need(*keys):
        for key in keys:
            if key not in waited:
                waited.add(key)
                ready[key].wait()

    leaving = []
    for g, (slot, group, tiles) in enumerate(plan):
        width = keep_refs[g].shape[1]
        for index, _, _, a, b in tiles:
            need(("left", index), ("left got", index), ("keep", g, a), ("got", g, a))
            left = jnp.concatenate([left_ref[index], left_got_ref[index].astype(BF16)], axis=0)
            right = jnp.concatenate([keep_refs[g][:, a:b], got_refs[g][:, a:b].astype(BF16)], axis=0)
            value = mm(left, right, TN)
            if slot is None:
                part, base = (0, 0) if 2 * b <= width else (1, width // 2)
                stage_refs[g][part, :, a - base : b - base] = value
                parts = ((part, a - base, b - base),)
            else:
                pairs = value.reshape(model // (2 * group), 2, group, b - a)
                kept = bit_ref[slot] == 0
                first, second = pairs[:, 0], pairs[:, 1]
                for part, (one, other) in enumerate(((first, second), (second, first))):
                    picked = jnp.where(kept, one, other)
                    stage_refs[g][part, :, a:b] = picked.reshape(model // 2, b - a)
                parts = ((1, a, b), (0, a, b))
            for part, a, b in parts:
                copy = pltpu.make_async_copy(
                    stage_refs[g].at[part, :, a:b], outs[2 * g + part].at[:, a:b], out_sem.at[len(leaving)]
                )
                copy.start()
                leaving.append(copy)
    for copy in leaving:
        copy.wait()


def weight_grads(at, lefts, keeps, received, plan):
    depth, model = lefts[0].shape
    stages, shapes, steps = [], [], 0
    for (slot, _, tiles), keep in zip(plan, keeps):
        width = keep.shape[1]
        shape = (model, width // 2) if slot is None else (model // 2, width)
        stages.append(pltpu.VMEM((2, *shape), F32))
        shapes += [struct(shape, F32)] * 2
        steps += len(tiles)
    columns = sum(keep.shape[1] for keep in keeps)
    anywhere = pl.BlockSpec(memory_space=pl.ANY)
    return pl.pallas_call(
        functools.partial(weight_kernel, plan, len(received), len(lefts)),
        grid_spec=pltpu.PrefetchScalarGridSpec(
            num_scalar_prefetch=1,
            grid=(1,),
            in_specs=[anywhere] * (len(lefts) + len(keeps) + len(received)),
            out_specs=[anywhere] * len(shapes),
            scratch_shapes=[
                pltpu.VMEM((len(lefts), depth, model), BF16),
                pltpu.VMEM((len(lefts), depth, model), F32),
                *(pltpu.VMEM(keep.shape, BF16) for keep in keeps),
                *(pltpu.VMEM(keep.shape, F32) for keep in keeps),
                *stages,
                pltpu.SemaphoreType.DMA((2 * len(lefts) + 2 * steps,)),
                pltpu.SemaphoreType.DMA((2 * steps,)),
            ],
        ),
        out_shape=shapes,
        compiler_params=params(63),
        cost_estimate=cost(4 * depth * model * columns, 4 * model * columns + 8 * depth * columns),
        name="weight_grads",
    )(at, *lefts, *keeps, *received)


def combine_kernel(plan, count, bits_ref, *rest):
    outs = len(plan)
    arrays, targets = rest[:count], rest[count : count + outs]
    buffers, (in_sem, out_sem) = rest[count + outs : -2], rest[-2:]
    copies = []
    for pieces in plan:
        for _, terms in pieces:
            for array, chosen, a, b, _ in terms:
                index = [slice(None)] * len(arrays[array].shape)
                for axis, (bit, mine) in chosen:
                    index[axis] = pl.ds(bits_ref[bit] if mine else 1 - bits_ref[bit], 1)
                index[-1] = slice(a, b)
                k = len(copies)
                copies.append(pltpu.make_async_copy(arrays[array].at[tuple(index)], buffers[k], in_sem.at[k]))
    for copy in copies:
        copy.start()
    k = 0
    leaving = []
    for target, pieces in zip(targets, plan):
        for at, terms in pieces:
            first = k
            total = None
            for *_, gate in terms:
                copies[k].wait()
                value = buffers[k][...]
                if gate is not None:
                    value = jnp.where(bits_ref[0] == gate, value, 0.0)
                total = value if total is None else total + value
                k += 1
            if len(terms) > 1:
                buffers[first][...] = total
            width = buffers[first].shape[-1]
            index = (*[slice(None)] * (len(target.shape) - 1), slice(at, at + width))
            copy = pltpu.make_async_copy(buffers[first], target.at[index], out_sem.at[len(leaving)])
            copy.start()
            leaving.append(copy)
    for copy in leaving:
        copy.wait()


def combine(bit_values, outputs):
    arrays, plan, shapes, buffers, moved = [], [], [], [], 0
    for pieces in outputs:
        at, planned = 0, []
        for terms in pieces:
            named = []
            for array, chosen, a, b, gate in terms:
                place = [k for k, other in enumerate(arrays) if other is array]
                if not place:
                    place = [len(arrays)]
                    arrays.append(array)
                named.append((place[0], tuple(sorted(chosen.items())), a, b, gate))
                block = tuple(1 if k in chosen else size for k, size in enumerate(array.shape[:-1]))
                buffers.append(pltpu.VMEM((*block, b - a), F32))
                moved += 4 * math.prod(block) * (b - a)
            planned.append((at, named))
            at += b - a
        plan.append(planned)
        shapes.append(struct((*block, at), F32))
    anywhere = pl.BlockSpec(memory_space=pl.ANY)
    pieces = sum(len(planned) for planned in plan)
    return pl.pallas_call(
        functools.partial(combine_kernel, plan, len(arrays)),
        grid_spec=pltpu.PrefetchScalarGridSpec(
            num_scalar_prefetch=1,
            grid=(1,),
            in_specs=[anywhere] * len(arrays),
            out_specs=[anywhere] * len(shapes),
            scratch_shapes=[
                *buffers,
                pltpu.SemaphoreType.DMA((len(buffers),)),
                pltpu.SemaphoreType.DMA((pieces,)),
            ],
        ),
        out_shape=shapes,
        compiler_params=params(63),
        cost_estimate=cost(moved, 2 * moved),
        name="combine",
    )(bit_values, *arrays)


def turn_kernel(value_ref, out_ref):
    out_ref[...] = value_ref[...].astype(F32).T.astype(BF16)


def turn(value, columns=256):
    length, model = value.shape
    return pl.pallas_call(
        turn_kernel,
        grid=(model // columns,),
        in_specs=[pl.BlockSpec((length, columns), lambda i: (0, i))],
        out_specs=pl.BlockSpec((columns, length), lambda i: (i, 0)),
        out_shape=struct((model, length), BF16),
        compiler_params=params(63),
        cost_estimate=cost(length * model, 4 * length * model),
        name="turn",
    )(value)


def place_kernel(steps, y_ref, own_ref, first_ref, second_ref, out_ref):
    mine = pl.program_id(0) // steps == y_ref[0]
    got = jnp.concatenate([first_ref[...], second_ref[...]], axis=1)
    out_ref[...] = jnp.where(mine, own_ref[...].astype(F32), got).astype(BF16)


def place_rows(y, own, first, second):
    half, model = own.shape
    rows = min(128, half)
    steps = half // rows
    tile = lambda w: pl.BlockSpec((rows, w), lambda i, s: (i % steps, 0))
    return pl.pallas_call(
        functools.partial(place_kernel, steps),
        grid_spec=pltpu.PrefetchScalarGridSpec(
            num_scalar_prefetch=1,
            grid=(2 * steps,),
            in_specs=[tile(model), tile(model // 2), tile(model // 2)],
            out_specs=pl.BlockSpec((rows, model), lambda i, s: (i, 0)),
        ),
        out_shape=struct((2 * half, model), BF16),
        compiler_params=params(63),
        cost_estimate=cost(half * model, 12 * half * model),
        name="place_rows",
    )(y, own, first, second)


def per_device(
    devices,
    tokens,
    lengths,
    entity_flags,
    query_weight,
    query_bias,
    key_weight,
    key_bias,
    value_weight,
    value_bias,
    output_weight,
    output_bias,
    attn_gain,
    attn_shift,
    inner_weight,
    inner_bias,
    outer_weight,
    outer_bias,
    final_gain,
    final_shift,
    cotangent,
):
    x = tokens[0]
    length, model = x.shape
    width = key_weight.shape[1]
    hidden = inner_weight.shape[1]
    half = length // 2
    bits = devices.bit_length() - 1
    y = lax.axis_index("tensor")
    d = lax.axis_index("dp")

    def swap(value, mask):
        return lax.ppermute(value, "dp", [(i, i ^ mask) for i in range(devices)])

    def cross(value):
        return lax.ppermute(value, "tensor", [(0, 1), (1, 0)])

    me = d % SLICES
    core = d % 2
    rows = model // devices
    near_mask, far_mask = 192 // rows, 96 // rows
    at = jnp.stack([y, me, (d // near_mask) % 2, (d // far_mask) % 2]).astype(jnp.int32)
    tie = lax.optimization_barrier

    def cut(array, index):
        size = array.shape[0] // SLICES
        return lax.dynamic_slice_in_dim(array, index * size, size, 0)

    def pack(index):
        wide = cut(inner_weight, index)
        early = jnp.concatenate([cut(output_weight, index), wide[:, :model], wide[:, model:]], axis=0)
        return early.astype(F32)

    def pack_late(index):
        return cut(outer_weight, index).astype(F32)

    live = (lax.broadcasted_iota(jnp.int32, (length, 1), 0) < lengths[0]).astype(F32)
    kind = (entity_flags[0] == 1).astype(F32).reshape(length, 1)

    e0 = cross(pack(me))
    far_bias = cross(inner_bias)
    q2, k2, v = project(
        x, kind, query_weight, query_bias, key_weight, key_bias, value_weight, value_bias
    )
    e0, far_bias, l0, l6, q2 = tie((e0, far_bias, pack_late(me), pack_late(me ^ 6), q2))
    e2 = swap(e0, 2)
    e4 = swap(e0, 4)
    l0 = cross(l0)
    e1 = swap(e0, 1)
    context, extra = attend(q2, k2, v, live)
    sent = lax.dynamic_slice_in_dim(context, half * (1 - y), half, 0).astype(F32)
    e1, e2, e4, l0, l6, sent = tie((e1, e2, e4, l0, l6, sent))
    l2 = swap(l0, 2)
    l4 = swap(l0, 4)
    got = cross(sent)
    e6 = swap(e4, 2)
    l6 = cross(l6)
    per = width // devices
    where_row = lax.broadcasted_iota(jnp.int32, (model, width), 0)
    where_bias = lax.broadcasted_iota(jnp.int32, (model, width), 1)
    pick = (where_row == (where_bias // per) * rows + where_bias % per).astype(BF16)
    x_turned = turn(x)
    l2, l4, e2, e4, pick, x_turned = tie((l2, l4, e2, e4, pick, x_turned))
    e3 = swap(e2, 1)
    e5 = swap(e4, 1)
    got, e6, l6, e3, e5, l0, l2, l4 = tie((got, e6, l6, e3, e5, l0, l2, l4))
    l1 = swap(l0, 1)
    l3 = swap(l2, 1)
    l5 = swap(l4, 1)
    l7 = swap(l6, 1)
    e7 = swap(e6, 1)
    early = (e0, e1, e2, e3, e4, e5, e6, e7)
    late = (l0, l1, l2, l3, l4, l5, l6, l7)

    vec = jnp.stack(
        [output_bias, attn_gain, attn_shift, outer_bias, final_gain, final_shift, outer_bias, outer_bias]
    )
    bias = jnp.concatenate([inner_bias, far_bias, inner_bias, far_bias]).reshape(8, hidden // 2)
    ca, cb = first_cut(hidden // 2), hidden // 2
    da, db = hidden // 2 - ca, 0
    (
        out_rows, out_first, out_late, low, d_low, keep2, early_send, slope, n1, inv1, d_second, late_sums,
        far_early, far_late,
    ) = forward(
        at, x, cotangent[0], live, context, got, output_weight, inner_weight, outer_weight,
        early, late, vec, bias,
    )
    early_got = swap(early_send, 1)
    got_first = cross(out_first)
    d_first, dco, dcf, d_attn, keep0, keep1, late_send, first_sums, inner_sums = backward(
        at, slope, n1, inv1, d_second, d_low, context, got, output_weight, vec, inner_weight, outer_weight,
        far_early, far_late,
    )
    inner_columns = inner_sums[:4].reshape(2, model, 2)
    shared = [first_sums[:3].T, late_sums[:3].T]
    columns = jnp.concatenate([*shared, inner_columns[0], *shared, inner_columns[1]], axis=1)
    early_got, got_first, late_send, dcf, columns = tie((early_got, got_first, late_send, dcf, columns))
    late_got = swap(late_send, 1)
    d_got = cross(dcf)

    low_at, d_attn_at = (0, 2 * cb + model), (1, hidden)
    g2_keep, g2_send = weight_grads(
        at, (d_low,), (keep2,), (early_got,),
        (
            (
                3, far_mask * rows,
                ((0, (0, 0), (0, model), 0, cb), (0, (0, 0), (0, model + cb), cb, 2 * cb)),
            ),
        ),
    )
    g0_keep, g0_send, g1_keep, g1_send = weight_grads(
        at, (low, d_attn), (keep0, keep1), (early_got, late_got),
        (
            (
                2, near_mask * rows,
                (
                    (0, low_at, (1, 0), 0, ca), (0, low_at, (1, ca), ca, 2 * ca),
                    (1, d_attn_at, (0, 2 * model + hidden), 2 * ca, 2 * ca + width),
                ),
            ),
            (
                None, None,
                ((0, low_at, (1, 2 * ca), 0, da), (0, low_at, (1, 2 * ca + da), da, 2 * da)),
            ),
        ),
    )
    g0_send, g1_send, d_got = tie((g0_send, g1_send, d_got))
    g0_got = swap(g0_send, near_mask)
    g2_got = swap(g2_send, far_mask)
    g1_got = cross(g1_send)

    g0_send, g1_send, g2_send, dco, d_got = tie((g0_send, g1_send, g2_send, dco, d_got))
    chunks = tuple(length * k // 32 for k in (7, 16, 9))
    group = rows if rows % 8 == 0 else None
    results = attend_back(
        at, q2, extra, k2, v, context, dco, d_got, live, kind, columns, pick,
        query_weight, key_weight, value_weight, x_turned, d_first, chunks, group,
    )
    parts, products = results[: len(chunks)], results[len(chunks) :]
    got_out = cross(out_late)

    def spread(array, done):
        dims = [1 if (1 << (bits - 1 - k)) in done else 2 for k in range(bits)]
        return array.reshape(*dims, rows, array.shape[-1])

    bit_values = jnp.stack([(d >> k) % 2 for k in range(bits)]).astype(jnp.int32)
    rest_masks = [1 << k for k in range(1, bits) if (1 << k) not in (near_mask, far_mask)]

    def term(array, *done):
        array = spread(array, done)
        return (array, {}, 0, array.shape[-1], None)

    def half_of(terms, mask, mine):
        k = mask.bit_length() - 1
        return [(array, {**chosen, bits - 1 - k: (k, mine)}, a, b, gate) for array, chosen, a, b, gate in terms]

    def kept(terms, mask):
        return half_of(terms, mask, True)

    def other(terms, mask):
        return half_of(terms, mask, False)

    def columns_of(terms, first, last):
        return [(array, chosen, a + first, a + last, gate) for array, chosen, a, _, gate in terms]

    def on_core(terms, core_index):
        return [(array, chosen, a, b, core_index) for array, chosen, a, b, _ in terms]

    def whole_of(array):
        return (array, {}, 0, array.shape[-1], None)

    def part_of(array, a, b):
        return (array, {}, a, b, None)

    g0_got, g1_got, g2_got, got_out, parts, products = tie((g0_got, g1_got, g2_got, got_out, parts, products))
    if group is None:
        c = [term(products[0])]
        e = [term(products[1])]
        c_send, e_send = combine(bit_values, [[other(c, 1)], [other(e, 1)]])
        c, e = kept(c, 1), kept(e, 1)
    else:
        c, e = [term(products[0], 1)], [term(products[2], 1)]
        c_send, e_send = spread(products[1], (1,)), spread(products[3], (1,))
    e_got = swap(e_send, 1)
    c_got = swap(c_send, 1)
    g0 = [term(g0_keep, near_mask), term(g0_got, near_mask)]
    g1 = [term(g1_keep), term(g1_got)]
    g2 = [term(g2_keep, far_mask), term(g2_got, far_mask)]
    sends = combine(bit_values, [[columns_of(g0, ca, 2 * ca + width)], [other(g1, near_mask)]])
    _, late_bits = tie((sends, bit_values))
    (g2_send,) = combine(late_bits, [[other(g2, near_mask)]])
    e_got, c_got, parts, _ = tie((e_got, c_got, parts, g2_send))
    e.append(whole_of(e_got))
    c.append(whole_of(c_got))
    g1_got = swap(sends[1], near_mask)
    g0_got = cross(sends[0])
    g2_got = swap(g2_send, near_mask)
    e_send, c_send = combine(bit_values, [[other(e, far_mask)], [other(c, near_mask)]])
    e_got = swap(e_send, far_mask)
    part0 = cross(parts[0])
    near_bit, near_axis = (d // near_mask) % 2, bits - near_mask.bit_length()
    for array, *_ in g1:
        g1_got = tie(g1_got + lax.dynamic_slice_in_dim(array, near_bit, 1, near_axis))
    g0_got, g1_sum = tie((g0_got, g1_got))
    t = [
        *on_core(columns_of(g0, 2 * ca, 2 * ca + width), 0),
        *on_core([part_of(g0_got, ca, ca + width)], 1),
    ]
    g0 = [*columns_of(g0, 0, ca), part_of(g0_got, 0, ca)]
    g1 = [whole_of(g1_sum)]

    (three_send,) = combine(bit_values, [[other(terms, far_mask) for terms in (g0, t, g1)]])
    three_got = swap(three_send, far_mask)
    e_got, _ = tie((e_got, three_send))
    e = [*kept(e, far_mask), whole_of(e_got)]
    (small_send,) = combine(bit_values, [[columns_of(e, 3 * width + 128, 3 * width + 256)]])
    small_got = cross(small_send)
    g2_got, part0, parts, small_got = tie((g2_got, part0, parts, small_got))
    g2 = [*kept(g2, near_mask), whole_of(g2_got)]
    (g2_send,) = combine(bit_values, [[columns_of(g2, cb, 2 * cb)]])
    g2_got = cross(g2_send)
    c_got = swap(c_send, near_mask)
    three_got, c_got, own0, part0 = tie((three_got, c_got, parts[0], part0))
    in0 = (own0 + part0).astype(BF16)
    three_got, g2_got, c_got, small_got, in0, parts = tie((three_got, g2_got, c_got, small_got, in0, parts))
    small = [*columns_of(e, 3 * width, 3 * width + 128), whole_of(small_got)]
    e = columns_of(e, 0, 3 * width)
    g0 = [*kept(g0, far_mask), part_of(three_got, 0, ca)]
    t = [*kept(t, far_mask), part_of(three_got, ca, ca + width)]
    g1 = [*kept(g1, far_mask), part_of(three_got, ca + width, three_got.shape[-1])]
    g2 = [*columns_of(g2, 0, cb), whole_of(g2_got)]
    c = [*kept(c, near_mask), whole_of(c_got)]

    main = (g0, g1, g2, t)
    sizes = (ca, da + db, cb, width)
    ends = [sum(sizes[:k]) for k in range(len(sizes) + 1)]
    mask = rest_masks[0]
    (main_send,) = combine(bit_values, [[other(terms, mask) for terms in main]])
    _, late_bits = tie((main_send, bit_values))
    sends = combine(late_bits, [[other(e, near_mask), other(small, near_mask)], [other(c, far_mask)]])
    got_z = swap(main_send, mask)
    in1 = (parts[1] + cross(parts[1])).astype(BF16)
    c_got = swap(sends[1], far_mask)
    e_got = swap(sends[0], near_mask)
    layer_out = place_rows(at, out_rows, got_first, got_out)
    got_z, e_got, c_got, in1, parts, layer_out = tie((got_z, e_got, c_got, in1, parts, layer_out))
    main = [[*kept(terms, mask), part_of(got_z, ends[n], ends[n + 1])] for n, terms in enumerate(main)]
    e = [*kept(e, near_mask), part_of(e_got, 0, 3 * width)]
    small = [*kept(small, near_mask), part_of(e_got, 3 * width, 3 * width + 128)]
    c = [*kept(c, far_mask), whole_of(c_got)]
    for mask in rest_masks[1:]:
        (send,) = combine(bit_values, [[other(terms, mask) for terms in main]])
        got_z = swap(send, mask)
        main = [[*kept(terms, mask), part_of(got_z, ends[n], ends[n + 1])] for n, terms in enumerate(main)]

    for k, mask in enumerate(rest_masks):
        (pair_send,) = combine(bit_values, [[other(c, mask), other(e, mask), other(small, mask)]])
        outputs = [[kept(c, mask), kept(e, mask), kept(small, mask)]]
        if k == 0:
            outputs += [[other(terms, 1) for terms in main], [kept(terms, 1) for terms in main]]
        _, late_bits = tie((pair_send, bit_values))
        sends = combine(late_bits, outputs)
        pair_got = swap(pair_send, mask)
        if k == 0:
            in2 = (parts[2] + cross(parts[2])).astype(BF16)
            got_last = swap(sends[1], 1)
            keep = sends[2]
        pair_keep = sends[0]
        wide = pair_keep.shape[-1]
        c = [part_of(pair_keep, 0, 3 * width), part_of(pair_got, 0, 3 * width)]
        e = [part_of(pair_keep, 3 * width, 6 * width), part_of(pair_got, 3 * width, 6 * width)]
        small = [part_of(pair_keep, 6 * width, wide), part_of(pair_got, 6 * width, wide)]

    input_grad = jnp.concatenate([in0, in1, in2], axis=0)
    got_last, keep, input_grad = tie((got_last, keep, input_grad))
    got_last = got_last.reshape(rows, -1)
    keep = keep.reshape(rows, -1)
    low_half = jnp.where(core == 0, keep, got_last)
    high_half = jnp.where(core == 0, got_last, keep)
    at2 = ca + da + db
    inner_half = lambda array: [array[:, : ca + da]]
    at3 = at2 + cb
    outer_half = lambda array: [array[:, at2:at3], array[:, ca + da : at2]]
    t = keep[:, at3:] + got_last[:, at3:]
    grad_inner = jnp.concatenate(inner_half(low_half) + inner_half(high_half), axis=1)
    grad_outer = jnp.concatenate(outer_half(low_half) + outer_half(high_half), axis=1).T
    grad_output = t.T
    pair_got, grad_inner, grad_outer, grad_output = tie((pair_got, grad_inner, grad_outer, grad_output))
    pair = (pair_keep + pair_got).reshape(rows, -1)
    c, e = pair[:, : 3 * width], pair[:, 3 * width :]
    small = e[:, 3 * width + 6 : 3 * width + 12]
    inner_two = e[:, 3 * width + 12 : 3 * width + 14]

    piece = lambda array, k: array[:, width * k : width * (k + 1)]
    grad_query_weight = jnp.stack([piece(c, 0), piece(c, 1), piece(c, 2), piece(e, 0)])
    biases = e[:per, 3 * width : 3 * width + 6].T
    return (
        layer_out[None],
        input_grad[None],
        grad_query_weight,
        biases[:4],
        piece(e, 1),
        biases[4],
        piece(e, 2),
        biases[5],
        grad_output,
        small[:, 0],
        small[:, 1],
        small[:, 2],
        grad_inner,
        inner_two.reshape(2 * rows),
        grad_outer,
        small[:, 3],
        small[:, 4],
        small[:, 5],
    )


def solution(mesh):
    return jax.shard_map(
        functools.partial(per_device, mesh.shape["dp"]),
        mesh=mesh,
        in_specs=(
            P("dp", None, None),
            P("dp"),
            P("dp", None),
            P(None, None, "tensor"),
            P(None, "tensor"),
            P(None, "tensor"),
            P("tensor"),
            P(None, "tensor"),
            P("tensor"),
            P("tensor", None),
            P(),
            P(),
            P(),
            P(None, "tensor"),
            P("tensor"),
            P("tensor", None),
            P(),
            P(),
            P(),
            P("dp", None, None),
        ),
        out_specs=(
            P("dp", None, None),
            P("dp", None, None),
            P(None, "dp", "tensor"),
            P(None, ("tensor", "dp")),
            P("dp", "tensor"),
            P(("tensor", "dp")),
            P("dp", "tensor"),
            P(("tensor", "dp")),
            P("tensor", "dp"),
            P("dp"),
            P("dp"),
            P("dp"),
            P("dp", "tensor"),
            P(("tensor", "dp")),
            P("tensor", "dp"),
            P("dp"),
            P("dp"),
            P("dp"),
        ),
        check_vma=False,
    )
```

```python
import functools
import math

import jax
import jax.numpy as jnp
from jax import lax
from jax.experimental import pallas as pl
from jax.experimental.pallas import tpu as pltpu
from jax.sharding import PartitionSpec as P

HD = 64
SLICES = 8
MASKED = -1e30
NORM_EPS = 1e-05

F32 = jnp.float32
BF16 = jnp.bfloat16
NN = (((1,), (0,)), ((), ()))
NT = (((1,), (1,)), ((), ()))
TN = (((0,), (0,)), ((), ()))


def mm(left, right, dims):
    return lax.dot_general(left, right, dims, preferred_element_type=F32)


def struct(shape, kind):
    return jax.ShapeDtypeStruct(shape, kind)


def params(mib):
    return pltpu.CompilerParams(vmem_limit_bytes=mib << 20)


def cost(flops, moved, special=0):
    return pl.CostEstimate(flops=int(flops), bytes_accessed=int(moved), transcendentals=int(special))


def whole_block(shape):
    return pl.BlockSpec(shape, lambda *_: (0,) * len(shape), pipeline_mode=pl.Buffered(1))


def three_pieces(value):
    high = value.astype(BF16).astype(F32)
    rest = value - high
    middle = rest.astype(BF16).astype(F32)
    return high, middle, rest - middle


def project_kernel(x_ref, kind_ref, wq_ref, bq_ref, wk_ref, bk_ref, wv_ref, bv_ref, q2_ref, k2_ref, v_ref):
    x = x_ref[...]
    entity = kind_ref[...] > 0.5
    rows = x.shape[0]
    width = wk_ref.shape[1]

    weights = jnp.concatenate([*(wq_ref[c] for c in range(4)), wk_ref[...], wv_ref[...]], axis=1)
    biases = jnp.concatenate([*(bq_ref[c : c + 1, :] for c in range(4)), bk_ref[...], bv_ref[...]], axis=1)
    products = mm(x, weights, NN) + biases

    def query(c):
        return products[:, width * c : width * (c + 1)]

    scale = 1.0 / math.sqrt(HD)
    to_word = jnp.where(entity, query(2), query(0)).astype(BF16).astype(F32) * scale
    to_entity = jnp.where(entity, query(3), query(1)).astype(BF16).astype(F32) * scale
    keys = query(4).astype(BF16).astype(F32)
    v_ref[...] = query(5).astype(BF16)
    left = lax.broadcasted_iota(jnp.int32, (rows, 2 * HD), 1) < HD
    held = left != entity
    for p in range(width // (2 * HD)):
        cols = slice(2 * HD * p, 2 * HD * (p + 1))
        w, e, k = to_word[:, cols], to_entity[:, cols], keys[:, cols]
        w_roll, e_roll, k_roll = (pltpu.roll(t, HD, 1) for t in (w, e, k))
        even = slice(4 * HD * p, 4 * HD * p + 2 * HD)
        odd = slice(4 * HD * p + 2 * HD, 4 * HD * (p + 1))
        q2_ref[:, even] = jnp.where(left, w, e_roll).astype(BF16)
        q2_ref[:, odd] = jnp.where(left, w_roll, e).astype(BF16)
        k2_ref[:, even] = jnp.where(held, jnp.where(left, k, k_roll), 0.0).astype(BF16)
        k2_ref[:, odd] = jnp.where(held, jnp.where(left, k_roll, k), 0.0).astype(BF16)


def project(x, kind, wq, bq, wk, bk, wv, bv, rows=256):
    length, model = x.shape
    width = wk.shape[1]
    rows = min(rows, length)
    tile = lambda w: pl.BlockSpec((rows, w), lambda i: (i, 0))
    return pl.pallas_call(
        project_kernel,
        grid=(length // rows,),
        in_specs=[
            tile(model),
            tile(1),
            whole_block(wq.shape),
            whole_block(bq.shape),
            whole_block(wk.shape),
            whole_block((1, width)),
            whole_block(wv.shape),
            whole_block((1, width)),
        ],
        out_specs=[tile(2 * width), tile(2 * width), tile(width)],
        out_shape=[
            struct((length, 2 * width), BF16),
            struct((length, 2 * width), BF16),
            struct((length, width), BF16),
        ],
        compiler_params=params(63),
        cost_estimate=cost(12 * length * model * width, 16 * model * width + 12 * length * width),
        name="project",
    )(x, kind, wq, bq, wk, bk.reshape(1, width), wv, bv.reshape(1, width))


def key_extra(live, rows):
    lane = lax.broadcasted_iota(jnp.int32, (rows, 2 * HD), 1)
    return jnp.where(
        lane == 0, jnp.where(live, 0.0, MASKED), jnp.where(lane < 4, 1.0, 0.0)
    ).astype(BF16)


def attend_kernel(q2_ref, k2_ref, v_ref, live_ref, out_ref, extra_ref, turned_ref, both_ref):
    length = k2_ref.shape[0]
    h = pl.program_id(1)

    @pl.when(h == 0)
    def _():
        turned = v_ref[...].astype(F32).T.astype(BF16)
        turned_ref[0] = turned[:HD]
        turned_ref[1] = turned[HD:]

    lane = lax.broadcasted_iota(jnp.int32, (length, 2 * HD), 1)
    one = jnp.where(lane == 0, 1.0, 0.0).astype(BF16)
    keys = jnp.concatenate([k2_ref[...], key_extra(live_ref[...] > 0.5, length)], axis=1)
    query = jnp.concatenate([q2_ref[...], one], axis=1)
    scores = mm(keys, query, NT)
    top = jnp.max(scores, axis=0, keepdims=True)
    weights = jnp.exp(scores - top)
    norm = jnp.sum(weights, axis=0, keepdims=True)
    summed = mm(turned_ref[h], weights.astype(BF16), NN)
    both_ref[h] = summed * (1.0 / norm)
    pieces = three_pieces(-(top + jnp.log(norm)))
    filled = jnp.concatenate(
        [jnp.ones((1, length), F32), *pieces, jnp.zeros((2 * HD - 4, length), F32)], axis=0
    )
    extra_ref[...] = filled.T.astype(BF16)

    @pl.when(h == 1)
    def _():
        out_ref[...] = jnp.concatenate([both_ref[0], both_ref[1]], axis=0).T.astype(BF16)


def attend(q2, k2, v, live):
    length, width = v.shape
    head = pl.BlockSpec((length, 2 * HD), lambda p, h: (0, 2 * p + h))
    pair = pl.BlockSpec((length, 2 * HD), lambda p, h: (0, p))
    return pl.pallas_call(
        attend_kernel,
        grid=(width // (2 * HD), 2),
        in_specs=[head, head, pair, whole_block((length, 1))],
        out_specs=[pair, head],
        out_shape=[struct((length, width), BF16), struct((length, 2 * width), BF16)],
        scratch_shapes=[pltpu.VMEM((2, HD, length), BF16), pltpu.VMEM((2, HD, length), F32)],
        compiler_params=params(63),
        cost_estimate=cost(10 * length * length * width, 20 * length * width, length * length * width // HD),
        name="attend",
    )(q2, k2, v, live)


def attend_back_kernel(
    count, group, y_ref, q2_ref, extra_ref, k2_ref, v_ref, o_ref, own_ref, got_ref, live_ref, kind_ref, columns_ref, pick_ref,
    wq_hbm, wk_hbm, wv_hbm, turned_hbm, first_hbm, *rest,
):
    outs = count + (2 if group is None else 4)
    part_hbm, grads_hbm = rest[:count], rest[count:outs]
    (
        dk_ref, dv_ref, dq_ref, product_ref, d_ref, all_ref, sums_ref, weights_ref, turned_ref, first_ref,
        part_ref, grads_ref, in_sem, out_sem,
    ) = rest[outs:]
    length = k2_ref.shape[0]
    width = wk_hbm.shape[1]
    p, h = pl.program_id(0), pl.program_id(1)
    pairs = width // (2 * HD)
    lane = lax.broadcasted_iota(jnp.int32, (length, 2 * HD), 1)
    left = lane < HD

    def arriving():
        copies = [
            pltpu.make_async_copy(wq_hbm.at[c], weights_ref.at[:, width * c : width * (c + 1)], in_sem.at[c])
            for c in range(4)
        ]
        copies.append(pltpu.make_async_copy(wk_hbm, weights_ref.at[:, 4 * width : 5 * width], in_sem.at[4]))
        copies.append(pltpu.make_async_copy(wv_hbm, weights_ref.at[:, 5 * width : 6 * width], in_sem.at[5]))
        copies.append(pltpu.make_async_copy(turned_hbm, turned_ref, in_sem.at[6]))
        copies.append(pltpu.make_async_copy(first_hbm, first_ref, in_sem.at[7]))
        return copies

    @pl.when(jnp.logical_and(p == 0, h == 0))
    def _():
        for copy in arriving():
            copy.start()

    @pl.when(h == 0)
    def _():
        first = y_ref[0] == 0
        own, got = own_ref[...], got_ref[...]
        joined = jnp.concatenate([jnp.where(first, own, got), jnp.where(first, got, own)], axis=0)
        product_ref[...] = joined * o_ref[...].astype(F32)
        d_ref[...] = joined.astype(BF16)

    d_context = d_ref[...]
    base = HD * (1 - h)
    mine = jnp.logical_and(lane >= HD - base, lane < 2 * HD - base)
    delta = jnp.sum(jnp.where(mine, product_ref[...], 0.0), axis=1, keepdims=True)
    high, middle, low = three_pieces(-delta)
    pieces = jnp.where(
        lane == base, high, jnp.where(lane == base + 1, middle, jnp.where(lane == base + 2, low, 0.0))
    ).astype(BF16)
    d_wide = jnp.where(mine, d_context, pieces)
    q2, k2 = q2_ref[...], k2_ref[...]
    query = jnp.concatenate([q2, extra_ref[...]], axis=1)
    keys = jnp.concatenate([k2, key_extra(live_ref[...] > 0.5, length)], axis=1)
    probs = jnp.exp(mm(keys, query, NT))
    ones = jnp.where((lane >= base) & (lane < base + 3), 1.0, 0.0).astype(BF16)
    d_probs = mm(jnp.where(mine, v_ref[...], ones), d_wide, NT)
    d_scores = (probs * d_probs).astype(BF16)
    dv_ref[h] = mm(probs.astype(BF16), d_context, NN)
    dk_ref[h] = mm(d_scores, q2, NN)
    dq_ref[h] = mm(k2, d_scores, TN).T * (1.0 / math.sqrt(HD))

    @pl.when(h == 1)
    def _():
        entity = kind_ref[...] > 0.5
        even, odd = dq_ref[0], dq_ref[1]
        to_word = jnp.where(left, even, pltpu.roll(odd, HD, 1)).astype(BF16).astype(F32)
        to_entity = jnp.where(left, pltpu.roll(even, HD, 1), odd).astype(BF16).astype(F32)
        even, odd = dk_ref[0], dk_ref[1]
        even = jnp.where(entity, pltpu.roll(even, HD, 1), even)
        odd = jnp.where(entity, odd, pltpu.roll(odd, HD, 1))
        grads = [
            jnp.where(entity, 0.0, to_word),
            jnp.where(entity, 0.0, to_entity),
            jnp.where(entity, to_word, 0.0),
            jnp.where(entity, to_entity, 0.0),
            jnp.where(left, even, odd).astype(BF16).astype(F32),
            jnp.where(left, dv_ref[0], dv_ref[1]).astype(BF16).astype(F32),
        ]
        for c, grad in enumerate(grads):
            all_ref[p, c] = grad.astype(BF16)
        sums = [jnp.sum(grad, axis=0, keepdims=True) for grad in grads]
        sums_ref[p] = jnp.concatenate([*sums, jnp.zeros((2, 2 * HD), F32)], axis=0)

    @pl.when(jnp.logical_and(p == pairs - 1, h == 1))
    def _():
        for copy in arriving():
            copy.wait()
        grads = jnp.concatenate([all_ref[k, c] for c in range(6) for k in range(pairs)], axis=1)
        half = first_ref.shape[0]
        leaving = []

        def leave(source, target):
            copy = pltpu.make_async_copy(source, target, out_sem.at[len(leaving)])
            copy.start()
            leaving.append(copy)

        for i in range(2):
            rows = slice(i * half, (i + 1) * half)
            total = mm(grads[rows], weights_ref[...], NT)
            part_ref[rows, :] = total + jnp.where(y_ref[0] == i, first_ref[...], 0.0)
        begin = 0
        for target in part_hbm:
            leave(part_ref.at[begin : begin + target.shape[0], :], target)
            begin += target.shape[0]
        model = turned_ref.shape[0]
        sums = jnp.concatenate([sums_ref[k] for k in range(pairs)], axis=1)
        pieces = jnp.concatenate([piece.astype(BF16) for piece in three_pieces(sums)], axis=0)
        picked = mm(pick_ref[...], pieces, NT)
        biases = picked[:, :6] + picked[:, 8:14] + picked[:, 16:22]
        seen = columns_ref.shape[1] // 2
        rest_zero = jnp.zeros((model, 128 - 6 - seen), F32)
        extra = jnp.concatenate(
            [
                biases, columns_ref[:, :seen], rest_zero,
                jnp.zeros((model, 6), F32), columns_ref[:, seen:], rest_zero,
            ],
            axis=1,
        )
        lower = y_ref[1] % 2 == 0

        def place(array, cols, value):
            if group is None:
                grads_ref[array, :, cols] = value
                return
            blocks = value.reshape(model // (2 * group), 2, group, value.shape[1])
            first, second = blocks[:, 0], blocks[:, 1]
            for k, (one, other) in enumerate(((first, second), (second, first))):
                picked_rows = jnp.where(lower, one, other).reshape(model // 2, value.shape[1])
                grads_ref[array, k * (model // 2) : (k + 1) * (model // 2), cols] = picked_rows

        for array in range(2):

            def one(i, carry, array=array):
                grad = jnp.concatenate([all_ref[k, 3 * array + i] for k in range(pairs)], axis=1)
                at = pl.multiple_of(width * i, 128)
                place(array, pl.ds(at, width), mm(turned_ref[...], grad, NN))
                return carry

            lax.fori_loop(0, 3, one, 0)
            wide = 3 * width
            if array:
                place(array, slice(wide, wide + 256), extra)
                wide += 256
            if group is None:
                leave(grads_ref.at[array, :, :wide], grads_hbm[array])
            else:
                for k in (1, 0):
                    rows = slice(k * (model // 2), (k + 1) * (model // 2))
                    leave(grads_ref.at[array, rows, :wide], grads_hbm[2 * array + k])
        for copy in leaving:
            copy.wait()


def attend_back(
    y, q2, extra, k2, v, o, own, got, live, kind, columns, pick, wq, wk, wv, turned, first, chunks, group
):
    length, width = v.shape
    half, model = first.shape
    pairs = width // (2 * HD)
    head = pl.BlockSpec((length, 2 * HD), lambda p, h, *_: (0, 2 * p + h))
    pair = pl.BlockSpec((length, 2 * HD), lambda p, h, *_: (0, p))
    part = pl.BlockSpec((half, 2 * HD), lambda p, h, *_: (0, p))
    anywhere = pl.BlockSpec(memory_space=pl.ANY)
    shapes = [struct((rows, model), F32) for rows in chunks]
    for wide in (3 * width, 3 * width + 256):
        shapes += [struct((model, wide), F32)] if group is None else [struct((model // 2, wide), F32)] * 2
    return pl.pallas_call(
        functools.partial(attend_back_kernel, len(chunks), group),
        grid_spec=pltpu.PrefetchScalarGridSpec(
            num_scalar_prefetch=1,
            grid=(pairs, 2),
            in_specs=[
                head, head, head, pair, pair, part, part, whole_block((length, 1)), whole_block((length, 1)),
                whole_block(columns.shape), whole_block(pick.shape),
                *[anywhere] * 5,
            ],
            out_specs=[anywhere] * len(shapes),
            scratch_shapes=[
                *[pltpu.VMEM((2, length, 2 * HD), F32)] * 3,
                pltpu.VMEM((length, 2 * HD), F32),
                pltpu.VMEM((length, 2 * HD), BF16),
                pltpu.VMEM((pairs, 6, length, 2 * HD), BF16),
                pltpu.VMEM((pairs, 8, 2 * HD), F32),
                pltpu.VMEM((model, 6 * width), BF16),
                pltpu.VMEM((model, length), BF16),
                pltpu.VMEM((half, model), F32),
                pltpu.VMEM((length, model), F32),
                pltpu.VMEM((2, model, 3 * width + 256), F32),
                pltpu.SemaphoreType.DMA((8,)),
                pltpu.SemaphoreType.DMA((len(shapes),)),
            ],
        ),
        out_shape=shapes,
        compiler_params=params(63),
        cost_estimate=cost(20 * length * length * width, 40 * length * width, length * length * width // HD),
        name="attend_back",
    )(y, q2, extra, k2, v, o, own, got, live, kind, columns, pick, wq, wk, wv, turned, first)


def normalise(value):
    centre = value - jnp.mean(value, axis=-1, keepdims=True)
    inverse = lax.rsqrt(jnp.mean(centre * centre, axis=-1, keepdims=True) + NORM_EPS)
    return centre * inverse, inverse


def normalise_back(scaled, normal, inverse):
    return inverse * (
        scaled
        - jnp.mean(scaled, axis=-1, keepdims=True)
        - normal * jnp.mean(scaled * normal, axis=-1, keepdims=True)
    )


def gelu_pair(values):
    cumulative = 0.5 * (1.0 + lax.erf(values * (1.0 / math.sqrt(2.0))))
    density = jnp.exp(-0.5 * values * values) * (1.0 / math.sqrt(2.0 * math.pi))
    return values * cumulative, cumulative + values * density


def column_sum(value):
    return jnp.sum(value, axis=0, keepdims=True)


def first_cut(half):
    return half // 2


def middle_sizes(wi, wo, early):
    hidden, model, width = wi.shape[1], wo.shape[1], wo.shape[0]
    cut = [width // SLICES, (width + model) // SLICES, (width + 2 * model) // SLICES]
    return hidden, hidden // 2, model, width, cut


def far_block(ref, a, b):
    return ref[:, a:b, :].reshape(SLICES * (b - a), ref.shape[2])


def far_outer(ref, part, half):
    per = SLICES // 2
    return ref[per * (part - 2) : per * (part - 1), :, :].reshape(half, ref.shape[2])


def by_core(lower, values):
    first, second = (value.astype(F32) for value in values)
    keep = jnp.where(lower, first, second).astype(BF16)
    return keep, jnp.where(lower, second, first)


def forward_kernel(at_ref, x_ref, cot_ref, live_ref, own_ref, got_ref, wo_ref, wi_hbm, wu_hbm, *rest):
    arrived = rest[:SLICES]
    arrived_late = rest[SLICES : 2 * SLICES]
    (
        vec_ref, bias_ref, out_ref, out_first_ref, out_late_ref, low_ref, d_low_ref, keep_ref, send_ref,
        slope_ref, n1_ref, inv1_ref, d_second_ref, sums_ref, early_hbm, late_hbm,
        early_ref, late_ref, wi_ref, wu_ref, raw_ref, raw_late_ref, in_sem, out_sem,
    ) = rest[2 * SLICES :]
    step = pl.program_id(0)
    me = at_ref[1]
    lower = me % 2 == 0
    hidden, half, model, width, cut = middle_sizes(wi_hbm, wo_ref, early_ref)

    def weight_copies():
        stages = [[], [], [], [], []]
        for k in range(SLICES):
            for stage, source, target in (
                (0, arrived[k].at[: cut[0], :], raw_ref.at[k, : cut[0], :]),
                (2, arrived[k].at[cut[0] :, :], raw_ref.at[k, cut[0] :, :]),
                (4, arrived_late[k], raw_late_ref.at[k]),
            ):
                stages[stage].append(pltpu.make_async_copy(source, target, in_sem.at[stage * SLICES + k]))
        stages[1].append(pltpu.make_async_copy(wi_hbm, wi_ref, in_sem.at[SLICES]))
        stages[3].append(pltpu.make_async_copy(wu_hbm, wu_ref, in_sem.at[3 * SLICES]))
        return stages

    def leaving():
        return [
            pltpu.make_async_copy(early_ref, early_hbm, out_sem.at[0]),
            pltpu.make_async_copy(late_ref, late_hbm, out_sem.at[1]),
        ]

    def arrive(*wanted):
        @pl.when(step == 0)
        def _():
            stages = weight_copies()
            for stage in wanted:
                for copy in stages[stage]:
                    copy.wait()
            for k in range(SLICES):
                if 0 in wanted:
                    early_ref[me ^ k, : cut[0], :] = raw_ref[k, : cut[0], :].astype(BF16)
                if 2 in wanted:
                    early_ref[me ^ k, cut[0] :, :] = raw_ref[k, cut[0] :, :].astype(BF16)
                if 4 in wanted:
                    late_ref[me ^ k] = raw_late_ref[k].astype(BF16)
            if 4 in wanted:
                for copy in leaving():
                    copy.start()

    @pl.when(step == 0)
    def _():
        for stage in weight_copies():
            for copy in stage:
                copy.start()

    arrive(0)
    vec = [vec_ref[k : k + 1, :] for k in range(6)]
    got = got_ref[...].astype(BF16)
    own = own_ref[...]
    first = mm(own, wo_ref[...], NN) + mm(got, far_block(early_ref, 0, cut[0]), NN) + vec[0] + x_ref[...].astype(F32)
    n1, inv1 = normalise(first)
    n1_ref[...] = n1
    inv1_ref[...] = inv1
    normed = n1 * vec[1] + vec[2]
    low = normed.astype(BF16)
    low_ref[...] = low
    at_low = model + hidden
    send_ref[:, at_low : at_low + model] = low.astype(F32)
    _, send = by_core(lower, (own, got))
    send_ref[:, at_low + model :] = send
    second = vec[3] + normed
    arrive(1, 3)
    for far in range(2):
        if far:
            arrive(2, 4)
        pair = []
        for part in (2 * far, 2 * far + 1):
            inner = wi_ref[:, half * part : half * (part + 1)] if part < 2 else far_block(early_ref, cut[part - 2], cut[part - 1])
            pre = mm(low, inner, NN) + bias_ref[part : part + 1, :]
            active, slope = gelu_pair(pre)
            active = active.astype(BF16)
            slope_ref[:, half * part : half * (part + 1)] = slope.astype(BF16)
            pair.append(active)
            outer = wu_ref[half * part : half * (part + 1), :] if part < 2 else far_outer(late_ref, part, half)
            second = second + mm(active, outer, NN)
        keep, send = by_core(lower, pair)
        keep_ref[:, half * far : half * (far + 1)] = keep
        send_ref[:, model + half * far : model + half * (far + 1)] = send
    n2, inv2 = normalise(second)
    live = live_ref[...] > 0.5
    result = jnp.where(live, n2 * vec[4] + vec[5], 0.0).astype(BF16)
    out_ref[...] = result
    out_first_ref[...] = result[:, : model // 2].astype(F32)
    out_late_ref[...] = result[:, model // 2 :].astype(F32)
    dz = jnp.where(live, cot_ref[...].astype(F32), 0.0)
    d_second = normalise_back(dz * vec[4], n2, inv2)
    d_second_ref[...] = d_second
    d_low = d_second.astype(BF16)
    d_low_ref[...] = d_low
    send_ref[:, :model] = d_low.astype(F32)
    sums = jnp.concatenate(
        [column_sum(d_second), column_sum(dz * n2), column_sum(dz), jnp.zeros((5, model), F32)], axis=0
    )

    @pl.when(step == 0)
    def _():
        sums_ref[...] = sums

    @pl.when(step != 0)
    def _():
        sums_ref[...] += sums

    @pl.when(step == pl.num_programs(0) - 1)
    def _():
        for copy in leaving():
            copy.wait()


def forward(at, x, cot, live, context, got, wo, wi, wu, early, late, vec, bias, rows=256):
    half, width = got.shape
    model, hidden = wi.shape
    rows = min(rows, half)
    steps = half // rows
    mine = lambda w: pl.BlockSpec((rows, w), lambda i, s: (i + s[0] * steps, 0))
    tile = lambda w: pl.BlockSpec((rows, w), lambda i, s: (i, 0))
    anywhere = pl.BlockSpec(memory_space=pl.ANY)
    widths = (
        (model, BF16), (model // 2, F32), (model // 2, F32), (model, BF16), (model, BF16), (hidden, BF16),
        (2 * model + hidden + width, F32), (2 * hidden, BF16), (model, F32), (1, F32), (model, F32),
    )
    far_shapes = [(SLICES, *early[0].shape), (SLICES, *late[0].shape)]
    return pl.pallas_call(
        forward_kernel,
        grid_spec=pltpu.PrefetchScalarGridSpec(
            num_scalar_prefetch=1,
            grid=(steps,),
            in_specs=[
                mine(model), mine(model), mine(1), mine(width), tile(width),
                whole_block(wo.shape), *[anywhere] * (2 + 2 * SLICES),
                whole_block(vec.shape), whole_block(bias.shape),
            ],
            out_specs=[
                *(tile(w) for w, _ in widths), pl.BlockSpec((8, model), lambda i, s: (0, 0)), anywhere, anywhere,
            ],
            scratch_shapes=[
                *(pltpu.VMEM(shape, BF16) for shape in far_shapes),
                pltpu.VMEM(wi.shape, BF16),
                pltpu.VMEM(wu.shape, BF16),
                *(pltpu.VMEM(shape, F32) for shape in far_shapes),
                pltpu.SemaphoreType.DMA((5 * SLICES,)),
                pltpu.SemaphoreType.DMA((2,)),
            ],
        ),
        out_shape=[
            *(struct((half, w), kind) for w, kind in widths), struct((8, model), F32),
            *(struct(shape, BF16) for shape in far_shapes),
        ],
        compiler_params=params(63),
        cost_estimate=cost(8 * half * model * hidden, 24 * model * hidden, 4 * half * hidden),
        name="forward",
    )(at, x, cot, live, context, got, wo, wi, wu, *early, *late, vec, bias)


def backward_kernel(
    at_ref, slope_ref, n1_ref, inv1_ref, d_second_ref, d_low_ref, own_ref, got_ref, wo_ref, vec_ref,
    wi_hbm, wu_hbm, early_hbm, late_hbm,
    first_ref, dco_ref, dcf_ref, d_attn_ref, keep0_ref, keep1_ref, send_ref, sums_ref, inner_sums_ref,
    wi_ref, wu_ref, early_ref, late_ref, in_sem,
):
    step = pl.program_id(0)
    lower = at_ref[1] % 2 == 0
    hidden, half, model, width, cut = middle_sizes(wi_hbm, wo_ref, early_ref)
    ca = first_cut(half)

    def copies():
        pairs = ((wu_hbm, wu_ref), (wi_hbm, wi_ref), (late_hbm, late_ref), (early_hbm, early_ref))
        return [pltpu.make_async_copy(*pair, in_sem.at[k]) for k, pair in enumerate(pairs)]

    @pl.when(step == 0)
    def _():
        for copy in copies():
            copy.start()

    d_low = d_low_ref[...]
    n1 = n1_ref[...]
    d_normed = d_second_ref[...]
    inner_sums = []
    for far in range(2):

        @pl.when(step == 0)
        def _():
            for copy in copies()[2 * far : 2 * far + 2]:
                copy.wait()

        pair = []
        for part in (2 * far, 2 * far + 1):
            outer = wu_ref[half * part : half * (part + 1), :] if part < 2 else far_outer(late_ref, part, half)
            inner = wi_ref[:, half * part : half * (part + 1)] if part < 2 else far_block(early_ref, cut[part - 2], cut[part - 1])
            d_hidden = mm(d_low, outer, NT)
            d_inner = (d_hidden * slope_ref[:, half * part : half * (part + 1)].astype(F32)).astype(BF16)
            pair.append(d_inner)
            inner_sums.append(column_sum(d_inner.astype(F32)))
            d_normed = d_normed + mm(d_inner, inner, NT)
        keep, send = by_core(lower, pair)
        da = half - ca
        keep0_ref[:, ca * far : ca * (far + 1)] = keep[:, :ca]
        keep1_ref[:, da * far : da * (far + 1)] = keep[:, ca:]
        send_ref[:, ca * far : ca * (far + 1)] = send[:, :ca]
        send_ref[:, 2 * ca + da * far : 2 * ca + da * (far + 1)] = send[:, ca:]
    d_first = normalise_back(d_normed * vec_ref[1:2, :], n1, inv1_ref[...])
    first_ref[...] = d_first
    d_attn = d_first.astype(BF16)
    d_attn_ref[...] = d_attn
    send_ref[:, hidden:] = d_attn.astype(F32)
    dco_ref[...] = mm(d_attn, wo_ref[...], NT).astype(BF16).astype(F32)
    dcf_ref[...] = mm(d_attn, far_block(early_ref, 0, cut[0]), NT).astype(BF16).astype(F32)
    keep, _ = by_core(lower, (own_ref[...], got_ref[...]))
    keep0_ref[:, 2 * ca :] = keep
    sums = jnp.concatenate(
        [column_sum(d_first), column_sum(d_normed * n1), column_sum(d_normed), jnp.zeros((5, model), F32)], axis=0
    )
    inner_sums = jnp.concatenate([*inner_sums, jnp.zeros((4, half), F32)], axis=0)

    @pl.when(step == 0)
    def _():
        sums_ref[...] = sums
        inner_sums_ref[...] = inner_sums

    @pl.when(step != 0)
    def _():
        sums_ref[...] += sums
        inner_sums_ref[...] += inner_sums


def backward(at, slope, n1, inv1, d_second, d_low, context, got, wo, vec, wi, wu, early, late, rows=256):
    half, width = got.shape
    model, hidden = wi.shape
    rows = min(rows, half)
    steps = half // rows
    ca = first_cut(hidden // 2)
    mine = lambda w: pl.BlockSpec((rows, w), lambda i, s: (i + s[0] * steps, 0))
    tile = lambda w: pl.BlockSpec((rows, w), lambda i, s: (i, 0))
    anywhere = pl.BlockSpec(memory_space=pl.ANY)
    widths = (
        (model, F32), (width, F32), (width, F32), (model, BF16), (2 * ca + width, BF16), (hidden - 2 * ca, BF16),
        (hidden + model, F32),
    )
    return pl.pallas_call(
        backward_kernel,
        grid_spec=pltpu.PrefetchScalarGridSpec(
            num_scalar_prefetch=1,
            grid=(steps,),
            in_specs=[
                tile(2 * hidden), tile(model), tile(1), tile(model), tile(model), mine(width), tile(width),
                whole_block(wo.shape), whole_block(vec.shape), *[anywhere] * 4,
            ],
            out_specs=[
                *(tile(w) for w, _ in widths),
                pl.BlockSpec((8, model), lambda i, s: (0, 0)),
                pl.BlockSpec((8, hidden // 2), lambda i, s: (0, 0)),
            ],
            scratch_shapes=[
                *(pltpu.VMEM(a.shape, BF16) for a in (wi, wu, early, late)),
                pltpu.SemaphoreType.DMA((4,)),
            ],
        ),
        out_shape=[
            *(struct((half, w), kind) for w, kind in widths), struct((8, model), F32), struct((8, hidden // 2), F32),
        ],
        compiler_params=params(63),
        cost_estimate=cost(8 * half * model * hidden, 24 * model * hidden),
        name="backward",
    )(at, slope, n1, inv1, d_second, d_low, context, got, wo, vec, wi, wu, early, late)


def weight_kernel(plan, count, kinds, bit_ref, *rest):
    groups = len(plan)
    left_hbm, rest = rest[:kinds], rest[kinds:]
    keep_hbm, rest = rest[:groups], rest[groups:]
    got_hbm, rest = rest[:count], rest[count:]
    outs, rest = rest[: 2 * groups], rest[2 * groups :]
    left_ref, left_got_ref, rest = rest[0], rest[1], rest[2:]
    keep_refs, rest = rest[:groups], rest[groups:]
    got_refs, rest = rest[:groups], rest[groups:]
    stage_refs, (in_sem, out_sem) = rest[:groups], rest[groups:]
    model = left_ref.shape[2]

    arriving, ready = [], {}

    def bring(key, source, target):
        if key not in ready:
            ready[key] = pltpu.make_async_copy(source, target, in_sem.at[len(arriving)])
            ready[key].start()
            arriving.append(key)

    for g, (_, _, tiles) in enumerate(plan):
        for index, (left_array, left_at), (right_array, right_at), a, b in tiles:
            bring(("left", index), left_hbm[index], left_ref.at[index])
            if ("left got", index) not in ready:
                columns = slice(left_at, left_at + model)
                bring(("left got", index), got_hbm[left_array].at[:, columns], left_got_ref.at[index])
            bring(("keep", g, a), keep_hbm[g].at[:, a:b], keep_refs[g].at[:, a:b])
            columns = slice(right_at, right_at + b - a)
            bring(("got", g, a), got_hbm[right_array].at[:, columns], got_refs[g].at[:, a:b])
    waited = set()

    def need(*keys):
        for key in keys:
            if key not in waited:
                waited.add(key)
                ready[key].wait()

    leaving = []
    for g, (slot, group, tiles) in enumerate(plan):
        width = keep_refs[g].shape[1]
        for index, _, _, a, b in tiles:
            need(("left", index), ("left got", index), ("keep", g, a), ("got", g, a))
            left = jnp.concatenate([left_ref[index], left_got_ref[index].astype(BF16)], axis=0)
            right = jnp.concatenate([keep_refs[g][:, a:b], got_refs[g][:, a:b].astype(BF16)], axis=0)
            value = mm(left, right, TN)
            if slot is None:
                part, base = (0, 0) if 2 * b <= width else (1, width // 2)
                stage_refs[g][part, :, a - base : b - base] = value
                parts = ((part, a - base, b - base),)
            else:
                pairs = value.reshape(model // (2 * group), 2, group, b - a)
                kept = bit_ref[slot] == 0
                first, second = pairs[:, 0], pairs[:, 1]
                for part, (one, other) in enumerate(((first, second), (second, first))):
                    picked = jnp.where(kept, one, other)
                    stage_refs[g][part, :, a:b] = picked.reshape(model // 2, b - a)
                parts = ((1, a, b), (0, a, b))
            for part, a, b in parts:
                copy = pltpu.make_async_copy(
                    stage_refs[g].at[part, :, a:b], outs[2 * g + part].at[:, a:b], out_sem.at[len(leaving)]
                )
                copy.start()
                leaving.append(copy)
    for copy in leaving:
        copy.wait()


def weight_grads(at, lefts, keeps, received, plan):
    depth, model = lefts[0].shape
    stages, shapes, steps = [], [], 0
    for (slot, _, tiles), keep in zip(plan, keeps):
        width = keep.shape[1]
        shape = (model, width // 2) if slot is None else (model // 2, width)
        stages.append(pltpu.VMEM((2, *shape), F32))
        shapes += [struct(shape, F32)] * 2
        steps += len(tiles)
    columns = sum(keep.shape[1] for keep in keeps)
    anywhere = pl.BlockSpec(memory_space=pl.ANY)
    return pl.pallas_call(
        functools.partial(weight_kernel, plan, len(received), len(lefts)),
        grid_spec=pltpu.PrefetchScalarGridSpec(
            num_scalar_prefetch=1,
            grid=(1,),
            in_specs=[anywhere] * (len(lefts) + len(keeps) + len(received)),
            out_specs=[anywhere] * len(shapes),
            scratch_shapes=[
                pltpu.VMEM((len(lefts), depth, model), BF16),
                pltpu.VMEM((len(lefts), depth, model), F32),
                *(pltpu.VMEM(keep.shape, BF16) for keep in keeps),
                *(pltpu.VMEM(keep.shape, F32) for keep in keeps),
                *stages,
                pltpu.SemaphoreType.DMA((2 * len(lefts) + 2 * steps,)),
                pltpu.SemaphoreType.DMA((2 * steps,)),
            ],
        ),
        out_shape=shapes,
        compiler_params=params(63),
        cost_estimate=cost(4 * depth * model * columns, 4 * model * columns + 8 * depth * columns),
        name="weight_grads",
    )(at, *lefts, *keeps, *received)


def combine_kernel(plan, count, bits_ref, *rest):
    outs = len(plan)
    arrays, targets = rest[:count], rest[count : count + outs]
    buffers, (in_sem, out_sem) = rest[count + outs : -2], rest[-2:]
    copies = []
    for pieces in plan:
        for _, terms in pieces:
            for array, chosen, a, b, _ in terms:
                index = [slice(None)] * len(arrays[array].shape)
                for axis, (bit, mine) in chosen:
                    index[axis] = pl.ds(bits_ref[bit] if mine else 1 - bits_ref[bit], 1)
                index[-1] = slice(a, b)
                k = len(copies)
                copies.append(pltpu.make_async_copy(arrays[array].at[tuple(index)], buffers[k], in_sem.at[k]))
    for copy in copies:
        copy.start()
    k = 0
    leaving = []
    for target, pieces in zip(targets, plan):
        for at, terms in pieces:
            first = k
            total = None
            for *_, gate in terms:
                copies[k].wait()
                value = buffers[k][...]
                if gate is not None:
                    value = jnp.where(bits_ref[0] == gate, value, 0.0)
                total = value if total is None else total + value
                k += 1
            if len(terms) > 1:
                buffers[first][...] = total
            width = buffers[first].shape[-1]
            index = (*[slice(None)] * (len(target.shape) - 1), slice(at, at + width))
            copy = pltpu.make_async_copy(buffers[first], target.at[index], out_sem.at[len(leaving)])
            copy.start()
            leaving.append(copy)
    for copy in leaving:
        copy.wait()


def combine(bit_values, outputs):
    arrays, plan, shapes, buffers, moved = [], [], [], [], 0
    for pieces in outputs:
        at, planned = 0, []
        for terms in pieces:
            named = []
            for array, chosen, a, b, gate in terms:
                place = [k for k, other in enumerate(arrays) if other is array]
                if not place:
                    place = [len(arrays)]
                    arrays.append(array)
                named.append((place[0], tuple(sorted(chosen.items())), a, b, gate))
                block = tuple(1 if k in chosen else size for k, size in enumerate(array.shape[:-1]))
                buffers.append(pltpu.VMEM((*block, b - a), F32))
                moved += 4 * math.prod(block) * (b - a)
            planned.append((at, named))
            at += b - a
        plan.append(planned)
        shapes.append(struct((*block, at), F32))
    anywhere = pl.BlockSpec(memory_space=pl.ANY)
    pieces = sum(len(planned) for planned in plan)
    return pl.pallas_call(
        functools.partial(combine_kernel, plan, len(arrays)),
        grid_spec=pltpu.PrefetchScalarGridSpec(
            num_scalar_prefetch=1,
            grid=(1,),
            in_specs=[anywhere] * len(arrays),
            out_specs=[anywhere] * len(shapes),
            scratch_shapes=[
                *buffers,
                pltpu.SemaphoreType.DMA((len(buffers),)),
                pltpu.SemaphoreType.DMA((pieces,)),
            ],
        ),
        out_shape=shapes,
        compiler_params=params(63),
        cost_estimate=cost(moved, 2 * moved),
        name="combine",
    )(bit_values, *arrays)


def turn_kernel(value_ref, out_ref):
    out_ref[...] = value_ref[...].astype(F32).T.astype(BF16)


def turn(value, columns=256):
    length, model = value.shape
    return pl.pallas_call(
        turn_kernel,
        grid=(model // columns,),
        in_specs=[pl.BlockSpec((length, columns), lambda i: (0, i))],
        out_specs=pl.BlockSpec((columns, length), lambda i: (i, 0)),
        out_shape=struct((model, length), BF16),
        compiler_params=params(63),
        cost_estimate=cost(length * model, 4 * length * model),
        name="turn",
    )(value)


def place_kernel(steps, y_ref, own_ref, first_ref, second_ref, out_ref):
    mine = pl.program_id(0) // steps == y_ref[0]
    got = jnp.concatenate([first_ref[...], second_ref[...]], axis=1)
    out_ref[...] = jnp.where(mine, own_ref[...].astype(F32), got).astype(BF16)


def place_rows(y, own, first, second):
    half, model = own.shape
    rows = min(128, half)
    steps = half // rows
    tile = lambda w: pl.BlockSpec((rows, w), lambda i, s: (i % steps, 0))
    return pl.pallas_call(
        functools.partial(place_kernel, steps),
        grid_spec=pltpu.PrefetchScalarGridSpec(
            num_scalar_prefetch=1,
            grid=(2 * steps,),
            in_specs=[tile(model), tile(model // 2), tile(model // 2)],
            out_specs=pl.BlockSpec((rows, model), lambda i, s: (i, 0)),
        ),
        out_shape=struct((2 * half, model), BF16),
        compiler_params=params(63),
        cost_estimate=cost(half * model, 12 * half * model),
        name="place_rows",
    )(y, own, first, second)


def per_device(
    devices,
    tokens,
    lengths,
    entity_flags,
    query_weight,
    query_bias,
    key_weight,
    key_bias,
    value_weight,
    value_bias,
    output_weight,
    output_bias,
    attn_gain,
    attn_shift,
    inner_weight,
    inner_bias,
    outer_weight,
    outer_bias,
    final_gain,
    final_shift,
    cotangent,
):
    x = tokens[0]
    length, model = x.shape
    width = key_weight.shape[1]
    hidden = inner_weight.shape[1]
    half = length // 2
    bits = devices.bit_length() - 1
    y = lax.axis_index("tensor")
    d = lax.axis_index("dp")

    def swap(value, mask):
        return lax.ppermute(value, "dp", [(i, i ^ mask) for i in range(devices)])

    def cross(value):
        return lax.ppermute(value, "tensor", [(0, 1), (1, 0)])

    me = d % SLICES
    core = d % 2
    rows = model // devices
    near_mask, far_mask = 192 // rows, 96 // rows
    at = jnp.stack([y, me, (d // near_mask) % 2, (d // far_mask) % 2]).astype(jnp.int32)
    tie = lax.optimization_barrier

    def cut(array, index):
        size = array.shape[0] // SLICES
        return lax.dynamic_slice_in_dim(array, index * size, size, 0)

    def pack(index):
        wide = cut(inner_weight, index)
        early = jnp.concatenate([cut(output_weight, index), wide[:, :model], wide[:, model:]], axis=0)
        return early.astype(F32)

    def pack_late(index):
        return cut(outer_weight, index).astype(F32)

    live = (lax.broadcasted_iota(jnp.int32, (length, 1), 0) < lengths[0]).astype(F32)
    kind = (entity_flags[0] == 1).astype(F32).reshape(length, 1)

    e0 = cross(pack(me))
    far_bias = cross(inner_bias)
    q2, k2, v = project(
        x, kind, query_weight, query_bias, key_weight, key_bias, value_weight, value_bias
    )
    e0, far_bias, l0, l6, q2 = tie((e0, far_bias, pack_late(me), pack_late(me ^ 6), q2))
    e2 = swap(e0, 2)
    e4 = swap(e0, 4)
    l0 = cross(l0)
    e1 = swap(e0, 1)
    context, extra = attend(q2, k2, v, live)
    sent = lax.dynamic_slice_in_dim(context, half * (1 - y), half, 0).astype(F32)
    e1, e2, e4, l0, l6, sent = tie((e1, e2, e4, l0, l6, sent))
    l2 = swap(l0, 2)
    l4 = swap(l0, 4)
    got = cross(sent)
    e6 = swap(e4, 2)
    l6 = cross(l6)
    per = width // devices
    where_row = lax.broadcasted_iota(jnp.int32, (model, width), 0)
    where_bias = lax.broadcasted_iota(jnp.int32, (model, width), 1)
    pick = (where_row == (where_bias // per) * rows + where_bias % per).astype(BF16)
    x_turned = turn(x)
    l2, l4, e2, e4, pick, x_turned = tie((l2, l4, e2, e4, pick, x_turned))
    e3 = swap(e2, 1)
    e5 = swap(e4, 1)
    got, e6, l6, e3, e5, l0, l2, l4 = tie((got, e6, l6, e3, e5, l0, l2, l4))
    l1 = swap(l0, 1)
    l3 = swap(l2, 1)
    l5 = swap(l4, 1)
    l7 = swap(l6, 1)
    e7 = swap(e6, 1)
    early = (e0, e1, e2, e3, e4, e5, e6, e7)
    late = (l0, l1, l2, l3, l4, l5, l6, l7)

    vec = jnp.stack(
        [output_bias, attn_gain, attn_shift, outer_bias, final_gain, final_shift, outer_bias, outer_bias]
    )
    bias = jnp.concatenate([inner_bias, far_bias, inner_bias, far_bias]).reshape(8, hidden // 2)
    ca, cb = first_cut(hidden // 2), hidden // 2
    da, db = hidden // 2 - ca, 0
    (
        out_rows, out_first, out_late, low, d_low, keep2, early_send, slope, n1, inv1, d_second, late_sums,
        far_early, far_late,
    ) = forward(
        at, x, cotangent[0], live, context, got, output_weight, inner_weight, outer_weight,
        early, late, vec, bias,
    )
    early_got = swap(early_send, 1)
    got_first = cross(out_first)
    d_first, dco, dcf, d_attn, keep0, keep1, late_send, first_sums, inner_sums = backward(
        at, slope, n1, inv1, d_second, d_low, context, got, output_weight, vec, inner_weight, outer_weight,
        far_early, far_late,
    )
    inner_columns = inner_sums[:4].reshape(2, model, 2)
    shared = [first_sums[:3].T, late_sums[:3].T]
    columns = jnp.concatenate([*shared, inner_columns[0], *shared, inner_columns[1]], axis=1)
    early_got, got_first, late_send, dcf, columns = tie((early_got, got_first, late_send, dcf, columns))
    late_got = swap(late_send, 1)
    d_got = cross(dcf)

    low_at, d_attn_at = (0, 2 * cb + model), (1, hidden)
    g2_keep, g2_send = weight_grads(
        at, (d_low,), (keep2,), (early_got,),
        (
            (
                3, far_mask * rows,
                ((0, (0, 0), (0, model), 0, cb), (0, (0, 0), (0, model + cb), cb, 2 * cb)),
            ),
        ),
    )
    g0_keep, g0_send, g1_keep, g1_send = weight_grads(
        at, (low, d_attn), (keep0, keep1), (early_got, late_got),
        (
            (
                2, near_mask * rows,
                (
                    (0, low_at, (1, 0), 0, ca), (0, low_at, (1, ca), ca, 2 * ca),
                    (1, d_attn_at, (0, 2 * model + hidden), 2 * ca, 2 * ca + width),
                ),
            ),
            (
                None, None,
                ((0, low_at, (1, 2 * ca), 0, da), (0, low_at, (1, 2 * ca + da), da, 2 * da)),
            ),
        ),
    )
    g0_send, g1_send, d_got = tie((g0_send, g1_send, d_got))
    g0_got = swap(g0_send, near_mask)
    g2_got = swap(g2_send, far_mask)
    g1_got = cross(g1_send)

    g0_send, g1_send, g2_send, dco, d_got = tie((g0_send, g1_send, g2_send, dco, d_got))
    chunks = tuple(length * k // 32 for k in (7, 17, 8))
    group = rows if rows % 8 == 0 else None
    results = attend_back(
        at, q2, extra, k2, v, context, dco, d_got, live, kind, columns, pick,
        query_weight, key_weight, value_weight, x_turned, d_first, chunks, group,
    )
    parts, products = results[: len(chunks)], results[len(chunks) :]
    got_out = cross(out_late)

    def spread(array, done):
        dims = [1 if (1 << (bits - 1 - k)) in done else 2 for k in range(bits)]
        return array.reshape(*dims, rows, array.shape[-1])

    bit_values = jnp.stack([(d >> k) % 2 for k in range(bits)]).astype(jnp.int32)
    rest_masks = [1 << k for k in range(1, bits) if (1 << k) not in (near_mask, far_mask)]

    def term(array, *done):
        array = spread(array, done)
        return (array, {}, 0, array.shape[-1], None)

    def half_of(terms, mask, mine):
        k = mask.bit_length() - 1
        return [(array, {**chosen, bits - 1 - k: (k, mine)}, a, b, gate) for array, chosen, a, b, gate in terms]

    def kept(terms, mask):
        return half_of(terms, mask, True)

    def other(terms, mask):
        return half_of(terms, mask, False)

    def columns_of(terms, first, last):
        return [(array, chosen, a + first, a + last, gate) for array, chosen, a, _, gate in terms]

    def on_core(terms, core_index):
        return [(array, chosen, a, b, core_index) for array, chosen, a, b, _ in terms]

    def whole_of(array):
        return (array, {}, 0, array.shape[-1], None)

    def part_of(array, a, b):
        return (array, {}, a, b, None)

    g0_got, g1_got, g2_got, got_out, parts, products = tie((g0_got, g1_got, g2_got, got_out, parts, products))
    if group is None:
        c = [term(products[0])]
        e = [term(products[1])]
        c_send, e_send = combine(bit_values, [[other(c, 1)], [other(e, 1)]])
        c, e = kept(c, 1), kept(e, 1)
    else:
        c, e = [term(products[0], 1)], [term(products[2], 1)]
        c_send, e_send = spread(products[1], (1,)), spread(products[3], (1,))
    e_got = swap(e_send, 1)
    c_got = swap(c_send, 1)
    g0 = [term(g0_keep, near_mask), term(g0_got, near_mask)]
    g1 = [term(g1_keep), term(g1_got)]
    g2 = [term(g2_keep, far_mask), term(g2_got, far_mask)]
    sends = combine(bit_values, [[columns_of(g0, ca, 2 * ca + width)], [other(g1, near_mask)]])
    _, late_bits = tie((sends, bit_values))
    (g2_send,) = combine(late_bits, [[other(g2, near_mask)]])
    e_got, c_got, parts, _ = tie((e_got, c_got, parts, g2_send))
    e.append(whole_of(e_got))
    c.append(whole_of(c_got))
    g1_got = swap(sends[1], near_mask)
    g0_got = cross(sends[0])
    g2_got = swap(g2_send, near_mask)
    e_send, c_send = combine(bit_values, [[other(e, far_mask)], [other(c, near_mask)]])
    e_got = swap(e_send, far_mask)
    part0 = cross(parts[0])
    near_bit, near_axis = (d // near_mask) % 2, bits - near_mask.bit_length()
    for array, *_ in g1:
        g1_got = tie(g1_got + lax.dynamic_slice_in_dim(array, near_bit, 1, near_axis))
    g0_got, g1_sum = tie((g0_got, g1_got))
    t = [
        *on_core(columns_of(g0, 2 * ca, 2 * ca + width), 0),
        *on_core([part_of(g0_got, ca, ca + width)], 1),
    ]
    g0 = [*columns_of(g0, 0, ca), part_of(g0_got, 0, ca)]
    g1 = [whole_of(g1_sum)]

    (three_send,) = combine(bit_values, [[other(terms, far_mask) for terms in (g0, t, g1)]])
    three_got = swap(three_send, far_mask)
    e_got, _ = tie((e_got, three_send))
    e = [*kept(e, far_mask), whole_of(e_got)]
    (small_send,) = combine(bit_values, [[columns_of(e, 3 * width + 128, 3 * width + 256)]])
    small_got = cross(small_send)
    g2_got, part0, parts, small_got = tie((g2_got, part0, parts, small_got))
    g2 = [*kept(g2, near_mask), whole_of(g2_got)]
    (g2_send,) = combine(bit_values, [[columns_of(g2, cb, 2 * cb)]])
    g2_got = cross(g2_send)
    c_got = swap(c_send, near_mask)
    three_got, c_got, own0, part0 = tie((three_got, c_got, parts[0], part0))
    in0 = (own0 + part0).astype(BF16)
    three_got, g2_got, c_got, small_got, in0, parts = tie((three_got, g2_got, c_got, small_got, in0, parts))
    small = [*columns_of(e, 3 * width, 3 * width + 128), whole_of(small_got)]
    e = columns_of(e, 0, 3 * width)
    g0 = [*kept(g0, far_mask), part_of(three_got, 0, ca)]
    t = [*kept(t, far_mask), part_of(three_got, ca, ca + width)]
    g1 = [*kept(g1, far_mask), part_of(three_got, ca + width, three_got.shape[-1])]
    g2 = [*columns_of(g2, 0, cb), whole_of(g2_got)]
    c = [*kept(c, near_mask), whole_of(c_got)]

    main = (g0, g1, g2, t)
    sizes = (ca, da + db, cb, width)
    ends = [sum(sizes[:k]) for k in range(len(sizes) + 1)]
    mask = rest_masks[0]
    (main_send,) = combine(bit_values, [[other(terms, mask) for terms in main]])
    _, late_bits = tie((main_send, bit_values))
    sends = combine(late_bits, [[other(e, near_mask), other(small, near_mask)], [other(c, far_mask)]])
    got_z = swap(main_send, mask)
    in1 = (parts[1] + cross(parts[1])).astype(BF16)
    c_got = swap(sends[1], far_mask)
    e_got = swap(sends[0], near_mask)
    layer_out = place_rows(at, out_rows, got_first, got_out)
    got_z, e_got, c_got, in1, parts, layer_out = tie((got_z, e_got, c_got, in1, parts, layer_out))
    main = [[*kept(terms, mask), part_of(got_z, ends[n], ends[n + 1])] for n, terms in enumerate(main)]
    e = [*kept(e, near_mask), part_of(e_got, 0, 3 * width)]
    small = [*kept(small, near_mask), part_of(e_got, 3 * width, 3 * width + 128)]
    c = [*kept(c, far_mask), whole_of(c_got)]
    for mask in rest_masks[1:]:
        (send,) = combine(bit_values, [[other(terms, mask) for terms in main]])
        got_z = swap(send, mask)
        main = [[*kept(terms, mask), part_of(got_z, ends[n], ends[n + 1])] for n, terms in enumerate(main)]

    for k, mask in enumerate(rest_masks):
        (pair_send,) = combine(bit_values, [[other(c, mask), other(e, mask), other(small, mask)]])
        outputs = [[kept(c, mask), kept(e, mask), kept(small, mask)]]
        if k == 0:
            outputs += [[other(terms, 1) for terms in main], [kept(terms, 1) for terms in main]]
        _, late_bits = tie((pair_send, bit_values))
        sends = combine(late_bits, outputs)
        pair_got = swap(pair_send, mask)
        if k == 0:
            in2 = (parts[2] + cross(parts[2])).astype(BF16)
            got_last = swap(sends[1], 1)
            keep = sends[2]
        pair_keep = sends[0]
        wide = pair_keep.shape[-1]
        c = [part_of(pair_keep, 0, 3 * width), part_of(pair_got, 0, 3 * width)]
        e = [part_of(pair_keep, 3 * width, 6 * width), part_of(pair_got, 3 * width, 6 * width)]
        small = [part_of(pair_keep, 6 * width, wide), part_of(pair_got, 6 * width, wide)]

    input_grad = jnp.concatenate([in0, in1, in2], axis=0)
    got_last, keep, input_grad = tie((got_last, keep, input_grad))
    got_last = got_last.reshape(rows, -1)
    keep = keep.reshape(rows, -1)
    low_half = jnp.where(core == 0, keep, got_last)
    high_half = jnp.where(core == 0, got_last, keep)
    at2 = ca + da + db
    inner_half = lambda array: [array[:, : ca + da]]
    at3 = at2 + cb
    outer_half = lambda array: [array[:, at2:at3], array[:, ca + da : at2]]
    t = keep[:, at3:] + got_last[:, at3:]
    grad_inner = jnp.concatenate(inner_half(low_half) + inner_half(high_half), axis=1)
    grad_outer = jnp.concatenate(outer_half(low_half) + outer_half(high_half), axis=1).T
    grad_output = t.T
    pair_got, grad_inner, grad_outer, grad_output = tie((pair_got, grad_inner, grad_outer, grad_output))
    pair = (pair_keep + pair_got).reshape(rows, -1)
    c, e = pair[:, : 3 * width], pair[:, 3 * width :]
    small = e[:, 3 * width + 6 : 3 * width + 12]
    inner_two = e[:, 3 * width + 12 : 3 * width + 14]

    piece = lambda array, k: array[:, width * k : width * (k + 1)]
    grad_query_weight = jnp.stack([piece(c, 0), piece(c, 1), piece(c, 2), piece(e, 0)])
    biases = e[:per, 3 * width : 3 * width + 6].T
    return (
        layer_out[None],
        input_grad[None],
        grad_query_weight,
        biases[:4],
        piece(e, 1),
        biases[4],
        piece(e, 2),
        biases[5],
        grad_output,
        small[:, 0],
        small[:, 1],
        small[:, 2],
        grad_inner,
        inner_two.reshape(2 * rows),
        grad_outer,
        small[:, 3],
        small[:, 4],
        small[:, 5],
    )


def solution(mesh):
    return jax.shard_map(
        functools.partial(per_device, mesh.shape["dp"]),
        mesh=mesh,
        in_specs=(
            P("dp", None, None),
            P("dp"),
            P("dp", None),
            P(None, None, "tensor"),
            P(None, "tensor"),
            P(None, "tensor"),
            P("tensor"),
            P(None, "tensor"),
            P("tensor"),
            P("tensor", None),
            P(),
            P(),
            P(),
            P(None, "tensor"),
            P("tensor"),
            P("tensor", None),
            P(),
            P(),
            P(),
            P("dp", None, None),
        ),
        out_specs=(
            P("dp", None, None),
            P("dp", None, None),
            P(None, "dp", "tensor"),
            P(None, ("tensor", "dp")),
            P("dp", "tensor"),
            P(("tensor", "dp")),
            P("dp", "tensor"),
            P(("tensor", "dp")),
            P("tensor", "dp"),
            P("dp"),
            P("dp"),
            P("dp"),
            P("dp", "tensor"),
            P(("tensor", "dp")),
            P("tensor", "dp"),
            P("dp"),
            P("dp"),
            P("dp"),
        ),
        check_vma=False,
    )
```
